32 devices in a mesh: section: 2 (over core), ctx: 4 (over y, x), wt: 4 (over z).
Axes of the slice: x: 2, y: 2, z: 4, core: 2. Of those that a mesh axis runs over, the one named last changes fastest.
Arguments:
- block_input: bfloat16 [2, 4, 512, 1024], P(None, 'wt', 'ctx'), may hold values from -6 to 6
- output_grad: bfloat16 [2, 4, 512, 1024], P(None, 'wt', 'ctx'), may hold values from -6 to 6
- doc_lengths: int32 [2, 4, 8], P(None, 'wt'), may hold values from 1 to 256, 512 in all within a row
- first_gain: bfloat16 [2, 1024], P('section', 'wt'), may hold values from 0.5 to 1.5
- mixer_in: bfloat16 [2, 1024, 3352], P('section', 'wt'), may hold values from -0.1875 to 0.1875
- conv_kernel: bfloat16 [2, 4, 1792], P('section', None, 'wt'), may hold values from -3 to 3
- conv_bias: bfloat16 [2, 1792], P('section', 'wt'), may hold values from -3 to 3
- step_bias: float32 [2, 24], P('section'), may hold values from -3 to 0
- decay_log: float32 [2, 24], P('section'), may hold values from -6.9 to -1.9
- skip_gain: float32 [2, 24], P('section'), may hold values from -3 to 3
- mixer_out: bfloat16 [2, 1536, 1024], P('section', 'wt'), may hold values from -0.0390625 to 0.0390625
- attention_in: bfloat16 [2, 1024, 768], P('section', 'wt'), may hold values from -0.1875 to 0.1875
- attention_out: bfloat16 [2, 512, 1024], P('section', 'wt'), may hold values from -2 to 2
- second_gain: bfloat16 [2, 1024], P('section', 'wt'), may hold values from 0.5 to 1.5
- gate_up: bfloat16 [2, 1024, 4096], P('section', 'wt'), may hold values from -0.1875 to 0.1875
- down_weight: bfloat16 [2, 2048, 1024], P('section', 'wt'), may hold values from -0.125 to 0.125
Outputs:
- section_output: bfloat16 [2, 2, 4, 512, 1024], P('section', None, 'wt', 'ctx')
- input_grad: bfloat16 [2, 2, 4, 512, 1024], P('section', None, 'wt', 'ctx')
- first_gain_grad: float32 [2, 1024], P('section', 'wt')
- mixer_in_grad: float32 [2, 1024, 3352], P('section', 'wt')
- conv_kernel_grad: float32 [2, 4, 1792], P('section', None, 'wt')
- conv_bias_grad: float32 [2, 1792], P('section', 'wt')
- step_bias_grad: float32 [2, 24], P('section')
- decay_log_grad: float32 [2, 24], P('section')
- skip_gain_grad: float32 [2, 24], P('section')
- mixer_out_grad: float32 [2, 1536, 1024], P('section', 'wt')
- attention_in_grad: float32 [2, 1024, 768], P('section', 'wt')
- attention_out_grad: float32 [2, 512, 1024], P('section', 'wt')
- second_gain_grad: float32 [2, 1024], P('section', 'wt')
- gate_up_grad: float32 [2, 1024, 4096], P('section', 'wt')
- down_weight_grad: float32 [2, 2048, 1024], P('section', 'wt')
The draws below stay inside these ranges and needn't reach their ends.
Inputs may be any that keep to these rules, and one draw needn't show every extreme that they name: `doc_lengths`: each row holds the lengths of the 8 documents that fill one sequence of 512 tokens in order; one of them has exactly 256 tokens.
All inputs are finite; a program needn't handle non-finite values.
Results may differ from the reference program's by a relative error of at most 0.033.
Values may be sent and summed in bfloat16 or wider, within the bound.
No kernel may reach another device: no remote copies, remote signals or barrier semaphores. Data moves between devices by JAX's collectives and lax.ppermute only.
A program may use at most 320 MiB of HBM per device.

```python
import math
import jax
import jax.numpy as jnp
import numpy as np
from jax import lax

D = 1024
FF = 2048
MH = 24
MP = 64
NS = 128
QH = 8
KVH = 2
HD = 64
CONV = 4
MICRO = 2
DOCS = 8
SPAN = 128
QUERY_BLOCK = 512
DS = 1536
CONVD = 1792
INW = 3352
QD = 512
KVD = 128
QKVW = 768
LENGTH = 512
SEQS = 4
DOC_MOST = 256


def levels(key, extent, split, least, top_value):
    loudness = 1.0
    for axis_at, shards_of in split:
        draws = jax.random.uniform(jax.random.fold_in(jax.random.fold_in(key, 6), axis_at), (shards_of,), jnp.float32, least / len(split), top_value / len(split))
        loudness = loudness * jnp.repeat(jnp.exp(draws), extent[axis_at] // shards_of).reshape((-1,) + (1,) * (len(extent) - 1 - axis_at))
    return loudness


def length_profile(count, total, bound, lean):
    portions = [(1 << 20) // math.isqrt(rank ** lean) + 1 for rank in range(2, count + 1)]
    spare, counts = total - bound - (count - 1), [1] * (count - 1)
    while spare > 0:
        free = [i for i in range(count - 1) if counts[i] < bound]
        mass, remaining = sum([portions[i] for i in free]), spare
        for i in free:
            more = min(bound - counts[i], max(1, remaining * portions[i] // mass), spare)
            counts[i] = counts[i] + more
            spare = spare - more
    return np.array([bound] + counts)


def uneven_parts(key, count, total, most, lean):
    if count == 2:
        one = jax.random.randint(key, (), max(1, total - most), min(most, total - 1) + 1)
        return jnp.stack([one, total - one])
    sizes = jnp.asarray(length_profile(count, total, most, lean), jnp.int32)
    couples = (count - 1) // 2
    giver, taker = sizes[1:1 + 2 * couples:2], sizes[2:2 + 2 * couples:2]
    room = jnp.minimum(giver - 1, most - taker)
    moved = jax.random.randint(jax.random.fold_in(key, 1), (couples,), 0, 1 << 20) % (room + 1)
    sizes = sizes.at[1:1 + 2 * couples:2].set(giver - moved).at[2:2 + 2 * couples:2].set(taker + moved)
    return sizes[jax.random.permutation(jax.random.fold_in(key, 2), count)]


def scatter_about(own_key, shape, scale, reach, cuts=(), kind=jnp.bfloat16):
    level = levels(own_key, shape, cuts, -0.22, 0.18) if cuts else 1.0
    drawn = jax.random.normal(own_key, shape, jnp.float32) * scale * level
    return jnp.minimum(jnp.maximum(drawn, -reach), reach).astype(kind)


def setup_inputs(seed: int = 0) -> dict:
    streams_of = jax.random.split(jax.random.key(seed), 17)
    return {
        "block_input": scatter_about(streams_of[0], (MICRO, SEQS, LENGTH, D), 1.0, 6.0, ((1, 4), (2, 4))),
        "output_grad": scatter_about(streams_of[1], (MICRO, SEQS, LENGTH, D), 1.0, 6.0, ((1, 4), (2, 4))),
        "doc_lengths": jax.vmap(lambda own: uneven_parts(own, DOCS, LENGTH, DOC_MOST, 2))(jax.random.split(streams_of[2], MICRO * SEQS)).reshape((MICRO, SEQS, DOCS)).astype(jnp.int32),
        "first_gain": jnp.clip(1.0 + 0.1 * jax.random.normal(streams_of[3], (2, D), jnp.float32), 0.5, 1.5).astype(jnp.bfloat16),
        "mixer_in": scatter_about(streams_of[4], (2, D, INW), D ** -0.5, 0.1875, ((0, 2), (1, 4))),
        "conv_kernel": scatter_about(streams_of[5], (2, CONV, CONVD), CONV ** -0.5, 3.0, ((0, 2), (2, 4))),
        "conv_bias": scatter_about(streams_of[6], (2, CONVD), 0.5, 3.0, ((0, 2), (1, 4))),
        "step_bias": jnp.clip(-3.0 + 3.0 * jax.random.uniform(streams_of[7], (2, MH), jnp.float32) ** levels(streams_of[7], (2, MH), ((0, 2),), -0.2, 0.2), -3.0, 0.0),
        "decay_log": jnp.clip(-6.9 + 5 * jax.random.uniform(streams_of[8], (2, MH), jnp.float32) ** levels(streams_of[8], (2, MH), ((0, 2),), -0.2, 0.2), -6.9, -1.9),
        "skip_gain": scatter_about(streams_of[9], (2, MH), 1.0, 3.0, ((0, 2),), jnp.float32),
        "mixer_out": scatter_about(streams_of[10], (2, DS, D), (16 * DS) ** -0.5, 0.0390625, ((0, 2), (1, 4))),
        "attention_in": scatter_about(streams_of[11], (2, D, QKVW), D ** -0.5, 0.1875, ((0, 2), (1, 4))),
        "attention_out": scatter_about(streams_of[12], (2, QD, D), (QD // 64) ** -0.5, 2.0, ((0, 2), (1, 4))),
        "second_gain": jnp.clip(1.0 + 0.1 * jax.random.normal(streams_of[13], (2, D), jnp.float32), 0.5, 1.5).astype(jnp.bfloat16),
        "gate_up": scatter_about(streams_of[14], (2, D, 2 * FF), D ** -0.5, 0.1875, ((0, 2), (1, 4))),
        "down_weight": scatter_about(streams_of[15], (2, FF, D), FF ** -0.5, 0.125, ((0, 2), (1, 4))),
    }


epsilon = 1e-05
masked_value = -1e+30
highest = lax.Precision.HIGHEST

@jax.custom_vjp
def low(v):
    return lax.optimization_barrier(v.astype(jnp.bfloat16)).astype(jnp.float32)

@jax.custom_vjp
def low_back(v):
    return v

def low_keep(v):
    return (low(v), None)

def low_pass(kept, grad):
    return (grad,)

def back_keep(v):
    return (v, None)

def back_low(kept, grad):
    return (low(grad),)
low.defvjp(low_keep, low_pass)
low_back.defvjp(back_keep, back_low)

def matmul(left, right):
    return jnp.dot(left, right, precision=highest, preferred_element_type=jnp.float32)

def norm_apply(hidden_in, gain_vec):
    return hidden_in * lax.rsqrt(lax.optimization_barrier(jnp.mean(hidden_in * hidden_in, axis=-1, keepdims=True)) + epsilon) * gain_vec

def doc_layout(doc_sizes, positions):
    bounds = jnp.cumsum(doc_sizes).astype(jnp.int32)[:-1]
    doc_ids = lax.optimization_barrier(jnp.sum((positions[:, None] >= bounds[None, :]).astype(jnp.int32), axis=1))
    starts = jnp.any(positions[:, None] == bounds[None, :], axis=1)
    return (doc_ids, starts)

def conv_apply(extended, ext_ids, kernel, offset_vec):
    amount = extended.shape[0] - CONV + 1
    own_ids = ext_ids[CONV - 1:]
    summed = offset_vec[None, :] + jnp.zeros((amount, 1), extended.dtype)
    for tap_index in range(CONV):
        same_doc = (ext_ids[tap_index:tap_index + amount] == own_ids).astype(extended.dtype)
        summed = summed + kernel[tap_index][None, :] * extended[tap_index:tap_index + amount] * same_doc[:, None]
    return jax.nn.silu(summed)

def span_pass(carried_state, pieces):
    values, write_vec, read_vec, step_size, log_decay, doc_ids, before = pieces
    amount = values.shape[0]
    running = jnp.cumsum(log_decay, axis=0)
    row_ids = lax.broadcasted_iota(jnp.int32, (amount, amount), 0)
    col_ids = lax.broadcasted_iota(jnp.int32, (amount, amount), 1)
    allowed = (col_ids <= row_ids) & (doc_ids[:, None] == doc_ids[None, :])
    log_gap = jnp.where(allowed[:, :, None], running[:, None, :] - running[None, :, :], masked_value)
    intersection = jnp.einsum('in,jn->ij', read_vec, write_vec, precision=highest)
    mixing = intersection[:, :, None] * jnp.exp(log_gap) * step_size[None, :, :]
    within = jnp.einsum('ijh,jhp->ihp', mixing, values, precision=highest)
    inflow = jnp.exp(running) * (doc_ids == before)[:, None].astype(running.dtype)
    carried = jnp.einsum('in,hpn->ihp', read_vec, carried_state, precision=highest) * inflow[:, :, None]
    to_end = jnp.exp(running[-1][None, :] - running) * (doc_ids == doc_ids[-1])[:, None].astype(running.dtype) * step_size
    increment = jnp.einsum('jh,jhp,jn->hpn', to_end, values, write_vec, precision=highest)
    return (inflow[-1][:, None, None] * carried_state + increment, within + carried)

def mixer(projected, kernel, offset_vec, step_bias, decay_log, skip_gain, doc_ids, starts):
    length = projected.shape[0]
    gate_value = projected[:, :DS]
    extended = jnp.concatenate([jnp.zeros((CONV - 1, CONVD), projected.dtype), projected[:, DS:DS + CONVD]], axis=0)
    ext_ids = jnp.concatenate([jnp.full((CONV - 1,), -1, jnp.int32), doc_ids.astype(jnp.int32)])
    conv_out = conv_apply(extended, ext_ids, kernel, offset_vec)
    values = conv_out[:, :DS].reshape(length, MH, MP)
    step_size = jax.nn.softplus(projected[:, DS + CONVD:] + step_bias)
    log_decay = -step_size * jnp.exp(decay_log)
    blocks = length // SPAN
    pieces = (values.reshape(blocks, SPAN, MH, MP), conv_out[:, DS:DS + NS].reshape(blocks, SPAN, NS), conv_out[:, DS + NS:].reshape(blocks, SPAN, NS), step_size.reshape(blocks, SPAN, MH), log_decay.reshape(blocks, SPAN, MH), doc_ids.reshape(blocks, SPAN), doc_ids[::SPAN] - starts[::SPAN].astype(jnp.int32))
    initial = jnp.zeros((MH, MP, NS), projected.dtype)
    unused, outputs = lax.scan(jax.checkpoint(span_pass), initial, pieces)
    ssm_out = outputs.reshape(length, MH, MP) + skip_gain[None, :, None] * values
    return ssm_out.reshape(length, DS) * jax.nn.silu(gate_value)

def attend(heads_in, doc_ids):
    length = heads_in.shape[0]
    per_group = QH // KVH
    queries = heads_in[:, :QD].reshape(length, KVH, per_group, HD)
    key_part = heads_in[:, QD:QD + KVD].reshape(length, KVH, HD)
    value_part = heads_in[:, QD + KVD:].reshape(length, KVH, HD)
    positions = jnp.arange(length, dtype=jnp.int32)
    blocks = length // QUERY_BLOCK

    def block_pass(pieces):
        query_block, query_pos, query_ids = pieces
        scores = low_back(jnp.einsum('igjd,kgd->gjik', query_block, key_part, precision=highest) * 0.125)
        allowed = (positions[None, :] <= query_pos[:, None]) & (doc_ids[None, :] == query_ids[:, None])
        scores = jnp.where(allowed[None, None], scores, masked_value)
        chances = low(jax.nn.softmax(scores, axis=-1))
        return jnp.einsum('gjik,kgd->igjd', chances, value_part, precision=highest)
    outputs = lax.map(jax.checkpoint(block_pass), (queries.reshape(blocks, QUERY_BLOCK, KVH, per_group, HD), positions.reshape(blocks, QUERY_BLOCK), doc_ids.reshape(blocks, QUERY_BLOCK)))
    return outputs.reshape(length, QD)

def layer(hidden_in, weights, doc_ids, starts):
    normed = low(norm_apply(hidden_in, weights['first_gain']))
    projected = low_back(low(matmul(normed, weights['mixer_in'])))
    gated_out = low(mixer(projected, weights['conv_kernel'], weights['conv_bias'], weights['step_bias'], weights['decay_log'], weights['skip_gain'], doc_ids, starts))
    mixer_term = low_back(matmul(gated_out, weights['mixer_out']))
    heads_in = low_back(low(matmul(normed, weights['attention_in'])))
    attention_raw = low_back(low(attend(heads_in, doc_ids)))
    attention_term = low_back(matmul(attention_raw, weights['attention_out']))
    middle = hidden_in + mixer_term + attention_term
    normed_mid = low(norm_apply(middle, weights['second_gain']))
    expanded = low_back(matmul(normed_mid, weights['gate_up']))
    hidden = low(jax.nn.silu(expanded[:, :FF]) * expanded[:, FF:])
    return middle + low_back(matmul(hidden, weights['down_weight']))
weight_names = ('first_gain', 'mixer_in', 'conv_kernel', 'conv_bias', 'step_bias', 'decay_log', 'skip_gain', 'mixer_out', 'attention_in', 'attention_out', 'second_gain', 'gate_up', 'down_weight')

def reference(block_input, output_grad, doc_lengths, first_gain, mixer_in, conv_kernel, conv_bias, step_bias, decay_log, skip_gain, mixer_out, attention_in, attention_out, second_gain, gate_up, down_weight):
    arrays = (first_gain, mixer_in, conv_kernel, conv_bias, step_bias, decay_log, skip_gain, mixer_out, attention_in, attention_out, second_gain, gate_up, down_weight)
    sections = [dict(zip(weight_names, [array[section_index].astype(jnp.float32) for array in arrays])) for section_index in range(2)]
    positions = jnp.arange(LENGTH, dtype=jnp.int32)
    amount = MICRO * SEQS
    inputs = block_input.reshape(amount, LENGTH, D)
    cotangents = output_grad.reshape(amount, LENGTH, D)
    lengths = doc_lengths.reshape(amount, DOCS)
    zeros = (jax.tree.map(jnp.zeros_like, sections[0]), jax.tree.map(jnp.zeros_like, sections[1]))

    def sequence(carry, pieces):
        block_row, cotangent, doc_sizes = pieces
        doc_ids, starts = doc_layout(doc_sizes, positions)

        def apply_layer(hidden_in, weights):
            return layer(hidden_in, weights, doc_ids, starts)
        first_out, first_pull = jax.vjp(apply_layer, block_row.astype(jnp.float32), sections[0])
        middle = first_out.astype(jnp.bfloat16)
        second_out, second_pull = jax.vjp(apply_layer, middle.astype(jnp.float32), sections[1])
        middle_grad, second_grads = second_pull(cotangent.astype(jnp.float32))
        middle_low = middle_grad.astype(jnp.bfloat16)
        first_grad, first_grads = first_pull(middle_low.astype(jnp.float32))
        carry = (jax.tree.map(jnp.add, carry[0], first_grads), jax.tree.map(jnp.add, carry[1], second_grads))
        return (carry, (middle, second_out.astype(jnp.bfloat16), first_grad.astype(jnp.bfloat16), middle_low))
    totals, (middles, lasts, first_grads, second_grads) = lax.scan(sequence, zeros, (inputs, cotangents, lengths))
    layout = (MICRO, SEQS, LENGTH, D)
    section_output = jnp.stack([middles.reshape(layout), lasts.reshape(layout)])
    input_grad = jnp.stack([first_grads.reshape(layout), second_grads.reshape(layout)])
    summed = [jnp.stack([totals[0][name], totals[1][name]]) for name in weight_names]
    return (section_output, input_grad, summed[0], summed[1], summed[2], summed[3], summed[4], summed[5], summed[6], summed[7], summed[8], summed[9], summed[10], summed[11], summed[12])
```

```python
import math

import jax
import jax.numpy as jnp
from jax import lax
from jax.sharding import Mesh, PartitionSpec as P

D = 1024
FF = 2048
MH = 24
MP = 64
NS = 128
QH = 8
KVH = 2
HD = 64
CONV = 4
MICRO = 2
SPAN = 128
KEY_BLOCK = 1024
DS = 1536
CONVD = 1792
QD = 512
KVD = 128


epsilon = 1e-05
masked_value = -1e30
highest = lax.Precision.HIGHEST
weight_names = (
    "first_gain",
    "mixer_in",
    "conv_kernel",
    "conv_bias",
    "mixer_out",
    "attention_in",
    "attention_out",
    "second_gain",
    "gate_up",
    "down_weight",
)


def passed_along(value, axis, by):
    length = lax.axis_size(axis)
    pairs = [(i, i + by) for i in range(length) if 0 <= i + by < length]
    return lax.ppermute(value, axis, pairs)


def prefix(value, axis, combine, identity):
    length, position = (lax.axis_size(axis), lax.axis_index(axis))
    everything = jax.tree.map(
        lambda part, kind: lax.all_gather(part.astype(kind), axis),
        value,
        (jnp.bfloat16, jnp.bfloat16),
    )
    start = jax.tree.map(
        lambda part, zero: jnp.broadcast_to(jnp.asarray(zero, part.dtype), part.shape),
        value,
        identity,
    )

    def step(k, before):
        reached = k < position
        new = combine(
            before, jax.tree.map(lambda part, own: part[k].astype(own.dtype), everything, value)
        )
        return jax.tree.map(lambda a, b: jnp.where(reached, a, b), new, before)

    return lax.fori_loop(0, length, step, start)


def prefix_2(value, axis, join, neutral):
    count = lax.axis_size(axis)
    place = lax.axis_index(axis)
    ahead = count - 1 - place
    gathered = jax.tree.map(
        lambda a, kind: lax.all_gather(a.astype(kind), axis),
        value,
        jax.tree.map(lambda a: jnp.bfloat16 if a.dtype == jnp.float32 else a.dtype, value),
    )
    state = jax.tree.map(lambda a, e: jnp.zeros_like(a) + jnp.asarray(e, a.dtype), value, neutral)

    def one(step, state):
        source = count - 1 - step
        return join(
            state,
            jax.tree.map(
                lambda a, own: lax.dynamic_index_in_dim(a, source, 0, False).astype(own.dtype),
                gathered,
                value,
            ),
        )

    return lax.fori_loop(0, ahead, one, state)


def inner_rows(left, right):
    return lax.dot_general(
        left, right, (((0,), (0,)), ((), ())), preferred_element_type=jnp.float32
    )


def outer_cols(left, right):
    return lax.dot_general(
        left, right, (((1,), (1,)), ((), ())), preferred_element_type=jnp.float32
    )


def norm_apply(hidden_in, gain_vec):
    return (
        hidden_in
        * lax.rsqrt(jnp.mean(hidden_in * hidden_in, axis=-1, keepdims=True) + epsilon)
        * gain_vec
    )


def norm_back(hidden_in, gain_vec, upstream):
    scale = lax.rsqrt(jnp.mean(hidden_in * hidden_in, axis=-1, keepdims=True) + epsilon)
    normed = hidden_in * scale
    weighted = upstream * gain_vec
    hidden_grad = scale * (weighted - normed * jnp.mean(weighted * normed, axis=-1, keepdims=True))
    return (hidden_grad, jnp.sum(upstream * normed, axis=0))


def running_sum(value):
    count = value.shape[0]
    until = lax.broadcasted_iota(jnp.int32, (count, count), 0) >= lax.broadcasted_iota(
        jnp.int32, (count, count), 1
    )
    return jnp.dot(until.astype(jnp.float32), value, precision=highest)


def doc_layout(doc_sizes, positions):
    count = doc_sizes.shape[0]
    until = lax.broadcasted_iota(jnp.int32, (count, count), 0) >= lax.broadcasted_iota(
        jnp.int32, (count, count), 1
    )
    bounds = jnp.sum(jnp.where(until, doc_sizes[None, :], 0), axis=1)[:-1]
    doc_ids = jnp.sum((positions[:, None] >= bounds[None, :]).astype(jnp.int32), axis=1)
    starts = jnp.any(positions[:, None] == bounds[None, :], axis=1)
    return (doc_ids, starts)


def conv_apply(extended, ext_ids, kernel, offset_vec):
    amount = extended.shape[0] - CONV + 1
    own_ids = ext_ids[CONV - 1 :]
    summed = offset_vec[None, :] + jnp.zeros((amount, 1), extended.dtype)
    for tap_index in range(CONV):
        same_doc = (ext_ids[tap_index : tap_index + amount] == own_ids).astype(extended.dtype)
        summed = (
            summed
            + kernel[tap_index][None, :]
            * extended[tap_index : tap_index + amount]
            * same_doc[:, None]
        )
    return jax.nn.silu(summed)


def span_pass(carried_state, pieces):
    values, write_vec, read_vec, step_size, log_decay, doc_ids, before = pieces
    amount = values.shape[0]
    running = running_sum(log_decay)
    row_ids = lax.broadcasted_iota(jnp.int32, (amount, amount), 0)
    col_ids = lax.broadcasted_iota(jnp.int32, (amount, amount), 1)
    allowed = (col_ids <= row_ids) & (doc_ids[:, None] == doc_ids[None, :])
    log_gap = jnp.where(
        allowed[:, :, None], running[:, None, :] - running[None, :, :], masked_value
    )
    intersection = jnp.einsum("in,jn->ij", read_vec, write_vec, precision=highest)
    mixing = intersection[:, :, None] * jnp.exp(log_gap) * step_size[None, :, :]
    within = jnp.einsum("ijh,jhp->ihp", mixing, values, precision=highest)
    inflow = jnp.exp(running) * (doc_ids == before)[:, None].astype(jnp.float32)
    carried = (
        jnp.einsum("in,hpn->ihp", read_vec, carried_state, precision=highest) * inflow[:, :, None]
    )
    to_end = (
        jnp.exp(running[-1][None, :] - running)
        * (doc_ids == doc_ids[-1])[:, None].astype(jnp.float32)
        * step_size
    )
    increment = jnp.einsum("jh,jhp,jn->hpn", to_end, values, write_vec, precision=highest)
    return (inflow[-1][:, None, None] * carried_state + increment, within + carried)


def mixer_local(
    extended,
    raw_rate,
    kernel,
    offset_vec,
    step_bias,
    decay_log,
    skip_gain,
    state_in,
    ext_ids,
    doc_ids,
    starts,
):
    tokens = raw_rate.shape[0]
    conv_out = conv_apply(extended, ext_ids, kernel, offset_vec)
    values = conv_out[:, :DS].reshape(tokens, MH, MP)
    read_vector = conv_out[:, DS + NS :]
    step_size = jax.nn.softplus(raw_rate + step_bias)
    log_decay = -step_size * jnp.exp(decay_log)
    blocks = tokens // SPAN
    pieces = (
        values.reshape(blocks, SPAN, MH, MP),
        conv_out[:, DS : DS + NS].reshape(blocks, SPAN, NS),
        read_vector.reshape(blocks, SPAN, NS),
        step_size.reshape(blocks, SPAN, MH),
        log_decay.reshape(blocks, SPAN, MH),
        doc_ids.reshape(blocks, SPAN),
        doc_ids[::SPAN] - starts[::SPAN].astype(jnp.int32),
    )
    state_out, outputs = lax.scan(span_pass, state_in, pieces)
    result = outputs.reshape(tokens, MH, MP) + skip_gain[None, :, None] * values
    return ((result.reshape(tokens, DS), state_out), (read_vector, log_decay))


def device_inflow(log_decay, doc_ids, starts):
    same_doc = (doc_ids == doc_ids[0] - starts[0].astype(jnp.int32)).astype(jnp.float32)
    return jnp.exp(running_sum(log_decay)) * same_doc[:, None]


def chain_affine(earlier, later):
    return (earlier[0] * later[0], later[0][:, None, None] * earlier[1] + later[1])


def query_groups(flat):
    tokens = flat.shape[0]
    per_group = QH // KVH
    return (
        flat.reshape(tokens, KVH, per_group, HD)
        .transpose(1, 2, 0, 3)
        .reshape(KVH, per_group * tokens, HD)
    )


def query_flat(grouped, tokens):
    per_group = QH // KVH
    return grouped.reshape(KVH, per_group, tokens, HD).transpose(2, 0, 1, 3).reshape(tokens, QD)


def score_block(queries, key_rows, query_pos, query_ids, all_ids, offset, block_len):
    key_block = lax.dynamic_slice_in_dim(key_rows, offset, block_len, 0)
    key_part = key_block[:, :KVD].reshape(block_len, KVH, HD)
    value_part = key_block[:, KVD:].reshape(block_len, KVH, HD)
    key_pos = offset + jnp.arange(block_len, dtype=jnp.int32)
    key_ids = lax.dynamic_slice_in_dim(all_ids, offset, block_len, 0)
    allowed = (key_pos[None, :] <= query_pos[:, None]) & (key_ids[None, :] == query_ids[:, None])
    scores = (
        jnp.einsum("grd,kgd->grk", queries, key_part, preferred_element_type=jnp.float32) * 0.125
    )
    return (jnp.where(allowed[None], scores, masked_value), allowed, key_part, value_part)


def attend_forward(queries_flat, key_rows, positions, doc_ids, all_ids, ctx_index):
    tokens = queries_flat.shape[0]
    per_group = QH // KVH
    queries = query_groups(queries_flat)
    query_pos = jnp.tile(positions, per_group)
    query_ids = jnp.tile(doc_ids, per_group)
    block_len = math.gcd(key_rows.shape[0], KEY_BLOCK)
    block_count = ((ctx_index + 1) * tokens + block_len - 1) // block_len

    def visit_block(block_index, carry):
        running_max, running_sum, accumulated = carry
        scores, allowed, key_part, value_part = score_block(
            queries, key_rows, query_pos, query_ids, all_ids, block_index * block_len, block_len
        )
        new_max = jnp.maximum(running_max, jnp.max(scores, axis=-1))
        chances = jnp.where(allowed[None], jnp.exp(scores - new_max[..., None]), 0.0)
        rescale = jnp.exp(running_max - new_max)
        running_sum = running_sum * rescale + jnp.sum(chances, axis=-1)
        accumulated = accumulated * rescale[..., None] + jnp.einsum(
            "grk,kgd->grd",
            chances.astype(jnp.bfloat16),
            value_part,
            preferred_element_type=jnp.float32,
        )
        return (new_max, running_sum, accumulated)

    row_count = per_group * tokens
    start_carry = (
        jnp.full((KVH, row_count), masked_value, jnp.float32),
        jnp.zeros((KVH, row_count), jnp.float32),
        jnp.zeros((KVH, row_count, HD), jnp.float32),
    )
    running_max, running_sum, accumulated = lax.fori_loop(0, block_count, visit_block, start_carry)
    output = accumulated / running_sum[..., None]
    return (query_flat(output, tokens), running_max + jnp.log(running_sum))


def attend_backward(
    queries_flat,
    key_rows,
    attention_raw,
    log_norm,
    grad_low,
    positions,
    doc_ids,
    all_ids,
    ctx_index,
):
    tokens = queries_flat.shape[0]
    length = key_rows.shape[0]
    per_group = QH // KVH
    queries = query_groups(queries_flat)
    grad_rows = query_groups(grad_low)
    grad_wide = grad_rows.astype(jnp.float32)
    delta = jnp.sum(grad_wide * query_groups(attention_raw), axis=-1)
    query_pos = jnp.tile(positions, per_group)
    query_ids = jnp.tile(doc_ids, per_group)
    block_len = math.gcd(length, KEY_BLOCK)
    block_count = ((ctx_index + 1) * tokens + block_len - 1) // block_len

    def visit_block(block_index, carry):
        query_grad, key_grad, value_grad = carry
        offset = block_index * block_len
        scores, allowed, key_part, value_part = score_block(
            queries, key_rows, query_pos, query_ids, all_ids, offset, block_len
        )
        chances = jnp.where(allowed[None], jnp.exp(scores - log_norm[..., None]), 0.0)
        prob_grad = jnp.einsum(
            "grd,kgd->grk", grad_rows, value_part, preferred_element_type=jnp.float32
        )
        score_grad = (chances * (prob_grad - delta[..., None])).astype(jnp.bfloat16)
        query_grad = query_grad + jnp.einsum(
            "grk,kgd->grd", score_grad, key_part, preferred_element_type=jnp.float32
        )
        key_piece = (
            jnp.einsum("grk,grd->kgd", score_grad, queries, preferred_element_type=jnp.float32)
            * 0.125
        )
        value_piece = jnp.einsum(
            "grk,grd->kgd",
            chances.astype(jnp.bfloat16),
            grad_rows,
            preferred_element_type=jnp.float32,
        )
        key_grad = lax.dynamic_update_slice_in_dim(
            key_grad,
            lax.dynamic_slice_in_dim(key_grad, offset, block_len, 0)
            + key_piece.reshape(block_len, KVD),
            offset,
            0,
        )
        value_grad = lax.dynamic_update_slice_in_dim(
            value_grad,
            lax.dynamic_slice_in_dim(value_grad, offset, block_len, 0)
            + value_piece.reshape(block_len, KVD),
            offset,
            0,
        )
        return (query_grad, key_grad, value_grad)

    start_carry = (
        jnp.zeros((KVH, per_group * tokens, HD), jnp.float32),
        jnp.zeros((length, KVD), jnp.float32),
        jnp.zeros((length, KVD), jnp.float32),
    )
    query_grad, key_grad, value_grad = lax.fori_loop(0, block_count, visit_block, start_carry)
    return (query_flat(query_grad * 0.125, tokens), key_grad, value_grad)


def layer_layout(doc_sizes, tokens, ctx_index, ctx_count):
    positions = ctx_index * tokens + jnp.arange(tokens, dtype=jnp.int32)
    doc_ids, starts = doc_layout(doc_sizes, positions)
    all_ids = doc_layout(doc_sizes, jnp.arange(tokens * ctx_count, dtype=jnp.int32))[0]
    ext_ids = doc_layout(
        doc_sizes, ctx_index * tokens - (CONV - 1) + jnp.arange(tokens + CONV - 1, dtype=jnp.int32)
    )[0]
    return (positions, doc_ids, starts, all_ids, ext_ids)


def layer_forward(hidden_in, weights_full, head_params, doc_sizes, ctx_index, ctx_count):
    tokens = hidden_in.shape[0]
    positions, doc_ids, starts, all_ids, ext_ids = layer_layout(
        doc_sizes, tokens, ctx_index, ctx_count
    )
    normed = norm_apply(hidden_in, weights_full["first_gain"].astype(jnp.float32)).astype(
        jnp.bfloat16
    )
    projected = jnp.dot(
        normed, weights_full["mixer_in"], preferred_element_type=jnp.float32
    ).astype(jnp.bfloat16)
    edge_rows = passed_along(projected[tokens - (CONV - 1) :, DS : DS + CONVD], "ctx", 1)
    extended = jnp.concatenate([edge_rows, projected[:, DS : DS + CONVD]], axis=0).astype(
        jnp.float32
    )
    raw_rate = projected[:, DS + CONVD :].astype(jnp.float32)
    step_bias, decay_log, skip_gain = head_params
    empty_state = jnp.zeros((MH, MP, NS), jnp.float32)
    (partial_out, local_state), (read_vector, log_decay) = mixer_local(
        extended,
        raw_rate,
        weights_full["conv_kernel"].astype(jnp.float32),
        weights_full["conv_bias"].astype(jnp.float32),
        step_bias,
        decay_log,
        skip_gain,
        empty_state,
        ext_ids,
        doc_ids,
        starts,
    )
    inflow = device_inflow(log_decay, doc_ids, starts)
    state_in = prefix(
        (inflow[-1], local_state), "ctx", chain_affine, (jnp.ones((MH,), jnp.float32), empty_state)
    )[1]
    carried = (
        jnp.einsum("tn,hpn->thp", read_vector, state_in, precision=highest) * inflow[:, :, None]
    )
    ssm_out = partial_out + carried.reshape(tokens, DS)
    gate_value = projected[:, :DS].astype(jnp.float32)
    gated_out = (ssm_out * jax.nn.silu(gate_value)).astype(jnp.bfloat16)
    mixer_term = jnp.dot(gated_out, weights_full["mixer_out"], preferred_element_type=jnp.float32)
    heads_in = jnp.dot(
        normed, weights_full["attention_in"], preferred_element_type=jnp.float32
    ).astype(jnp.bfloat16)
    key_rows = lax.all_gather(heads_in[:, QD:], "ctx", axis=0, tiled=True)
    attention_raw, log_norm = attend_forward(
        heads_in[:, :QD], key_rows, positions, doc_ids, all_ids, ctx_index
    )
    attention_term = jnp.dot(
        attention_raw.astype(jnp.bfloat16),
        weights_full["attention_out"],
        preferred_element_type=jnp.float32,
    )
    middle = hidden_in + mixer_term + attention_term
    normed_mid = norm_apply(middle, weights_full["second_gain"].astype(jnp.float32)).astype(
        jnp.bfloat16
    )
    expanded = jnp.dot(normed_mid, weights_full["gate_up"], preferred_element_type=jnp.float32)
    hidden = (jax.nn.silu(expanded[:, :FF]) * expanded[:, FF:]).astype(jnp.bfloat16)
    result = middle + jnp.dot(
        hidden, weights_full["down_weight"], preferred_element_type=jnp.float32
    )
    stored = (
        hidden_in,
        middle,
        projected,
        edge_rows,
        state_in,
        ssm_out,
        heads_in,
        key_rows,
        attention_raw,
        log_norm,
        expanded,
    )
    return (result, stored)


def layer_backward(grad_in, stored, weights_full, head_params, doc_sizes, ctx_index, ctx_count):
    (
        hidden_in,
        middle,
        projected,
        edge_rows,
        state_in,
        ssm_out,
        heads_in,
        key_rows,
        attention_raw,
        log_norm,
        expanded,
    ) = stored
    tokens = hidden_in.shape[0]
    positions, doc_ids, starts, all_ids, ext_ids = layer_layout(
        doc_sizes, tokens, ctx_index, ctx_count
    )
    first_gain = weights_full["first_gain"].astype(jnp.float32)
    second_gain = weights_full["second_gain"].astype(jnp.float32)
    down_low = grad_in.astype(jnp.bfloat16)
    gate_vals = expanded[:, :FF]
    up_vals = expanded[:, FF:]
    gate_sig = jax.nn.sigmoid(gate_vals)
    hidden = (jax.nn.silu(gate_vals) * up_vals).astype(jnp.bfloat16)
    down_weight_grad = inner_rows(hidden, down_low)
    hidden_grad = outer_cols(down_low, weights_full["down_weight"])
    slope = gate_sig * (1.0 + gate_vals * (1.0 - gate_sig))
    expand_grad = jnp.concatenate(
        [hidden_grad * up_vals * slope, hidden_grad * jax.nn.silu(gate_vals)], axis=1
    ).astype(jnp.bfloat16)
    normed_mid = norm_apply(middle, second_gain).astype(jnp.bfloat16)
    gate_up_grad = inner_rows(normed_mid, expand_grad)
    mid_norm_grad, second_gain_grad = norm_back(
        middle, second_gain, outer_cols(expand_grad, weights_full["gate_up"])
    )
    middle_grad = grad_in + mid_norm_grad
    residual_low = middle_grad.astype(jnp.bfloat16)
    attention_out_grad = inner_rows(attention_raw.astype(jnp.bfloat16), residual_low)
    output_low = outer_cols(residual_low, weights_full["attention_out"]).astype(jnp.bfloat16)
    query_grad, key_grad, value_grad = attend_backward(
        heads_in[:, :QD],
        key_rows,
        attention_raw,
        log_norm,
        output_low,
        positions,
        doc_ids,
        all_ids,
        ctx_index,
    )
    key_share, value_share = (
        lax.psum_scatter(
            key_grad.astype(jnp.bfloat16), "ctx", scatter_dimension=0, tiled=True
        ).astype(jnp.float32),
        lax.psum_scatter(
            value_grad.astype(jnp.bfloat16), "ctx", scatter_dimension=0, tiled=True
        ).astype(jnp.float32),
    )
    heads_grad = jnp.concatenate([query_grad, key_share, value_share], axis=1).astype(jnp.bfloat16)
    gate_value = projected[:, :DS].astype(jnp.float32)
    gate_sig_z = jax.nn.sigmoid(gate_value)
    gated_out = (ssm_out * jax.nn.silu(gate_value)).astype(jnp.bfloat16)
    mixer_out_grad = inner_rows(gated_out, residual_low)
    gated_grad = outer_cols(residual_low, weights_full["mixer_out"])
    ssm_grad = gated_grad * jax.nn.silu(gate_value)
    gate_grad = gated_grad * ssm_out * gate_sig_z * (1.0 + gate_value * (1.0 - gate_sig_z))
    extended = jnp.concatenate([edge_rows, projected[:, DS : DS + CONVD]], axis=0).astype(
        jnp.float32
    )
    raw_rate = projected[:, DS + CONVD :].astype(jnp.float32)
    step_bias, decay_log, skip_gain = head_params

    def local_piece(
        extended, raw_rate, kernel, offset_vec, step_bias, decay_log, skip_gain, state_in
    ):
        return mixer_local(
            extended,
            raw_rate,
            kernel,
            offset_vec,
            step_bias,
            decay_log,
            skip_gain,
            state_in,
            ext_ids,
            doc_ids,
            starts,
        )

    primal, pullback, (read_vector, log_decay) = jax.vjp(
        local_piece,
        extended,
        raw_rate,
        weights_full["conv_kernel"].astype(jnp.float32),
        weights_full["conv_bias"].astype(jnp.float32),
        step_bias,
        decay_log,
        skip_gain,
        state_in,
        has_aux=True,
    )
    inflow = device_inflow(log_decay, doc_ids, starts)
    local_grad = jnp.einsum(
        "th,thp,tn->hpn", inflow, ssm_grad.reshape(tokens, MH, MP), read_vector, precision=highest
    )
    state_back = prefix_2(
        (inflow[-1], local_grad),
        "ctx",
        chain_affine,
        (jnp.ones((MH,), jnp.float32), jnp.zeros((MH, MP, NS), jnp.float32)),
    )[1]
    ext_grad, raw_grad, kernel_grad, offset_grad, step_grad, decay_grad, skip_grad, unused = (
        pullback((ssm_grad, state_back))
    )
    rim_grad = passed_along(ext_grad[: CONV - 1], "ctx", -1)
    pre_grad = ext_grad[CONV - 1 :]
    pre_grad = jnp.concatenate(
        [pre_grad[: tokens - (CONV - 1)], pre_grad[tokens - (CONV - 1) :] + rim_grad], axis=0
    )
    mixer_grad = jnp.concatenate([gate_grad, pre_grad, raw_grad], axis=1).astype(jnp.bfloat16)
    normed = norm_apply(hidden_in, first_gain).astype(jnp.bfloat16)
    mixer_in_grad = inner_rows(normed, mixer_grad)
    attention_in_grad = inner_rows(normed, heads_grad)
    normed_grad = outer_cols(mixer_grad, weights_full["mixer_in"]) + outer_cols(
        heads_grad, weights_full["attention_in"]
    )
    in_norm_grad, first_gain_grad = norm_back(hidden_in, first_gain, normed_grad)
    block_grad = middle_grad + in_norm_grad
    weight_grads = (
        first_gain_grad,
        mixer_in_grad,
        kernel_grad,
        offset_grad,
        mixer_out_grad,
        attention_in_grad,
        attention_out_grad,
        second_gain_grad,
        gate_up_grad,
        down_weight_grad,
    )
    return (block_grad, weight_grads, (step_grad, decay_grad, skip_grad))


def local(
    block_input,
    output_grad,
    doc_lengths,
    first_gain,
    mixer_in,
    conv_kernel,
    conv_bias,
    step_bias,
    decay_log,
    skip_gain,
    mixer_out,
    attention_in,
    attention_out,
    second_gain,
    gate_up,
    down_weight,
):
    gathered = (
        lax.all_gather(first_gain[0], "wt", axis=0, tiled=True),
        lax.all_gather(mixer_in[0], "wt", axis=0, tiled=True),
        lax.all_gather(conv_kernel[0], "wt", axis=1, tiled=True),
        lax.all_gather(conv_bias[0], "wt", axis=0, tiled=True),
        lax.all_gather(mixer_out[0], "wt", axis=0, tiled=True),
        lax.all_gather(attention_in[0], "wt", axis=0, tiled=True),
        lax.all_gather(attention_out[0], "wt", axis=0, tiled=True),
        lax.all_gather(second_gain[0], "wt", axis=0, tiled=True),
        lax.all_gather(gate_up[0], "wt", axis=0, tiled=True),
        lax.all_gather(down_weight[0], "wt", axis=0, tiled=True),
    )
    weights_full = dict(zip(weight_names, gathered))
    head_params = (step_bias[0], decay_log[0], skip_gain[0])
    head_section = lax.axis_index("section") == 0
    ctx_index = lax.axis_index("ctx")
    ctx_count = lax.axis_size("ctx")
    tokens = block_input.shape[2]
    received = jnp.zeros((tokens, D), jnp.bfloat16)
    results = []
    stored_list = []
    for moment in range(MICRO + 1):
        own_block = block_input[min(moment, MICRO - 1), 0].astype(jnp.float32)
        entry = jnp.where(head_section, own_block, received.astype(jnp.float32))
        doc_sizes = jnp.where(
            head_section, doc_lengths[min(moment, MICRO - 1), 0], doc_lengths[max(moment - 1, 0), 0]
        )
        layer_result, stored = layer_forward(
            entry, weights_full, head_params, doc_sizes, ctx_index, ctx_count
        )
        sent = layer_result.astype(jnp.bfloat16)
        results.append(sent)
        stored_list.append((stored, doc_sizes))
        if moment < MICRO:
            received = passed_along(sent, "section", 1)
    back_received = jnp.zeros((tokens, D), jnp.bfloat16)
    total_grads = tuple((jnp.zeros(weight_full.shape, jnp.float32) for weight_full in gathered))
    total_heads = tuple((jnp.zeros(param_vec.shape, jnp.float32) for param_vec in head_params))
    sent_grads = []
    for moment in range(MICRO + 1):
        given_grad = output_grad[min(moment, MICRO - 1), 0].astype(jnp.float32)
        cotangent = jnp.where(head_section, back_received.astype(jnp.float32), given_grad)
        chosen = jax.tree.map(
            lambda left, right: jnp.where(head_section, left, right),
            stored_list[max(moment - 1, 0)],
            stored_list[min(moment + 1, MICRO)],
        )
        valid = jnp.where(head_section, moment >= 1, moment < MICRO)
        stored, doc_sizes = chosen
        block_grad, weight_grads, head_grads = layer_backward(
            cotangent, stored, weights_full, head_params, doc_sizes, ctx_index, ctx_count
        )
        total_grads = tuple(
            (old + jnp.where(valid, new, 0.0) for old, new in zip(total_grads, weight_grads))
        )
        total_heads = tuple(
            (old + jnp.where(valid, new, 0.0) for old, new in zip(total_heads, head_grads))
        )
        sent = block_grad.astype(jnp.bfloat16)
        sent_grads.append(sent)
        if moment < MICRO:
            back_received = passed_along(sent, "section", -1)
    section_output = jnp.stack(
        [
            jnp.where(head_section, results[batch_index], results[batch_index + 1])
            for batch_index in range(MICRO)
        ]
    ).reshape(1, MICRO, 1, tokens, D)
    input_grad = jnp.stack(
        [
            jnp.where(head_section, sent_grads[batch_index + 1], sent_grads[batch_index])
            for batch_index in range(MICRO)
        ]
    ).reshape(1, MICRO, 1, tokens, D)
    shares = (
        lax.psum_scatter(
            total_grads[0].astype(jnp.bfloat16), "wt", scatter_dimension=0, tiled=True
        ).astype(jnp.float32),
        lax.psum_scatter(
            total_grads[1].astype(jnp.bfloat16), "wt", scatter_dimension=0, tiled=True
        ).astype(jnp.float32),
        lax.psum_scatter(
            total_grads[2].astype(jnp.bfloat16), "wt", scatter_dimension=1, tiled=True
        ).astype(jnp.float32),
        lax.psum_scatter(
            total_grads[3].astype(jnp.bfloat16), "wt", scatter_dimension=0, tiled=True
        ).astype(jnp.float32),
        lax.psum_scatter(
            total_grads[4].astype(jnp.bfloat16), "wt", scatter_dimension=0, tiled=True
        ).astype(jnp.float32),
        lax.psum_scatter(
            total_grads[5].astype(jnp.bfloat16), "wt", scatter_dimension=0, tiled=True
        ).astype(jnp.float32),
        lax.psum_scatter(
            total_grads[6].astype(jnp.bfloat16), "wt", scatter_dimension=0, tiled=True
        ).astype(jnp.float32),
        lax.psum_scatter(
            total_grads[7].astype(jnp.bfloat16), "wt", scatter_dimension=0, tiled=True
        ).astype(jnp.float32),
        lax.psum_scatter(
            total_grads[8].astype(jnp.bfloat16), "wt", scatter_dimension=0, tiled=True
        ).astype(jnp.float32),
        lax.psum_scatter(
            total_grads[9].astype(jnp.bfloat16), "wt", scatter_dimension=0, tiled=True
        ).astype(jnp.float32),
    )
    reduced = (
        lax.psum(shares[0].astype(jnp.bfloat16), "ctx").astype(jnp.float32),
        lax.psum(shares[1].astype(jnp.bfloat16), "ctx").astype(jnp.float32),
        lax.psum(shares[2].astype(jnp.bfloat16), "ctx").astype(jnp.float32),
        lax.psum(shares[3].astype(jnp.bfloat16), "ctx").astype(jnp.float32),
        lax.psum(shares[4].astype(jnp.bfloat16), "ctx").astype(jnp.float32),
        lax.psum(shares[5].astype(jnp.bfloat16), "ctx").astype(jnp.float32),
        lax.psum(shares[6].astype(jnp.bfloat16), "ctx").astype(jnp.float32),
        lax.psum(shares[7].astype(jnp.bfloat16), "ctx").astype(jnp.float32),
        lax.psum(shares[8].astype(jnp.bfloat16), "ctx").astype(jnp.float32),
        lax.psum(shares[9].astype(jnp.bfloat16), "ctx").astype(jnp.float32),
    )
    head_sums = lax.psum((total_heads[0], total_heads[1], total_heads[2]), ("ctx", "wt"))
    return (
        section_output,
        input_grad,
        reduced[0][None],
        reduced[1][None],
        reduced[2][None],
        reduced[3][None],
        head_sums[0][None],
        head_sums[1][None],
        head_sums[2][None],
        reduced[4][None],
        reduced[5][None],
        reduced[6][None],
        reduced[7][None],
        reduced[8][None],
        reduced[9][None],
    )


def spread(mesh):
    placed = (
        P(None, "wt", "ctx", None),
        P(None, "wt", "ctx", None),
        P(None, "wt", None),
        P("section", "wt"),
        P("section", "wt", None),
        P("section", None, "wt"),
        P("section", "wt"),
        P("section", None),
        P("section", None),
        P("section", None),
        P("section", "wt", None),
        P("section", "wt", None),
        P("section", "wt", None),
        P("section", "wt"),
        P("section", "wt", None),
        P("section", "wt", None),
    )
    return jax.shard_map(
        local,
        mesh=mesh,
        in_specs=placed,
        out_specs=(
            P("section", None, "wt", "ctx", None),
            P("section", None, "wt", "ctx", None),
            P("section", "wt"),
            P("section", "wt", None),
            P("section", None, "wt"),
            P("section", "wt"),
            P("section", None),
            P("section", None),
            P("section", None),
            P("section", "wt", None),
            P("section", "wt", None),
            P("section", "wt", None),
            P("section", "wt"),
            P("section", "wt", None),
            P("section", "wt", None),
        ),
        check_vma=False,
    )


TP = 4
RH = MH // TP
RD = DS // TP
RQ = QD // TP
RF = FF // TP
TAIL = 2 * NS + 128
INC = 2 * RD + TAIL + RQ + 2 * KVD
RAW_AT = 2 * RD + 2 * NS
Q_AT = 2 * RD + TAIL
OUTR = RD + RQ
AXES = ("core", "y", "x", "z")
f32, bf16 = jnp.float32, jnp.bfloat16


def swapped(value, axis):
    return lax.ppermute(value, axis, [(0, 1), (1, 0)])


def across(value):
    return lax.ppermute(value, ("y", "x"), [(0, 3), (1, 2), (2, 1), (3, 0)])


def turned(value, by):
    return lax.ppermute(value, "z", [(i, (i + by) % 4) for i in range(4)])


def place(core, y, x, z):
    return ((core * 2 + y) * 2 + x) * 4 + z


def sent(value, pairs):
    return lax.ppermute(value, AXES, [(place(*a), place(*b)) for a, b in pairs])


every = [(c, y, x, z) for c in range(2) for y in range(2) for x in range(2) for z in range(4)]


def ordered(flag, own, other):
    return jnp.where(flag == 0, jnp.stack([own, other]), jnp.stack([other, own]))


def whole_rows(pair, y, x):
    own = lax.dynamic_index_in_dim(pair, y, 0, False)
    other = lax.dynamic_index_in_dim(pair, 1 - y, 0, False)
    near = ordered(x, own, swapped(own, "x"))
    far = ordered(x, swapped(other, "y"), across(other))
    return ordered(y, near, far).reshape(4 * own.shape[0], own.shape[1])


def back_rows(rows, y, x):
    blocks = rows.reshape(2, 2, rows.shape[0] // 4, rows.shape[1])
    own = blocks[y, x]
    other = swapped(blocks[1 - y, x], "y")
    return ordered(y, own, other)


def quarter_sum(part, c):
    half = part.shape[0] // 2
    mine = lax.dynamic_slice_in_dim(part, c * half, half, 0)
    theirs = lax.dynamic_slice_in_dim(part, (1 - c) * half, half, 0)
    low = (mine + swapped(theirs.astype(bf16), "core").astype(f32)).astype(bf16)
    both = (low.astype(f32) + swapped(low, "x").astype(f32)).astype(bf16)
    return ordered(c, both, swapped(both, "core")).reshape(part.shape)


def rank_cut(mixer_in, attention_in, gate_up, down, rank):
    cut = lax.dynamic_slice_in_dim
    columns = jnp.concatenate(
        [
            cut(mixer_in, rank * RD, RD, 1),
            cut(mixer_in, DS + rank * RD, RD, 1),
            jnp.pad(mixer_in[:, 2 * DS :], ((0, 0), (0, TAIL - 2 * NS - MH))),
            cut(attention_in, rank * RQ, RQ, 1),
            attention_in[:, QD:],
        ],
        axis=1,
    )
    hidden = jnp.concatenate(
        [cut(gate_up, h * FF + g * RF + rank * 128, 128, 1) for h in range(2) for g in range(4)], axis=1
    )
    return columns, hidden, cut(down, rank * 128, 128, 0)


def gathered_rows(own, y, z):
    half = lax.dynamic_index_in_dim(own, y, 0, False)
    got = [turned(half, k) for k in (1, 2, 3)]
    pairs = [own] + [ordered(y, g, swapped(g, "y")) for g in got]
    rows = jnp.zeros((4,) + own.shape, own.dtype)
    for k, pair in enumerate(pairs):
        rows = lax.dynamic_update_index_in_dim(rows, pair, (z - k) % 4, 0)
    return rows.reshape(8 * own.shape[1], own.shape[2])


def bring_weights(mixer_in, attention_in, gate_up, down, mixer_out, attention_out, c, y, x, z):
    keep = rank_cut(mixer_in, attention_in, gate_up, down, 2 * c + x)
    give = rank_cut(mixer_in, attention_in, gate_up, down, 2 * (1 - c) + x)
    take = [swapped(g, "core") for g in give]
    outer = jnp.concatenate([mixer_out, attention_out], axis=0)
    out_take = sent(
        outer, [((1 - b // 2, y_, b % 2, b), (b // 2, y_, b % 2, b)) for y_ in range(2) for b in range(4)]
    )
    rank = 2 * c + x
    sections = []
    for s in range(2):
        mine = c == s
        inner, hidden, down_rows = [jnp.where(mine, k, t) for k, t in zip(keep, take)]
        out_own = jnp.where(mine, outer, out_take)
        wi = gathered_rows(inner.reshape(2, 128, INC), y, z)
        wgu = gathered_rows(hidden.reshape(2, 128, 2 * RF), y, z)
        wd = gathered_rows(down_rows.reshape(2, 64, D), y, z)
        half = lax.dynamic_slice_in_dim(out_own, y * (OUTR // 2), OUTR // 2, 0)
        arrived = sum(
            sent(half, [(p, p[:3] + ((p[3] + k) % 4,)) for p in every if p[3] == 2 * p[0] + p[2]])
            for k in (1, 2, 3)
        )
        pair = ordered(y, arrived, swapped(arrived, "y")).reshape(OUTR, D)
        wo = jnp.where(z == rank, out_own, pair)
        sections.append((wi, wgu, wd, wo[:RD], wo[RD:]))
    return sections


def rolled(value, by):
    return jnp.roll(value, by, axis=0)


def heads_apart(flat, count):
    return flat.reshape(flat.shape[0], count, flat.shape[1] // count).transpose(1, 0, 2)


def heads_joined(apart):
    return apart.transpose(1, 0, 2).reshape(apart.shape[1], -1)


def silu_slope(value, sig):
    return sig * (1.0 + value * (1.0 - sig))


def mixer_values(proj, small, taps):
    pre = proj[:, RD : 2 * RD + 2 * NS].astype(f32)
    summed = small["conv_bias"] + pre * small["conv_kernel"][CONV - 1 :]
    for by in range(1, CONV):
        summed = summed + small["conv_kernel"][CONV - 1 - by : CONV - by] * rolled(pre, by) * taps[by]
    return pre, summed


def layer_first(x, small, w, masks, rank):
    wi, wgu, wd, wmo, wao = w
    same, causal, taps = masks
    allowed = same & causal
    scale = lax.rsqrt(jnp.mean(x * x, axis=-1, keepdims=True) + epsilon)
    h1 = (x * scale * small["first_gain"]).astype(bf16)
    proj = jnp.dot(h1, wi, preferred_element_type=f32).astype(bf16)
    pre, summed = mixer_values(proj, small, taps)
    conv = jax.nn.silu(summed)
    vals = heads_apart(conv[:, :RD], RH)
    raw = lax.dynamic_slice_in_dim(proj[:, RAW_AT : RAW_AT + 128].astype(f32), rank * RH, RH, 1)
    dt = jax.nn.softplus(raw + small["step_bias"])
    rate = -dt * jnp.exp(small["decay_log"])
    run = running_sum(rate)
    gram = outer_cols(conv[:, RD + NS :].astype(bf16), conv[:, RD : RD + NS].astype(bf16))
    gap = run.T[:, :, None] - run.T[:, None, :]
    decay = jnp.exp(jnp.where(allowed[None], gap, masked_value))
    mixing = (gram[None] * decay).astype(bf16)
    fed = (vals * dt.T[:, :, None]).astype(bf16)
    state_out = jnp.einsum("hij,hjp->hip", mixing, fed, preferred_element_type=f32)
    ssm = heads_joined(state_out + small["skip_gain"][:, None, None] * vals)
    z_value = proj[:, :RD].astype(f32)
    gated = (ssm * jax.nn.silu(z_value)).astype(bf16)
    queries = heads_apart(proj[:, Q_AT : Q_AT + RQ], 2)
    kv = proj[:, Q_AT + RQ :]
    group = rank // 2
    keys = jnp.where(group == 0, kv[:, :HD], kv[:, HD : 2 * HD])
    values = jnp.where(group == 0, kv[:, 2 * HD : 3 * HD], kv[:, 3 * HD :])
    scores = jnp.einsum("hid,jd->hij", queries, keys, preferred_element_type=f32) * 0.125
    scores = jnp.where(allowed[None], scores, masked_value)
    probs = jax.nn.softmax(scores, axis=-1)
    attn = heads_joined(
        jnp.einsum("hij,jd->hid", probs.astype(bf16), values, preferred_element_type=f32)
    ).astype(bf16)
    part = jnp.dot(gated, wmo, preferred_element_type=f32) + jnp.dot(attn, wao, preferred_element_type=f32)
    return part, (proj, state_out, gated, attn)


def layer_second(mid, small, w):
    wi, wgu, wd, wmo, wao = w
    scale = lax.rsqrt(jnp.mean(mid * mid, axis=-1, keepdims=True) + epsilon)
    h2 = (mid * scale * small["second_gain"]).astype(bf16)
    gu = jnp.dot(h2, wgu, preferred_element_type=f32)
    hidden = (jax.nn.silu(gu[:, :RF]) * gu[:, RF:]).astype(bf16)
    return jnp.dot(hidden, wd, preferred_element_type=f32), gu


def back_second(cot, mid, gu, small, w):
    wi, wgu, wd, wmo, wao = w
    low = cot.astype(bf16)
    gate, up = gu[:, :RF], gu[:, RF:]
    sig = jax.nn.sigmoid(gate)
    hidden = (gate * sig * up).astype(bf16)
    wd_grad = inner_rows(hidden, low)
    hidden_grad = outer_cols(low, wd)
    gu_grad = jnp.concatenate(
        [hidden_grad * up * silu_slope(gate, sig), hidden_grad * gate * sig], axis=1
    ).astype(bf16)
    scale = lax.rsqrt(jnp.mean(mid * mid, axis=-1, keepdims=True) + epsilon)
    h2 = (mid * scale * small["second_gain"]).astype(bf16)
    wgu_grad = inner_rows(h2, gu_grad)
    return outer_cols(gu_grad, wgu), wgu_grad, wd_grad


def back_first(mid_grad, x, saved, small, w, masks, rank):
    wi, wgu, wd, wmo, wao = w
    proj, state_out, gated, attn = saved
    same, causal, taps = masks
    allowed = same & causal
    low = mid_grad.astype(bf16)
    wo_grad = jnp.concatenate([inner_rows(gated, low), inner_rows(attn, low)], axis=0)
    gated_grad = outer_cols(low, wmo)
    attn_grad = heads_apart(outer_cols(low, wao).astype(bf16), 2)
    queries = heads_apart(proj[:, Q_AT : Q_AT + RQ], 2)
    kv = proj[:, Q_AT + RQ :]
    group = rank // 2
    keys = jnp.where(group == 0, kv[:, :HD], kv[:, HD : 2 * HD])
    values = jnp.where(group == 0, kv[:, 2 * HD : 3 * HD], kv[:, 3 * HD :])
    scores = jnp.einsum("hid,jd->hij", queries, keys, preferred_element_type=f32) * 0.125
    probs = jax.nn.softmax(jnp.where(allowed[None], scores, masked_value), axis=-1)
    prob_grad = jnp.einsum("hid,jd->hij", attn_grad, values, preferred_element_type=f32)
    score_grad = (probs * (prob_grad - jnp.sum(probs * prob_grad, axis=-1, keepdims=True))).astype(bf16)
    query_grad = heads_joined(jnp.einsum("hij,jd->hid", score_grad, keys, preferred_element_type=f32)) * 0.125
    key_grad = jnp.einsum("hij,hid->jd", score_grad, queries, preferred_element_type=f32) * 0.125
    value_grad = jnp.einsum("hij,hid->jd", probs.astype(bf16), attn_grad, preferred_element_type=f32)
    nothing = jnp.zeros_like(key_grad)
    kv_grad = jnp.where(
        group == 0,
        jnp.concatenate([key_grad, nothing, value_grad, nothing], axis=1),
        jnp.concatenate([nothing, key_grad, nothing, value_grad], axis=1),
    )
    z_value = proj[:, :RD].astype(f32)
    z_sig = jax.nn.sigmoid(z_value)
    pre, summed = mixer_values(proj, small, taps)
    conv_sig = jax.nn.sigmoid(summed)
    conv = summed * conv_sig
    vals = heads_apart(conv[:, :RD], RH)
    write_low, read_low = conv[:, RD : RD + NS].astype(bf16), conv[:, RD + NS :].astype(bf16)
    ssm = heads_joined(state_out + small["skip_gain"][:, None, None] * vals)
    z_grad = gated_grad * ssm * silu_slope(z_value, z_sig)
    ssm_grad = heads_apart(gated_grad * z_value * z_sig, RH)
    ssm_low = ssm_grad.astype(bf16)
    raw = lax.dynamic_slice_in_dim(proj[:, RAW_AT : RAW_AT + 128].astype(f32), rank * RH, RH, 1)
    stepped = raw + small["step_bias"]
    dt = jax.nn.softplus(stepped)
    rate_scale = jnp.exp(small["decay_log"])
    rate = -dt * rate_scale
    run = running_sum(rate)
    gram = outer_cols(read_low, write_low)
    gap = run.T[:, :, None] - run.T[:, None, :]
    decay = jnp.exp(jnp.where(allowed[None], gap, masked_value))
    mixing = (gram[None] * decay).astype(bf16)
    fed = (vals * dt.T[:, :, None]).astype(bf16)
    mixing_grad = jnp.einsum("hip,hjp->hij", ssm_low, fed, preferred_element_type=f32)
    fed_grad = jnp.einsum("hij,hip->hjp", mixing, ssm_low, preferred_element_type=f32)
    gram_grad = jnp.sum(mixing_grad * decay, axis=0).astype(bf16)
    read_grad = jnp.dot(gram_grad, write_low, preferred_element_type=f32)
    write_grad = inner_rows(gram_grad, read_low)
    run_grad = (
        jnp.sum(ssm_low.astype(f32) * state_out, axis=-1) - jnp.sum(fed.astype(f32) * fed_grad, axis=-1)
    )
    later = (allowed.T).astype(f32)
    rate_grad = jnp.einsum("kp,hp->kh", later, run_grad, precision=highest)
    dt_grad = jnp.sum(vals * fed_grad, axis=-1).T - rate_grad * rate_scale
    decay_grad = jnp.sum(rate_grad * rate, axis=0)
    raw_grad = dt_grad * jax.nn.sigmoid(stepped)
    step_grad = jnp.sum(raw_grad, axis=0)
    skip_grad = jnp.sum(ssm_grad * vals, axis=(1, 2))
    vals_grad = heads_joined(dt.T[:, :, None] * fed_grad + small["skip_gain"][:, None, None] * ssm_grad)
    summed_grad = jnp.concatenate([vals_grad, write_grad, read_grad], axis=1) * silu_slope(summed, conv_sig)
    bias_grad = jnp.sum(summed_grad, axis=0)
    kernel_grads = [jnp.sum(summed_grad * pre, axis=0)]
    pre_grad = summed_grad * small["conv_kernel"][CONV - 1 :]
    for by in range(1, CONV):
        kept = summed_grad * taps[by]
        kernel_grads.insert(0, jnp.sum(kept * rolled(pre, by), axis=0))
        pre_grad = pre_grad + rolled(kept * small["conv_kernel"][CONV - 1 - by : CONV - by], -by)
    raw_wide = lax.dynamic_update_slice_in_dim(
        jnp.zeros((raw_grad.shape[0], 128), f32), raw_grad, rank * RH, 1
    )
    proj_grad = jnp.concatenate([z_grad, pre_grad, raw_wide, query_grad, kv_grad], axis=1).astype(bf16)
    scale = lax.rsqrt(jnp.mean(x * x, axis=-1, keepdims=True) + epsilon)
    h1 = (x * scale * small["first_gain"]).astype(bf16)
    wi_grad = inner_rows(h1, proj_grad)
    conv_grads = jnp.concatenate([jnp.stack(kernel_grads), bias_grad[None]], axis=0)
    return outer_cols(proj_grad, wi), wi_grad, wo_grad, conv_grads, (step_grad, decay_grad, skip_grad)


def reduced_rows(grad, y, z, rows):
    parts = grad.astype(bf16).reshape(4, 2, rows, grad.shape[1])
    mine = lax.dynamic_index_in_dim(parts, y, 1, False)
    theirs = lax.dynamic_index_in_dim(parts, 1 - y, 1, False)
    low = (mine.astype(f32) + swapped(theirs, "y").astype(f32)).astype(bf16)
    total = lax.dynamic_index_in_dim(low, z, 0, False).astype(f32)
    for k in (1, 2, 3):
        total = total + turned(lax.dynamic_index_in_dim(low, (z + k) % 4, 0, False), k).astype(f32)
    return total.astype(bf16)


def reduced_out(grad, y, z, rank):
    parts = grad.astype(bf16).reshape(2, OUTR // 2, D)
    mine = lax.dynamic_index_in_dim(parts, y, 0, False)
    theirs = lax.dynamic_index_in_dim(parts, 1 - y, 0, False)
    low = (mine.astype(f32) + swapped(theirs, "y").astype(f32)).astype(bf16)
    total = low.astype(f32)
    for k in (1, 2, 3):
        pairs = [(p, p[:3] + (2 * p[0] + p[2],)) for p in every if p[3] == (2 * p[0] + p[2] + k) % 4]
        total = total + sent(low, pairs).astype(f32)
    return total.astype(bf16)


def on_core(value, s, flip):
    return sent(
        value,
        [(p, (s, p[1] ^ flip[0], p[2] ^ flip[1], p[3])) for p in every if p[0] == s],
    )


def spread_plane(pieces, s, c, y, x):
    results = []
    for piece in pieces:
        given = sent(piece, [(p, (s,) + p[1:]) for p in every if p[0] != s])
        block = jnp.stack([piece, given] if s == 0 else [given, piece])
        near = ordered(x, block, on_core(block, s, (0, 1)))
        far = ordered(x, on_core(block, s, (1, 0)), on_core(block, s, (1, 1)))
        results.append(ordered(y, near, far))
    return results


def spread_out(piece, s, z):
    def holder(y, z):
        return (z // 2, y, z % 2, z)

    moves = [sent(piece, [(holder(y, z_), (s, y, z_ % 2, z_)) for y in range(2) for z_ in range(4) if z_ // 2 != s])]
    here = jnp.where(z // 2 == s, piece, moves[0])
    other_x = sent(here, [((s, y, z_ % 2, z_), (s, y, 1 - z_ % 2, z_)) for y in range(2) for z_ in range(4)])
    x = lax.axis_index("x")
    row = jnp.where(x == z % 2, here, other_x)
    return ordered(lax.axis_index("y"), row, on_core(row, s, (1, 0)))


def weight_outputs(inner, hidden, down, out):
    def ranks(value):
        return value.transpose(2, 1, 0, 3, 4).reshape(4, 2 * value.shape[3], value.shape[4]).astype(f32)

    inner, hidden, down = ranks(inner), ranks(hidden), ranks(down)

    def joined(part):
        return part.transpose(1, 0, 2).reshape(part.shape[1], -1)

    shared = jnp.sum(inner[:, :, 2 * RD : 2 * RD + 2 * NS + MH], axis=0)
    mixer_in = jnp.concatenate([joined(inner[:, :, :RD]), joined(inner[:, :, RD : 2 * RD]), shared], axis=1)
    attention_in = jnp.concatenate(
        [joined(inner[:, :, Q_AT : Q_AT + RQ]), jnp.sum(inner[:, :, Q_AT + RQ :], axis=0)], axis=1
    )
    gate_up = hidden.reshape(4, 2 * 128, 2, 4, 128).transpose(1, 2, 3, 0, 4).reshape(2 * 128, 2 * FF)
    rows = down.reshape(RF, D)
    out = out.reshape(OUTR, D).astype(f32)
    return mixer_in, out[:RD], attention_in, out[RD:], gate_up, rows


def paired(
    block_input,
    output_grad,
    doc_lengths,
    first_gain,
    mixer_in,
    conv_kernel,
    conv_bias,
    step_bias,
    decay_log,
    skip_gain,
    mixer_out,
    attention_in,
    attention_out,
    second_gain,
    gate_up,
    down_weight,
):
    c, y, x, z = (lax.axis_index(a) for a in AXES)
    rank = 2 * c + x
    sections = bring_weights(
        mixer_in[0], attention_in[0], gate_up[0], down_weight[0], mixer_out[0], attention_out[0], c, y, x, z
    )
    x0 = whole_rows(block_input[:, 0], y, x).astype(f32)
    cot = whole_rows(output_grad[:, 0], y, x).astype(f32)
    lead = jnp.concatenate(
        [
            conv_kernel[0].astype(f32).reshape(-1),
            conv_bias[0].astype(f32),
            first_gain[0].astype(f32),
            second_gain[0].astype(f32),
            step_bias[0],
            decay_log[0],
            skip_gain[0],
        ]
    )
    packed = lax.all_gather(lead, ("core", "z"))
    packed = packed.reshape(2, 4, -1)
    quarter = CONVD // 4
    smalls = []
    cut = lax.dynamic_slice_in_dim
    for s in range(2):
        conv = packed[s, :, : 5 * quarter].reshape(4, 5, quarter).transpose(1, 0, 2).reshape(5, CONVD)
        conv = jnp.concatenate([cut(conv, rank * RD, RD, 1), conv[:, DS:]], axis=1)
        at = 5 * quarter
        gains = packed[s, :, at : at + 512].reshape(4, 2, 256).transpose(1, 0, 2).reshape(2, D)
        at += 512
        per_head = [cut(packed[s, 0, at + i * MH : at + (i + 1) * MH], rank * RH, RH, 0) for i in range(3)]
        smalls.append(
            {
                "conv_kernel": conv[:4],
                "conv_bias": conv[4],
                "first_gain": gains[0],
                "second_gain": gains[1],
                "step_bias": per_head[0],
                "decay_log": per_head[1],
                "skip_gain": per_head[2],
            }
        )
    doc_sizes = lax.dynamic_index_in_dim(doc_lengths[:, 0], y, 0, False)
    length = x0.shape[0]
    positions = jnp.arange(length, dtype=jnp.int32)
    ids = doc_layout(doc_sizes, positions)[0]
    same = ids[:, None] == ids[None, :]
    causal = positions[:, None] >= positions[None, :]
    taps = [None] + [
        ((positions >= by) & (jnp.roll(ids, by) == ids)).astype(f32)[:, None] for by in range(1, CONV)
    ]
    masks = (same, causal, taps)

    entry = x0
    kept = []
    outputs = []
    for s in range(2):
        part, saved = layer_first(entry, smalls[s], sections[s], masks, rank)
        mid = entry + quarter_sum(part, c).astype(f32)
        part, gu = layer_second(mid, smalls[s], sections[s])
        result = (mid + quarter_sum(part, c).astype(f32)).astype(bf16)
        outputs.append(result)
        kept.append((entry, saved, mid, gu))
        entry = result.astype(f32)

    input_grads = [None, None]
    small_grads = [None, None]
    finished = [None, None]
    for s in (1, 0):
        entry, saved, mid, gu = kept[s]
        part, wgu_grad, wd_grad = back_second(cot, mid, gu, smalls[s], sections[s])
        mid_norm, second_grad = norm_back(mid, smalls[s]["second_gain"], quarter_sum(part, c).astype(f32))
        mid_grad = cot + mid_norm
        part, wi_grad, wo_grad, conv_grads, head_grads = back_first(
            mid_grad, entry, saved, smalls[s], sections[s], masks, rank
        )
        in_norm, first_grad = norm_back(entry, smalls[s]["first_gain"], quarter_sum(part, c).astype(f32))
        low = (mid_grad + in_norm).astype(bf16)
        input_grads[s] = low
        cot = low.astype(f32)
        first = (rank == 0).astype(f32)
        wide = jnp.zeros((5, CONVD), f32)
        wide = lax.dynamic_update_slice_in_dim(wide, conv_grads[:, :RD], rank * RD, 1)
        wide = wide.at[:, DS:].set(conv_grads[:, RD:])
        heads = jnp.zeros((3, MH), f32)
        heads = lax.dynamic_update_slice_in_dim(heads, jnp.stack(head_grads), rank * RH, 1)
        small_grads[s] = jnp.concatenate(
            [wide.reshape(-1), first_grad * first, second_grad * first, heads.reshape(-1)]
        )
        hidden = reduced_rows(wgu_grad, y, z, 128)
        down = reduced_rows(wd_grad, y, z, 64)
        out = reduced_out(wo_grad, y, z, rank)
        inner = reduced_rows(wi_grad, y, z, 128)
        hidden, down, inner = spread_plane((hidden, down, inner), s, c, y, x)
        finished[s] = weight_outputs(inner, hidden, down, spread_out(out, s, z))

    weights = [jnp.where(c == 0, a, b) for a, b in zip(*finished)]
    sums = lax.psum(jnp.stack(small_grads), AXES)
    sums = lax.dynamic_index_in_dim(sums, c, 0, False)
    wide = sums[: 5 * CONVD].reshape(5, CONVD)
    at = 5 * CONVD
    conv_out = cut(wide, z * quarter, quarter, 1)
    first_out = cut(sums[at : at + D], z * 256, 256, 0)
    second_out = cut(sums[at + D : at + 2 * D], z * 256, 256, 0)
    head_out = sums[at + 2 * D :].reshape(3, MH)
    outs = [back_rows(o, y, x) for o in outputs]
    ins = [back_rows(o, y, x) for o in input_grads]
    section_output = jnp.where(c == 0, outs[0], outs[1])[None, :, None]
    input_grad = jnp.where(c == 0, ins[0], ins[1])[None, :, None]
    mixer_in_grad, mixer_out_grad, attention_in_grad, attention_out_grad, gate_up_grad, down_grad = weights
    return (
        section_output,
        input_grad,
        first_out[None],
        mixer_in_grad[None],
        conv_out[None, :4],
        conv_out[None, 4],
        head_out[None, 0],
        head_out[None, 1],
        head_out[None, 2],
        mixer_out_grad[None],
        attention_in_grad[None],
        attention_out_grad[None],
        second_out[None],
        gate_up_grad[None],
        down_grad[None],
    )


def paired_specs():
    plane = ("y", "x")
    rows = P("core", "z", None)
    placed = (
        P(None, "z", plane, None),
        P(None, "z", plane, None),
        P(None, "z", None),
        P("core", "z"),
        rows,
        P("core", None, "z"),
        P("core", "z"),
        P("core", None),
        P("core", None),
        P("core", None),
        rows,
        rows,
        rows,
        P("core", "z"),
        rows,
        rows,
    )
    given = (
        P("core", None, "z", plane, None),
        P("core", None, "z", plane, None),
        P("core", "z"),
        rows,
        P("core", None, "z"),
        P("core", "z"),
        P("core", None),
        P("core", None),
        P("core", None),
        rows,
        rows,
        rows,
        P("core", "z"),
        rows,
        rows,
    )
    return placed, given


def solution(mesh):
    if tuple(mesh.devices.shape) == (2, 4, 4):
        fine = Mesh(mesh.devices.reshape(2, 2, 2, 4), AXES)
        placed, given = paired_specs()
        return jax.shard_map(paired, mesh=fine, in_specs=placed, out_specs=given, check_vma=False)
    return spread(mesh)
```

```python
import functools
import math

import jax
import jax.numpy as jnp
from jax import lax
from jax.experimental import pallas as pl
from jax.experimental.pallas import tpu as pltpu
from jax.sharding import Mesh, PartitionSpec as P

D = 1024
FF = 2048
MH = 24
MP = 64
NS = 128
QH = 8
KVH = 2
HD = 64
CONV = 4
MICRO = 2
SPAN = 128
KEY_BLOCK = 1024
DS = 1536
CONVD = 1792
QD = 512
KVD = 128


epsilon = 1e-05
masked_value = -1e30
highest = lax.Precision.HIGHEST
weight_names = (
    "first_gain",
    "mixer_in",
    "conv_kernel",
    "conv_bias",
    "mixer_out",
    "attention_in",
    "attention_out",
    "second_gain",
    "gate_up",
    "down_weight",
)


def passed_along(value, axis, by):
    length = lax.axis_size(axis)
    pairs = [(i, i + by) for i in range(length) if 0 <= i + by < length]
    return lax.ppermute(value, axis, pairs)


def prefix(value, axis, combine, identity):
    length, position = (lax.axis_size(axis), lax.axis_index(axis))
    everything = jax.tree.map(
        lambda part, kind: lax.all_gather(part.astype(kind), axis),
        value,
        (jnp.bfloat16, jnp.bfloat16),
    )
    start = jax.tree.map(
        lambda part, zero: jnp.broadcast_to(jnp.asarray(zero, part.dtype), part.shape),
        value,
        identity,
    )

    def step(k, before):
        reached = k < position
        new = combine(
            before, jax.tree.map(lambda part, own: part[k].astype(own.dtype), everything, value)
        )
        return jax.tree.map(lambda a, b: jnp.where(reached, a, b), new, before)

    return lax.fori_loop(0, length, step, start)


def prefix_2(value, axis, join, neutral):
    count = lax.axis_size(axis)
    place = lax.axis_index(axis)
    ahead = count - 1 - place
    gathered = jax.tree.map(
        lambda a, kind: lax.all_gather(a.astype(kind), axis),
        value,
        jax.tree.map(lambda a: jnp.bfloat16 if a.dtype == jnp.float32 else a.dtype, value),
    )
    state = jax.tree.map(lambda a, e: jnp.zeros_like(a) + jnp.asarray(e, a.dtype), value, neutral)

    def one(step, state):
        source = count - 1 - step
        return join(
            state,
            jax.tree.map(
                lambda a, own: lax.dynamic_index_in_dim(a, source, 0, False).astype(own.dtype),
                gathered,
                value,
            ),
        )

    return lax.fori_loop(0, ahead, one, state)


def inner_rows(left, right):
    return lax.dot_general(
        left, right, (((0,), (0,)), ((), ())), preferred_element_type=jnp.float32
    )


def outer_cols(left, right):
    return lax.dot_general(
        left, right, (((1,), (1,)), ((), ())), preferred_element_type=jnp.float32
    )


def norm_apply(hidden_in, gain_vec):
    return (
        hidden_in
        * lax.rsqrt(jnp.mean(hidden_in * hidden_in, axis=-1, keepdims=True) + epsilon)
        * gain_vec
    )


def norm_back(hidden_in, gain_vec, upstream):
    scale = lax.rsqrt(jnp.mean(hidden_in * hidden_in, axis=-1, keepdims=True) + epsilon)
    normed = hidden_in * scale
    weighted = upstream * gain_vec
    hidden_grad = scale * (weighted - normed * jnp.mean(weighted * normed, axis=-1, keepdims=True))
    return (hidden_grad, jnp.sum(upstream * normed, axis=0))


def running_sum(value):
    count = value.shape[0]
    until = lax.broadcasted_iota(jnp.int32, (count, count), 0) >= lax.broadcasted_iota(
        jnp.int32, (count, count), 1
    )
    return jnp.dot(until.astype(jnp.float32), value, precision=highest)


def doc_layout(doc_sizes, positions):
    count = doc_sizes.shape[0]
    until = lax.broadcasted_iota(jnp.int32, (count, count), 0) >= lax.broadcasted_iota(
        jnp.int32, (count, count), 1
    )
    bounds = jnp.sum(jnp.where(until, doc_sizes[None, :], 0), axis=1)[:-1]
    doc_ids = jnp.sum((positions[:, None] >= bounds[None, :]).astype(jnp.int32), axis=1)
    starts = jnp.any(positions[:, None] == bounds[None, :], axis=1)
    return (doc_ids, starts)


def conv_apply(extended, ext_ids, kernel, offset_vec):
    amount = extended.shape[0] - CONV + 1
    own_ids = ext_ids[CONV - 1 :]
    summed = offset_vec[None, :] + jnp.zeros((amount, 1), extended.dtype)
    for tap_index in range(CONV):
        same_doc = (ext_ids[tap_index : tap_index + amount] == own_ids).astype(extended.dtype)
        summed = (
            summed
            + kernel[tap_index][None, :]
            * extended[tap_index : tap_index + amount]
            * same_doc[:, None]
        )
    return jax.nn.silu(summed)


def span_pass(carried_state, pieces):
    values, write_vec, read_vec, step_size, log_decay, doc_ids, before = pieces
    amount = values.shape[0]
    running = running_sum(log_decay)
    row_ids = lax.broadcasted_iota(jnp.int32, (amount, amount), 0)
    col_ids = lax.broadcasted_iota(jnp.int32, (amount, amount), 1)
    allowed = (col_ids <= row_ids) & (doc_ids[:, None] == doc_ids[None, :])
    log_gap = jnp.where(
        allowed[:, :, None], running[:, None, :] - running[None, :, :], masked_value
    )
    intersection = jnp.einsum("in,jn->ij", read_vec, write_vec, precision=highest)
    mixing = intersection[:, :, None] * jnp.exp(log_gap) * step_size[None, :, :]
    within = jnp.einsum("ijh,jhp->ihp", mixing, values, precision=highest)
    inflow = jnp.exp(running) * (doc_ids == before)[:, None].astype(jnp.float32)
    carried = (
        jnp.einsum("in,hpn->ihp", read_vec, carried_state, precision=highest) * inflow[:, :, None]
    )
    to_end = (
        jnp.exp(running[-1][None, :] - running)
        * (doc_ids == doc_ids[-1])[:, None].astype(jnp.float32)
        * step_size
    )
    increment = jnp.einsum("jh,jhp,jn->hpn", to_end, values, write_vec, precision=highest)
    return (inflow[-1][:, None, None] * carried_state + increment, within + carried)


def mixer_local(
    extended,
    raw_rate,
    kernel,
    offset_vec,
    step_bias,
    decay_log,
    skip_gain,
    state_in,
    ext_ids,
    doc_ids,
    starts,
):
    tokens = raw_rate.shape[0]
    conv_out = conv_apply(extended, ext_ids, kernel, offset_vec)
    values = conv_out[:, :DS].reshape(tokens, MH, MP)
    read_vector = conv_out[:, DS + NS :]
    step_size = jax.nn.softplus(raw_rate + step_bias)
    log_decay = -step_size * jnp.exp(decay_log)
    blocks = tokens // SPAN
    pieces = (
        values.reshape(blocks, SPAN, MH, MP),
        conv_out[:, DS : DS + NS].reshape(blocks, SPAN, NS),
        read_vector.reshape(blocks, SPAN, NS),
        step_size.reshape(blocks, SPAN, MH),
        log_decay.reshape(blocks, SPAN, MH),
        doc_ids.reshape(blocks, SPAN),
        doc_ids[::SPAN] - starts[::SPAN].astype(jnp.int32),
    )
    state_out, outputs = lax.scan(span_pass, state_in, pieces)
    result = outputs.reshape(tokens, MH, MP) + skip_gain[None, :, None] * values
    return ((result.reshape(tokens, DS), state_out), (read_vector, log_decay))


def device_inflow(log_decay, doc_ids, starts):
    same_doc = (doc_ids == doc_ids[0] - starts[0].astype(jnp.int32)).astype(jnp.float32)
    return jnp.exp(running_sum(log_decay)) * same_doc[:, None]


def chain_affine(earlier, later):
    return (earlier[0] * later[0], later[0][:, None, None] * earlier[1] + later[1])


def query_groups(flat):
    tokens = flat.shape[0]
    per_group = QH // KVH
    return (
        flat.reshape(tokens, KVH, per_group, HD)
        .transpose(1, 2, 0, 3)
        .reshape(KVH, per_group * tokens, HD)
    )


def query_flat(grouped, tokens):
    per_group = QH // KVH
    return grouped.reshape(KVH, per_group, tokens, HD).transpose(2, 0, 1, 3).reshape(tokens, QD)


def score_block(queries, key_rows, query_pos, query_ids, all_ids, offset, block_len):
    key_block = lax.dynamic_slice_in_dim(key_rows, offset, block_len, 0)
    key_part = key_block[:, :KVD].reshape(block_len, KVH, HD)
    value_part = key_block[:, KVD:].reshape(block_len, KVH, HD)
    key_pos = offset + jnp.arange(block_len, dtype=jnp.int32)
    key_ids = lax.dynamic_slice_in_dim(all_ids, offset, block_len, 0)
    allowed = (key_pos[None, :] <= query_pos[:, None]) & (key_ids[None, :] == query_ids[:, None])
    scores = (
        jnp.einsum("grd,kgd->grk", queries, key_part, preferred_element_type=jnp.float32) * 0.125
    )
    return (jnp.where(allowed[None], scores, masked_value), allowed, key_part, value_part)


def attend_forward(queries_flat, key_rows, positions, doc_ids, all_ids, ctx_index):
    tokens = queries_flat.shape[0]
    per_group = QH // KVH
    queries = query_groups(queries_flat)
    query_pos = jnp.tile(positions, per_group)
    query_ids = jnp.tile(doc_ids, per_group)
    block_len = math.gcd(key_rows.shape[0], KEY_BLOCK)
    block_count = ((ctx_index + 1) * tokens + block_len - 1) // block_len

    def visit_block(block_index, carry):
        running_max, running_sum, accumulated = carry
        scores, allowed, key_part, value_part = score_block(
            queries, key_rows, query_pos, query_ids, all_ids, block_index * block_len, block_len
        )
        new_max = jnp.maximum(running_max, jnp.max(scores, axis=-1))
        chances = jnp.where(allowed[None], jnp.exp(scores - new_max[..., None]), 0.0)
        rescale = jnp.exp(running_max - new_max)
        running_sum = running_sum * rescale + jnp.sum(chances, axis=-1)
        accumulated = accumulated * rescale[..., None] + jnp.einsum(
            "grk,kgd->grd",
            chances.astype(jnp.bfloat16),
            value_part,
            preferred_element_type=jnp.float32,
        )
        return (new_max, running_sum, accumulated)

    row_count = per_group * tokens
    start_carry = (
        jnp.full((KVH, row_count), masked_value, jnp.float32),
        jnp.zeros((KVH, row_count), jnp.float32),
        jnp.zeros((KVH, row_count, HD), jnp.float32),
    )
    running_max, running_sum, accumulated = lax.fori_loop(0, block_count, visit_block, start_carry)
    output = accumulated / running_sum[..., None]
    return (query_flat(output, tokens), running_max + jnp.log(running_sum))


def attend_backward(
    queries_flat,
    key_rows,
    attention_raw,
    log_norm,
    grad_low,
    positions,
    doc_ids,
    all_ids,
    ctx_index,
):
    tokens = queries_flat.shape[0]
    length = key_rows.shape[0]
    per_group = QH // KVH
    queries = query_groups(queries_flat)
    grad_rows = query_groups(grad_low)
    grad_wide = grad_rows.astype(jnp.float32)
    delta = jnp.sum(grad_wide * query_groups(attention_raw), axis=-1)
    query_pos = jnp.tile(positions, per_group)
    query_ids = jnp.tile(doc_ids, per_group)
    block_len = math.gcd(length, KEY_BLOCK)
    block_count = ((ctx_index + 1) * tokens + block_len - 1) // block_len

    def visit_block(block_index, carry):
        query_grad, key_grad, value_grad = carry
        offset = block_index * block_len
        scores, allowed, key_part, value_part = score_block(
            queries, key_rows, query_pos, query_ids, all_ids, offset, block_len
        )
        chances = jnp.where(allowed[None], jnp.exp(scores - log_norm[..., None]), 0.0)
        prob_grad = jnp.einsum(
            "grd,kgd->grk", grad_rows, value_part, preferred_element_type=jnp.float32
        )
        score_grad = (chances * (prob_grad - delta[..., None])).astype(jnp.bfloat16)
        query_grad = query_grad + jnp.einsum(
            "grk,kgd->grd", score_grad, key_part, preferred_element_type=jnp.float32
        )
        key_piece = (
            jnp.einsum("grk,grd->kgd", score_grad, queries, preferred_element_type=jnp.float32)
            * 0.125
        )
        value_piece = jnp.einsum(
            "grk,grd->kgd",
            chances.astype(jnp.bfloat16),
            grad_rows,
            preferred_element_type=jnp.float32,
        )
        key_grad = lax.dynamic_update_slice_in_dim(
            key_grad,
            lax.dynamic_slice_in_dim(key_grad, offset, block_len, 0)
            + key_piece.reshape(block_len, KVD),
            offset,
            0,
        )
        value_grad = lax.dynamic_update_slice_in_dim(
            value_grad,
            lax.dynamic_slice_in_dim(value_grad, offset, block_len, 0)
            + value_piece.reshape(block_len, KVD),
            offset,
            0,
        )
        return (query_grad, key_grad, value_grad)

    start_carry = (
        jnp.zeros((KVH, per_group * tokens, HD), jnp.float32),
        jnp.zeros((length, KVD), jnp.float32),
        jnp.zeros((length, KVD), jnp.float32),
    )
    query_grad, key_grad, value_grad = lax.fori_loop(0, block_count, visit_block, start_carry)
    return (query_flat(query_grad * 0.125, tokens), key_grad, value_grad)


def layer_layout(doc_sizes, tokens, ctx_index, ctx_count):
    positions = ctx_index * tokens + jnp.arange(tokens, dtype=jnp.int32)
    doc_ids, starts = doc_layout(doc_sizes, positions)
    all_ids = doc_layout(doc_sizes, jnp.arange(tokens * ctx_count, dtype=jnp.int32))[0]
    ext_ids = doc_layout(
        doc_sizes, ctx_index * tokens - (CONV - 1) + jnp.arange(tokens + CONV - 1, dtype=jnp.int32)
    )[0]
    return (positions, doc_ids, starts, all_ids, ext_ids)


def layer_forward(hidden_in, weights_full, head_params, doc_sizes, ctx_index, ctx_count):
    tokens = hidden_in.shape[0]
    positions, doc_ids, starts, all_ids, ext_ids = layer_layout(
        doc_sizes, tokens, ctx_index, ctx_count
    )
    normed = norm_apply(hidden_in, weights_full["first_gain"].astype(jnp.float32)).astype(
        jnp.bfloat16
    )
    projected = jnp.dot(
        normed, weights_full["mixer_in"], preferred_element_type=jnp.float32
    ).astype(jnp.bfloat16)
    edge_rows = passed_along(projected[tokens - (CONV - 1) :, DS : DS + CONVD], "ctx", 1)
    extended = jnp.concatenate([edge_rows, projected[:, DS : DS + CONVD]], axis=0).astype(
        jnp.float32
    )
    raw_rate = projected[:, DS + CONVD :].astype(jnp.float32)
    step_bias, decay_log, skip_gain = head_params
    empty_state = jnp.zeros((MH, MP, NS), jnp.float32)
    (partial_out, local_state), (read_vector, log_decay) = mixer_local(
        extended,
        raw_rate,
        weights_full["conv_kernel"].astype(jnp.float32),
        weights_full["conv_bias"].astype(jnp.float32),
        step_bias,
        decay_log,
        skip_gain,
        empty_state,
        ext_ids,
        doc_ids,
        starts,
    )
    inflow = device_inflow(log_decay, doc_ids, starts)
    state_in = prefix(
        (inflow[-1], local_state), "ctx", chain_affine, (jnp.ones((MH,), jnp.float32), empty_state)
    )[1]
    carried = (
        jnp.einsum("tn,hpn->thp", read_vector, state_in, precision=highest) * inflow[:, :, None]
    )
    ssm_out = partial_out + carried.reshape(tokens, DS)
    gate_value = projected[:, :DS].astype(jnp.float32)
    gated_out = (ssm_out * jax.nn.silu(gate_value)).astype(jnp.bfloat16)
    mixer_term = jnp.dot(gated_out, weights_full["mixer_out"], preferred_element_type=jnp.float32)
    heads_in = jnp.dot(
        normed, weights_full["attention_in"], preferred_element_type=jnp.float32
    ).astype(jnp.bfloat16)
    key_rows = lax.all_gather(heads_in[:, QD:], "ctx", axis=0, tiled=True)
    attention_raw, log_norm = attend_forward(
        heads_in[:, :QD], key_rows, positions, doc_ids, all_ids, ctx_index
    )
    attention_term = jnp.dot(
        attention_raw.astype(jnp.bfloat16),
        weights_full["attention_out"],
        preferred_element_type=jnp.float32,
    )
    middle = hidden_in + mixer_term + attention_term
    normed_mid = norm_apply(middle, weights_full["second_gain"].astype(jnp.float32)).astype(
        jnp.bfloat16
    )
    expanded = jnp.dot(normed_mid, weights_full["gate_up"], preferred_element_type=jnp.float32)
    hidden = (jax.nn.silu(expanded[:, :FF]) * expanded[:, FF:]).astype(jnp.bfloat16)
    result = middle + jnp.dot(
        hidden, weights_full["down_weight"], preferred_element_type=jnp.float32
    )
    stored = (
        hidden_in,
        middle,
        projected,
        edge_rows,
        state_in,
        ssm_out,
        heads_in,
        key_rows,
        attention_raw,
        log_norm,
        expanded,
    )
    return (result, stored)


def layer_backward(grad_in, stored, weights_full, head_params, doc_sizes, ctx_index, ctx_count):
    (
        hidden_in,
        middle,
        projected,
        edge_rows,
        state_in,
        ssm_out,
        heads_in,
        key_rows,
        attention_raw,
        log_norm,
        expanded,
    ) = stored
    tokens = hidden_in.shape[0]
    positions, doc_ids, starts, all_ids, ext_ids = layer_layout(
        doc_sizes, tokens, ctx_index, ctx_count
    )
    first_gain = weights_full["first_gain"].astype(jnp.float32)
    second_gain = weights_full["second_gain"].astype(jnp.float32)
    down_low = grad_in.astype(jnp.bfloat16)
    gate_vals = expanded[:, :FF]
    up_vals = expanded[:, FF:]
    gate_sig = jax.nn.sigmoid(gate_vals)
    hidden = (jax.nn.silu(gate_vals) * up_vals).astype(jnp.bfloat16)
    down_weight_grad = inner_rows(hidden, down_low)
    hidden_grad = outer_cols(down_low, weights_full["down_weight"])
    slope = gate_sig * (1.0 + gate_vals * (1.0 - gate_sig))
    expand_grad = jnp.concatenate(
        [hidden_grad * up_vals * slope, hidden_grad * jax.nn.silu(gate_vals)], axis=1
    ).astype(jnp.bfloat16)
    normed_mid = norm_apply(middle, second_gain).astype(jnp.bfloat16)
    gate_up_grad = inner_rows(normed_mid, expand_grad)
    mid_norm_grad, second_gain_grad = norm_back(
        middle, second_gain, outer_cols(expand_grad, weights_full["gate_up"])
    )
    middle_grad = grad_in + mid_norm_grad
    residual_low = middle_grad.astype(jnp.bfloat16)
    attention_out_grad = inner_rows(attention_raw.astype(jnp.bfloat16), residual_low)
    output_low = outer_cols(residual_low, weights_full["attention_out"]).astype(jnp.bfloat16)
    query_grad, key_grad, value_grad = attend_backward(
        heads_in[:, :QD],
        key_rows,
        attention_raw,
        log_norm,
        output_low,
        positions,
        doc_ids,
        all_ids,
        ctx_index,
    )
    key_share, value_share = (
        lax.psum_scatter(
            key_grad.astype(jnp.bfloat16), "ctx", scatter_dimension=0, tiled=True
        ).astype(jnp.float32),
        lax.psum_scatter(
            value_grad.astype(jnp.bfloat16), "ctx", scatter_dimension=0, tiled=True
        ).astype(jnp.float32),
    )
    heads_grad = jnp.concatenate([query_grad, key_share, value_share], axis=1).astype(jnp.bfloat16)
    gate_value = projected[:, :DS].astype(jnp.float32)
    gate_sig_z = jax.nn.sigmoid(gate_value)
    gated_out = (ssm_out * jax.nn.silu(gate_value)).astype(jnp.bfloat16)
    mixer_out_grad = inner_rows(gated_out, residual_low)
    gated_grad = outer_cols(residual_low, weights_full["mixer_out"])
    ssm_grad = gated_grad * jax.nn.silu(gate_value)
    gate_grad = gated_grad * ssm_out * gate_sig_z * (1.0 + gate_value * (1.0 - gate_sig_z))
    extended = jnp.concatenate([edge_rows, projected[:, DS : DS + CONVD]], axis=0).astype(
        jnp.float32
    )
    raw_rate = projected[:, DS + CONVD :].astype(jnp.float32)
    step_bias, decay_log, skip_gain = head_params

    def local_piece(
        extended, raw_rate, kernel, offset_vec, step_bias, decay_log, skip_gain, state_in
    ):
        return mixer_local(
            extended,
            raw_rate,
            kernel,
            offset_vec,
            step_bias,
            decay_log,
            skip_gain,
            state_in,
            ext_ids,
            doc_ids,
            starts,
        )

    primal, pullback, (read_vector, log_decay) = jax.vjp(
        local_piece,
        extended,
        raw_rate,
        weights_full["conv_kernel"].astype(jnp.float32),
        weights_full["conv_bias"].astype(jnp.float32),
        step_bias,
        decay_log,
        skip_gain,
        state_in,
        has_aux=True,
    )
    inflow = device_inflow(log_decay, doc_ids, starts)
    local_grad = jnp.einsum(
        "th,thp,tn->hpn", inflow, ssm_grad.reshape(tokens, MH, MP), read_vector, precision=highest
    )
    state_back = prefix_2(
        (inflow[-1], local_grad),
        "ctx",
        chain_affine,
        (jnp.ones((MH,), jnp.float32), jnp.zeros((MH, MP, NS), jnp.float32)),
    )[1]
    ext_grad, raw_grad, kernel_grad, offset_grad, step_grad, decay_grad, skip_grad, unused = (
        pullback((ssm_grad, state_back))
    )
    rim_grad = passed_along(ext_grad[: CONV - 1], "ctx", -1)
    pre_grad = ext_grad[CONV - 1 :]
    pre_grad = jnp.concatenate(
        [pre_grad[: tokens - (CONV - 1)], pre_grad[tokens - (CONV - 1) :] + rim_grad], axis=0
    )
    mixer_grad = jnp.concatenate([gate_grad, pre_grad, raw_grad], axis=1).astype(jnp.bfloat16)
    normed = norm_apply(hidden_in, first_gain).astype(jnp.bfloat16)
    mixer_in_grad = inner_rows(normed, mixer_grad)
    attention_in_grad = inner_rows(normed, heads_grad)
    normed_grad = outer_cols(mixer_grad, weights_full["mixer_in"]) + outer_cols(
        heads_grad, weights_full["attention_in"]
    )
    in_norm_grad, first_gain_grad = norm_back(hidden_in, first_gain, normed_grad)
    block_grad = middle_grad + in_norm_grad
    weight_grads = (
        first_gain_grad,
        mixer_in_grad,
        kernel_grad,
        offset_grad,
        mixer_out_grad,
        attention_in_grad,
        attention_out_grad,
        second_gain_grad,
        gate_up_grad,
        down_weight_grad,
    )
    return (block_grad, weight_grads, (step_grad, decay_grad, skip_grad))


def local(
    block_input,
    output_grad,
    doc_lengths,
    first_gain,
    mixer_in,
    conv_kernel,
    conv_bias,
    step_bias,
    decay_log,
    skip_gain,
    mixer_out,
    attention_in,
    attention_out,
    second_gain,
    gate_up,
    down_weight,
):
    gathered = (
        lax.all_gather(first_gain[0], "wt", axis=0, tiled=True),
        lax.all_gather(mixer_in[0], "wt", axis=0, tiled=True),
        lax.all_gather(conv_kernel[0], "wt", axis=1, tiled=True),
        lax.all_gather(conv_bias[0], "wt", axis=0, tiled=True),
        lax.all_gather(mixer_out[0], "wt", axis=0, tiled=True),
        lax.all_gather(attention_in[0], "wt", axis=0, tiled=True),
        lax.all_gather(attention_out[0], "wt", axis=0, tiled=True),
        lax.all_gather(second_gain[0], "wt", axis=0, tiled=True),
        lax.all_gather(gate_up[0], "wt", axis=0, tiled=True),
        lax.all_gather(down_weight[0], "wt", axis=0, tiled=True),
    )
    weights_full = dict(zip(weight_names, gathered))
    head_params = (step_bias[0], decay_log[0], skip_gain[0])
    head_section = lax.axis_index("section") == 0
    ctx_index = lax.axis_index("ctx")
    ctx_count = lax.axis_size("ctx")
    tokens = block_input.shape[2]
    received = jnp.zeros((tokens, D), jnp.bfloat16)
    results = []
    stored_list = []
    for moment in range(MICRO + 1):
        own_block = block_input[min(moment, MICRO - 1), 0].astype(jnp.float32)
        entry = jnp.where(head_section, own_block, received.astype(jnp.float32))
        doc_sizes = jnp.where(
            head_section, doc_lengths[min(moment, MICRO - 1), 0], doc_lengths[max(moment - 1, 0), 0]
        )
        layer_result, stored = layer_forward(
            entry, weights_full, head_params, doc_sizes, ctx_index, ctx_count
        )
        sent = layer_result.astype(jnp.bfloat16)
        results.append(sent)
        stored_list.append((stored, doc_sizes))
        if moment < MICRO:
            received = passed_along(sent, "section", 1)
    back_received = jnp.zeros((tokens, D), jnp.bfloat16)
    total_grads = tuple((jnp.zeros(weight_full.shape, jnp.float32) for weight_full in gathered))
    total_heads = tuple((jnp.zeros(param_vec.shape, jnp.float32) for param_vec in head_params))
    sent_grads = []
    for moment in range(MICRO + 1):
        given_grad = output_grad[min(moment, MICRO - 1), 0].astype(jnp.float32)
        cotangent = jnp.where(head_section, back_received.astype(jnp.float32), given_grad)
        chosen = jax.tree.map(
            lambda left, right: jnp.where(head_section, left, right),
            stored_list[max(moment - 1, 0)],
            stored_list[min(moment + 1, MICRO)],
        )
        valid = jnp.where(head_section, moment >= 1, moment < MICRO)
        stored, doc_sizes = chosen
        block_grad, weight_grads, head_grads = layer_backward(
            cotangent, stored, weights_full, head_params, doc_sizes, ctx_index, ctx_count
        )
        total_grads = tuple(
            (old + jnp.where(valid, new, 0.0) for old, new in zip(total_grads, weight_grads))
        )
        total_heads = tuple(
            (old + jnp.where(valid, new, 0.0) for old, new in zip(total_heads, head_grads))
        )
        sent = block_grad.astype(jnp.bfloat16)
        sent_grads.append(sent)
        if moment < MICRO:
            back_received = passed_along(sent, "section", -1)
    section_output = jnp.stack(
        [
            jnp.where(head_section, results[batch_index], results[batch_index + 1])
            for batch_index in range(MICRO)
        ]
    ).reshape(1, MICRO, 1, tokens, D)
    input_grad = jnp.stack(
        [
            jnp.where(head_section, sent_grads[batch_index + 1], sent_grads[batch_index])
            for batch_index in range(MICRO)
        ]
    ).reshape(1, MICRO, 1, tokens, D)
    shares = (
        lax.psum_scatter(
            total_grads[0].astype(jnp.bfloat16), "wt", scatter_dimension=0, tiled=True
        ).astype(jnp.float32),
        lax.psum_scatter(
            total_grads[1].astype(jnp.bfloat16), "wt", scatter_dimension=0, tiled=True
        ).astype(jnp.float32),
        lax.psum_scatter(
            total_grads[2].astype(jnp.bfloat16), "wt", scatter_dimension=1, tiled=True
        ).astype(jnp.float32),
        lax.psum_scatter(
            total_grads[3].astype(jnp.bfloat16), "wt", scatter_dimension=0, tiled=True
        ).astype(jnp.float32),
        lax.psum_scatter(
            total_grads[4].astype(jnp.bfloat16), "wt", scatter_dimension=0, tiled=True
        ).astype(jnp.float32),
        lax.psum_scatter(
            total_grads[5].astype(jnp.bfloat16), "wt", scatter_dimension=0, tiled=True
        ).astype(jnp.float32),
        lax.psum_scatter(
            total_grads[6].astype(jnp.bfloat16), "wt", scatter_dimension=0, tiled=True
        ).astype(jnp.float32),
        lax.psum_scatter(
            total_grads[7].astype(jnp.bfloat16), "wt", scatter_dimension=0, tiled=True
        ).astype(jnp.float32),
        lax.psum_scatter(
            total_grads[8].astype(jnp.bfloat16), "wt", scatter_dimension=0, tiled=True
        ).astype(jnp.float32),
        lax.psum_scatter(
            total_grads[9].astype(jnp.bfloat16), "wt", scatter_dimension=0, tiled=True
        ).astype(jnp.float32),
    )
    reduced = (
        lax.psum(shares[0].astype(jnp.bfloat16), "ctx").astype(jnp.float32),
        lax.psum(shares[1].astype(jnp.bfloat16), "ctx").astype(jnp.float32),
        lax.psum(shares[2].astype(jnp.bfloat16), "ctx").astype(jnp.float32),
        lax.psum(shares[3].astype(jnp.bfloat16), "ctx").astype(jnp.float32),
        lax.psum(shares[4].astype(jnp.bfloat16), "ctx").astype(jnp.float32),
        lax.psum(shares[5].astype(jnp.bfloat16), "ctx").astype(jnp.float32),
        lax.psum(shares[6].astype(jnp.bfloat16), "ctx").astype(jnp.float32),
        lax.psum(shares[7].astype(jnp.bfloat16), "ctx").astype(jnp.float32),
        lax.psum(shares[8].astype(jnp.bfloat16), "ctx").astype(jnp.float32),
        lax.psum(shares[9].astype(jnp.bfloat16), "ctx").astype(jnp.float32),
    )
    head_sums = lax.psum((total_heads[0], total_heads[1], total_heads[2]), ("ctx", "wt"))
    return (
        section_output,
        input_grad,
        reduced[0][None],
        reduced[1][None],
        reduced[2][None],
        reduced[3][None],
        head_sums[0][None],
        head_sums[1][None],
        head_sums[2][None],
        reduced[4][None],
        reduced[5][None],
        reduced[6][None],
        reduced[7][None],
        reduced[8][None],
        reduced[9][None],
    )


def spread(mesh):
    placed = (
        P(None, "wt", "ctx", None),
        P(None, "wt", "ctx", None),
        P(None, "wt", None),
        P("section", "wt"),
        P("section", "wt", None),
        P("section", None, "wt"),
        P("section", "wt"),
        P("section", None),
        P("section", None),
        P("section", None),
        P("section", "wt", None),
        P("section", "wt", None),
        P("section", "wt", None),
        P("section", "wt"),
        P("section", "wt", None),
        P("section", "wt", None),
    )
    return jax.shard_map(
        local,
        mesh=mesh,
        in_specs=placed,
        out_specs=(
            P("section", None, "wt", "ctx", None),
            P("section", None, "wt", "ctx", None),
            P("section", "wt"),
            P("section", "wt", None),
            P("section", None, "wt"),
            P("section", "wt"),
            P("section", None),
            P("section", None),
            P("section", None),
            P("section", "wt", None),
            P("section", "wt", None),
            P("section", "wt", None),
            P("section", "wt"),
            P("section", "wt", None),
            P("section", "wt", None),
        ),
        check_vma=False,
    )


f32, bf16 = jnp.float32, jnp.bfloat16
RH = MH // 4
RD = DS // 4
RQ = QD // 4
RF = FF // 4
RAW_AT = 2 * RD + 2 * NS
Q_AT = RAW_AT + 128
K_AT = Q_AT + RQ
INC = K_AT + 2 * HD
OUTR = RD + RQ
GROUP_A = INC + D // 2
GROUP_B = 2 * RF + D // 2
AXES = CORE, ROW, COL, LINE = tuple("cyxz")


def swapped(value, axis):
    return lax.ppermute(value, axis, [(0, 1), (1, 0)])


def across(value):
    return lax.ppermute(value, (ROW, COL), [(0, 3), (1, 2), (2, 1), (3, 0)])


def place(p):
    return ((p[0] * 2 + p[1]) * 2 + p[2]) * 4 + p[3]


def sent(value, pairs):
    return lax.ppermute(value, AXES, [(place(a), place(b)) for a, b in pairs])


every = [(c, y, x, z) for c in range(2) for y in range(2) for x in range(2) for z in range(4)]


def turned(value, by):
    return lax.ppermute(value, LINE, [(i, (i + by) % 4) for i in range(4)])


def paired_lines(value, by):
    return lax.ppermute(value, LINE, [(i, i ^ by) for i in range(4)])


def after(value, *others):
    return lax.optimization_barrier((value,) + others)[0]


def ordered(flag, own, other):
    return jnp.where(flag == 0, jnp.stack([own, other]), jnp.stack([other, own]))


def whole_rows(pair, y, x):
    own = lax.dynamic_index_in_dim(pair, y, 0, False)
    other = lax.dynamic_index_in_dim(pair, 1 - y, 0, False)
    near = ordered(x, own, swapped(own, COL))
    far = ordered(x, swapped(other, ROW), across(other))
    return ordered(y, near, far).reshape(4 * own.shape[0], own.shape[1])


def back_rows(rows, y, x):
    blocks = rows.reshape(2, 2, rows.shape[0] // 4, rows.shape[1])
    return ordered(y, blocks[y, x], swapped(blocks[1 - y, x], ROW))


def quarter_sum(keep, give):
    low = (keep.astype(f32) + swapped(give, CORE).astype(f32)).astype(bf16)
    both = (low.astype(f32) + swapped(low, COL).astype(f32)).astype(bf16)
    return both, swapped(both, CORE)


BLOCK = 128
REACH = 2
CONVR = RD + 2 * NS
OUT_BLOCKS = [(j, y, c) for j in range(2) for y, c in ((0, 0), (0, 1), (1, 0))] + [(0, 1, 1), (1, 1, 1)]
WIDE = D // 2
LIMIT = 56 << 20


def mm(left, right, dims=((1,), (0,)), precision=None):
    return lax.dot_general(left, right, (dims, ((), ())), precision=precision, preferred_element_type=f32)


NT = ((1,), (1,))
TN = ((0,), (0,))


def logistic(value):
    return 1.0 / (1.0 + jnp.exp(-value))


def slope(value, sig):
    return sig * (1.0 + value * (1.0 - sig))


def unit_scale(rows):
    return lax.rsqrt(jnp.mean(rows * rows, axis=-1, keepdims=True) + epsilon)


def conv_chunk(proj_ref, ck_ref, tok_ref, j):
    lanes = slice(128 * j, 128 * (j + 1))
    pre = proj_ref[:, RD + 128 * j : RD + 128 * (j + 1)].astype(f32)
    summed = ck_ref[4:5, lanes] + pre * ck_ref[3:4, lanes]
    for by in range(1, CONV):
        summed = summed + pltpu.roll(pre, by, 0) * (ck_ref[3 - by : 4 - by, lanes] * tok_ref[:, by : by + 1])
    return pre, summed


def step_sizes(proj_ref, hp_ref):
    stepped = proj_ref[:, RAW_AT : RAW_AT + 128].astype(f32) + hp_ref[0:1, :]
    dt = jnp.maximum(stepped, 0.0) + jnp.log1p(jnp.exp(-jnp.abs(stepped)))
    return stepped, dt


def running(dt, hp_ref, run_s, run_t):
    count = dt.shape[0]
    rate = -dt * hp_ref[1:2, :]
    until = (
        lax.broadcasted_iota(jnp.int32, (count, count), 0) >= lax.broadcasted_iota(jnp.int32, (count, count), 1)
    ).astype(f32)
    run = mm(until, rate, precision=highest)
    run_s[...] = run
    run_t[...] = run.T
    return rate


def spans(count):
    for i in range(count // BLOCK):
        start = BLOCK * max(0, i - REACH)
        yield slice(BLOCK * i, BLOCK * (i + 1)), slice(start, BLOCK * (i + 1)), start


def barred(tok_ref, idr_ref, rows, keys):
    shape = (rows.stop - rows.start, keys.stop - keys.start)
    query = lax.broadcasted_iota(jnp.int32, shape, 0) + rows.start
    key = lax.broadcasted_iota(jnp.int32, shape, 1) + keys.start
    ok = (query >= key) & (tok_ref[rows, 0:1] == idr_ref[0:1, keys])
    return jnp.where(ok, 0.0, masked_value)


def fed_chunk(dt, conv, j, count):
    lane = lax.broadcasted_iota(jnp.int32, (count, 128), 1)
    return jnp.where(lane < MP, dt[:, 2 * j : 2 * j + 1], dt[:, 2 * j + 1 : 2 * j + 2]) * conv


def split_rows(c_ref, keep_ref, give_ref, half, value):
    @pl.when(c_ref[0] == half)
    def _():
        keep_ref[...] = value

    @pl.when(c_ref[0] != half)
    def _():
        give_ref[...] = value


def first_kernel(
    c_ref, mid_ref, own_ref, other_ref, gain_ref, wi_ref, mine_ref, got_ref, ck_ref, hp_ref, tok_ref, idr_ref,
    keep_ref, give_ref, x_ref, proj_ref, state_ref, ga_ref, h_s, wo_ref,
    vals_s, bc_s, fed_s, run_s, run_t,
):
    count = mid_ref.shape[0]
    for b, (j, y, c) in enumerate(OUT_BLOCKS):
        rows = slice(128 * j + 64 * y, 128 * j + 64 * y + 64)
        wo_ref[64 * b : 64 * b + 64, :] = jnp.where(c_ref[0] == c, mine_ref[rows, :], got_ref[rows, :])
    for i in range(count // BLOCK):
        rows = slice(BLOCK * i, BLOCK * (i + 1))
        low = mid_ref[rows, :]
        if mid_ref.dtype == f32:
            low = (low + added_rows(c_ref, own_ref, other_ref, i, count)).astype(bf16)
        x_ref[rows, :] = low
        x = low.astype(f32)
        h_s[rows, :] = (x * unit_scale(x) * gain_ref[...]).astype(bf16)
    for at in range(0, INC, 256):
        cols = slice(at, min(at + 256, INC))
        proj_ref[:, cols] = mm(h_s[...], wi_ref[:, cols]).astype(bf16)
    stepped, dt = step_sizes(proj_ref, hp_ref)
    running(dt, hp_ref, run_s, run_t)
    for j in range(CONVR // 128):
        pre, summed = conv_chunk(proj_ref, ck_ref, tok_ref, j)
        conv = summed * logistic(summed)
        if j < RD // 128:
            vals_s[:, 128 * j : 128 * (j + 1)] = conv
            fed_s[:, 128 * j : 128 * (j + 1)] = fed_chunk(dt, conv, j, count).astype(bf16)
        else:
            bc_s[:, 128 * j - RD : 128 * (j + 1) - RD] = conv.astype(bf16)
    for rows, keys, start in spans(count):
        bar = barred(tok_ref, idr_ref, rows, keys)
        gram = mm(bc_s[rows, NS:], bc_s[keys, :NS], NT)
        for h in range(RH):
            lanes = slice(MP * h, MP * (h + 1))
            decay = jnp.exp(run_s[rows, h : h + 1] - run_t[h : h + 1, keys] + bar)
            state_ref[rows, lanes] = mm((gram * decay).astype(bf16), fed_s[keys, lanes])
        for h in range(RQ // HD):
            lanes = slice(Q_AT + HD * h, Q_AT + HD * (h + 1))
            scores = mm(proj_ref[rows, lanes], proj_ref[keys, K_AT : K_AT + HD], NT) * 0.125 + bar
            chances = jnp.exp(scores - jnp.max(scores, axis=-1, keepdims=True))
            probs = (chances / jnp.sum(chances, axis=-1, keepdims=True)).astype(bf16)
            ga_ref[rows, RD + HD * h : RD + HD * (h + 1)] = mm(
                probs, proj_ref[keys, K_AT + HD : K_AT + 2 * HD]
            ).astype(bf16)
        z = proj_ref[rows, :RD].astype(f32)
        ssm = state_ref[rows, :] + ck_ref[5:6, :RD] * vals_s[rows, :]
        ga_ref[rows, :RD] = (ssm * z * logistic(z)).astype(bf16)
    for half in range(2):
        rows = slice(count // 2 * half, count // 2 * (half + 1))
        split_rows(c_ref, keep_ref, give_ref, half, mm(ga_ref[rows, :], wo_ref[...]).astype(bf16))


def added_rows(c_ref, own_ref, other_ref, i, count):
    half, at = divmod(BLOCK * i, count // 2)
    rows = slice(at, at + BLOCK)
    return jnp.where(c_ref[0] == half, own_ref[rows, :], other_ref[rows, :]).astype(f32)


def second_kernel(
    c_ref, x_ref, own_ref, other_ref, gain_ref, wgu_ref, wd_ref,
    keep_ref, give_ref, mid_ref, h_ref, gu_ref, hid_ref,
):
    count = x_ref.shape[0]
    for i in range(count // BLOCK):
        rows = slice(BLOCK * i, BLOCK * (i + 1))
        mid = x_ref[rows, :].astype(f32) + added_rows(c_ref, own_ref, other_ref, i, count)
        mid_ref[rows, :] = mid
        h_ref[rows, :] = (mid * unit_scale(mid) * gain_ref[...]).astype(bf16)
    for at in range(0, RF, 256):
        cols = slice(at, at + 256)
        ups = slice(RF + at, RF + at + 256)
        gate = mm(h_ref[...], wgu_ref[:, cols])
        up = mm(h_ref[...], wgu_ref[:, ups])
        gu_ref[:, cols] = gate
        gu_ref[:, ups] = up
        hid_ref[:, cols] = (gate * logistic(gate) * up).astype(bf16)
    for half in range(2):
        rows = slice(count // 2 * half, count // 2 * (half + 1))
        split_rows(c_ref, keep_ref, give_ref, half, mm(hid_ref[rows, :], wd_ref[...]).astype(bf16))


def back_second_kernel(c_ref, cot_ref, gu_ref, wgu_ref, wd_ref, keep_ref, give_ref, gug_ref):
    count = cot_ref.shape[0]
    for at in range(0, RF, 256):
        cols = slice(at, at + 256)
        ups = slice(RF + at, RF + at + 256)
        hidden_grad = mm(cot_ref[...], wd_ref[cols, :], NT)
        gate, up = gu_ref[:, cols], gu_ref[:, ups]
        sig = logistic(gate)
        gug_ref[:, cols] = (hidden_grad * up * slope(gate, sig)).astype(bf16)
        gug_ref[:, ups] = (hidden_grad * gate * sig).astype(bf16)
    for half in range(2):
        rows = slice(count // 2 * half, count // 2 * (half + 1))
        split_rows(c_ref, keep_ref, give_ref, half, mm(gug_ref[rows, :], wgu_ref[...], NT).astype(bf16))


def norm_back_rows(rows, gain, grad):
    scale = unit_scale(rows)
    normed = rows * scale
    weighted = grad * gain
    back = scale * (weighted - normed * jnp.mean(weighted * normed, axis=-1, keepdims=True))
    return back, jnp.sum(grad * normed, axis=0, keepdims=True)


def back_first_kernel(
    c_ref, cot_ref, own_ref, other_ref, mid_ref, gain_ref, proj_ref, state_ref, ga_ref, wi_ref, wo_ref, ck_ref,
    hp_ref, tok_ref, idr_ref,
    keep_ref, give_ref, outk_ref, outg_ref, midg_ref, projg_ref, gaing_ref, convg_ref, headg_ref,
    low_ref, gag_s, vals_s, bc_s, fed_s, run_s, run_t, sg_s, fedg_s, bcg_s, kvg_s, valg_s,
):
    count = cot_ref.shape[0]
    gain_grad = jnp.zeros((1, D), f32)
    for i in range(count // BLOCK):
        rows = slice(BLOCK * i, BLOCK * (i + 1))
        back, more = norm_back_rows(
            mid_ref[rows, :], gain_ref[...], added_rows(c_ref, own_ref, other_ref, i, count)
        )
        gain_grad = gain_grad + more
        total = cot_ref[rows, :].astype(f32) + back
        midg_ref[rows, :] = total
        low_ref[rows, :] = total.astype(bf16)
    gaing_ref[...] = gain_grad
    for q in range(OUTR // 128):
        grad = mm(ga_ref[:, 128 * q : 128 * (q + 1)], low_ref[...], TN).astype(bf16)
        for b in (2 * q, 2 * q + 1):
            j, y, c = OUT_BLOCKS[b]
            rows = slice(128 * j + 64 * y, 128 * j + 64 * y + 64)
            part = grad[64 * (b % 2) : 64 * (b % 2) + 64, :]

            @pl.when(c_ref[0] == c)
            def _(rows=rows, part=part):
                outk_ref[rows, :] = part

            @pl.when(c_ref[0] != c)
            def _(rows=rows, part=part):
                outg_ref[rows, :] = part

    for at in range(0, OUTR, 256):
        cols = slice(at, at + 256)
        gag_s[:, cols] = mm(low_ref[...], wo_ref[cols, :], NT)
    stepped, dt = step_sizes(proj_ref, hp_ref)
    rate = running(dt, hp_ref, run_s, run_t)
    for j in range(CONVR // 128):
        lanes = slice(128 * j, 128 * (j + 1))
        pre, summed = conv_chunk(proj_ref, ck_ref, tok_ref, j)
        conv = summed * logistic(summed)
        if j < RD // 128:
            vals_s[:, lanes] = conv
            fed_s[:, lanes] = fed_chunk(dt, conv, j, count).astype(bf16)
            z = proj_ref[:, lanes].astype(f32)
            sig = logistic(z)
            skip = ck_ref[5:6, lanes]
            grad = gag_s[:, lanes]
            ssm = state_ref[:, lanes] + skip * conv
            projg_ref[:, lanes] = (grad * ssm * slope(z, sig)).astype(bf16)
            ssm_grad = grad * z * sig
            sg_s[:, lanes] = ssm_grad.astype(bf16)
            valg_s[:, lanes] = ssm_grad * skip
            convg_ref[5:6, lanes] = jnp.sum(ssm_grad * conv, axis=0, keepdims=True)
        else:
            bc_s[:, 128 * j - RD : 128 * (j + 1) - RD] = conv.astype(bf16)
    fedg_s[...] = jnp.zeros_like(fedg_s)
    bcg_s[:, :NS] = jnp.zeros((count, NS), f32)
    kvg_s[...] = jnp.zeros_like(kvg_s)
    for rows, keys, start in spans(count):
        bar = barred(tok_ref, idr_ref, rows, keys)
        gram = mm(bc_s[rows, NS:], bc_s[keys, :NS], NT)
        gram_grad = jnp.zeros_like(gram)
        for h in range(RH):
            lanes = slice(MP * h, MP * (h + 1))
            decay = jnp.exp(run_s[rows, h : h + 1] - run_t[h : h + 1, keys] + bar)
            grad = sg_s[rows, lanes]
            gram_grad = gram_grad + mm(grad, fed_s[keys, lanes], NT) * decay
            fedg_s[keys, lanes] += mm((gram * decay).astype(bf16), grad, TN)
        gram_low = gram_grad.astype(bf16)
        bcg_s[rows, NS:] = mm(gram_low, bc_s[keys, :NS])
        bcg_s[keys, :NS] += mm(gram_low, bc_s[rows, NS:], TN)
        for h in range(RQ // HD):
            lanes = slice(Q_AT + HD * h, Q_AT + HD * (h + 1))
            query, key = proj_ref[rows, lanes], proj_ref[keys, K_AT : K_AT + HD]
            scores = mm(query, key, NT) * 0.125 + bar
            chances = jnp.exp(scores - jnp.max(scores, axis=-1, keepdims=True))
            probs = chances / jnp.sum(chances, axis=-1, keepdims=True)
            grad = gag_s[rows, RD + HD * h : RD + HD * (h + 1)].astype(bf16)
            prob_grad = mm(grad, proj_ref[keys, K_AT + HD : K_AT + 2 * HD], NT)
            score_grad = probs * (prob_grad - jnp.sum(probs * prob_grad, axis=-1, keepdims=True))
            score_grad = score_grad.astype(bf16)
            projg_ref[rows, lanes] = (mm(score_grad, key) * 0.125).astype(bf16)
            kvg_s[keys, :HD] += mm(score_grad, query, TN) * 0.125
            kvg_s[keys, HD:] += mm(probs.astype(bf16), grad, TN)
    projg_ref[:, K_AT:] = kvg_s[...].astype(bf16)
    head_of = lax.broadcasted_iota(jnp.int32, (RD, 128), 0) // MP
    picks = (head_of == lax.broadcasted_iota(jnp.int32, (RD, 128), 1)).astype(f32)
    run_grad = mm(
        sg_s[...].astype(f32) * state_ref[...] - fed_s[...].astype(f32) * fedg_s[...], picks, precision=highest
    )
    shape = (count, count)
    later = (
        (lax.broadcasted_iota(jnp.int32, shape, 1) >= lax.broadcasted_iota(jnp.int32, shape, 0))
        & (tok_ref[:, 0:1] == idr_ref[0:1, :])
    ).astype(f32)
    rate_grad = mm(later, run_grad, precision=highest)
    dt_grad = mm(vals_s[...] * fedg_s[...], picks, precision=highest) - rate_grad * hp_ref[1:2, :]
    raw_grad = dt_grad * logistic(stepped)
    headg_ref[0:1, :] = jnp.sum(raw_grad, axis=0, keepdims=True)
    headg_ref[1:2, :] = jnp.sum(rate_grad * rate, axis=0, keepdims=True)
    lane = lax.broadcasted_iota(jnp.int32, raw_grad.shape, 1)
    projg_ref[:, RAW_AT : RAW_AT + 128] = jnp.where(lane < RH, raw_grad, 0.0).astype(bf16)
    for j in range(CONVR // 128):
        lanes = slice(128 * j, 128 * (j + 1))
        pre, summed = conv_chunk(proj_ref, ck_ref, tok_ref, j)
        if j < RD // 128:
            grad = valg_s[:, lanes] + fed_chunk(dt, fedg_s[:, lanes], j, count)
        else:
            grad = bcg_s[:, 128 * j - RD : 128 * (j + 1) - RD]
        grad = grad * slope(summed, logistic(summed))
        convg_ref[4:5, lanes] = jnp.sum(grad, axis=0, keepdims=True)
        convg_ref[3:4, lanes] = jnp.sum(grad * pre, axis=0, keepdims=True)
        total = grad * ck_ref[3:4, lanes]
        for by in range(1, CONV):
            kept = grad * tok_ref[:, by : by + 1]
            convg_ref[3 - by : 4 - by, lanes] = jnp.sum(kept * pltpu.roll(pre, by, 0), axis=0, keepdims=True)
            total = total + pltpu.roll(kept * ck_ref[3 - by : 4 - by, lanes], count - by, 0)
        projg_ref[:, RD + 128 * j : RD + 128 * (j + 1)] = total.astype(bf16)
    for half in range(2):
        rows = slice(count // 2 * half, count // 2 * (half + 1))
        split_rows(c_ref, keep_ref, give_ref, half, mm(projg_ref[rows, :], wi_ref[...], NT).astype(bf16))


def back_input_kernel(c_ref, x_ref, own_ref, other_ref, gain_ref, midg_ref, low_ref, gaing_ref):
    count = x_ref.shape[0]
    gain_grad = jnp.zeros((1, D), f32)
    for i in range(count // BLOCK):
        rows = slice(BLOCK * i, BLOCK * (i + 1))
        back, more = norm_back_rows(
            x_ref[rows, :].astype(f32), gain_ref[...], added_rows(c_ref, own_ref, other_ref, i, count)
        )
        gain_grad = gain_grad + more
        low_ref[rows, :] = (midg_ref[rows, :] + back).astype(bf16)
    gaing_ref[...] = gain_grad


def chosen(shape, source):
    lane = lax.broadcasted_iota(jnp.int32, shape, 1)
    return (lax.broadcasted_iota(jnp.int32, shape, 0) == source(lane)).astype(bf16)


def heads_from(x, width):
    return lambda d: d + x * width + jnp.where(d >= width, width, 0)


def steps_from(x, core):
    return lambda d: jnp.where(d < RH, 12 * core + 3 * x + d + jnp.where(d >= 3, 3, 0), -1)


def keys_from(core):
    return lambda d: HD * core + d + jnp.where(d >= HD, HD, 0)


def aligned(value, by):
    return pl.multiple_of(value, by)


def folded(ref, index, at, rows):
    ref[index + (slice(0, 64), slice(at, at + WIDE))] = rows[:, :WIDE]
    ref[index + (slice(64, 128), slice(at, at + WIDE))] = rows[:, WIDE:]


def prepare_kernel(c_ref, mi_ref, ai_ref, gu_ref, dn_ref, mo_ref, ao_ref, a_ref, b_ref):
    core, x = c_ref[0], c_ref[2]
    pick = chosen((2 * RD, RD), heads_from(x, RD // 2))
    pick_query = chosen((2 * RQ, RQ), heads_from(x, HD))
    for t in range(2):
        slot = lax.rem(core + t, 2)
        pick_step = chosen((MH, 128), steps_from(x, t))
        pick_key = chosen((2 * KVD, 2 * HD), keys_from(t))
        for y in range(2):
            rows = slice(128 * y, 128 * (y + 1))

            def put(at, value):
                a_ref[slot, y, :, at : at + value.shape[1]] = value.astype(bf16)

            for h in range(2):
                put(RD * h, mm(mi_ref[DS * h + 2 * RD * t : DS * h + 2 * RD * (t + 1), rows], pick, TN))
            put(2 * RD, mi_ref[2 * DS : 2 * DS + 2 * NS, rows].T)
            put(RAW_AT, mm(mi_ref[DS + CONVD :, rows], pick_step, TN))
            put(Q_AT, mm(ai_ref[rows, 2 * RQ * t : 2 * RQ * (t + 1)], pick_query))
            put(K_AT, mm(ai_ref[rows, QD:], pick_key))
            for h in range(8):
                at = aligned(RF * h + 256 * t + 128 * x, 128)
                b_ref[slot, y, :, 128 * h : 128 * (h + 1)] = gu_ref[rows, pl.ds(at, 128)]
            at = aligned(256 * t + 128 * x + 64 * y, 64)
            folded(b_ref, (slot, y), 2 * RF, dn_ref[pl.ds(at, 64), :])
        half = RD // 2
        folded(a_ref, (slot, 0), INC, mo_ref[pl.ds(aligned(half * x + 64 * t, 64), 64), :])
        last = mo_ref[pl.ds(aligned(half * x + 128, 64), 64), :] if t == 0 else ao_ref[pl.ds(aligned(64 * x, 64), 64), :]
        folded(a_ref, (slot, 1), INC, last)


def sources(c_ref, own, keep_ref, got_ref, near, far):
    y, z = c_ref[1], c_ref[3]
    for k in range(2):
        yield z, k, lambda *at, k=k: jnp.where(c_ref[0] == own, keep_ref[(0, k) + at], got_ref[(k,) + at])
    for k in range(3):
        line = lax.rem(z + 3 - k, 4)
        yield line, y, lambda *at, k=k: near[k][at]
        yield line, 1 - y, lambda *at, k=k: far[k][at]


def unpack_a_kernel(own, c_ref, keep_ref, got_ref, n0, n1, n2, f0, f1, f2, wi_ref, mine_ref, give_ref):
    parts = sources(c_ref, own, keep_ref, got_ref, (n0, n1, n2), (f0, f1, f2))
    unpack_a_from(c_ref, parts, wi_ref, mine_ref, give_ref)


def unpack_a_from(c_ref, parts, wi_ref, mine_ref, give_ref):
    for line, y, load in parts:
        wi_ref[pl.ds(aligned(256 * line + 128 * y, 128), 128), :] = load(slice(None), slice(0, INC))
        rows = pl.ds(aligned(128 * lax.rem(line, 2) + 64 * y, 64), 64)
        left = load(slice(0, 64), slice(INC, GROUP_A))
        right = load(slice(64, 128), slice(INC, GROUP_A))

        @pl.when(line // 2 == c_ref[0])
        def _(rows=rows, left=left, right=right):
            mine_ref[rows, :WIDE] = left
            mine_ref[rows, WIDE:] = right

        @pl.when(line // 2 != c_ref[0])
        def _(rows=rows, left=left, right=right):
            give_ref[rows, :WIDE] = left
            give_ref[rows, WIDE:] = right


def halves_of(c_ref, keep_ref, got_ref, near_ref, far_ref):
    y, z = c_ref[1], c_ref[3]
    for k in range(4):
        line = lax.rem(z + k, 4)
        yield line, y, lambda *at, line=line: near_ref[(line,) + at]
        if k == 0:
            yield line, 1 - y, lambda *at: jnp.where(
                c_ref[0] == 1, keep_ref[(0, 1 - y) + at], got_ref[(1 - y,) + at]
            )
        else:
            yield line, 1 - y, lambda *at, k=k: far_ref[(k - 1,) + at]


def lines_a_kernel(c_ref, keep_ref, got_ref, near_ref, far_ref, wi_ref, mine_ref, give_ref):
    unpack_a_from(c_ref, halves_of(c_ref, keep_ref, got_ref, near_ref, far_ref), wi_ref, mine_ref, give_ref)


def lines_b_kernel(c_ref, keep_ref, got_ref, near_ref, far_ref, wgu_ref, wd_ref):
    unpack_b_from(halves_of(c_ref, keep_ref, got_ref, near_ref, far_ref), wgu_ref, wd_ref)


def unpack_b_kernel(own, c_ref, keep_ref, got_ref, n0, n1, n2, f0, f1, f2, wgu_ref, wd_ref):
    unpack_b_from(sources(c_ref, own, keep_ref, got_ref, (n0, n1, n2), (f0, f1, f2)), wgu_ref, wd_ref)


def unpack_b_from(parts, wgu_ref, wd_ref):
    for line, y, load in parts:
        wgu_ref[pl.ds(aligned(256 * line + 128 * y, 128), 128), :] = load(slice(None), slice(0, 2 * RF))
        rows = pl.ds(aligned(128 * line + 64 * y, 64), 64)
        wd_ref[rows, :WIDE] = load(slice(0, 64), slice(2 * RF, GROUP_B))
        wd_ref[rows, WIDE:] = load(slice(64, 128), slice(2 * RF, GROUP_B))


def split_halves(c_ref, y, line, refs, width, value, folds):
    def put(ref, index):
        ref[index + (slice(None), slice(0, width))] = value
        folded(ref, index, width, folds)

    if len(refs) == 1:
        put(refs[0], (line, y))
        return
    for k, ref in enumerate(refs):

        @pl.when((c_ref[1] == y) if k == 0 else (c_ref[1] != y))
        def _(ref=ref):
            put(ref, (line,))


def grads_b_kernel(c_ref, h_ref, gug_ref, hid_ref, cot_ref, *refs):
    for line in range(4):
        down = mm(hid_ref[:, 128 * line : 128 * (line + 1)], cot_ref[...], TN).astype(bf16)
        for y in range(2):
            at = 256 * line + 128 * y
            grad = mm(h_ref[:, at : at + 128], gug_ref[...], TN).astype(bf16)
            split_halves(c_ref, y, line, refs, 2 * RF, grad, down[64 * y : 64 * (y + 1), :])


def grads_a_kernel(c_ref, h_ref, projg_ref, mine_ref, got_ref, *refs):
    for line in range(4):
        for y in range(2):
            at = 256 * line + 128 * y
            grad = mm(h_ref[:, at : at + 128], projg_ref[...], TN).astype(bf16)
            rows = slice(128 * (line % 2) + 64 * y, 128 * (line % 2) + 64 * y + 64)
            out = jnp.where(c_ref[0] == line // 2, mine_ref[rows, :], got_ref[rows, :])
            split_halves(c_ref, y, line, refs, INC, grad, out)


def lines_kernel(c_ref, keep_ref, got_ref, own_ref, one_ref, two_ref, three_ref):
    for k, ref in enumerate((own_ref, one_ref, two_ref, three_ref)):
        line = lax.rem(c_ref[3] + k, 4)
        ref[...] = (keep_ref[line].astype(f32) + got_ref[line].astype(f32)).astype(bf16)


def final_b_kernel(c_ref, near, far, q0, q1, q2, q3, gu_ref, dn_ref):
    @pl.when(c_ref[0] == 0)
    def _():
        final_b_of(c_ref, [near.at[0], near.at[1], far.at[0], far.at[1]], gu_ref, dn_ref)

    @pl.when(c_ref[0] == 1)
    def _():
        final_b_of(c_ref, [q0, q1, q2, q3], gu_ref, dn_ref)


def final_b_of(c_ref, refs, gu_ref, dn_ref):
    for i, ref in enumerate(refs):
        y, x = lax.rem(c_ref[1] + i // 2, 2), lax.rem(c_ref[2] + i, 2)
        rows = pl.ds(aligned(128 * y, 128), 128)
        for t in range(2):
            for h in range(8):
                at = aligned(RF * h + 256 * t + 128 * x, 128)
                gu_ref[rows, pl.ds(at, 128)] = ref[t, :, 128 * h : 128 * (h + 1)].astype(f32)
            down = pl.ds(aligned(256 * t + 128 * x + 64 * y, 64), 64)
            dn_ref[down, :WIDE] = ref[t, :64, 2 * RF : GROUP_B].astype(f32)
            dn_ref[down, WIDE:] = ref[t, 64:, 2 * RF : GROUP_B].astype(f32)


def final_a_kernel(c_ref, p0, p1, p2, p3, near, far, mi_ref, ai_ref, mo_ref, ao_ref):
    @pl.when(c_ref[0] == 0)
    def _():
        final_a_of(c_ref, p0, p1, p2, p3, mi_ref, ai_ref, mo_ref, ao_ref)

    @pl.when(c_ref[0] == 1)
    def _():
        final_a_of(c_ref, near.at[0], near.at[1], far.at[0], far.at[1], mi_ref, ai_ref, mo_ref, ao_ref)


def final_a_of(c_ref, p0, p1, p2, p3, mi_ref, ai_ref, mo_ref, ao_ref):
    for i in range(2):
        y = lax.rem(c_ref[1] + i, 2)
        rows = pl.ds(aligned(128 * y, 128), 128)
        shared = jnp.zeros((128, 2 * NS), f32)
        steps = jnp.zeros((MH, 128), f32)
        keys = jnp.zeros((128, 2 * KVD), f32)
        for t in range(2):
            gate = jnp.zeros((2 * RD, 128), f32)
            vals = jnp.zeros((2 * RD, 128), f32)
            query = jnp.zeros((128, 2 * RQ), f32)
            for k in range(2):
                ref = (p0, p1, p2, p3)[2 * i + k]
                x = lax.rem(c_ref[2] + k, 2)
                pick = chosen((2 * RD, RD), heads_from(x, RD // 2))
                gate = gate + mm(pick, ref[t, :, :RD], NT)
                vals = vals + mm(pick, ref[t, :, RD : 2 * RD], NT)
                shared = shared + ref[t, :, 2 * RD : RAW_AT].astype(f32)
                steps = steps + mm(chosen((MH, 128), steps_from(x, t)), ref[t, :, RAW_AT:Q_AT], NT)
                query = query + mm(ref[t, :, Q_AT:K_AT], chosen((2 * RQ, RQ), heads_from(x, HD)), NT)
                keys = keys + mm(ref[t, :, K_AT:INC], chosen((2 * KVD, 2 * HD), keys_from(t)), NT)
                left, right = ref[t, :64, INC:].astype(f32), ref[t, 64:, INC:].astype(f32)
                half = RD // 2

                def put(out_ref, at, left=left, right=right):
                    out_ref[pl.ds(aligned(at, 64), 64), :WIDE] = left
                    out_ref[pl.ds(aligned(at, 64), 64), WIDE:] = right

                @pl.when(y == 0)
                def _(put=put, x=x, t=t):
                    put(mo_ref, half * x + 64 * t)

                @pl.when(y == 1)
                def _(put=put, x=x, t=t):
                    if t == 0:
                        put(mo_ref, half * x + 128)
                    else:
                        put(ao_ref, 64 * x)

            mi_ref[2 * RD * t : 2 * RD * (t + 1), rows] = gate
            mi_ref[DS + 2 * RD * t : DS + 2 * RD * (t + 1), rows] = vals
            ai_ref[rows, 2 * RQ * t : 2 * RQ * (t + 1)] = query
        mi_ref[2 * DS : 2 * DS + 2 * NS, rows] = shared.T
        mi_ref[DS + CONVD :, rows] = steps
        ai_ref[rows, QD:] = keys


def on_chip(kernel, c, inputs, outs, scratch=(), micros=2):
    inside = pl.BlockSpec(memory_space=pltpu.VMEM)
    return pl.pallas_call(
        kernel,
        in_specs=[pl.BlockSpec(memory_space=pltpu.SMEM)] + [inside] * len(inputs),
        out_specs=[inside] * len(outs),
        out_shape=[jax.ShapeDtypeStruct(*o) for o in outs],
        scratch_shapes=[pltpu.VMEM(*s) for s in scratch],
        compiler_params=pltpu.CompilerParams(vmem_limit_bytes=LIMIT),
        cost_estimate=pl.CostEstimate(flops=micros * 10**9, bytes_accessed=micros * 3 * 10**6, transcendentals=0),
    )(c, *inputs)


def all_lines(values, z):
    got = [turned(values, k) for k in (1, 2, 3)]
    lines = jnp.zeros((4,) + values.shape, f32)
    for k, piece in enumerate([values] + got):
        lines = lax.dynamic_update_index_in_dim(lines, piece, (z - k) % 4, 0)
    return lines, got


def small_parameters(packed, c, x):
    quarter = CONVD // 4
    cut = lax.dynamic_slice_in_dim

    def heads(values, width):
        parts = cut(values, c * 12 * width, 12 * width, values.ndim - 1)
        parts = [cut(parts, (6 * j + 3 * x) * width, 3 * width, values.ndim - 1) for j in range(2)]
        return jnp.concatenate(parts, axis=-1)

    result = []
    for s in range(2):
        one = packed[s]
        conv = one[:, : 5 * quarter].reshape(4, 5, quarter).transpose(1, 0, 2).reshape(5, CONVD)
        conv = jnp.concatenate([heads(conv[:, :DS], MP), conv[:, DS:]], axis=1)
        at = 5 * quarter
        gains = one[:, at : at + 512].reshape(4, 2, 256).transpose(1, 0, 2).reshape(2, D)
        at += 512
        per_head = heads(one[0, at : at + 3 * MH].reshape(3, MH), 1)
        skip = jnp.pad(jnp.repeat(per_head[2], MP), (0, CONVR - RD))
        conv = jnp.pad(jnp.concatenate([conv, skip[None]], axis=0), ((0, 2), (0, 0)))
        per_head = jnp.pad(jnp.stack([per_head[0], jnp.exp(per_head[1])]), ((0, 6), (0, 128 - RH)))
        result.append((gains[0:1], gains[1:2], conv, per_head))
    return result


def small_gradients(conv_grad, head_grad, first_grad, second_grad, c, x):
    def heads(values, width):
        out = jnp.zeros(values.shape[:-1] + (MH * width,), f32)
        for j in range(2):
            part = values[..., 3 * width * j : 3 * width * (j + 1)]
            out = lax.dynamic_update_slice_in_dim(out, part, (12 * c + 6 * j + 3 * x) * width, values.ndim - 1)
        return out

    first = ((c == 0) & (x == 0)).astype(f32)
    wide = jnp.concatenate([heads(conv_grad[:5, :RD], MP), conv_grad[:5, RD:]], axis=1)
    skip = conv_grad[5, :RD].reshape(RH, MP).sum(axis=1)
    per_head = heads(jnp.stack([head_grad[0, :RH], head_grad[1, :RH], skip]), 1)
    flat = jnp.concatenate([wide.reshape(-1), first_grad[0] * first, second_grad[0] * first, per_head.reshape(-1)])
    return jnp.pad(flat, (0, 88 * 128 - flat.shape[0])).reshape(88, 128)


def summed_small(grads, c, last):
    total = jnp.where(c == 0, grads[0], grads[1]) + swapped(jnp.where(c == 0, grads[1], grads[0]), CORE)
    total = total + swapped(total, COL)
    total = after(total + swapped(total, ROW), last)
    total = total + paired_lines(total, 1)
    return total + paired_lines(total, 2)


def paired(
    block_input,
    output_grad,
    doc_lengths,
    first_gain,
    mixer_in,
    conv_kernel,
    conv_bias,
    step_bias,
    decay_log,
    skip_gain,
    mixer_out,
    attention_in,
    attention_out,
    second_gain,
    gate_up,
    down_weight,
):
    c, y, x, z = (lax.axis_index(a) for a in AXES)
    at = jnp.stack([c, y, x, z]).astype(jnp.int32)
    cut = lax.dynamic_slice_in_dim
    quarter = CONVD // 4

    lead = jnp.concatenate(
        [
            conv_kernel[0].astype(f32).reshape(-1),
            conv_bias[0].astype(f32),
            first_gain[0].astype(f32),
            second_gain[0].astype(f32),
            step_bias[0],
            decay_log[0],
            skip_gain[0],
        ]
    )
    lead = jnp.pad(lead, (0, 24 * 128 - lead.shape[0])).reshape(24, 128)
    lines, lines_got = all_lines(lead, z)

    keep_a, keep_b = on_chip(
        prepare_kernel,
        at,
        (mixer_in[0].T, attention_in[0], gate_up[0], down_weight[0], mixer_out[0], attention_out[0]),
        [((2, 2, 128, GROUP_A), bf16), ((2, 2, 128, GROUP_B), bf16)],
    )
    got_a = swapped(keep_a[1], CORE)
    got_b = swapped(keep_b[1], CORE)

    def halves(keep, got, s):
        return jnp.where(c == s, lax.dynamic_index_in_dim(keep[0], y, 0, False), lax.dynamic_index_in_dim(got, y, 0, False))

    def lines_of(half):
        one, three = turned(half, 1), turned(half, 3)
        return [one, turned(after(half, one, three), 2), three]

    half_a0 = after(halves(keep_a, got_a, 0), *lines_got)
    near_a0 = lines_of(half_a0)
    rows_in = jnp.concatenate([block_input[:, 0], output_grad[:, 0]], axis=2)
    rows_in = after(rows_in, half_a0)
    whole = whole_rows(rows_in, y, x)
    x0, cot = whole[:, :D], whole[:, D:]
    lines = after(lines, half_a0)
    smalls = small_parameters(ordered(c, lines, swapped(lines, CORE)).reshape(2, 4, -1), c, x)
    doc_sizes = lax.dynamic_index_in_dim(doc_lengths[:, 0], y, 0, False)
    length = x0.shape[0]
    positions = jnp.arange(length, dtype=jnp.int32)
    ids = doc_layout(doc_sizes, positions)[0]
    taps = [(positions >= by) & (jnp.roll(ids, by) == ids) for by in range(1, CONV)]
    tok = jnp.pad(jnp.stack([ids.astype(f32)] + [t.astype(f32) for t in taps], axis=1), ((0, 0), (0, 128 - CONV)))
    idr = jnp.broadcast_to(ids.astype(f32)[None], (8, length))
    half = length // 2
    partial = [((half, D), bf16), ((half, D), bf16)]

    def far_of(near, *waits):
        return [swapped(after(n, *waits), ROW) for n in near]

    def others(lines):
        return jnp.stack([lax.dynamic_index_in_dim(lines, (z + k) % 4, 0, False) for k in (1, 2, 3)])

    def unpack_a(s, near, far):
        wi, mine, give = on_chip(
            functools.partial(unpack_a_kernel, s),
            at,
            (keep_a, got_a, *near, *far),
            [((D, INC), bf16), ((256, D), bf16), ((256, D), bf16)],
        )
        return wi, mine, swapped(give, CORE)

    def unpack_b(s, near, far):
        return on_chip(
            functools.partial(unpack_b_kernel, s),
            at,
            (keep_b, got_b, *near, *far),
            [((D, 2 * RF), bf16), ((RF, D), bf16)],
        )

    def first_part(entry, own, other, s, wi, mine, got):
        gain, _, conv, per_head = smalls[s]
        return on_chip(
            first_kernel,
            at,
            (entry, own, other, gain, wi, mine, got, conv, per_head, tok, idr),
            partial
            + [
                ((length, D), bf16),
                ((length, INC), bf16),
                ((length, RD), f32),
                ((length, OUTR), bf16),
                ((length, D), bf16),
                ((OUTR, D), bf16),
            ],
            [
                ((length, RD), f32),
                ((length, 2 * NS), bf16),
                ((length, RD), bf16),
                ((length, 128), f32),
                ((128, length), f32),
            ],
            15,
        )

    def second_part(entry, own, other, s, wgu, wd):
        return on_chip(
            second_kernel,
            at,
            (entry, own, other, smalls[s][1], wgu, wd),
            partial
            + [((length, D), f32), ((length, D), bf16), ((length, 2 * RF), f32), ((length, RF), bf16)],
            micros=8,
        )

    far_a0 = far_of(near_a0, whole)
    near_b0 = lines_of(after(halves(keep_b, got_b, 0), *near_a0))
    wi0, mine, got = unpack_a(0, near_a0, [after(f, *near_b0) for f in far_a0])
    lines_a1 = lax.all_gather(after(halves(keep_a, got_a, 1), *near_a0), LINE)
    lines_b1 = lax.all_gather(after(halves(keep_b, got_b, 1), lines_a1), LINE)
    far_b0 = far_of(near_b0)
    keep, give, x0, proj0, state0, ga0, h0, wo0 = first_part(x0, smalls[0][0], smalls[0][0], 0, wi0, mine, got)
    give = after(give, *far_b0)
    own, other = quarter_sum(keep, give)
    wgu0, wd0 = unpack_b(0, near_b0, far_b0)
    keep, give, mid0, g0, gu0, hid0 = second_part(x0, own, other, 0, wgu0, wd0)
    give = after(give, lines_a1)
    far_a1 = swapped(others(lines_a1), ROW)
    own, other = quarter_sum(keep, give)
    wi1, mine, give_out = on_chip(
        lines_a_kernel, at, (keep_a, got_a, lines_a1, far_a1), [((D, INC), bf16), ((256, D), bf16), ((256, D), bf16)]
    )
    got = swapped(give_out, CORE)
    keep, give, x1, proj1, state1, ga1, h1, wo1 = first_part(mid0, own, other, 1, wi1, mine, got)
    far_b1 = swapped(others(lines_b1), ROW)
    own, other = quarter_sum(keep, give)
    wgu1, wd1 = on_chip(lines_b_kernel, at, (keep_b, got_b, lines_b1, far_b1), [((D, 2 * RF), bf16), ((RF, D), bf16)])
    late_keep, late_give, mid1, g1, gu1, hid1 = second_part(x1, own, other, 1, wgu1, wd1)

    def back_second(cot, s, gu, wgu, wd):
        return on_chip(
            back_second_kernel, at, (cot, gu, wgu, wd), partial + [((length, 2 * RF), bf16)], micros=7
        )

    def back_first(cot, own, other, s, mid, proj, state, ga, wi, wo):
        gain, conv, per_head = smalls[s][1:]
        return on_chip(
            back_first_kernel,
            at,
            (cot, own, other, mid, gain, proj, state, ga, wi, wo, conv, per_head, tok, idr),
            partial
            + [
                ((256, D), bf16),
                ((256, D), bf16),
                ((length, D), f32),
                ((length, INC), bf16),
                ((1, D), f32),
                ((8, CONVR), f32),
                ((8, 128), f32),
            ],
            [
                ((length, D), bf16),
                ((length, OUTR), f32),
                ((length, RD), f32),
                ((length, 2 * NS), bf16),
                ((length, RD), bf16),
                ((length, 128), f32),
                ((128, length), f32),
                ((length, RD), bf16),
                ((length, RD), f32),
                ((length, 2 * NS), f32),
                ((length, 2 * HD), f32),
                ((length, RD), f32),
            ],
            25,
        )

    def back_input(s, entry, own, other, mid_grad):
        return on_chip(
            back_input_kernel,
            at,
            (entry, own, other, smalls[s][0], mid_grad),
            [((length, D), bf16), ((1, D), f32)],
            micros=4,
        )

    def shapes(split, columns):
        return [((4, 128, columns), bf16)] * 2 if split else [((4, 2, 128, columns), bf16)]

    def grads_b(split, *inputs):
        return on_chip(grads_b_kernel, at, inputs, shapes(split, GROUP_B), micros=5)

    def grads_a(split, h, proj_grad, mine, give):
        inputs = (h, proj_grad, mine, swapped(give, CORE))
        return on_chip(grads_a_kernel, at, inputs, shapes(split, GROUP_A), micros=5)

    def scattered(grads):
        grads = grads[0]
        return lax.psum_scatter(grads.reshape(8, 128, grads.shape[3]), (LINE, ROW), scatter_dimension=0)

    def row_sent(grads):
        return swapped(grads[1], ROW)

    def line_sent(grads, got):
        columns = got.shape[2]
        own, one, two, three = on_chip(lines_kernel, at, (grads[0], got), [((128, columns), bf16)] * 4)
        one, three = turned(one, 1), turned(three, 3)
        return own, [one, turned(after(two, one, three), 2), three]

    def line_summed(own, parts):
        return sum([p.astype(f32) for p in parts], own.astype(f32)).astype(bf16)

    def spread_two(first, second, *waits):
        block = ordered(c, jnp.where(c == 0, first, second), swapped(jnp.where(c == 0, second, first), CORE))
        block = after(block, *waits)
        near = jnp.stack([block, swapped(block, COL)])
        return near, swapped(near, ROW)

    def spread_one(piece, s):
        given = sent(piece, [(p, (s,) + p[1:]) for p in every if p[0] != s])
        block = jnp.stack([piece, given] if s == 0 else [given, piece])
        mine = [p for p in every if p[0] == s]
        flips = [[(p, (s, p[1] ^ i, p[2] ^ k, p[3])) for p in mine] for i, k in ((0, 1), (1, 0), (1, 1))]
        return [block] + [sent(block, f) for f in flips]

    cot1 = cot
    keep, give, gu_grad = back_second(cot1, 1, gu1, wgu1, wd1)
    own, other = quarter_sum(keep, give)
    late_give = after(late_give, own)
    late, late_other = quarter_sum(late_keep, late_give)
    sum_b1 = scattered(grads_b(False, g1, gu_grad, hid1, cot1))
    keep, give, mine, give_out, mid_grad, proj_grad, second1, conv1, head1 = back_first(
        cot1, own, other, 1, mid1, proj1, state1, ga1, wi1, wo1
    )
    give = after(give, late)
    own, other = quarter_sum(keep, give)
    sum_a1 = scattered(grads_a(False, h1, proj_grad, mine, give_out))
    cot0, first1 = back_input(1, x1, own, other, mid_grad)
    keep, give, gu_grad = back_second(cot0, 0, gu0, wgu0, wd0)
    own, other = quarter_sum(keep, give)
    gb0 = grads_b(True, g0, gu_grad, hid0, cot0)
    gb0_got = row_sent(gb0)
    keep, give, mine, give_out, mid_grad, proj_grad, second0, conv0, head0 = back_first(
        cot0, own, other, 0, mid0, proj0, state0, ga0, wi0, wo0
    )
    plane_b1 = spread_one(sum_b1, 1)
    give = after(give, *plane_b1[1:])
    ga0_ = grads_a(True, h0, proj_grad, mine, give_out)
    ga0_got = row_sent(ga0_)
    sum_b0 = line_sent(gb0, after(gb0_got, ga0_[0]))
    b0 = line_summed(*sum_b0)
    sum_a0 = line_sent(ga0_, after(ga0_got, b0))
    own, other = quarter_sum(keep, after(give, sum_a0[0]))
    low0, first0 = back_input(0, x0, own, other, mid_grad)
    plane_two = spread_two(jnp.pad(b0, ((0, 0), (0, GROUP_A - GROUP_B))), sum_a1, sum_a0[0])
    gate_up_grad, down_grad = on_chip(
        final_b_kernel, at, (*plane_two, *plane_b1), [((256, 2 * FF), f32), ((RF, D), f32)], micros=4
    )
    a0 = line_summed(sum_a0[0], [after(p, *plane_two, first0) for p in sum_a0[1]])
    plane_a0 = spread_one(a0, 0)
    mixer_in_grad, attention_in_grad, mixer_out_grad, attention_out_grad = on_chip(
        final_a_kernel,
        at,
        (*plane_a0, *plane_two),
        [((DS + CONVD + MH, 256), f32), ((256, QD + 2 * KVD), f32), ((RD, D), f32), ((128, D), f32)],
        micros=4,
    )

    out1 = (mid1 + ordered(c, late, late_other).reshape(length, D).astype(f32)).astype(bf16)
    section_output = back_rows(jnp.where(c == 0, x1, out1), y, x)
    input_grad = back_rows(jnp.where(c == 0, low0, cot0), y, x)
    grads = [small_gradients(conv0, head0, first0, second0, c, x), small_gradients(conv1, head1, first1, second1, c, x)]
    grads = [after(g, sum_a0[0]) for g in grads]
    sums = summed_small(grads, c, a0).reshape(-1)
    wide = sums[: 5 * CONVD].reshape(5, CONVD)
    start = 5 * CONVD
    conv_out = cut(wide, z * quarter, quarter, 1)
    first_out = cut(sums[start : start + D], z * 256, 256, 0)
    second_out = cut(sums[start + D : start + 2 * D], z * 256, 256, 0)
    head_out = sums[start + 2 * D : start + 2 * D + 3 * MH].reshape(3, MH)
    return (
        section_output[None, :, None],
        input_grad[None, :, None],
        first_out[None],
        mixer_in_grad.T[None],
        conv_out[None, :4],
        conv_out[None, 4],
        head_out[None, 0],
        head_out[None, 1],
        head_out[None, 2],
        mixer_out_grad[None],
        attention_in_grad[None],
        attention_out_grad[None],
        second_out[None],
        gate_up_grad[None],
        down_grad[None],
    )


def paired_specs():
    plane = (ROW, COL)
    rows = P(CORE, LINE, None)
    placed = (
        P(None, LINE, plane, None),
        P(None, LINE, plane, None),
        P(None, LINE, None),
        P(CORE, LINE),
        rows,
        P(CORE, None, LINE),
        P(CORE, LINE),
        P(CORE, None),
        P(CORE, None),
        P(CORE, None),
        rows,
        rows,
        rows,
        P(CORE, LINE),
        rows,
        rows,
    )
    given = (
        P(CORE, None, LINE, plane, None),
        P(CORE, None, LINE, plane, None),
        P(CORE, LINE),
        rows,
        P(CORE, None, LINE),
        P(CORE, LINE),
        P(CORE, None),
        P(CORE, None),
        P(CORE, None),
        rows,
        rows,
        rows,
        P(CORE, LINE),
        rows,
        rows,
    )
    return placed, given


def solution(mesh):
    if tuple(mesh.devices.shape) == (2, 4, 4):
        fine = Mesh(mesh.devices.reshape(2, 2, 2, 4), AXES)
        placed, given = paired_specs()
        return jax.shard_map(paired, mesh=fine, in_specs=placed, out_specs=given, check_vma=False)
    return spread(mesh)
```

```python
import functools
import math

import jax
import jax.numpy as jnp
from jax import lax
from jax.experimental import pallas as pl
from jax.experimental.pallas import tpu as pltpu
from jax.sharding import Mesh, PartitionSpec as P

D = 1024
FF = 2048
MH = 24
MP = 64
NS = 128
QH = 8
KVH = 2
HD = 64
CONV = 4
MICRO = 2
SPAN = 128
KEY_BLOCK = 1024
DS = 1536
CONVD = 1792
QD = 512
KVD = 128


epsilon = 1e-05
masked_value = -1e30
highest = lax.Precision.HIGHEST
weight_names = (
    "first_gain",
    "mixer_in",
    "conv_kernel",
    "conv_bias",
    "mixer_out",
    "attention_in",
    "attention_out",
    "second_gain",
    "gate_up",
    "down_weight",
)


def passed_along(value, axis, by):
    length = lax.axis_size(axis)
    pairs = [(i, i + by) for i in range(length) if 0 <= i + by < length]
    return lax.ppermute(value, axis, pairs)


def prefix(value, axis, combine, identity):
    length, position = (lax.axis_size(axis), lax.axis_index(axis))
    everything = jax.tree.map(
        lambda part, kind: lax.all_gather(part.astype(kind), axis),
        value,
        (jnp.bfloat16, jnp.bfloat16),
    )
    start = jax.tree.map(
        lambda part, zero: jnp.broadcast_to(jnp.asarray(zero, part.dtype), part.shape),
        value,
        identity,
    )

    def step(k, before):
        reached = k < position
        new = combine(
            before, jax.tree.map(lambda part, own: part[k].astype(own.dtype), everything, value)
        )
        return jax.tree.map(lambda a, b: jnp.where(reached, a, b), new, before)

    return lax.fori_loop(0, length, step, start)


def prefix_2(value, axis, join, neutral):
    count = lax.axis_size(axis)
    place = lax.axis_index(axis)
    ahead = count - 1 - place
    gathered = jax.tree.map(
        lambda a, kind: lax.all_gather(a.astype(kind), axis),
        value,
        jax.tree.map(lambda a: jnp.bfloat16 if a.dtype == jnp.float32 else a.dtype, value),
    )
    state = jax.tree.map(lambda a, e: jnp.zeros_like(a) + jnp.asarray(e, a.dtype), value, neutral)

    def one(step, state):
        source = count - 1 - step
        return join(
            state,
            jax.tree.map(
                lambda a, own: lax.dynamic_index_in_dim(a, source, 0, False).astype(own.dtype),
                gathered,
                value,
            ),
        )

    return lax.fori_loop(0, ahead, one, state)


def inner_rows(left, right):
    return lax.dot_general(
        left, right, (((0,), (0,)), ((), ())), preferred_element_type=jnp.float32
    )


def outer_cols(left, right):
    return lax.dot_general(
        left, right, (((1,), (1,)), ((), ())), preferred_element_type=jnp.float32
    )


def norm_apply(hidden_in, gain_vec):
    return (
        hidden_in
        * lax.rsqrt(jnp.mean(hidden_in * hidden_in, axis=-1, keepdims=True) + epsilon)
        * gain_vec
    )


def norm_back(hidden_in, gain_vec, upstream):
    scale = lax.rsqrt(jnp.mean(hidden_in * hidden_in, axis=-1, keepdims=True) + epsilon)
    normed = hidden_in * scale
    weighted = upstream * gain_vec
    hidden_grad = scale * (weighted - normed * jnp.mean(weighted * normed, axis=-1, keepdims=True))
    return (hidden_grad, jnp.sum(upstream * normed, axis=0))


def running_sum(value):
    count = value.shape[0]
    until = lax.broadcasted_iota(jnp.int32, (count, count), 0) >= lax.broadcasted_iota(
        jnp.int32, (count, count), 1
    )
    return jnp.dot(until.astype(jnp.float32), value, precision=highest)


def doc_layout(doc_sizes, positions):
    count = doc_sizes.shape[0]
    until = lax.broadcasted_iota(jnp.int32, (count, count), 0) >= lax.broadcasted_iota(
        jnp.int32, (count, count), 1
    )
    bounds = jnp.sum(jnp.where(until, doc_sizes[None, :], 0), axis=1)[:-1]
    doc_ids = jnp.sum((positions[:, None] >= bounds[None, :]).astype(jnp.int32), axis=1)
    starts = jnp.any(positions[:, None] == bounds[None, :], axis=1)
    return (doc_ids, starts)


def conv_apply(extended, ext_ids, kernel, offset_vec):
    amount = extended.shape[0] - CONV + 1
    own_ids = ext_ids[CONV - 1 :]
    summed = offset_vec[None, :] + jnp.zeros((amount, 1), extended.dtype)
    for tap_index in range(CONV):
        same_doc = (ext_ids[tap_index : tap_index + amount] == own_ids).astype(extended.dtype)
        summed = (
            summed
            + kernel[tap_index][None, :]
            * extended[tap_index : tap_index + amount]
            * same_doc[:, None]
        )
    return jax.nn.silu(summed)


def span_pass(carried_state, pieces):
    values, write_vec, read_vec, step_size, log_decay, doc_ids, before = pieces
    amount = values.shape[0]
    running = running_sum(log_decay)
    row_ids = lax.broadcasted_iota(jnp.int32, (amount, amount), 0)
    col_ids = lax.broadcasted_iota(jnp.int32, (amount, amount), 1)
    allowed = (col_ids <= row_ids) & (doc_ids[:, None] == doc_ids[None, :])
    log_gap = jnp.where(
        allowed[:, :, None], running[:, None, :] - running[None, :, :], masked_value
    )
    intersection = jnp.einsum("in,jn->ij", read_vec, write_vec, precision=highest)
    mixing = intersection[:, :, None] * jnp.exp(log_gap) * step_size[None, :, :]
    within = jnp.einsum("ijh,jhp->ihp", mixing, values, precision=highest)
    inflow = jnp.exp(running) * (doc_ids == before)[:, None].astype(jnp.float32)
    carried = (
        jnp.einsum("in,hpn->ihp", read_vec, carried_state, precision=highest) * inflow[:, :, None]
    )
    to_end = (
        jnp.exp(running[-1][None, :] - running)
        * (doc_ids == doc_ids[-1])[:, None].astype(jnp.float32)
        * step_size
    )
    increment = jnp.einsum("jh,jhp,jn->hpn", to_end, values, write_vec, precision=highest)
    return (inflow[-1][:, None, None] * carried_state + increment, within + carried)


def mixer_local(
    extended,
    raw_rate,
    kernel,
    offset_vec,
    step_bias,
    decay_log,
    skip_gain,
    state_in,
    ext_ids,
    doc_ids,
    starts,
):
    tokens = raw_rate.shape[0]
    conv_out = conv_apply(extended, ext_ids, kernel, offset_vec)
    values = conv_out[:, :DS].reshape(tokens, MH, MP)
    read_vector = conv_out[:, DS + NS :]
    step_size = jax.nn.softplus(raw_rate + step_bias)
    log_decay = -step_size * jnp.exp(decay_log)
    blocks = tokens // SPAN
    pieces = (
        values.reshape(blocks, SPAN, MH, MP),
        conv_out[:, DS : DS + NS].reshape(blocks, SPAN, NS),
        read_vector.reshape(blocks, SPAN, NS),
        step_size.reshape(blocks, SPAN, MH),
        log_decay.reshape(blocks, SPAN, MH),
        doc_ids.reshape(blocks, SPAN),
        doc_ids[::SPAN] - starts[::SPAN].astype(jnp.int32),
    )
    state_out, outputs = lax.scan(span_pass, state_in, pieces)
    result = outputs.reshape(tokens, MH, MP) + skip_gain[None, :, None] * values
    return ((result.reshape(tokens, DS), state_out), (read_vector, log_decay))


def device_inflow(log_decay, doc_ids, starts):
    same_doc = (doc_ids == doc_ids[0] - starts[0].astype(jnp.int32)).astype(jnp.float32)
    return jnp.exp(running_sum(log_decay)) * same_doc[:, None]


def chain_affine(earlier, later):
    return (earlier[0] * later[0], later[0][:, None, None] * earlier[1] + later[1])


def query_groups(flat):
    tokens = flat.shape[0]
    per_group = QH // KVH
    return (
        flat.reshape(tokens, KVH, per_group, HD)
        .transpose(1, 2, 0, 3)
        .reshape(KVH, per_group * tokens, HD)
    )


def query_flat(grouped, tokens):
    per_group = QH // KVH
    return grouped.reshape(KVH, per_group, tokens, HD).transpose(2, 0, 1, 3).reshape(tokens, QD)


def score_block(queries, key_rows, query_pos, query_ids, all_ids, offset, block_len):
    key_block = lax.dynamic_slice_in_dim(key_rows, offset, block_len, 0)
    key_part = key_block[:, :KVD].reshape(block_len, KVH, HD)
    value_part = key_block[:, KVD:].reshape(block_len, KVH, HD)
    key_pos = offset + jnp.arange(block_len, dtype=jnp.int32)
    key_ids = lax.dynamic_slice_in_dim(all_ids, offset, block_len, 0)
    allowed = (key_pos[None, :] <= query_pos[:, None]) & (key_ids[None, :] == query_ids[:, None])
    scores = (
        jnp.einsum("grd,kgd->grk", queries, key_part, preferred_element_type=jnp.float32) * 0.125
    )
    return (jnp.where(allowed[None], scores, masked_value), allowed, key_part, value_part)


def attend_forward(queries_flat, key_rows, positions, doc_ids, all_ids, ctx_index):
    tokens = queries_flat.shape[0]
    per_group = QH // KVH
    queries = query_groups(queries_flat)
    query_pos = jnp.tile(positions, per_group)
    query_ids = jnp.tile(doc_ids, per_group)
    block_len = math.gcd(key_rows.shape[0], KEY_BLOCK)
    block_count = ((ctx_index + 1) * tokens + block_len - 1) // block_len

    def visit_block(block_index, carry):
        running_max, running_sum, accumulated = carry
        scores, allowed, key_part, value_part = score_block(
            queries, key_rows, query_pos, query_ids, all_ids, block_index * block_len, block_len
        )
        new_max = jnp.maximum(running_max, jnp.max(scores, axis=-1))
        chances = jnp.where(allowed[None], jnp.exp(scores - new_max[..., None]), 0.0)
        rescale = jnp.exp(running_max - new_max)
        running_sum = running_sum * rescale + jnp.sum(chances, axis=-1)
        accumulated = accumulated * rescale[..., None] + jnp.einsum(
            "grk,kgd->grd",
            chances.astype(jnp.bfloat16),
            value_part,
            preferred_element_type=jnp.float32,
        )
        return (new_max, running_sum, accumulated)

    row_count = per_group * tokens
    start_carry = (
        jnp.full((KVH, row_count), masked_value, jnp.float32),
        jnp.zeros((KVH, row_count), jnp.float32),
        jnp.zeros((KVH, row_count, HD), jnp.float32),
    )
    running_max, running_sum, accumulated = lax.fori_loop(0, block_count, visit_block, start_carry)
    output = accumulated / running_sum[..., None]
    return (query_flat(output, tokens), running_max + jnp.log(running_sum))


def attend_backward(
    queries_flat,
    key_rows,
    attention_raw,
    log_norm,
    grad_low,
    positions,
    doc_ids,
    all_ids,
    ctx_index,
):
    tokens = queries_flat.shape[0]
    length = key_rows.shape[0]
    per_group = QH // KVH
    queries = query_groups(queries_flat)
    grad_rows = query_groups(grad_low)
    grad_wide = grad_rows.astype(jnp.float32)
    delta = jnp.sum(grad_wide * query_groups(attention_raw), axis=-1)
    query_pos = jnp.tile(positions, per_group)
    query_ids = jnp.tile(doc_ids, per_group)
    block_len = math.gcd(length, KEY_BLOCK)
    block_count = ((ctx_index + 1) * tokens + block_len - 1) // block_len

    def visit_block(block_index, carry):
        query_grad, key_grad, value_grad = carry
        offset = block_index * block_len
        scores, allowed, key_part, value_part = score_block(
            queries, key_rows, query_pos, query_ids, all_ids, offset, block_len
        )
        chances = jnp.where(allowed[None], jnp.exp(scores - log_norm[..., None]), 0.0)
        prob_grad = jnp.einsum(
            "grd,kgd->grk", grad_rows, value_part, preferred_element_type=jnp.float32
        )
        score_grad = (chances * (prob_grad - delta[..., None])).astype(jnp.bfloat16)
        query_grad = query_grad + jnp.einsum(
            "grk,kgd->grd", score_grad, key_part, preferred_element_type=jnp.float32
        )
        key_piece = (
            jnp.einsum("grk,grd->kgd", score_grad, queries, preferred_element_type=jnp.float32)
            * 0.125
        )
        value_piece = jnp.einsum(
            "grk,grd->kgd",
            chances.astype(jnp.bfloat16),
            grad_rows,
            preferred_element_type=jnp.float32,
        )
        key_grad = lax.dynamic_update_slice_in_dim(
            key_grad,
            lax.dynamic_slice_in_dim(key_grad, offset, block_len, 0)
            + key_piece.reshape(block_len, KVD),
            offset,
            0,
        )
        value_grad = lax.dynamic_update_slice_in_dim(
            value_grad,
            lax.dynamic_slice_in_dim(value_grad, offset, block_len, 0)
            + value_piece.reshape(block_len, KVD),
            offset,
            0,
        )
        return (query_grad, key_grad, value_grad)

    start_carry = (
        jnp.zeros((KVH, per_group * tokens, HD), jnp.float32),
        jnp.zeros((length, KVD), jnp.float32),
        jnp.zeros((length, KVD), jnp.float32),
    )
    query_grad, key_grad, value_grad = lax.fori_loop(0, block_count, visit_block, start_carry)
    return (query_flat(query_grad * 0.125, tokens), key_grad, value_grad)


def layer_layout(doc_sizes, tokens, ctx_index, ctx_count):
    positions = ctx_index * tokens + jnp.arange(tokens, dtype=jnp.int32)
    doc_ids, starts = doc_layout(doc_sizes, positions)
    all_ids = doc_layout(doc_sizes, jnp.arange(tokens * ctx_count, dtype=jnp.int32))[0]
    ext_ids = doc_layout(
        doc_sizes, ctx_index * tokens - (CONV - 1) + jnp.arange(tokens + CONV - 1, dtype=jnp.int32)
    )[0]
    return (positions, doc_ids, starts, all_ids, ext_ids)


def layer_forward(hidden_in, weights_full, head_params, doc_sizes, ctx_index, ctx_count):
    tokens = hidden_in.shape[0]
    positions, doc_ids, starts, all_ids, ext_ids = layer_layout(
        doc_sizes, tokens, ctx_index, ctx_count
    )
    normed = norm_apply(hidden_in, weights_full["first_gain"].astype(jnp.float32)).astype(
        jnp.bfloat16
    )
    projected = jnp.dot(
        normed, weights_full["mixer_in"], preferred_element_type=jnp.float32
    ).astype(jnp.bfloat16)
    edge_rows = passed_along(projected[tokens - (CONV - 1) :, DS : DS + CONVD], "ctx", 1)
    extended = jnp.concatenate([edge_rows, projected[:, DS : DS + CONVD]], axis=0).astype(
        jnp.float32
    )
    raw_rate = projected[:, DS + CONVD :].astype(jnp.float32)
    step_bias, decay_log, skip_gain = head_params
    empty_state = jnp.zeros((MH, MP, NS), jnp.float32)
    (partial_out, local_state), (read_vector, log_decay) = mixer_local(
        extended,
        raw_rate,
        weights_full["conv_kernel"].astype(jnp.float32),
        weights_full["conv_bias"].astype(jnp.float32),
        step_bias,
        decay_log,
        skip_gain,
        empty_state,
        ext_ids,
        doc_ids,
        starts,
    )
    inflow = device_inflow(log_decay, doc_ids, starts)
    state_in = prefix(
        (inflow[-1], local_state), "ctx", chain_affine, (jnp.ones((MH,), jnp.float32), empty_state)
    )[1]
    carried = (
        jnp.einsum("tn,hpn->thp", read_vector, state_in, precision=highest) * inflow[:, :, None]
    )
    ssm_out = partial_out + carried.reshape(tokens, DS)
    gate_value = projected[:, :DS].astype(jnp.float32)
    gated_out = (ssm_out * jax.nn.silu(gate_value)).astype(jnp.bfloat16)
    mixer_term = jnp.dot(gated_out, weights_full["mixer_out"], preferred_element_type=jnp.float32)
    heads_in = jnp.dot(
        normed, weights_full["attention_in"], preferred_element_type=jnp.float32
    ).astype(jnp.bfloat16)
    key_rows = lax.all_gather(heads_in[:, QD:], "ctx", axis=0, tiled=True)
    attention_raw, log_norm = attend_forward(
        heads_in[:, :QD], key_rows, positions, doc_ids, all_ids, ctx_index
    )
    attention_term = jnp.dot(
        attention_raw.astype(jnp.bfloat16),
        weights_full["attention_out"],
        preferred_element_type=jnp.float32,
    )
    middle = hidden_in + mixer_term + attention_term
    normed_mid = norm_apply(middle, weights_full["second_gain"].astype(jnp.float32)).astype(
        jnp.bfloat16
    )
    expanded = jnp.dot(normed_mid, weights_full["gate_up"], preferred_element_type=jnp.float32)
    hidden = (jax.nn.silu(expanded[:, :FF]) * expanded[:, FF:]).astype(jnp.bfloat16)
    result = middle + jnp.dot(
        hidden, weights_full["down_weight"], preferred_element_type=jnp.float32
    )
    stored = (
        hidden_in,
        middle,
        projected,
        edge_rows,
        state_in,
        ssm_out,
        heads_in,
        key_rows,
        attention_raw,
        log_norm,
        expanded,
    )
    return (result, stored)


def layer_backward(grad_in, stored, weights_full, head_params, doc_sizes, ctx_index, ctx_count):
    (
        hidden_in,
        middle,
        projected,
        edge_rows,
        state_in,
        ssm_out,
        heads_in,
        key_rows,
        attention_raw,
        log_norm,
        expanded,
    ) = stored
    tokens = hidden_in.shape[0]
    positions, doc_ids, starts, all_ids, ext_ids = layer_layout(
        doc_sizes, tokens, ctx_index, ctx_count
    )
    first_gain = weights_full["first_gain"].astype(jnp.float32)
    second_gain = weights_full["second_gain"].astype(jnp.float32)
    down_low = grad_in.astype(jnp.bfloat16)
    gate_vals = expanded[:, :FF]
    up_vals = expanded[:, FF:]
    gate_sig = jax.nn.sigmoid(gate_vals)
    hidden = (jax.nn.silu(gate_vals) * up_vals).astype(jnp.bfloat16)
    down_weight_grad = inner_rows(hidden, down_low)
    hidden_grad = outer_cols(down_low, weights_full["down_weight"])
    slope = gate_sig * (1.0 + gate_vals * (1.0 - gate_sig))
    expand_grad = jnp.concatenate(
        [hidden_grad * up_vals * slope, hidden_grad * jax.nn.silu(gate_vals)], axis=1
    ).astype(jnp.bfloat16)
    normed_mid = norm_apply(middle, second_gain).astype(jnp.bfloat16)
    gate_up_grad = inner_rows(normed_mid, expand_grad)
    mid_norm_grad, second_gain_grad = norm_back(
        middle, second_gain, outer_cols(expand_grad, weights_full["gate_up"])
    )
    middle_grad = grad_in + mid_norm_grad
    residual_low = middle_grad.astype(jnp.bfloat16)
    attention_out_grad = inner_rows(attention_raw.astype(jnp.bfloat16), residual_low)
    output_low = outer_cols(residual_low, weights_full["attention_out"]).astype(jnp.bfloat16)
    query_grad, key_grad, value_grad = attend_backward(
        heads_in[:, :QD],
        key_rows,
        attention_raw,
        log_norm,
        output_low,
        positions,
        doc_ids,
        all_ids,
        ctx_index,
    )
    key_share, value_share = (
        lax.psum_scatter(
            key_grad.astype(jnp.bfloat16), "ctx", scatter_dimension=0, tiled=True
        ).astype(jnp.float32),
        lax.psum_scatter(
            value_grad.astype(jnp.bfloat16), "ctx", scatter_dimension=0, tiled=True
        ).astype(jnp.float32),
    )
    heads_grad = jnp.concatenate([query_grad, key_share, value_share], axis=1).astype(jnp.bfloat16)
    gate_value = projected[:, :DS].astype(jnp.float32)
    gate_sig_z = jax.nn.sigmoid(gate_value)
    gated_out = (ssm_out * jax.nn.silu(gate_value)).astype(jnp.bfloat16)
    mixer_out_grad = inner_rows(gated_out, residual_low)
    gated_grad = outer_cols(residual_low, weights_full["mixer_out"])
    ssm_grad = gated_grad * jax.nn.silu(gate_value)
    gate_grad = gated_grad * ssm_out * gate_sig_z * (1.0 + gate_value * (1.0 - gate_sig_z))
    extended = jnp.concatenate([edge_rows, projected[:, DS : DS + CONVD]], axis=0).astype(
        jnp.float32
    )
    raw_rate = projected[:, DS + CONVD :].astype(jnp.float32)
    step_bias, decay_log, skip_gain = head_params

    def local_piece(
        extended, raw_rate, kernel, offset_vec, step_bias, decay_log, skip_gain, state_in
    ):
        return mixer_local(
            extended,
            raw_rate,
            kernel,
            offset_vec,
            step_bias,
            decay_log,
            skip_gain,
            state_in,
            ext_ids,
            doc_ids,
            starts,
        )

    primal, pullback, (read_vector, log_decay) = jax.vjp(
        local_piece,
        extended,
        raw_rate,
        weights_full["conv_kernel"].astype(jnp.float32),
        weights_full["conv_bias"].astype(jnp.float32),
        step_bias,
        decay_log,
        skip_gain,
        state_in,
        has_aux=True,
    )
    inflow = device_inflow(log_decay, doc_ids, starts)
    local_grad = jnp.einsum(
        "th,thp,tn->hpn", inflow, ssm_grad.reshape(tokens, MH, MP), read_vector, precision=highest
    )
    state_back = prefix_2(
        (inflow[-1], local_grad),
        "ctx",
        chain_affine,
        (jnp.ones((MH,), jnp.float32), jnp.zeros((MH, MP, NS), jnp.float32)),
    )[1]
    ext_grad, raw_grad, kernel_grad, offset_grad, step_grad, decay_grad, skip_grad, unused = (
        pullback((ssm_grad, state_back))
    )
    rim_grad = passed_along(ext_grad[: CONV - 1], "ctx", -1)
    pre_grad = ext_grad[CONV - 1 :]
    pre_grad = jnp.concatenate(
        [pre_grad[: tokens - (CONV - 1)], pre_grad[tokens - (CONV - 1) :] + rim_grad], axis=0
    )
    mixer_grad = jnp.concatenate([gate_grad, pre_grad, raw_grad], axis=1).astype(jnp.bfloat16)
    normed = norm_apply(hidden_in, first_gain).astype(jnp.bfloat16)
    mixer_in_grad = inner_rows(normed, mixer_grad)
    attention_in_grad = inner_rows(normed, heads_grad)
    normed_grad = outer_cols(mixer_grad, weights_full["mixer_in"]) + outer_cols(
        heads_grad, weights_full["attention_in"]
    )
    in_norm_grad, first_gain_grad = norm_back(hidden_in, first_gain, normed_grad)
    block_grad = middle_grad + in_norm_grad
    weight_grads = (
        first_gain_grad,
        mixer_in_grad,
        kernel_grad,
        offset_grad,
        mixer_out_grad,
        attention_in_grad,
        attention_out_grad,
        second_gain_grad,
        gate_up_grad,
        down_weight_grad,
    )
    return (block_grad, weight_grads, (step_grad, decay_grad, skip_grad))


def local(
    block_input,
    output_grad,
    doc_lengths,
    first_gain,
    mixer_in,
    conv_kernel,
    conv_bias,
    step_bias,
    decay_log,
    skip_gain,
    mixer_out,
    attention_in,
    attention_out,
    second_gain,
    gate_up,
    down_weight,
):
    gathered = (
        lax.all_gather(first_gain[0], "wt", axis=0, tiled=True),
        lax.all_gather(mixer_in[0], "wt", axis=0, tiled=True),
        lax.all_gather(conv_kernel[0], "wt", axis=1, tiled=True),
        lax.all_gather(conv_bias[0], "wt", axis=0, tiled=True),
        lax.all_gather(mixer_out[0], "wt", axis=0, tiled=True),
        lax.all_gather(attention_in[0], "wt", axis=0, tiled=True),
        lax.all_gather(attention_out[0], "wt", axis=0, tiled=True),
        lax.all_gather(second_gain[0], "wt", axis=0, tiled=True),
        lax.all_gather(gate_up[0], "wt", axis=0, tiled=True),
        lax.all_gather(down_weight[0], "wt", axis=0, tiled=True),
    )
    weights_full = dict(zip(weight_names, gathered))
    head_params = (step_bias[0], decay_log[0], skip_gain[0])
    head_section = lax.axis_index("section") == 0
    ctx_index = lax.axis_index("ctx")
    ctx_count = lax.axis_size("ctx")
    tokens = block_input.shape[2]
    received = jnp.zeros((tokens, D), jnp.bfloat16)
    results = []
    stored_list = []
    for moment in range(MICRO + 1):
        own_block = block_input[min(moment, MICRO - 1), 0].astype(jnp.float32)
        entry = jnp.where(head_section, own_block, received.astype(jnp.float32))
        doc_sizes = jnp.where(
            head_section, doc_lengths[min(moment, MICRO - 1), 0], doc_lengths[max(moment - 1, 0), 0]
        )
        layer_result, stored = layer_forward(
            entry, weights_full, head_params, doc_sizes, ctx_index, ctx_count
        )
        sent = layer_result.astype(jnp.bfloat16)
        results.append(sent)
        stored_list.append((stored, doc_sizes))
        if moment < MICRO:
            received = passed_along(sent, "section", 1)
    back_received = jnp.zeros((tokens, D), jnp.bfloat16)
    total_grads = tuple((jnp.zeros(weight_full.shape, jnp.float32) for weight_full in gathered))
    total_heads = tuple((jnp.zeros(param_vec.shape, jnp.float32) for param_vec in head_params))
    sent_grads = []
    for moment in range(MICRO + 1):
        given_grad = output_grad[min(moment, MICRO - 1), 0].astype(jnp.float32)
        cotangent = jnp.where(head_section, back_received.astype(jnp.float32), given_grad)
        chosen = jax.tree.map(
            lambda left, right: jnp.where(head_section, left, right),
            stored_list[max(moment - 1, 0)],
            stored_list[min(moment + 1, MICRO)],
        )
        valid = jnp.where(head_section, moment >= 1, moment < MICRO)
        stored, doc_sizes = chosen
        block_grad, weight_grads, head_grads = layer_backward(
            cotangent, stored, weights_full, head_params, doc_sizes, ctx_index, ctx_count
        )
        total_grads = tuple(
            (old + jnp.where(valid, new, 0.0) for old, new in zip(total_grads, weight_grads))
        )
        total_heads = tuple(
            (old + jnp.where(valid, new, 0.0) for old, new in zip(total_heads, head_grads))
        )
        sent = block_grad.astype(jnp.bfloat16)
        sent_grads.append(sent)
        if moment < MICRO:
            back_received = passed_along(sent, "section", -1)
    section_output = jnp.stack(
        [
            jnp.where(head_section, results[batch_index], results[batch_index + 1])
            for batch_index in range(MICRO)
        ]
    ).reshape(1, MICRO, 1, tokens, D)
    input_grad = jnp.stack(
        [
            jnp.where(head_section, sent_grads[batch_index + 1], sent_grads[batch_index])
            for batch_index in range(MICRO)
        ]
    ).reshape(1, MICRO, 1, tokens, D)
    shares = (
        lax.psum_scatter(
            total_grads[0].astype(jnp.bfloat16), "wt", scatter_dimension=0, tiled=True
        ).astype(jnp.float32),
        lax.psum_scatter(
            total_grads[1].astype(jnp.bfloat16), "wt", scatter_dimension=0, tiled=True
        ).astype(jnp.float32),
        lax.psum_scatter(
            total_grads[2].astype(jnp.bfloat16), "wt", scatter_dimension=1, tiled=True
        ).astype(jnp.float32),
        lax.psum_scatter(
            total_grads[3].astype(jnp.bfloat16), "wt", scatter_dimension=0, tiled=True
        ).astype(jnp.float32),
        lax.psum_scatter(
            total_grads[4].astype(jnp.bfloat16), "wt", scatter_dimension=0, tiled=True
        ).astype(jnp.float32),
        lax.psum_scatter(
            total_grads[5].astype(jnp.bfloat16), "wt", scatter_dimension=0, tiled=True
        ).astype(jnp.float32),
        lax.psum_scatter(
            total_grads[6].astype(jnp.bfloat16), "wt", scatter_dimension=0, tiled=True
        ).astype(jnp.float32),
        lax.psum_scatter(
            total_grads[7].astype(jnp.bfloat16), "wt", scatter_dimension=0, tiled=True
        ).astype(jnp.float32),
        lax.psum_scatter(
            total_grads[8].astype(jnp.bfloat16), "wt", scatter_dimension=0, tiled=True
        ).astype(jnp.float32),
        lax.psum_scatter(
            total_grads[9].astype(jnp.bfloat16), "wt", scatter_dimension=0, tiled=True
        ).astype(jnp.float32),
    )
    reduced = (
        lax.psum(shares[0].astype(jnp.bfloat16), "ctx").astype(jnp.float32),
        lax.psum(shares[1].astype(jnp.bfloat16), "ctx").astype(jnp.float32),
        lax.psum(shares[2].astype(jnp.bfloat16), "ctx").astype(jnp.float32),
        lax.psum(shares[3].astype(jnp.bfloat16), "ctx").astype(jnp.float32),
        lax.psum(shares[4].astype(jnp.bfloat16), "ctx").astype(jnp.float32),
        lax.psum(shares[5].astype(jnp.bfloat16), "ctx").astype(jnp.float32),
        lax.psum(shares[6].astype(jnp.bfloat16), "ctx").astype(jnp.float32),
        lax.psum(shares[7].astype(jnp.bfloat16), "ctx").astype(jnp.float32),
        lax.psum(shares[8].astype(jnp.bfloat16), "ctx").astype(jnp.float32),
        lax.psum(shares[9].astype(jnp.bfloat16), "ctx").astype(jnp.float32),
    )
    head_sums = lax.psum((total_heads[0], total_heads[1], total_heads[2]), ("ctx", "wt"))
    return (
        section_output,
        input_grad,
        reduced[0][None],
        reduced[1][None],
        reduced[2][None],
        reduced[3][None],
        head_sums[0][None],
        head_sums[1][None],
        head_sums[2][None],
        reduced[4][None],
        reduced[5][None],
        reduced[6][None],
        reduced[7][None],
        reduced[8][None],
        reduced[9][None],
    )


def spread(mesh):
    placed = (
        P(None, "wt", "ctx", None),
        P(None, "wt", "ctx", None),
        P(None, "wt", None),
        P("section", "wt"),
        P("section", "wt", None),
        P("section", None, "wt"),
        P("section", "wt"),
        P("section", None),
        P("section", None),
        P("section", None),
        P("section", "wt", None),
        P("section", "wt", None),
        P("section", "wt", None),
        P("section", "wt"),
        P("section", "wt", None),
        P("section", "wt", None),
    )
    return jax.shard_map(
        local,
        mesh=mesh,
        in_specs=placed,
        out_specs=(
            P("section", None, "wt", "ctx", None),
            P("section", None, "wt", "ctx", None),
            P("section", "wt"),
            P("section", "wt", None),
            P("section", None, "wt"),
            P("section", "wt"),
            P("section", None),
            P("section", None),
            P("section", None),
            P("section", "wt", None),
            P("section", "wt", None),
            P("section", "wt", None),
            P("section", "wt"),
            P("section", "wt", None),
            P("section", "wt", None),
        ),
        check_vma=False,
    )


f32, bf16 = jnp.float32, jnp.bfloat16
RH = MH // 4
RD = DS // 4
RQ = QD // 4
RF = FF // 4
RAW_AT = 2 * RD + 2 * NS
Q_AT = RAW_AT + 128
K_AT = Q_AT + RQ
INC = K_AT + 2 * HD
OUTR = RD + RQ
FREE = 22
GROUP_A = INC + D // 2
GROUP_B = 2 * RF + D // 2
AXES = CORE, ROW, COL, LINE = tuple("cyxz")


def swapped(value, axis):
    return lax.ppermute(value, axis, [(0, 1), (1, 0)])


def across(value):
    return lax.ppermute(value, (ROW, COL), [(0, 3), (1, 2), (2, 1), (3, 0)])


def place(p):
    return ((p[0] * 2 + p[1]) * 2 + p[2]) * 4 + p[3]


def sent(value, pairs):
    return lax.ppermute(value, AXES, [(place(a), place(b)) for a, b in pairs])


every = [(c, y, x, z) for c in range(2) for y in range(2) for x in range(2) for z in range(4)]


def turned(value, by):
    return lax.ppermute(value, LINE, [(i, (i + by) % 4) for i in range(4)])


def paired_lines(value, by):
    return lax.ppermute(value, LINE, [(i, i ^ by) for i in range(4)])


def after(value, *others):
    return lax.optimization_barrier((value,) + others)[0]


def ordered(flag, own, other):
    return jnp.where(flag == 0, jnp.stack([own, other]), jnp.stack([other, own]))


def whole_rows(pair, y, x):
    own = lax.dynamic_index_in_dim(pair, y, 0, False)
    other = lax.dynamic_index_in_dim(pair, 1 - y, 0, False)
    near = ordered(x, own, swapped(own, COL))
    far = ordered(x, swapped(other, ROW), across(other))
    return ordered(y, near, far).reshape(4 * own.shape[0], own.shape[1])


def back_rows(rows, y, x):
    blocks = rows.reshape(2, 2, rows.shape[0] // 4, rows.shape[1])
    return ordered(y, blocks[y, x], swapped(blocks[1 - y, x], ROW))


def half_sum(keep, give):
    low = (keep.astype(f32) + swapped(give, CORE).astype(f32)).astype(bf16)
    return (low.astype(f32) + swapped(low, COL).astype(f32)).astype(bf16)


def quarter_sum(keep, give):
    both = half_sum(keep, give)
    return both, swapped(both, CORE)


BLOCK = 128
REACH = 2
CONVR = RD + 2 * NS
OUT_BLOCKS = [(j, y, c) for j in range(2) for y, c in ((0, 0), (0, 1), (1, 0))] + [(0, 1, 1), (1, 1, 1)]
WIDE = D // 2
LIMIT = 56 << 20


def mm(left, right, dims=((1,), (0,)), precision=None):
    return lax.dot_general(left, right, (dims, ((), ())), precision=precision, preferred_element_type=f32)


NT = ((1,), (1,))
TN = ((0,), (0,))


def logistic(value):
    return 1.0 / (1.0 + jnp.exp(-value))


def slope(value, sig):
    return sig * (1.0 + value * (1.0 - sig))


def unit_scale(rows):
    return lax.rsqrt(jnp.mean(rows * rows, axis=-1, keepdims=True) + epsilon)


def conv_chunk(proj_ref, ck_ref, tok_ref, j):
    lanes = slice(128 * j, 128 * (j + 1))
    pre = proj_ref[:, RD + 128 * j : RD + 128 * (j + 1)].astype(f32)
    summed = ck_ref[4:5, lanes] + pre * ck_ref[3:4, lanes]
    for by in range(1, CONV):
        summed = summed + pltpu.roll(pre, by, 0) * (ck_ref[3 - by : 4 - by, lanes] * tok_ref[:, by : by + 1])
    return pre, summed


def step_sizes(proj_ref, hp_ref):
    stepped = proj_ref[:, RAW_AT : RAW_AT + 128].astype(f32) + hp_ref[0:1, :]
    dt = jnp.maximum(stepped, 0.0) + jnp.log1p(jnp.exp(-jnp.abs(stepped)))
    return stepped, dt


def running(dt, hp_ref, run_s, run_t):
    count = dt.shape[0]
    rate = -dt * hp_ref[1:2, :]
    until = (
        lax.broadcasted_iota(jnp.int32, (count, count), 0) >= lax.broadcasted_iota(jnp.int32, (count, count), 1)
    ).astype(f32)
    run = mm(until, rate, precision=highest)
    run_s[...] = run
    run_t[...] = run.T
    return rate


def spans(count):
    for i in range(count // BLOCK):
        start = BLOCK * max(0, i - REACH)
        yield slice(BLOCK * i, BLOCK * (i + 1)), slice(start, BLOCK * (i + 1)), start


def barred(tok_ref, idr_ref, rows, keys):
    shape = (rows.stop - rows.start, keys.stop - keys.start)
    query = lax.broadcasted_iota(jnp.int32, shape, 0) + rows.start
    key = lax.broadcasted_iota(jnp.int32, shape, 1) + keys.start
    ok = (query >= key) & (tok_ref[rows, 0:1] == idr_ref[0:1, keys])
    return jnp.where(ok, 0.0, masked_value)


def fed_chunk(dt, conv, j, count):
    lane = lax.broadcasted_iota(jnp.int32, (count, 128), 1)
    return jnp.where(lane < MP, dt[:, 2 * j : 2 * j + 1], dt[:, 2 * j + 1 : 2 * j + 2]) * conv


def split_rows(c_ref, keep_ref, give_ref, half, value):
    @pl.when(c_ref[0] == half)
    def _():
        keep_ref[...] = value

    @pl.when(c_ref[0] != half)
    def _():
        give_ref[...] = value


def first_kernel(
    c_ref, mid_ref, own_ref, other_ref, gain_ref, wi_ref, mine_ref, got_ref, ck_ref, hp_ref, tok_ref, idr_ref,
    keep_ref, give_ref, x_ref, proj_ref, state_ref, ga_ref, h_s, wo_ref,
    vals_s, bc_s, fed_s, run_s, run_t,
):
    count = mid_ref.shape[0]
    for b, (j, y, c) in enumerate(OUT_BLOCKS):
        rows = slice(128 * j + 64 * y, 128 * j + 64 * y + 64)
        wo_ref[64 * b : 64 * b + 64, :] = jnp.where(c_ref[0] == c, mine_ref[rows, :], got_ref[rows, :])
    for i in range(count // BLOCK):
        rows = slice(BLOCK * i, BLOCK * (i + 1))
        low = mid_ref[rows, :]
        if mid_ref.dtype == f32:
            low = (low + added_rows(c_ref, own_ref, other_ref, i, count)).astype(bf16)
        x_ref[rows, :] = low
        x = low.astype(f32)
        h_s[rows, :] = (x * unit_scale(x) * gain_ref[...]).astype(bf16)
    for at in range(0, INC, 256):
        cols = slice(at, min(at + 256, INC))
        proj_ref[:, cols] = mm(h_s[...], wi_ref[:, cols]).astype(bf16)
    stepped, dt = step_sizes(proj_ref, hp_ref)
    running(dt, hp_ref, run_s, run_t)
    for j in range(CONVR // 128):
        pre, summed = conv_chunk(proj_ref, ck_ref, tok_ref, j)
        conv = summed * logistic(summed)
        if j < RD // 128:
            vals_s[:, 128 * j : 128 * (j + 1)] = conv
            fed_s[:, 128 * j : 128 * (j + 1)] = fed_chunk(dt, conv, j, count).astype(bf16)
        else:
            bc_s[:, 128 * j - RD : 128 * (j + 1) - RD] = conv.astype(bf16)
    for rows, keys, start in spans(count):
        bar = barred(tok_ref, idr_ref, rows, keys)
        gram = mm(bc_s[rows, NS:], bc_s[keys, :NS], NT)
        for h in range(RH):
            lanes = slice(MP * h, MP * (h + 1))
            decay = jnp.exp(run_s[rows, h : h + 1] - run_t[h : h + 1, keys] + bar)
            state_ref[rows, lanes] = mm((gram * decay).astype(bf16), fed_s[keys, lanes])
        for h in range(RQ // HD):
            lanes = slice(Q_AT + HD * h, Q_AT + HD * (h + 1))
            scores = mm(proj_ref[rows, lanes], proj_ref[keys, K_AT : K_AT + HD], NT) * 0.125 + bar
            chances = jnp.exp(scores - jnp.max(scores, axis=-1, keepdims=True))
            probs = (chances / jnp.sum(chances, axis=-1, keepdims=True)).astype(bf16)
            ga_ref[rows, RD + HD * h : RD + HD * (h + 1)] = mm(
                probs, proj_ref[keys, K_AT + HD : K_AT + 2 * HD]
            ).astype(bf16)
        z = proj_ref[rows, :RD].astype(f32)
        ssm = state_ref[rows, :] + ck_ref[5:6, :RD] * vals_s[rows, :]
        ga_ref[rows, :RD] = (ssm * z * logistic(z)).astype(bf16)
    for half in range(2):
        rows = slice(count // 2 * half, count // 2 * (half + 1))
        split_rows(c_ref, keep_ref, give_ref, half, mm(ga_ref[rows, :], wo_ref[...]).astype(bf16))


def added_rows(c_ref, own_ref, other_ref, i, count):
    half, at = divmod(BLOCK * i, count // 2)
    rows = slice(at, at + BLOCK)
    return jnp.where(c_ref[0] == half, own_ref[rows, :], other_ref[rows, :]).astype(f32)


def second_kernel(
    c_ref, x_ref, own_ref, other_ref, gain_ref, wgu_ref, wd_ref,
    keep_ref, give_ref, mid_ref, h_ref, gu_ref, hid_ref,
):
    count = x_ref.shape[0]
    for i in range(count // BLOCK):
        rows = slice(BLOCK * i, BLOCK * (i + 1))
        mid = x_ref[rows, :].astype(f32) + added_rows(c_ref, own_ref, other_ref, i, count)
        mid_ref[rows, :] = mid
        h_ref[rows, :] = (mid * unit_scale(mid) * gain_ref[...]).astype(bf16)
    for at in range(0, RF, 256):
        cols = slice(at, at + 256)
        ups = slice(RF + at, RF + at + 256)
        gate = mm(h_ref[...], wgu_ref[:, cols])
        up = mm(h_ref[...], wgu_ref[:, ups])
        gu_ref[:, cols] = gate
        gu_ref[:, ups] = up
        hid_ref[:, cols] = (gate * logistic(gate) * up).astype(bf16)
    for half in range(2):
        rows = slice(count // 2 * half, count // 2 * (half + 1))
        split_rows(c_ref, keep_ref, give_ref, half, mm(hid_ref[rows, :], wd_ref[...]).astype(bf16))


def back_second_kernel(c_ref, cot_ref, gu_ref, wgu_ref, wd_ref, keep_ref, give_ref, gug_ref):
    count = cot_ref.shape[0]
    for at in range(0, RF, 256):
        cols = slice(at, at + 256)
        ups = slice(RF + at, RF + at + 256)
        hidden_grad = mm(cot_ref[...], wd_ref[cols, :], NT)
        gate, up = gu_ref[:, cols], gu_ref[:, ups]
        sig = logistic(gate)
        gug_ref[:, cols] = (hidden_grad * up * slope(gate, sig)).astype(bf16)
        gug_ref[:, ups] = (hidden_grad * gate * sig).astype(bf16)
    for half in range(2):
        rows = slice(count // 2 * half, count // 2 * (half + 1))
        split_rows(c_ref, keep_ref, give_ref, half, mm(gug_ref[rows, :], wgu_ref[...], NT).astype(bf16))


def norm_back_rows(rows, gain, grad):
    scale = unit_scale(rows)
    normed = rows * scale
    weighted = grad * gain
    back = scale * (weighted - normed * jnp.mean(weighted * normed, axis=-1, keepdims=True))
    return back, jnp.sum(grad * normed, axis=0, keepdims=True)


def back_first_kernel(
    c_ref, cot_ref, own_ref, other_ref, mid_ref, gain_ref, proj_ref, state_ref, ga_ref, wi_ref, wo_ref, ck_ref,
    hp_ref, tok_ref, idr_ref,
    keep_ref, give_ref, outk_ref, outg_ref, midg_ref, projg_ref, gaing_ref, convg_ref, headg_ref,
    low_ref, gag_s, vals_s, bc_s, fed_s, run_s, run_t, sg_s, fedg_s, bcg_s, kvg_s, valg_s,
):
    count = cot_ref.shape[0]
    gain_grad = jnp.zeros((1, D), f32)
    for i in range(count // BLOCK):
        rows = slice(BLOCK * i, BLOCK * (i + 1))
        back, more = norm_back_rows(
            mid_ref[rows, :], gain_ref[...], added_rows(c_ref, own_ref, other_ref, i, count)
        )
        gain_grad = gain_grad + more
        total = cot_ref[rows, :].astype(f32) + back
        midg_ref[rows, :] = total
        low_ref[rows, :] = total.astype(bf16)
    gaing_ref[...] = gain_grad
    for q in range(OUTR // 128):
        grad = mm(ga_ref[:, 128 * q : 128 * (q + 1)], low_ref[...], TN).astype(bf16)
        for b in (2 * q, 2 * q + 1):
            j, y, c = OUT_BLOCKS[b]
            rows = slice(128 * j + 64 * y, 128 * j + 64 * y + 64)
            part = grad[64 * (b % 2) : 64 * (b % 2) + 64, :]

            @pl.when(c_ref[0] == c)
            def _(rows=rows, part=part):
                outk_ref[rows, :] = part

            @pl.when(c_ref[0] != c)
            def _(rows=rows, part=part):
                outg_ref[rows, :] = part

    for at in range(0, OUTR, 256):
        cols = slice(at, at + 256)
        gag_s[:, cols] = mm(low_ref[...], wo_ref[cols, :], NT)
    stepped, dt = step_sizes(proj_ref, hp_ref)
    rate = running(dt, hp_ref, run_s, run_t)
    for j in range(CONVR // 128):
        lanes = slice(128 * j, 128 * (j + 1))
        pre, summed = conv_chunk(proj_ref, ck_ref, tok_ref, j)
        conv = summed * logistic(summed)
        if j < RD // 128:
            vals_s[:, lanes] = conv
            fed_s[:, lanes] = fed_chunk(dt, conv, j, count).astype(bf16)
            z = proj_ref[:, lanes].astype(f32)
            sig = logistic(z)
            skip = ck_ref[5:6, lanes]
            grad = gag_s[:, lanes]
            ssm = state_ref[:, lanes] + skip * conv
            projg_ref[:, lanes] = (grad * ssm * slope(z, sig)).astype(bf16)
            ssm_grad = grad * z * sig
            sg_s[:, lanes] = ssm_grad.astype(bf16)
            valg_s[:, lanes] = ssm_grad * skip
            convg_ref[5:6, lanes] = jnp.sum(ssm_grad * conv, axis=0, keepdims=True)
        else:
            bc_s[:, 128 * j - RD : 128 * (j + 1) - RD] = conv.astype(bf16)
    fedg_s[...] = jnp.zeros_like(fedg_s)
    bcg_s[:, :NS] = jnp.zeros((count, NS), f32)
    kvg_s[...] = jnp.zeros_like(kvg_s)
    for rows, keys, start in spans(count):
        bar = barred(tok_ref, idr_ref, rows, keys)
        gram = mm(bc_s[rows, NS:], bc_s[keys, :NS], NT)
        gram_grad = jnp.zeros_like(gram)
        for h in range(RH):
            lanes = slice(MP * h, MP * (h + 1))
            decay = jnp.exp(run_s[rows, h : h + 1] - run_t[h : h + 1, keys] + bar)
            grad = sg_s[rows, lanes]
            gram_grad = gram_grad + mm(grad, fed_s[keys, lanes], NT) * decay
            fedg_s[keys, lanes] += mm((gram * decay).astype(bf16), grad, TN)
        gram_low = gram_grad.astype(bf16)
        bcg_s[rows, NS:] = mm(gram_low, bc_s[keys, :NS])
        bcg_s[keys, :NS] += mm(gram_low, bc_s[rows, NS:], TN)
        for h in range(RQ // HD):
            lanes = slice(Q_AT + HD * h, Q_AT + HD * (h + 1))
            query, key = proj_ref[rows, lanes], proj_ref[keys, K_AT : K_AT + HD]
            scores = mm(query, key, NT) * 0.125 + bar
            chances = jnp.exp(scores - jnp.max(scores, axis=-1, keepdims=True))
            probs = chances / jnp.sum(chances, axis=-1, keepdims=True)
            grad = gag_s[rows, RD + HD * h : RD + HD * (h + 1)].astype(bf16)
            prob_grad = mm(grad, proj_ref[keys, K_AT + HD : K_AT + 2 * HD], NT)
            score_grad = probs * (prob_grad - jnp.sum(probs * prob_grad, axis=-1, keepdims=True))
            score_grad = score_grad.astype(bf16)
            projg_ref[rows, lanes] = (mm(score_grad, key) * 0.125).astype(bf16)
            kvg_s[keys, :HD] += mm(score_grad, query, TN) * 0.125
            kvg_s[keys, HD:] += mm(probs.astype(bf16), grad, TN)
    projg_ref[:, K_AT:] = kvg_s[...].astype(bf16)
    head_of = lax.broadcasted_iota(jnp.int32, (RD, 128), 0) // MP
    picks = (head_of == lax.broadcasted_iota(jnp.int32, (RD, 128), 1)).astype(f32)
    run_grad = mm(
        sg_s[...].astype(f32) * state_ref[...] - fed_s[...].astype(f32) * fedg_s[...], picks, precision=highest
    )
    shape = (count, count)
    later = (
        (lax.broadcasted_iota(jnp.int32, shape, 1) >= lax.broadcasted_iota(jnp.int32, shape, 0))
        & (tok_ref[:, 0:1] == idr_ref[0:1, :])
    ).astype(f32)
    rate_grad = mm(later, run_grad, precision=highest)
    dt_grad = mm(vals_s[...] * fedg_s[...], picks, precision=highest) - rate_grad * hp_ref[1:2, :]
    raw_grad = dt_grad * logistic(stepped)
    headg_ref[0:1, :] = jnp.sum(raw_grad, axis=0, keepdims=True)
    headg_ref[1:2, :] = jnp.sum(rate_grad * rate, axis=0, keepdims=True)
    lane = lax.broadcasted_iota(jnp.int32, raw_grad.shape, 1)
    projg_ref[:, RAW_AT : RAW_AT + 128] = jnp.where(lane < RH, raw_grad, 0.0).astype(bf16)
    for j in range(CONVR // 128):
        lanes = slice(128 * j, 128 * (j + 1))
        pre, summed = conv_chunk(proj_ref, ck_ref, tok_ref, j)
        if j < RD // 128:
            grad = valg_s[:, lanes] + fed_chunk(dt, fedg_s[:, lanes], j, count)
        else:
            grad = bcg_s[:, 128 * j - RD : 128 * (j + 1) - RD]
        grad = grad * slope(summed, logistic(summed))
        convg_ref[4:5, lanes] = jnp.sum(grad, axis=0, keepdims=True)
        convg_ref[3:4, lanes] = jnp.sum(grad * pre, axis=0, keepdims=True)
        total = grad * ck_ref[3:4, lanes]
        for by in range(1, CONV):
            kept = grad * tok_ref[:, by : by + 1]
            convg_ref[3 - by : 4 - by, lanes] = jnp.sum(kept * pltpu.roll(pre, by, 0), axis=0, keepdims=True)
            total = total + pltpu.roll(kept * ck_ref[3 - by : 4 - by, lanes], count - by, 0)
        projg_ref[:, RD + 128 * j : RD + 128 * (j + 1)] = total.astype(bf16)
    for half in range(2):
        rows = slice(count // 2 * half, count // 2 * (half + 1))
        split_rows(c_ref, keep_ref, give_ref, half, mm(projg_ref[rows, :], wi_ref[...], NT).astype(bf16))


def back_input_kernel(c_ref, x_ref, own_ref, other_ref, gain_ref, midg_ref, low_ref, gaing_ref):
    count = x_ref.shape[0]
    gain_grad = jnp.zeros((1, D), f32)
    for i in range(count // BLOCK):
        rows = slice(BLOCK * i, BLOCK * (i + 1))
        back, more = norm_back_rows(
            x_ref[rows, :].astype(f32), gain_ref[...], added_rows(c_ref, own_ref, other_ref, i, count)
        )
        gain_grad = gain_grad + more
        low_ref[rows, :] = (midg_ref[rows, :] + back).astype(bf16)
    gaing_ref[...] = gain_grad


def back_half_kernel(c_ref, x_ref, own_ref, gain_ref, midg_ref, low_ref, gaing_ref):
    gain_grad = jnp.zeros((1, D), f32)
    for i in range(own_ref.shape[0] // BLOCK):
        rows = slice(BLOCK * i, BLOCK * (i + 1))
        at = pl.ds(pl.multiple_of(own_ref.shape[0] * c_ref[0] + BLOCK * i, BLOCK), BLOCK)
        back, more = norm_back_rows(x_ref[at, :].astype(f32), gain_ref[...], own_ref[rows, :].astype(f32))
        gain_grad = gain_grad + more
        low_ref[rows, :] = (midg_ref[at, :] + back).astype(bf16)
    gaing_ref[...] = gain_grad


def chosen(shape, source):
    lane = lax.broadcasted_iota(jnp.int32, shape, 1)
    return (lax.broadcasted_iota(jnp.int32, shape, 0) == source(lane)).astype(bf16)


def heads_from(x, width):
    return lambda d: d + x * width + jnp.where(d >= width, width, 0)


def steps_from(x, core):
    return lambda d: jnp.where(d < RH, 12 * core + 3 * x + d + jnp.where(d >= 3, 3, 0), -1)


def keys_from(core):
    return lambda d: HD * core + d + jnp.where(d >= HD, HD, 0)


def aligned(value, by):
    return pl.multiple_of(value, by)


def folded(ref, index, at, rows):
    ref[index + (slice(0, 64), slice(at, at + WIDE))] = rows[:, :WIDE]
    ref[index + (slice(64, 128), slice(at, at + WIDE))] = rows[:, WIDE:]


def prepare_a_kernel(c_ref, mi_ref, ai_ref, mo_ref, ao_ref, free_ref, keep_ref, give_ref):
    core, x = c_ref[0], c_ref[2]
    pick = chosen((2 * RD, RD), heads_from(x, RD // 2))
    pick_query = chosen((2 * RQ, RQ), heads_from(x, HD))
    half = RD // 2
    for t in range(2):
        pick_step = chosen((MH, 128), steps_from(x, t))
        pick_key = chosen((2 * KVD, 2 * HD), keys_from(t))
        for y in range(2):
            rows = slice(128 * y, 128 * (y + 1))
            parts = [mm(mi_ref[DS * h + 2 * RD * t : DS * h + 2 * RD * (t + 1), rows], pick, TN) for h in range(2)]
            parts.append(mi_ref[2 * DS : 2 * DS + 2 * NS, rows].T)
            parts.append(mm(mi_ref[DS + CONVD :, rows], pick_step, TN) + free_ref[...].astype(f32))
            parts.append(mm(ai_ref[rows, 2 * RQ * t : 2 * RQ * (t + 1)], pick_query))
            parts.append(mm(ai_ref[rows, QD:], pick_key))
            if y == 0:
                out = mo_ref[pl.ds(aligned(half * x + 64 * t, 64), 64), :]
            elif t == 0:
                out = mo_ref[pl.ds(aligned(half * x + 128, 64), 64), :]
            else:
                out = ao_ref[pl.ds(aligned(64 * x, 64), 64), :]
            for k, ref in enumerate((keep_ref, give_ref)):

                @pl.when((core == t) if k == 0 else (core != t))
                def _(ref=ref, parts=parts, out=out, y=y):
                    at = 0
                    for part in parts:
                        ref[y, :, at : at + part.shape[1]] = part.astype(bf16)
                        at += part.shape[1]
                    folded(ref, (y,), INC, out)


def prepare_b_kernel(c_ref, gu_ref, dn_ref, keep_ref, give_ref):
    core, x = c_ref[0], c_ref[2]
    for t in range(2):
        for k, ref in enumerate((keep_ref, give_ref)):

            @pl.when((core == t) if k == 0 else (core != t))
            def _(ref=ref, t=t):
                for y in range(2):
                    rows = slice(128 * y, 128 * (y + 1))
                    for h in range(8):
                        at = aligned(RF * h + 256 * t + 128 * x, 128)
                        ref[y, :, 128 * h : 128 * (h + 1)] = gu_ref[rows, pl.ds(at, 128)]
                    at = aligned(256 * t + 128 * x + 64 * y, 64)
                    folded(ref, (y,), 2 * RF, dn_ref[pl.ds(at, 64), :])


def unpack_a_from(c_ref, parts, wi_ref, mine_ref, give_ref):
    for line, y, load in parts:
        wi_ref[pl.ds(aligned(256 * line + 128 * y, 128), 128), :] = load(slice(None), slice(0, INC))
        rows = pl.ds(aligned(128 * lax.rem(line, 2) + 64 * y, 64), 64)
        left = load(slice(0, 64), slice(INC, GROUP_A))
        right = load(slice(64, 128), slice(INC, GROUP_A))

        @pl.when(line // 2 == c_ref[0])
        def _(rows=rows, left=left, right=right):
            mine_ref[rows, :WIDE] = left
            mine_ref[rows, WIDE:] = right

        @pl.when(line // 2 != c_ref[0])
        def _(rows=rows, left=left, right=right):
            give_ref[rows, :WIDE] = left
            give_ref[rows, WIDE:] = right


def unpack_b_from(parts, wgu_ref, wd_ref):
    for line, y, load in parts:
        wgu_ref[pl.ds(aligned(256 * line + 128 * y, 128), 128), :] = load(slice(None), slice(0, 2 * RF))
        rows = pl.ds(aligned(128 * line + 64 * y, 64), 64)
        wd_ref[rows, :WIDE] = load(slice(0, 64), slice(2 * RF, GROUP_B))
        wd_ref[rows, WIDE:] = load(slice(64, 128), slice(2 * RF, GROUP_B))


def halves_of(own, c_ref, keep_ref, got_ref, near_ref, far_ref):
    y, z = c_ref[1], c_ref[3]
    for k in range(4):
        line = lax.rem(z + k, 4)
        yield line, y, lambda *at, line=line: near_ref[(line,) + at]
        if k == 0:
            yield line, 1 - y, lambda *at: jnp.where(
                c_ref[0] == own, keep_ref[(1 - y,) + at], got_ref[(1 - y,) + at]
            )
        else:
            yield line, 1 - y, lambda *at, k=k: far_ref[(k - 1,) + at]


def lines_a_kernel(own, c_ref, keep_ref, got_ref, near_ref, far_ref, wi_ref, mine_ref, give_ref):
    unpack_a_from(c_ref, halves_of(own, c_ref, keep_ref, got_ref, near_ref, far_ref), wi_ref, mine_ref, give_ref)


def lines_b_kernel(own, c_ref, keep_ref, got_ref, near_ref, far_ref, wgu_ref, wd_ref):
    unpack_b_from(halves_of(own, c_ref, keep_ref, got_ref, near_ref, far_ref), wgu_ref, wd_ref)


def split_halves(c_ref, y, line, refs, width, value, folds):
    def put(ref, index):
        ref[index + (slice(None), slice(0, width))] = value
        folded(ref, index, width, folds)

    if len(refs) == 1:
        put(refs[0], (line, y))
        return
    far = refs[1 + line // 2] if len(refs) == 3 else refs[1]

    @pl.when(c_ref[1] == y)
    def _():
        put(refs[0], (line,))

    @pl.when(c_ref[1] != y)
    def _():
        put(far, (line % 2,) if len(refs) == 3 else (line,))


def grads_b_kernel(c_ref, h_ref, gug_ref, hid_ref, cot_ref, *refs):
    for line in range(4):
        down = mm(hid_ref[:, 128 * line : 128 * (line + 1)], cot_ref[...], TN).astype(bf16)
        for y in range(2):
            at = 256 * line + 128 * y
            grad = mm(h_ref[:, at : at + 128], gug_ref[...], TN).astype(bf16)
            split_halves(c_ref, y, line, refs, 2 * RF, grad, down[64 * y : 64 * (y + 1), :])


def grads_a_kernel(c_ref, h_ref, projg_ref, mine_ref, got_ref, *refs):
    for line in range(4):
        for y in range(2):
            at = 256 * line + 128 * y
            grad = mm(h_ref[:, at : at + 128], projg_ref[...], TN).astype(bf16)
            rows = slice(128 * (line % 2) + 64 * y, 128 * (line % 2) + 64 * y + 64)
            out = jnp.where(c_ref[0] == line // 2, mine_ref[rows, :], got_ref[rows, :])
            split_halves(c_ref, y, line, refs, INC, grad, out)


def final_b_kernel(c_ref, p0, p1, p2, p3, near, far, gu_ref, dn_ref):
    @pl.when(c_ref[0] == 0)
    def _():
        final_b_of(c_ref, [p0, p1, p2, p3], gu_ref, dn_ref)

    @pl.when(c_ref[0] == 1)
    def _():
        final_b_of(c_ref, [near.at[0], far.at[0], near.at[1], far.at[1]], gu_ref, dn_ref)


def final_b_of(c_ref, refs, gu_ref, dn_ref):
    for i, ref in enumerate(refs):
        y, x = lax.rem(c_ref[1] + i // 2, 2), lax.rem(c_ref[2] + i, 2)
        rows = pl.ds(aligned(128 * y, 128), 128)
        for t in range(2):
            for h in range(8):
                at = aligned(RF * h + 256 * t + 128 * x, 128)
                gu_ref[rows, pl.ds(at, 128)] = ref[t, :, 128 * h : 128 * (h + 1)].astype(f32)
            down = pl.ds(aligned(256 * t + 128 * x + 64 * y, 64), 64)
            dn_ref[down, :WIDE] = ref[t, :64, 2 * RF : GROUP_B].astype(f32)
            dn_ref[down, WIDE:] = ref[t, 64:, 2 * RF : GROUP_B].astype(f32)


def final_a_kernel(c_ref, p0, p1, p2, p3, q0, q1, q2, q3, mi_ref, ai_ref, mo_ref, ao_ref):
    @pl.when(c_ref[0] == 0)
    def _():
        final_a_of(c_ref, p0, p1, p2, p3, mi_ref, ai_ref, mo_ref, ao_ref)

    @pl.when(c_ref[0] == 1)
    def _():
        final_a_of(c_ref, q0, q1, q2, q3, mi_ref, ai_ref, mo_ref, ao_ref)


def final_a_of(c_ref, p0, p1, p2, p3, mi_ref, ai_ref, mo_ref, ao_ref):
    half = RD // 2
    for i in range(2):
        y = lax.rem(c_ref[1] + i, 2)
        rows = pl.ds(aligned(128 * y, 128), 128)
        shared = jnp.zeros((128, 2 * NS), f32)
        steps = jnp.zeros((MH, 128), f32)
        keys = jnp.zeros((128, 2 * KVD), f32)
        for t in range(2):
            query = jnp.zeros((128, 2 * RQ), f32)
            for k in range(2):
                ref = (p0, p1, p2, p3)[2 * i + k]
                x = lax.rem(c_ref[2] + k, 2)
                for h in range(2):
                    part = ref[t, :, RD * h : RD * (h + 1)].astype(f32).T
                    for j in range(2):
                        at = aligned(DS * h + 2 * RD * t + RD * j + half * x, 64)
                        mi_ref[pl.ds(at, half), rows] = part[half * j : half * (j + 1), :]
                shared = shared + ref[t, :, 2 * RD : RAW_AT].astype(f32)
                steps = steps + mm(chosen((MH, 128), steps_from(x, t)), ref[t, :, RAW_AT:Q_AT], NT)
                query = query + mm(ref[t, :, Q_AT:K_AT], chosen((2 * RQ, RQ), heads_from(x, HD)), NT)
                keys = keys + mm(ref[t, :, K_AT:INC], chosen((2 * KVD, 2 * HD), keys_from(t)), NT)
                left, right = ref[t, :64, INC:].astype(f32), ref[t, 64:, INC:].astype(f32)

                def put(out_ref, at, left=left, right=right):
                    out_ref[pl.ds(aligned(at, 64), 64), :WIDE] = left
                    out_ref[pl.ds(aligned(at, 64), 64), WIDE:] = right

                @pl.when(y == 0)
                def _(put=put, x=x, t=t):
                    put(mo_ref, half * x + 64 * t)

                @pl.when(y == 1)
                def _(put=put, x=x, t=t):
                    if t == 0:
                        put(mo_ref, half * x + 128)
                    else:
                        put(ao_ref, 64 * x)

            ai_ref[rows, 2 * RQ * t : 2 * RQ * (t + 1)] = query
        mi_ref[2 * DS : 2 * DS + 2 * NS, rows] = shared.T
        mi_ref[DS + CONVD :, rows] = steps
        ai_ref[rows, QD:] = keys


def on_chip(kernel, c, inputs, outs, scratch=(), micros=2):
    inside = pl.BlockSpec(memory_space=pltpu.VMEM)
    return pl.pallas_call(
        kernel,
        in_specs=[pl.BlockSpec(memory_space=pltpu.SMEM)] + [inside] * len(inputs),
        out_specs=[inside] * len(outs),
        out_shape=[jax.ShapeDtypeStruct(*o) for o in outs],
        scratch_shapes=[pltpu.VMEM(*s) for s in scratch],
        compiler_params=pltpu.CompilerParams(vmem_limit_bytes=LIMIT),
        cost_estimate=pl.CostEstimate(flops=micros * 10**9, bytes_accessed=micros * 3 * 10**6, transcendentals=0),
    )(c, *inputs)


def small_parameters(one, per_head, c, x):
    quarter = CONVD // 4
    cut = lax.dynamic_slice_in_dim

    def heads(values, width):
        parts = cut(values, c * 12 * width, 12 * width, values.ndim - 1)
        parts = [cut(parts, (6 * j + 3 * x) * width, 3 * width, values.ndim - 1) for j in range(2)]
        return jnp.concatenate(parts, axis=-1)

    conv = one[:, : 5 * quarter].reshape(4, 5, quarter).transpose(1, 0, 2).reshape(5, CONVD)
    conv = jnp.concatenate([heads(conv[:, :DS], MP), conv[:, DS:]], axis=1)
    at = 5 * quarter
    gains = one[:, at : at + 512].reshape(4, 2, 256).transpose(1, 0, 2).reshape(2, D)
    per_head = heads(per_head, 1)
    skip = jnp.pad(jnp.repeat(per_head[2], MP), (0, CONVR - RD))
    conv = jnp.pad(jnp.concatenate([conv, skip[None]], axis=0), ((0, 2), (0, 0)))
    per_head = jnp.pad(jnp.stack([per_head[0], jnp.exp(per_head[1])]), ((0, 6), (0, 128 - RH)))
    return gains[0:1], gains[1:2], conv, per_head


def small_gradients(conv_grad, head_grad, first_grad, second_grad, c, x, counted):
    def heads(values, width):
        out = jnp.zeros(values.shape[:-1] + (MH * width,), f32)
        for j in range(2):
            part = values[..., 3 * width * j : 3 * width * (j + 1)]
            out = lax.dynamic_update_slice_in_dim(out, part, (12 * c + 6 * j + 3 * x) * width, values.ndim - 1)
        return out

    first = ((c == 0) & (x == 0)).astype(f32)
    wide = jnp.concatenate([heads(conv_grad[:5, :RD], MP), conv_grad[:5, RD:]], axis=1)
    skip = conv_grad[5, :RD].reshape(RH, MP).sum(axis=1)
    per_head = heads(jnp.stack([head_grad[0, :RH], head_grad[1, :RH], skip]), 1)
    flat = jnp.concatenate(
        [wide.reshape(-1), first_grad[0] * counted.astype(f32), second_grad[0] * first, per_head.reshape(-1)]
    )
    return jnp.pad(flat, (0, 88 * 128 - flat.shape[0])).reshape(88, 128)


def summed_small(grads, c, wait, last):
    total = after(jnp.stack(grads), wait)
    total = total + paired_lines(total, 1)
    total = total + paired_lines(total, 2)
    first, second = total[0], total[1]
    total = jnp.where(c == 0, first, second) + swapped(jnp.where(c == 0, second, first), CORE)
    total = total + swapped(after(total, last), COL)
    return total + swapped(total, ROW)


def paired(
    block_input,
    output_grad,
    doc_lengths,
    first_gain,
    mixer_in,
    conv_kernel,
    conv_bias,
    step_bias,
    decay_log,
    skip_gain,
    mixer_out,
    attention_in,
    attention_out,
    second_gain,
    gate_up,
    down_weight,
):
    c, y, x, z = (lax.axis_index(a) for a in AXES)
    at = jnp.stack([c, y, x, z]).astype(jnp.int32)
    cut = lax.dynamic_slice_in_dim
    quarter = CONVD // 4

    free = jnp.concatenate([conv_kernel[0].reshape(-1), conv_bias[0], first_gain[0], second_gain[0]])
    free = jnp.pad(free, (0, FREE * 128 - free.shape[0])).reshape(FREE, 128).T
    free = jnp.pad(free, ((0, 0), (8, 120 - FREE)))

    keep_a, give_a = on_chip(
        prepare_a_kernel,
        at,
        (mixer_in[0].T, attention_in[0], mixer_out[0], attention_out[0], free),
        [((2, 128, GROUP_A), bf16)] * 2,
    )
    got_a = swapped(give_a, CORE)

    def halves(keep, got, s):
        return jnp.where(c == s, lax.dynamic_index_in_dim(keep, y, 0, False), lax.dynamic_index_in_dim(got, y, 0, False))

    half_a0 = halves(keep_a, got_a, 0)
    lines_a0 = lax.all_gather(half_a0, LINE)
    keep_b, give_b = on_chip(
        prepare_b_kernel, after(at, half_a0), (gate_up[0], down_weight[0]), [((2, 128, GROUP_B), bf16)] * 2
    )
    got_b = swapped(give_b, CORE)
    rows_in = jnp.concatenate([block_input[:, 0], output_grad[:, 0]], axis=2)
    rows_in = after(rows_in, half_a0)
    whole = whole_rows(rows_in, y, x)
    x0, cot = whole[:, :D], whole[:, D:]
    per_head = jnp.stack([step_bias[0], decay_log[0], skip_gain[0]])
    per_head = ordered(c, per_head, swapped(after(per_head, half_a0), CORE))

    def small_of(piece):
        return jnp.swapaxes(piece[..., RAW_AT + 8 : RAW_AT + 8 + FREE], -1, -2).astype(f32)

    smalls = [small_parameters(small_of(lines_a0).reshape(4, -1), per_head[0], c, x)]
    doc_sizes = lax.dynamic_index_in_dim(doc_lengths[:, 0], y, 0, False)
    length = x0.shape[0]
    positions = jnp.arange(length, dtype=jnp.int32)
    ids = doc_layout(doc_sizes, positions)[0]
    taps = [(positions >= by) & (jnp.roll(ids, by) == ids) for by in range(1, CONV)]
    tok = jnp.pad(jnp.stack([ids.astype(f32)] + [t.astype(f32) for t in taps], axis=1), ((0, 0), (0, 128 - CONV)))
    idr = jnp.broadcast_to(ids.astype(f32)[None], (8, length))
    half = length // 2
    partial = [((half, D), bf16), ((half, D), bf16)]

    def others(lines):
        return jnp.stack([lax.dynamic_index_in_dim(lines, (z + k) % 4, 0, False) for k in (1, 2, 3)])

    def unpack_a(s, near, far):
        wi, mine, give = on_chip(
            functools.partial(lines_a_kernel, s),
            at,
            (keep_a, got_a, near[:, :, :GROUP_A], far),
            [((D, INC), bf16), ((256, D), bf16), ((256, D), bf16)],
        )
        return wi, mine, swapped(give, CORE)

    def unpack_b(s, near, far):
        return on_chip(
            functools.partial(lines_b_kernel, s),
            at,
            (keep_b, got_b, near[:, :, -GROUP_B:], far),
            [((D, 2 * RF), bf16), ((RF, D), bf16)],
        )

    def first_part(entry, own, other, s, wi, mine, got):
        gain, _, conv, per_head = smalls[s]
        return on_chip(
            first_kernel,
            at,
            (entry, own, other, gain, wi, mine, got, conv, per_head, tok, idr),
            partial
            + [
                ((length, D), bf16),
                ((length, INC), bf16),
                ((length, RD), f32),
                ((length, OUTR), bf16),
                ((length, D), bf16),
                ((OUTR, D), bf16),
            ],
            [
                ((length, RD), f32),
                ((length, 2 * NS), bf16),
                ((length, RD), bf16),
                ((length, 128), f32),
                ((128, length), f32),
            ],
            15,
        )

    def second_part(entry, own, other, s, wgu, wd):
        return on_chip(
            second_kernel,
            at,
            (entry, own, other, smalls[s][1], wgu, wd),
            partial
            + [((length, D), f32), ((length, D), bf16), ((length, 2 * RF), f32), ((length, RF), bf16)],
            micros=8,
        )

    half_b0 = halves(keep_b, got_b, 0)
    lines_b0 = lax.all_gather(after(half_b0, lines_a0), LINE)
    far_a0 = swapped(after(others(lines_a0), whole, tok, idr, per_head), ROW)
    half_a1 = after(halves(keep_a, got_a, 1), lines_b0, far_a0)
    lines_a1 = lax.all_gather(half_a1, LINE)
    x0 = after(x0, half_a1)
    wi0, mine, got = unpack_a(0, lines_a0, far_a0)
    far_b0 = swapped(others(lines_b0), ROW)
    keep, give, x0, proj0, state0, ga0, h0, wo0 = first_part(x0, smalls[0][0], smalls[0][0], 0, wi0, mine, got)
    give = after(give, far_b0)
    own, other = quarter_sum(keep, give)
    wgu0, wd0 = unpack_b(0, lines_b0, far_b0)
    keep, give, mid0, g0, gu0, hid0 = second_part(x0, own, other, 0, wgu0, wd0)
    lines_b1 = lax.all_gather(after(halves(keep_b, got_b, 1), lines_a1, keep), LINE)
    far_a1 = swapped(others(lines_a1), ROW)
    smalls.append(small_parameters(small_of(after(lines_a1, mid0)).reshape(4, -1), per_head[1], c, x))
    own, other = quarter_sum(keep, give)
    wi1, mine, got = unpack_a(1, lines_a1, far_a1)
    keep, give, x1, proj1, state1, ga1, h1, wo1 = first_part(mid0, own, other, 1, wi1, mine, got)
    far_b1 = swapped(others(lines_b1), ROW)
    own, other = quarter_sum(keep, give)
    wgu1, wd1 = unpack_b(1, lines_b1, far_b1)
    late_keep, late_give, mid1, g1, gu1, hid1 = second_part(x1, own, other, 1, wgu1, wd1)

    def back_second(cot, s, gu, wgu, wd):
        return on_chip(
            back_second_kernel, at, (cot, gu, wgu, wd), partial + [((length, 2 * RF), bf16)], micros=7
        )

    def back_first(cot, own, other, s, mid, proj, state, ga, wi, wo):
        gain, conv, per_head = smalls[s][1:]
        return on_chip(
            back_first_kernel,
            at,
            (cot, own, other, mid, gain, proj, state, ga, wi, wo, conv, per_head, tok, idr),
            partial
            + [
                ((256, D), bf16),
                ((256, D), bf16),
                ((length, D), f32),
                ((length, INC), bf16),
                ((1, D), f32),
                ((8, CONVR), f32),
                ((8, 128), f32),
            ],
            [
                ((length, D), bf16),
                ((length, OUTR), f32),
                ((length, RD), f32),
                ((length, 2 * NS), bf16),
                ((length, RD), bf16),
                ((length, 128), f32),
                ((128, length), f32),
                ((length, RD), bf16),
                ((length, RD), f32),
                ((length, 2 * NS), f32),
                ((length, 2 * HD), f32),
                ((length, RD), f32),
            ],
            25,
        )

    def back_input(s, entry, own, other, mid_grad):
        return on_chip(
            back_input_kernel,
            at,
            (entry, own, other, smalls[s][0], mid_grad),
            [((length, D), bf16), ((1, D), f32)],
            micros=4,
        )

    def shapes(split, columns):
        if not split:
            return [((4, 2, 128, columns), bf16)]
        return [((4, 128, columns), bf16)] + [((4 // split, 128, columns), bf16)] * split

    def grads_b(split, *inputs):
        return on_chip(grads_b_kernel, at, inputs, shapes(split, GROUP_B), micros=5)

    def grads_a(split, h, proj_grad, mine, give):
        inputs = (h, proj_grad, mine, swapped(give, CORE))
        return on_chip(grads_a_kernel, at, inputs, shapes(split, GROUP_A), micros=5)

    def added(grads, *got):
        got = jnp.concatenate(got, axis=0) if len(got) > 1 else got[0]
        return (grads[0].astype(f32) + got.astype(f32)).astype(bf16)

    def lines_first(grads):
        columns = grads[0].shape[3]
        sums = scattered(grads[0].reshape(4, 256, columns)).reshape(2, 128, columns)
        mine = lax.dynamic_index_in_dim(sums, y, 0, False)
        theirs = lax.dynamic_index_in_dim(sums, 1 - y, 0, False)
        return (mine.astype(f32) + swapped(theirs, ROW).astype(f32)).astype(bf16)

    def scattered(lines):
        return lax.psum_scatter(lines, LINE, scatter_dimension=0)

    def both_ranks(first, second):
        return ordered(c, jnp.where(c == 0, first, second), swapped(jnp.where(c == 0, second, first), CORE))

    def spread_rows(piece, s):
        given = sent(piece, [(p, (s,) + p[1:]) for p in every if p[0] != s])
        block = jnp.stack([piece, given] if s == 0 else [given, piece])
        return jnp.stack([block, sent(block, [(p, (s, 1 - p[1], p[2], p[3])) for p in every if p[0] == s])])

    def spread_one(piece, s):
        given = sent(piece, [(p, (s,) + p[1:]) for p in every if p[0] != s])
        block = jnp.stack([piece, given] if s == 0 else [given, piece])
        mine = [p for p in every if p[0] == s]
        flips = [[(p, (s, p[1] ^ i, p[2] ^ k, p[3])) for p in mine] for i, k in ((0, 1), (1, 0), (1, 1))]
        return [block] + [sent(block, f) for f in flips]

    cot1 = cot
    keep, give, gu_grad = back_second(cot1, 1, gu1, wgu1, wd1)
    own, other = quarter_sum(keep, give)
    late_give = after(late_give, own)
    late, late_other = quarter_sum(late_keep, late_give)
    gb1 = grads_b(0, g1, gu_grad, hid1, cot1)
    own = after(own, gb1[0])
    sum_b1 = lines_first(gb1)
    keep, give, mine, give_out, mid_grad, proj_grad, second1, conv1, head1 = back_first(
        cot1, own, other, 1, mid1, proj1, state1, ga1, wi1, wo1
    )
    give = after(give, late)
    own, other = quarter_sum(keep, give)
    ga1_ = grads_a(0, h1, proj_grad, mine, give_out)
    own = after(own, ga1_[0], sum_b1, late_other)
    sum_a1 = lines_first(ga1_)
    cot0, first1 = back_input(1, x1, own, other, mid_grad)
    keep, give, gu_grad = back_second(cot0, 0, gu0, wgu0, wd0)
    own, other = quarter_sum(keep, give)
    gb0 = grads_b(1, g0, gu_grad, hid0, cot0)
    gb0_got = swapped(gb0[1], ROW)
    near_b1 = spread_rows(sum_b1, 1)
    own = after(own, gb0[0], near_b1)
    plane_b1 = near_b1, sent(near_b1, [(p, (1, p[1], 1 - p[2], p[3])) for p in every if p[0] == 1])
    keep, give, mine, give_out, mid_grad, proj_grad, second0, conv0, head0 = back_first(
        cot0, own, other, 0, mid0, proj0, state0, ga0, wi0, wo0
    )
    ga0_ = grads_a(2, h0, proj_grad, mine, give_out)
    ga0_got = [swapped(ga0_[1], ROW)]
    ga0_got.append(swapped(after(ga0_[2], ga0_got[0]), ROW))
    lines_gb0 = added(gb0, after(gb0_got, ga0_[0]))
    b0 = scattered(lines_gb0)
    own = half_sum(keep, after(give, ga0_[0]))
    low0, first0 = on_chip(
        back_half_kernel,
        at,
        (x0, own, smalls[0][0], mid_grad),
        [((half, D), bf16), ((1, D), f32)],
        micros=3,
    )
    block = both_ranks(jnp.pad(b0, ((0, 0), (0, GROUP_A - GROUP_B))), sum_a1)
    lines_ga0 = added(ga0_, ga0_got[0], after(ga0_got[1], first0, block, plane_b1[1]))
    a0 = scattered(lines_ga0)
    block = after(block, lines_ga0)
    plane_two = block, swapped(block, COL), swapped(block, ROW), across(block)
    gate_up_grad, down_grad = on_chip(
        final_b_kernel, at, (*plane_two, *plane_b1), [((256, 2 * FF), f32), ((RF, D), f32)], micros=4
    )
    plane_a0 = spread_one(after(a0, *plane_two), 0)
    mixer_in_grad, attention_in_grad, mixer_out_grad, attention_out_grad = on_chip(
        final_a_kernel,
        at,
        (*plane_a0, *plane_two),
        [((DS + CONVD + MH, 256), f32), ((256, QD + 2 * KVD), f32), ((RD, D), f32), ((128, D), f32)],
        micros=40,
    )

    out1 = (mid1 + ordered(c, late, late_other).reshape(length, D).astype(f32)).astype(bf16)
    section_output = back_rows(jnp.where(c == 0, x1, out1), y, x)
    part = lax.dynamic_slice_in_dim(low0, x * (half // 2), half // 2, 0)
    part = after(part, plane_a0[0])
    moved = [sent(part, [(p, (0, p[0], p[2], p[3])) for p in every if p[1] == m]) for m in range(2)]
    input_grad = jnp.where(c == 0, jnp.stack(moved), back_rows(cot0, y, x))
    grads = [
        small_gradients(conv0, head0, first0, second0, c, x, x == 0),
        small_gradients(conv1, head1, first1, second1, c, x, (c == 0) & (x == 0)),
    ]
    sums = summed_small(grads, c, first0, plane_a0[0]).reshape(-1)
    wide = sums[: 5 * CONVD].reshape(5, CONVD)
    start = 5 * CONVD
    conv_out = cut(wide, z * quarter, quarter, 1)
    first_out = cut(sums[start : start + D], z * 256, 256, 0)
    second_out = cut(sums[start + D : start + 2 * D], z * 256, 256, 0)
    head_out = sums[start + 2 * D : start + 2 * D + 3 * MH].reshape(3, MH)
    return (
        section_output[None, :, None],
        input_grad[None, :, None],
        first_out[None],
        mixer_in_grad.T[None],
        conv_out[None, :4],
        conv_out[None, 4],
        head_out[None, 0],
        head_out[None, 1],
        head_out[None, 2],
        mixer_out_grad[None],
        attention_in_grad[None],
        attention_out_grad[None],
        second_out[None],
        gate_up_grad[None],
        down_grad[None],
    )


def paired_specs():
    plane = (ROW, COL)
    rows = P(CORE, LINE, None)
    placed = (
        P(None, LINE, plane, None),
        P(None, LINE, plane, None),
        P(None, LINE, None),
        P(CORE, LINE),
        rows,
        P(CORE, None, LINE),
        P(CORE, LINE),
        P(CORE, None),
        P(CORE, None),
        P(CORE, None),
        rows,
        rows,
        rows,
        P(CORE, LINE),
        rows,
        rows,
    )
    given = (
        P(CORE, None, LINE, plane, None),
        P(CORE, None, LINE, plane, None),
        P(CORE, LINE),
        rows,
        P(CORE, None, LINE),
        P(CORE, LINE),
        P(CORE, None),
        P(CORE, None),
        P(CORE, None),
        rows,
        rows,
        rows,
        P(CORE, LINE),
        rows,
        rows,
    )
    return placed, given


def solution(mesh):
    if tuple(mesh.devices.shape) == (2, 4, 4):
        fine = Mesh(mesh.devices.reshape(2, 2, 2, 4), AXES)
        placed, given = paired_specs()
        return jax.shard_map(paired, mesh=fine, in_specs=placed, out_specs=given, check_vma=False)
    return spread(mesh)
```

```python
import functools
import math

import jax
import jax.numpy as jnp
from jax import lax
from jax.experimental import pallas as pl
from jax.experimental.pallas import tpu as pltpu
from jax.sharding import Mesh, PartitionSpec as P

D = 1024
FF = 2048
MH = 24
MP = 64
NS = 128
QH = 8
KVH = 2
HD = 64
CONV = 4
MICRO = 2
SPAN = 128
KEY_BLOCK = 1024
DS = 1536
CONVD = 1792
QD = 512
KVD = 128


epsilon = 1e-05
masked_value = -1e30
highest = lax.Precision.HIGHEST
weight_names = (
    "first_gain",
    "mixer_in",
    "conv_kernel",
    "conv_bias",
    "mixer_out",
    "attention_in",
    "attention_out",
    "second_gain",
    "gate_up",
    "down_weight",
)


def passed_along(value, axis, by):
    length = lax.axis_size(axis)
    pairs = [(i, i + by) for i in range(length) if 0 <= i + by < length]
    return lax.ppermute(value, axis, pairs)


def prefix(value, axis, combine, identity):
    length, position = (lax.axis_size(axis), lax.axis_index(axis))
    everything = jax.tree.map(
        lambda part, kind: lax.all_gather(part.astype(kind), axis),
        value,
        (jnp.bfloat16, jnp.bfloat16),
    )
    start = jax.tree.map(
        lambda part, zero: jnp.broadcast_to(jnp.asarray(zero, part.dtype), part.shape),
        value,
        identity,
    )

    def step(k, before):
        reached = k < position
        new = combine(
            before, jax.tree.map(lambda part, own: part[k].astype(own.dtype), everything, value)
        )
        return jax.tree.map(lambda a, b: jnp.where(reached, a, b), new, before)

    return lax.fori_loop(0, length, step, start)


def prefix_2(value, axis, join, neutral):
    count = lax.axis_size(axis)
    place = lax.axis_index(axis)
    ahead = count - 1 - place
    gathered = jax.tree.map(
        lambda a, kind: lax.all_gather(a.astype(kind), axis),
        value,
        jax.tree.map(lambda a: jnp.bfloat16 if a.dtype == jnp.float32 else a.dtype, value),
    )
    state = jax.tree.map(lambda a, e: jnp.zeros_like(a) + jnp.asarray(e, a.dtype), value, neutral)

    def one(step, state):
        source = count - 1 - step
        return join(
            state,
            jax.tree.map(
                lambda a, own: lax.dynamic_index_in_dim(a, source, 0, False).astype(own.dtype),
                gathered,
                value,
            ),
        )

    return lax.fori_loop(0, ahead, one, state)


def inner_rows(left, right):
    return lax.dot_general(
        left, right, (((0,), (0,)), ((), ())), preferred_element_type=jnp.float32
    )


def outer_cols(left, right):
    return lax.dot_general(
        left, right, (((1,), (1,)), ((), ())), preferred_element_type=jnp.float32
    )


def norm_apply(hidden_in, gain_vec):
    return (
        hidden_in
        * lax.rsqrt(jnp.mean(hidden_in * hidden_in, axis=-1, keepdims=True) + epsilon)
        * gain_vec
    )


def norm_back(hidden_in, gain_vec, upstream):
    scale = lax.rsqrt(jnp.mean(hidden_in * hidden_in, axis=-1, keepdims=True) + epsilon)
    normed = hidden_in * scale
    weighted = upstream * gain_vec
    hidden_grad = scale * (weighted - normed * jnp.mean(weighted * normed, axis=-1, keepdims=True))
    return (hidden_grad, jnp.sum(upstream * normed, axis=0))


def running_sum(value):
    count = value.shape[0]
    until = lax.broadcasted_iota(jnp.int32, (count, count), 0) >= lax.broadcasted_iota(
        jnp.int32, (count, count), 1
    )
    return jnp.dot(until.astype(jnp.float32), value, precision=highest)


def doc_layout(doc_sizes, positions):
    count = doc_sizes.shape[0]
    until = lax.broadcasted_iota(jnp.int32, (count, count), 0) >= lax.broadcasted_iota(
        jnp.int32, (count, count), 1
    )
    bounds = jnp.sum(jnp.where(until, doc_sizes[None, :], 0), axis=1)[:-1]
    doc_ids = jnp.sum((positions[:, None] >= bounds[None, :]).astype(jnp.int32), axis=1)
    starts = jnp.any(positions[:, None] == bounds[None, :], axis=1)
    return (doc_ids, starts)


def conv_apply(extended, ext_ids, kernel, offset_vec):
    amount = extended.shape[0] - CONV + 1
    own_ids = ext_ids[CONV - 1 :]
    summed = offset_vec[None, :] + jnp.zeros((amount, 1), extended.dtype)
    for tap_index in range(CONV):
        same_doc = (ext_ids[tap_index : tap_index + amount] == own_ids).astype(extended.dtype)
        summed = (
            summed
            + kernel[tap_index][None, :]
            * extended[tap_index : tap_index + amount]
            * same_doc[:, None]
        )
    return jax.nn.silu(summed)


def span_pass(carried_state, pieces):
    values, write_vec, read_vec, step_size, log_decay, doc_ids, before = pieces
    amount = values.shape[0]
    running = running_sum(log_decay)
    row_ids = lax.broadcasted_iota(jnp.int32, (amount, amount), 0)
    col_ids = lax.broadcasted_iota(jnp.int32, (amount, amount), 1)
    allowed = (col_ids <= row_ids) & (doc_ids[:, None] == doc_ids[None, :])
    log_gap = jnp.where(
        allowed[:, :, None], running[:, None, :] - running[None, :, :], masked_value
    )
    intersection = jnp.einsum("in,jn->ij", read_vec, write_vec, precision=highest)
    mixing = intersection[:, :, None] * jnp.exp(log_gap) * step_size[None, :, :]
    within = jnp.einsum("ijh,jhp->ihp", mixing, values, precision=highest)
    inflow = jnp.exp(running) * (doc_ids == before)[:, None].astype(jnp.float32)
    carried = (
        jnp.einsum("in,hpn->ihp", read_vec, carried_state, precision=highest) * inflow[:, :, None]
    )
    to_end = (
        jnp.exp(running[-1][None, :] - running)
        * (doc_ids == doc_ids[-1])[:, None].astype(jnp.float32)
        * step_size
    )
    increment = jnp.einsum("jh,jhp,jn->hpn", to_end, values, write_vec, precision=highest)
    return (inflow[-1][:, None, None] * carried_state + increment, within + carried)


def mixer_local(
    extended,
    raw_rate,
    kernel,
    offset_vec,
    step_bias,
    decay_log,
    skip_gain,
    state_in,
    ext_ids,
    doc_ids,
    starts,
):
    tokens = raw_rate.shape[0]
    conv_out = conv_apply(extended, ext_ids, kernel, offset_vec)
    values = conv_out[:, :DS].reshape(tokens, MH, MP)
    read_vector = conv_out[:, DS + NS :]
    step_size = jax.nn.softplus(raw_rate + step_bias)
    log_decay = -step_size * jnp.exp(decay_log)
    blocks = tokens // SPAN
    pieces = (
        values.reshape(blocks, SPAN, MH, MP),
        conv_out[:, DS : DS + NS].reshape(blocks, SPAN, NS),
        read_vector.reshape(blocks, SPAN, NS),
        step_size.reshape(blocks, SPAN, MH),
        log_decay.reshape(blocks, SPAN, MH),
        doc_ids.reshape(blocks, SPAN),
        doc_ids[::SPAN] - starts[::SPAN].astype(jnp.int32),
    )
    state_out, outputs = lax.scan(span_pass, state_in, pieces)
    result = outputs.reshape(tokens, MH, MP) + skip_gain[None, :, None] * values
    return ((result.reshape(tokens, DS), state_out), (read_vector, log_decay))


def device_inflow(log_decay, doc_ids, starts):
    same_doc = (doc_ids == doc_ids[0] - starts[0].astype(jnp.int32)).astype(jnp.float32)
    return jnp.exp(running_sum(log_decay)) * same_doc[:, None]


def chain_affine(earlier, later):
    return (earlier[0] * later[0], later[0][:, None, None] * earlier[1] + later[1])


def query_groups(flat):
    tokens = flat.shape[0]
    per_group = QH // KVH
    return (
        flat.reshape(tokens, KVH, per_group, HD)
        .transpose(1, 2, 0, 3)
        .reshape(KVH, per_group * tokens, HD)
    )


def query_flat(grouped, tokens):
    per_group = QH // KVH
    return grouped.reshape(KVH, per_group, tokens, HD).transpose(2, 0, 1, 3).reshape(tokens, QD)


def score_block(queries, key_rows, query_pos, query_ids, all_ids, offset, block_len):
    key_block = lax.dynamic_slice_in_dim(key_rows, offset, block_len, 0)
    key_part = key_block[:, :KVD].reshape(block_len, KVH, HD)
    value_part = key_block[:, KVD:].reshape(block_len, KVH, HD)
    key_pos = offset + jnp.arange(block_len, dtype=jnp.int32)
    key_ids = lax.dynamic_slice_in_dim(all_ids, offset, block_len, 0)
    allowed = (key_pos[None, :] <= query_pos[:, None]) & (key_ids[None, :] == query_ids[:, None])
    scores = (
        jnp.einsum("grd,kgd->grk", queries, key_part, preferred_element_type=jnp.float32) * 0.125
    )
    return (jnp.where(allowed[None], scores, masked_value), allowed, key_part, value_part)


def attend_forward(queries_flat, key_rows, positions, doc_ids, all_ids, ctx_index):
    tokens = queries_flat.shape[0]
    per_group = QH // KVH
    queries = query_groups(queries_flat)
    query_pos = jnp.tile(positions, per_group)
    query_ids = jnp.tile(doc_ids, per_group)
    block_len = math.gcd(key_rows.shape[0], KEY_BLOCK)
    block_count = ((ctx_index + 1) * tokens + block_len - 1) // block_len

    def visit_block(block_index, carry):
        running_max, running_sum, accumulated = carry
        scores, allowed, key_part, value_part = score_block(
            queries, key_rows, query_pos, query_ids, all_ids, block_index * block_len, block_len
        )
        new_max = jnp.maximum(running_max, jnp.max(scores, axis=-1))
        chances = jnp.where(allowed[None], jnp.exp(scores - new_max[..., None]), 0.0)
        rescale = jnp.exp(running_max - new_max)
        running_sum = running_sum * rescale + jnp.sum(chances, axis=-1)
        accumulated = accumulated * rescale[..., None] + jnp.einsum(
            "grk,kgd->grd",
            chances.astype(jnp.bfloat16),
            value_part,
            preferred_element_type=jnp.float32,
        )
        return (new_max, running_sum, accumulated)

    row_count = per_group * tokens
    start_carry = (
        jnp.full((KVH, row_count), masked_value, jnp.float32),
        jnp.zeros((KVH, row_count), jnp.float32),
        jnp.zeros((KVH, row_count, HD), jnp.float32),
    )
    running_max, running_sum, accumulated = lax.fori_loop(0, block_count, visit_block, start_carry)
    output = accumulated / running_sum[..., None]
    return (query_flat(output, tokens), running_max + jnp.log(running_sum))


def attend_backward(
    queries_flat,
    key_rows,
    attention_raw,
    log_norm,
    grad_low,
    positions,
    doc_ids,
    all_ids,
    ctx_index,
):
    tokens = queries_flat.shape[0]
    length = key_rows.shape[0]
    per_group = QH // KVH
    queries = query_groups(queries_flat)
    grad_rows = query_groups(grad_low)
    grad_wide = grad_rows.astype(jnp.float32)
    delta = jnp.sum(grad_wide * query_groups(attention_raw), axis=-1)
    query_pos = jnp.tile(positions, per_group)
    query_ids = jnp.tile(doc_ids, per_group)
    block_len = math.gcd(length, KEY_BLOCK)
    block_count = ((ctx_index + 1) * tokens + block_len - 1) // block_len

    def visit_block(block_index, carry):
        query_grad, key_grad, value_grad = carry
        offset = block_index * block_len
        scores, allowed, key_part, value_part = score_block(
            queries, key_rows, query_pos, query_ids, all_ids, offset, block_len
        )
        chances = jnp.where(allowed[None], jnp.exp(scores - log_norm[..., None]), 0.0)
        prob_grad = jnp.einsum(
            "grd,kgd->grk", grad_rows, value_part, preferred_element_type=jnp.float32
        )
        score_grad = (chances * (prob_grad - delta[..., None])).astype(jnp.bfloat16)
        query_grad = query_grad + jnp.einsum(
            "grk,kgd->grd", score_grad, key_part, preferred_element_type=jnp.float32
        )
        key_piece = (
            jnp.einsum("grk,grd->kgd", score_grad, queries, preferred_element_type=jnp.float32)
            * 0.125
        )
        value_piece = jnp.einsum(
            "grk,grd->kgd",
            chances.astype(jnp.bfloat16),
            grad_rows,
            preferred_element_type=jnp.float32,
        )
        key_grad = lax.dynamic_update_slice_in_dim(
            key_grad,
            lax.dynamic_slice_in_dim(key_grad, offset, block_len, 0)
            + key_piece.reshape(block_len, KVD),
            offset,
            0,
        )
        value_grad = lax.dynamic_update_slice_in_dim(
            value_grad,
            lax.dynamic_slice_in_dim(value_grad, offset, block_len, 0)
            + value_piece.reshape(block_len, KVD),
            offset,
            0,
        )
        return (query_grad, key_grad, value_grad)

    start_carry = (
        jnp.zeros((KVH, per_group * tokens, HD), jnp.float32),
        jnp.zeros((length, KVD), jnp.float32),
        jnp.zeros((length, KVD), jnp.float32),
    )
    query_grad, key_grad, value_grad = lax.fori_loop(0, block_count, visit_block, start_carry)
    return (query_flat(query_grad * 0.125, tokens), key_grad, value_grad)


def layer_layout(doc_sizes, tokens, ctx_index, ctx_count):
    positions = ctx_index * tokens + jnp.arange(tokens, dtype=jnp.int32)
    doc_ids, starts = doc_layout(doc_sizes, positions)
    all_ids = doc_layout(doc_sizes, jnp.arange(tokens * ctx_count, dtype=jnp.int32))[0]
    ext_ids = doc_layout(
        doc_sizes, ctx_index * tokens - (CONV - 1) + jnp.arange(tokens + CONV - 1, dtype=jnp.int32)
    )[0]
    return (positions, doc_ids, starts, all_ids, ext_ids)


def layer_forward(hidden_in, weights_full, head_params, doc_sizes, ctx_index, ctx_count):
    tokens = hidden_in.shape[0]
    positions, doc_ids, starts, all_ids, ext_ids = layer_layout(
        doc_sizes, tokens, ctx_index, ctx_count
    )
    normed = norm_apply(hidden_in, weights_full["first_gain"].astype(jnp.float32)).astype(
        jnp.bfloat16
    )
    projected = jnp.dot(
        normed, weights_full["mixer_in"], preferred_element_type=jnp.float32
    ).astype(jnp.bfloat16)
    edge_rows = passed_along(projected[tokens - (CONV - 1) :, DS : DS + CONVD], "ctx", 1)
    extended = jnp.concatenate([edge_rows, projected[:, DS : DS + CONVD]], axis=0).astype(
        jnp.float32
    )
    raw_rate = projected[:, DS + CONVD :].astype(jnp.float32)
    step_bias, decay_log, skip_gain = head_params
    empty_state = jnp.zeros((MH, MP, NS), jnp.float32)
    (partial_out, local_state), (read_vector, log_decay) = mixer_local(
        extended,
        raw_rate,
        weights_full["conv_kernel"].astype(jnp.float32),
        weights_full["conv_bias"].astype(jnp.float32),
        step_bias,
        decay_log,
        skip_gain,
        empty_state,
        ext_ids,
        doc_ids,
        starts,
    )
    inflow = device_inflow(log_decay, doc_ids, starts)
    state_in = prefix(
        (inflow[-1], local_state), "ctx", chain_affine, (jnp.ones((MH,), jnp.float32), empty_state)
    )[1]
    carried = (
        jnp.einsum("tn,hpn->thp", read_vector, state_in, precision=highest) * inflow[:, :, None]
    )
    ssm_out = partial_out + carried.reshape(tokens, DS)
    gate_value = projected[:, :DS].astype(jnp.float32)
    gated_out = (ssm_out * jax.nn.silu(gate_value)).astype(jnp.bfloat16)
    mixer_term = jnp.dot(gated_out, weights_full["mixer_out"], preferred_element_type=jnp.float32)
    heads_in = jnp.dot(
        normed, weights_full["attention_in"], preferred_element_type=jnp.float32
    ).astype(jnp.bfloat16)
    key_rows = lax.all_gather(heads_in[:, QD:], "ctx", axis=0, tiled=True)
    attention_raw, log_norm = attend_forward(
        heads_in[:, :QD], key_rows, positions, doc_ids, all_ids, ctx_index
    )
    attention_term = jnp.dot(
        attention_raw.astype(jnp.bfloat16),
        weights_full["attention_out"],
        preferred_element_type=jnp.float32,
    )
    middle = hidden_in + mixer_term + attention_term
    normed_mid = norm_apply(middle, weights_full["second_gain"].astype(jnp.float32)).astype(
        jnp.bfloat16
    )
    expanded = jnp.dot(normed_mid, weights_full["gate_up"], preferred_element_type=jnp.float32)
    hidden = (jax.nn.silu(expanded[:, :FF]) * expanded[:, FF:]).astype(jnp.bfloat16)
    result = middle + jnp.dot(
        hidden, weights_full["down_weight"], preferred_element_type=jnp.float32
    )
    stored = (
        hidden_in,
        middle,
        projected,
        edge_rows,
        state_in,
        ssm_out,
        heads_in,
        key_rows,
        attention_raw,
        log_norm,
        expanded,
    )
    return (result, stored)


def layer_backward(grad_in, stored, weights_full, head_params, doc_sizes, ctx_index, ctx_count):
    (
        hidden_in,
        middle,
        projected,
        edge_rows,
        state_in,
        ssm_out,
        heads_in,
        key_rows,
        attention_raw,
        log_norm,
        expanded,
    ) = stored
    tokens = hidden_in.shape[0]
    positions, doc_ids, starts, all_ids, ext_ids = layer_layout(
        doc_sizes, tokens, ctx_index, ctx_count
    )
    first_gain = weights_full["first_gain"].astype(jnp.float32)
    second_gain = weights_full["second_gain"].astype(jnp.float32)
    down_low = grad_in.astype(jnp.bfloat16)
    gate_vals = expanded[:, :FF]
    up_vals = expanded[:, FF:]
    gate_sig = jax.nn.sigmoid(gate_vals)
    hidden = (jax.nn.silu(gate_vals) * up_vals).astype(jnp.bfloat16)
    down_weight_grad = inner_rows(hidden, down_low)
    hidden_grad = outer_cols(down_low, weights_full["down_weight"])
    slope = gate_sig * (1.0 + gate_vals * (1.0 - gate_sig))
    expand_grad = jnp.concatenate(
        [hidden_grad * up_vals * slope, hidden_grad * jax.nn.silu(gate_vals)], axis=1
    ).astype(jnp.bfloat16)
    normed_mid = norm_apply(middle, second_gain).astype(jnp.bfloat16)
    gate_up_grad = inner_rows(normed_mid, expand_grad)
    mid_norm_grad, second_gain_grad = norm_back(
        middle, second_gain, outer_cols(expand_grad, weights_full["gate_up"])
    )
    middle_grad = grad_in + mid_norm_grad
    residual_low = middle_grad.astype(jnp.bfloat16)
    attention_out_grad = inner_rows(attention_raw.astype(jnp.bfloat16), residual_low)
    output_low = outer_cols(residual_low, weights_full["attention_out"]).astype(jnp.bfloat16)
    query_grad, key_grad, value_grad = attend_backward(
        heads_in[:, :QD],
        key_rows,
        attention_raw,
        log_norm,
        output_low,
        positions,
        doc_ids,
        all_ids,
        ctx_index,
    )
    key_share, value_share = (
        lax.psum_scatter(
            key_grad.astype(jnp.bfloat16), "ctx", scatter_dimension=0, tiled=True
        ).astype(jnp.float32),
        lax.psum_scatter(
            value_grad.astype(jnp.bfloat16), "ctx", scatter_dimension=0, tiled=True
        ).astype(jnp.float32),
    )
    heads_grad = jnp.concatenate([query_grad, key_share, value_share], axis=1).astype(jnp.bfloat16)
    gate_value = projected[:, :DS].astype(jnp.float32)
    gate_sig_z = jax.nn.sigmoid(gate_value)
    gated_out = (ssm_out * jax.nn.silu(gate_value)).astype(jnp.bfloat16)
    mixer_out_grad = inner_rows(gated_out, residual_low)
    gated_grad = outer_cols(residual_low, weights_full["mixer_out"])
    ssm_grad = gated_grad * jax.nn.silu(gate_value)
    gate_grad = gated_grad * ssm_out * gate_sig_z * (1.0 + gate_value * (1.0 - gate_sig_z))
    extended = jnp.concatenate([edge_rows, projected[:, DS : DS + CONVD]], axis=0).astype(
        jnp.float32
    )
    raw_rate = projected[:, DS + CONVD :].astype(jnp.float32)
    step_bias, decay_log, skip_gain = head_params

    def local_piece(
        extended, raw_rate, kernel, offset_vec, step_bias, decay_log, skip_gain, state_in
    ):
        return mixer_local(
            extended,
            raw_rate,
            kernel,
            offset_vec,
            step_bias,
            decay_log,
            skip_gain,
            state_in,
            ext_ids,
            doc_ids,
            starts,
        )

    primal, pullback, (read_vector, log_decay) = jax.vjp(
        local_piece,
        extended,
        raw_rate,
        weights_full["conv_kernel"].astype(jnp.float32),
        weights_full["conv_bias"].astype(jnp.float32),
        step_bias,
        decay_log,
        skip_gain,
        state_in,
        has_aux=True,
    )
    inflow = device_inflow(log_decay, doc_ids, starts)
    local_grad = jnp.einsum(
        "th,thp,tn->hpn", inflow, ssm_grad.reshape(tokens, MH, MP), read_vector, precision=highest
    )
    state_back = prefix_2(
        (inflow[-1], local_grad),
        "ctx",
        chain_affine,
        (jnp.ones((MH,), jnp.float32), jnp.zeros((MH, MP, NS), jnp.float32)),
    )[1]
    ext_grad, raw_grad, kernel_grad, offset_grad, step_grad, decay_grad, skip_grad, unused = (
        pullback((ssm_grad, state_back))
    )
    rim_grad = passed_along(ext_grad[: CONV - 1], "ctx", -1)
    pre_grad = ext_grad[CONV - 1 :]
    pre_grad = jnp.concatenate(
        [pre_grad[: tokens - (CONV - 1)], pre_grad[tokens - (CONV - 1) :] + rim_grad], axis=0
    )
    mixer_grad = jnp.concatenate([gate_grad, pre_grad, raw_grad], axis=1).astype(jnp.bfloat16)
    normed = norm_apply(hidden_in, first_gain).astype(jnp.bfloat16)
    mixer_in_grad = inner_rows(normed, mixer_grad)
    attention_in_grad = inner_rows(normed, heads_grad)
    normed_grad = outer_cols(mixer_grad, weights_full["mixer_in"]) + outer_cols(
        heads_grad, weights_full["attention_in"]
    )
    in_norm_grad, first_gain_grad = norm_back(hidden_in, first_gain, normed_grad)
    block_grad = middle_grad + in_norm_grad
    weight_grads = (
        first_gain_grad,
        mixer_in_grad,
        kernel_grad,
        offset_grad,
        mixer_out_grad,
        attention_in_grad,
        attention_out_grad,
        second_gain_grad,
        gate_up_grad,
        down_weight_grad,
    )
    return (block_grad, weight_grads, (step_grad, decay_grad, skip_grad))


def local(
    block_input,
    output_grad,
    doc_lengths,
    first_gain,
    mixer_in,
    conv_kernel,
    conv_bias,
    step_bias,
    decay_log,
    skip_gain,
    mixer_out,
    attention_in,
    attention_out,
    second_gain,
    gate_up,
    down_weight,
):
    gathered = (
        lax.all_gather(first_gain[0], "wt", axis=0, tiled=True),
        lax.all_gather(mixer_in[0], "wt", axis=0, tiled=True),
        lax.all_gather(conv_kernel[0], "wt", axis=1, tiled=True),
        lax.all_gather(conv_bias[0], "wt", axis=0, tiled=True),
        lax.all_gather(mixer_out[0], "wt", axis=0, tiled=True),
        lax.all_gather(attention_in[0], "wt", axis=0, tiled=True),
        lax.all_gather(attention_out[0], "wt", axis=0, tiled=True),
        lax.all_gather(second_gain[0], "wt", axis=0, tiled=True),
        lax.all_gather(gate_up[0], "wt", axis=0, tiled=True),
        lax.all_gather(down_weight[0], "wt", axis=0, tiled=True),
    )
    weights_full = dict(zip(weight_names, gathered))
    head_params = (step_bias[0], decay_log[0], skip_gain[0])
    head_section = lax.axis_index("section") == 0
    ctx_index = lax.axis_index("ctx")
    ctx_count = lax.axis_size("ctx")
    tokens = block_input.shape[2]
    received = jnp.zeros((tokens, D), jnp.bfloat16)
    results = []
    stored_list = []
    for moment in range(MICRO + 1):
        own_block = block_input[min(moment, MICRO - 1), 0].astype(jnp.float32)
        entry = jnp.where(head_section, own_block, received.astype(jnp.float32))
        doc_sizes = jnp.where(
            head_section, doc_lengths[min(moment, MICRO - 1), 0], doc_lengths[max(moment - 1, 0), 0]
        )
        layer_result, stored = layer_forward(
            entry, weights_full, head_params, doc_sizes, ctx_index, ctx_count
        )
        sent = layer_result.astype(jnp.bfloat16)
        results.append(sent)
        stored_list.append((stored, doc_sizes))
        if moment < MICRO:
            received = passed_along(sent, "section", 1)
    back_received = jnp.zeros((tokens, D), jnp.bfloat16)
    total_grads = tuple((jnp.zeros(weight_full.shape, jnp.float32) for weight_full in gathered))
    total_heads = tuple((jnp.zeros(param_vec.shape, jnp.float32) for param_vec in head_params))
    sent_grads = []
    for moment in range(MICRO + 1):
        given_grad = output_grad[min(moment, MICRO - 1), 0].astype(jnp.float32)
        cotangent = jnp.where(head_section, back_received.astype(jnp.float32), given_grad)
        chosen = jax.tree.map(
            lambda left, right: jnp.where(head_section, left, right),
            stored_list[max(moment - 1, 0)],
            stored_list[min(moment + 1, MICRO)],
        )
        valid = jnp.where(head_section, moment >= 1, moment < MICRO)
        stored, doc_sizes = chosen
        block_grad, weight_grads, head_grads = layer_backward(
            cotangent, stored, weights_full, head_params, doc_sizes, ctx_index, ctx_count
        )
        total_grads = tuple(
            (old + jnp.where(valid, new, 0.0) for old, new in zip(total_grads, weight_grads))
        )
        total_heads = tuple(
            (old + jnp.where(valid, new, 0.0) for old, new in zip(total_heads, head_grads))
        )
        sent = block_grad.astype(jnp.bfloat16)
        sent_grads.append(sent)
        if moment < MICRO:
            back_received = passed_along(sent, "section", -1)
    section_output = jnp.stack(
        [
            jnp.where(head_section, results[batch_index], results[batch_index + 1])
            for batch_index in range(MICRO)
        ]
    ).reshape(1, MICRO, 1, tokens, D)
    input_grad = jnp.stack(
        [
            jnp.where(head_section, sent_grads[batch_index + 1], sent_grads[batch_index])
            for batch_index in range(MICRO)
        ]
    ).reshape(1, MICRO, 1, tokens, D)
    shares = (
        lax.psum_scatter(
            total_grads[0].astype(jnp.bfloat16), "wt", scatter_dimension=0, tiled=True
        ).astype(jnp.float32),
        lax.psum_scatter(
            total_grads[1].astype(jnp.bfloat16), "wt", scatter_dimension=0, tiled=True
        ).astype(jnp.float32),
        lax.psum_scatter(
            total_grads[2].astype(jnp.bfloat16), "wt", scatter_dimension=1, tiled=True
        ).astype(jnp.float32),
        lax.psum_scatter(
            total_grads[3].astype(jnp.bfloat16), "wt", scatter_dimension=0, tiled=True
        ).astype(jnp.float32),
        lax.psum_scatter(
            total_grads[4].astype(jnp.bfloat16), "wt", scatter_dimension=0, tiled=True
        ).astype(jnp.float32),
        lax.psum_scatter(
            total_grads[5].astype(jnp.bfloat16), "wt", scatter_dimension=0, tiled=True
        ).astype(jnp.float32),
        lax.psum_scatter(
            total_grads[6].astype(jnp.bfloat16), "wt", scatter_dimension=0, tiled=True
        ).astype(jnp.float32),
        lax.psum_scatter(
            total_grads[7].astype(jnp.bfloat16), "wt", scatter_dimension=0, tiled=True
        ).astype(jnp.float32),
        lax.psum_scatter(
            total_grads[8].astype(jnp.bfloat16), "wt", scatter_dimension=0, tiled=True
        ).astype(jnp.float32),
        lax.psum_scatter(
            total_grads[9].astype(jnp.bfloat16), "wt", scatter_dimension=0, tiled=True
        ).astype(jnp.float32),
    )
    reduced = (
        lax.psum(shares[0].astype(jnp.bfloat16), "ctx").astype(jnp.float32),
        lax.psum(shares[1].astype(jnp.bfloat16), "ctx").astype(jnp.float32),
        lax.psum(shares[2].astype(jnp.bfloat16), "ctx").astype(jnp.float32),
        lax.psum(shares[3].astype(jnp.bfloat16), "ctx").astype(jnp.float32),
        lax.psum(shares[4].astype(jnp.bfloat16), "ctx").astype(jnp.float32),
        lax.psum(shares[5].astype(jnp.bfloat16), "ctx").astype(jnp.float32),
        lax.psum(shares[6].astype(jnp.bfloat16), "ctx").astype(jnp.float32),
        lax.psum(shares[7].astype(jnp.bfloat16), "ctx").astype(jnp.float32),
        lax.psum(shares[8].astype(jnp.bfloat16), "ctx").astype(jnp.float32),
        lax.psum(shares[9].astype(jnp.bfloat16), "ctx").astype(jnp.float32),
    )
    head_sums = lax.psum((total_heads[0], total_heads[1], total_heads[2]), ("ctx", "wt"))
    return (
        section_output,
        input_grad,
        reduced[0][None],
        reduced[1][None],
        reduced[2][None],
        reduced[3][None],
        head_sums[0][None],
        head_sums[1][None],
        head_sums[2][None],
        reduced[4][None],
        reduced[5][None],
        reduced[6][None],
        reduced[7][None],
        reduced[8][None],
        reduced[9][None],
    )


def spread(mesh):
    placed = (
        P(None, "wt", "ctx", None),
        P(None, "wt", "ctx", None),
        P(None, "wt", None),
        P("section", "wt"),
        P("section", "wt", None),
        P("section", None, "wt"),
        P("section", "wt"),
        P("section", None),
        P("section", None),
        P("section", None),
        P("section", "wt", None),
        P("section", "wt", None),
        P("section", "wt", None),
        P("section", "wt"),
        P("section", "wt", None),
        P("section", "wt", None),
    )
    return jax.shard_map(
        local,
        mesh=mesh,
        in_specs=placed,
        out_specs=(
            P("section", None, "wt", "ctx", None),
            P("section", None, "wt", "ctx", None),
            P("section", "wt"),
            P("section", "wt", None),
            P("section", None, "wt"),
            P("section", "wt"),
            P("section", None),
            P("section", None),
            P("section", None),
            P("section", "wt", None),
            P("section", "wt", None),
            P("section", "wt", None),
            P("section", "wt"),
            P("section", "wt", None),
            P("section", "wt", None),
        ),
        check_vma=False,
    )


f32, bf16 = jnp.float32, jnp.bfloat16
RH = MH // 4
RD = DS // 4
RQ = QD // 4
RF = FF // 4
RAW_AT = 2 * RD + 2 * NS
Q_AT = RAW_AT + 128
K_AT = Q_AT + RQ
INC = K_AT + 2 * HD
OUTR = RD + RQ
FREE = 22
GROUP_A = INC + D // 2
GROUP_B = 2 * RF + D // 2
AXES = CORE, ROW, COL, LINE = tuple("cyxz")


def swapped(value, axis):
    return lax.ppermute(value, axis, [(0, 1), (1, 0)])


def across(value):
    return lax.ppermute(value, (ROW, COL), [(0, 3), (1, 2), (2, 1), (3, 0)])


def place(p):
    return ((p[0] * 2 + p[1]) * 2 + p[2]) * 4 + p[3]


def sent(value, pairs):
    return lax.ppermute(value, AXES, [(place(a), place(b)) for a, b in pairs])


every = [(c, y, x, z) for c in range(2) for y in range(2) for x in range(2) for z in range(4)]


def turned(value, by):
    return lax.ppermute(value, LINE, [(i, (i + by) % 4) for i in range(4)])


def paired_lines(value, by):
    return lax.ppermute(value, LINE, [(i, i ^ by) for i in range(4)])


def after(value, *others):
    return lax.optimization_barrier((value,) + others)[0]


def ordered(flag, own, other):
    return jnp.where(flag == 0, jnp.stack([own, other]), jnp.stack([other, own]))


def whole_rows(pair, y, x):
    own = lax.dynamic_index_in_dim(pair, y, 0, False)
    other = lax.dynamic_index_in_dim(pair, 1 - y, 0, False)
    near = ordered(x, own, swapped(own, COL))
    far = ordered(x, swapped(other, ROW), across(other))
    return ordered(y, near, far).reshape(4 * own.shape[0], own.shape[1])


def back_rows(rows, y, x):
    blocks = rows.reshape(2, 2, rows.shape[0] // 4, rows.shape[1])
    return ordered(y, blocks[y, x], swapped(blocks[1 - y, x], ROW))


def half_sum(keep, give):
    low = (keep.astype(f32) + swapped(give, CORE).astype(f32)).astype(bf16)
    return (low.astype(f32) + swapped(low, COL).astype(f32)).astype(bf16)


def quarter_sum(keep, give):
    both = half_sum(keep, give)
    return both, swapped(both, CORE)


BLOCK = 128
REACH = 2
CONVR = RD + 2 * NS
OUT_BLOCKS = [(j, y, c) for j in range(2) for y, c in ((0, 0), (0, 1), (1, 0))] + [(0, 1, 1), (1, 1, 1)]
WIDE = D // 2
LIMIT = 56 << 20


def mm(left, right, dims=((1,), (0,)), precision=None):
    return lax.dot_general(left, right, (dims, ((), ())), precision=precision, preferred_element_type=f32)


NT = ((1,), (1,))
TN = ((0,), (0,))


def logistic(value):
    return 1.0 / (1.0 + jnp.exp(-value))


def slope(value, sig):
    return sig * (1.0 + value * (1.0 - sig))


def unit_scale(rows):
    return lax.rsqrt(jnp.mean(rows * rows, axis=-1, keepdims=True) + epsilon)


def conv_chunk(proj_ref, ck_ref, tok_ref, j):
    lanes = slice(128 * j, 128 * (j + 1))
    pre = proj_ref[:, RD + 128 * j : RD + 128 * (j + 1)].astype(f32)
    summed = ck_ref[4:5, lanes] + pre * ck_ref[3:4, lanes]
    for by in range(1, CONV):
        summed = summed + pltpu.roll(pre, by, 0) * (ck_ref[3 - by : 4 - by, lanes] * tok_ref[:, by : by + 1])
    return pre, summed


def step_sizes(proj_ref, hp_ref):
    stepped = proj_ref[:, RAW_AT : RAW_AT + 128].astype(f32) + hp_ref[0:1, :]
    dt = jnp.maximum(stepped, 0.0) + jnp.log1p(jnp.exp(-jnp.abs(stepped)))
    return stepped, dt


def running(dt, hp_ref, run_s, run_t):
    count = dt.shape[0]
    rate = -dt * hp_ref[1:2, :]
    until = (
        lax.broadcasted_iota(jnp.int32, (count, count), 0) >= lax.broadcasted_iota(jnp.int32, (count, count), 1)
    ).astype(f32)
    run = mm(until, rate, precision=highest)
    run_s[...] = run
    run_t[...] = run.T
    return rate


def spans(count):
    for i in range(count // BLOCK):
        start = BLOCK * max(0, i - REACH)
        yield slice(BLOCK * i, BLOCK * (i + 1)), slice(start, BLOCK * (i + 1)), start


def barred(tok_ref, idr_ref, rows, keys):
    shape = (rows.stop - rows.start, keys.stop - keys.start)
    query = lax.broadcasted_iota(jnp.int32, shape, 0) + rows.start
    key = lax.broadcasted_iota(jnp.int32, shape, 1) + keys.start
    ok = (query >= key) & (tok_ref[rows, 0:1] == idr_ref[0:1, keys])
    return jnp.where(ok, 0.0, masked_value)


def fed_chunk(dt, conv, j, count):
    lane = lax.broadcasted_iota(jnp.int32, (count, 128), 1)
    return jnp.where(lane < MP, dt[:, 2 * j : 2 * j + 1], dt[:, 2 * j + 1 : 2 * j + 2]) * conv


def split_rows(c_ref, keep_ref, give_ref, half, value):
    @pl.when(c_ref[0] == half)
    def _():
        keep_ref[...] = value

    @pl.when(c_ref[0] != half)
    def _():
        give_ref[...] = value


def first_kernel(
    c_ref, mid_ref, own_ref, other_ref, gain_ref, wi_ref, mine_ref, got_ref, ck_ref, hp_ref, tok_ref, idr_ref,
    keep_ref, give_ref, x_ref, proj_ref, state_ref, ga_ref, h_s, wo_ref,
    vals_s, bc_s, fed_s, run_s, run_t,
):
    count = mid_ref.shape[0]
    for b, (j, y, c) in enumerate(OUT_BLOCKS):
        rows = slice(128 * j + 64 * y, 128 * j + 64 * y + 64)
        wo_ref[64 * b : 64 * b + 64, :] = jnp.where(c_ref[0] == c, mine_ref[rows, :], got_ref[rows, :])
    for i in range(count // BLOCK):
        rows = slice(BLOCK * i, BLOCK * (i + 1))
        low = mid_ref[rows, :]
        if mid_ref.dtype == f32:
            low = (low + added_rows(c_ref, own_ref, other_ref, i, count)).astype(bf16)
        x_ref[rows, :] = low
        x = low.astype(f32)
        h_s[rows, :] = (x * unit_scale(x) * gain_ref[...]).astype(bf16)
    for at in range(0, INC, 256):
        cols = slice(at, min(at + 256, INC))
        proj_ref[:, cols] = mm(h_s[...], wi_ref[:, cols]).astype(bf16)
    stepped, dt = step_sizes(proj_ref, hp_ref)
    running(dt, hp_ref, run_s, run_t)
    for j in range(CONVR // 128):
        pre, summed = conv_chunk(proj_ref, ck_ref, tok_ref, j)
        conv = summed * logistic(summed)
        if j < RD // 128:
            vals_s[:, 128 * j : 128 * (j + 1)] = conv
            fed_s[:, 128 * j : 128 * (j + 1)] = fed_chunk(dt, conv, j, count).astype(bf16)
        else:
            bc_s[:, 128 * j - RD : 128 * (j + 1) - RD] = conv.astype(bf16)
    for rows, keys, start in spans(count):
        bar = barred(tok_ref, idr_ref, rows, keys)
        gram = mm(bc_s[rows, NS:], bc_s[keys, :NS], NT)
        for h in range(RH):
            lanes = slice(MP * h, MP * (h + 1))
            decay = jnp.exp(run_s[rows, h : h + 1] - run_t[h : h + 1, keys] + bar)
            state_ref[rows, lanes] = mm((gram * decay).astype(bf16), fed_s[keys, lanes])
        for h in range(RQ // HD):
            lanes = slice(Q_AT + HD * h, Q_AT + HD * (h + 1))
            scores = mm(proj_ref[rows, lanes], proj_ref[keys, K_AT : K_AT + HD], NT) * 0.125 + bar
            chances = jnp.exp(scores - jnp.max(scores, axis=-1, keepdims=True))
            probs = (chances / jnp.sum(chances, axis=-1, keepdims=True)).astype(bf16)
            ga_ref[rows, RD + HD * h : RD + HD * (h + 1)] = mm(
                probs, proj_ref[keys, K_AT + HD : K_AT + 2 * HD]
            ).astype(bf16)
        z = proj_ref[rows, :RD].astype(f32)
        ssm = state_ref[rows, :] + ck_ref[5:6, :RD] * vals_s[rows, :]
        ga_ref[rows, :RD] = (ssm * z * logistic(z)).astype(bf16)
    for half in range(2):
        rows = slice(count // 2 * half, count // 2 * (half + 1))
        split_rows(c_ref, keep_ref, give_ref, half, mm(ga_ref[rows, :], wo_ref[...]).astype(bf16))


def added_rows(c_ref, own_ref, other_ref, i, count):
    half, at = divmod(BLOCK * i, count // 2)
    rows = slice(at, at + BLOCK)
    return jnp.where(c_ref[0] == half, own_ref[rows, :], other_ref[rows, :]).astype(f32)


def second_kernel(
    c_ref, x_ref, own_ref, other_ref, gain_ref, wgu_ref, wd_ref,
    keep_ref, give_ref, mid_ref, h_ref, gu_ref, hid_ref,
):
    count = x_ref.shape[0]
    for i in range(count // BLOCK):
        rows = slice(BLOCK * i, BLOCK * (i + 1))
        mid = x_ref[rows, :].astype(f32) + added_rows(c_ref, own_ref, other_ref, i, count)
        mid_ref[rows, :] = mid
        h_ref[rows, :] = (mid * unit_scale(mid) * gain_ref[...]).astype(bf16)
    for at in range(0, RF, 256):
        cols = slice(at, at + 256)
        ups = slice(RF + at, RF + at + 256)
        gate = mm(h_ref[...], wgu_ref[:, cols])
        up = mm(h_ref[...], wgu_ref[:, ups])
        gu_ref[:, cols] = gate
        gu_ref[:, ups] = up
        hid_ref[:, cols] = (gate * logistic(gate) * up).astype(bf16)
    for half in range(2):
        rows = slice(count // 2 * half, count // 2 * (half + 1))
        split_rows(c_ref, keep_ref, give_ref, half, mm(hid_ref[rows, :], wd_ref[...]).astype(bf16))


def back_second_kernel(c_ref, cot_ref, gu_ref, wgu_ref, wd_ref, keep_ref, give_ref, gug_ref):
    count = cot_ref.shape[0]
    for at in range(0, RF, 256):
        cols = slice(at, at + 256)
        ups = slice(RF + at, RF + at + 256)
        hidden_grad = mm(cot_ref[...], wd_ref[cols, :], NT)
        gate, up = gu_ref[:, cols], gu_ref[:, ups]
        sig = logistic(gate)
        gug_ref[:, cols] = (hidden_grad * up * slope(gate, sig)).astype(bf16)
        gug_ref[:, ups] = (hidden_grad * gate * sig).astype(bf16)
    for half in range(2):
        rows = slice(count // 2 * half, count // 2 * (half + 1))
        split_rows(c_ref, keep_ref, give_ref, half, mm(gug_ref[rows, :], wgu_ref[...], NT).astype(bf16))


def norm_back_rows(rows, gain, grad):
    scale = unit_scale(rows)
    normed = rows * scale
    weighted = grad * gain
    back = scale * (weighted - normed * jnp.mean(weighted * normed, axis=-1, keepdims=True))
    return back, jnp.sum(grad * normed, axis=0, keepdims=True)


def back_first_kernel(
    c_ref, cot_ref, own_ref, other_ref, mid_ref, gain_ref, proj_ref, state_ref, ga_ref, wi_ref, wo_ref, ck_ref,
    hp_ref, tok_ref, idr_ref,
    keep_ref, give_ref, outk_ref, outg_ref, midg_ref, projg_ref, gaing_ref, convg_ref, headg_ref,
    low_ref, gag_s, vals_s, bc_s, fed_s, run_s, run_t, sg_s, fedg_s, bcg_s, kvg_s, valg_s,
):
    count = cot_ref.shape[0]
    gain_grad = jnp.zeros((1, D), f32)
    for i in range(count // BLOCK):
        rows = slice(BLOCK * i, BLOCK * (i + 1))
        back, more = norm_back_rows(
            mid_ref[rows, :], gain_ref[...], added_rows(c_ref, own_ref, other_ref, i, count)
        )
        gain_grad = gain_grad + more
        total = cot_ref[rows, :].astype(f32) + back
        midg_ref[rows, :] = total
        low_ref[rows, :] = total.astype(bf16)
    gaing_ref[...] = gain_grad
    for q in range(OUTR // 128):
        grad = mm(ga_ref[:, 128 * q : 128 * (q + 1)], low_ref[...], TN).astype(bf16)
        for b in (2 * q, 2 * q + 1):
            j, y, c = OUT_BLOCKS[b]
            rows = slice(128 * j + 64 * y, 128 * j + 64 * y + 64)
            part = grad[64 * (b % 2) : 64 * (b % 2) + 64, :]

            @pl.when(c_ref[0] == c)
            def _(rows=rows, part=part):
                outk_ref[rows, :] = part

            @pl.when(c_ref[0] != c)
            def _(rows=rows, part=part):
                outg_ref[rows, :] = part

    for at in range(0, OUTR, 256):
        cols = slice(at, at + 256)
        gag_s[:, cols] = mm(low_ref[...], wo_ref[cols, :], NT)
    stepped, dt = step_sizes(proj_ref, hp_ref)
    rate = running(dt, hp_ref, run_s, run_t)
    for j in range(CONVR // 128):
        lanes = slice(128 * j, 128 * (j + 1))
        pre, summed = conv_chunk(proj_ref, ck_ref, tok_ref, j)
        conv = summed * logistic(summed)
        if j < RD // 128:
            vals_s[:, lanes] = conv
            fed_s[:, lanes] = fed_chunk(dt, conv, j, count).astype(bf16)
            z = proj_ref[:, lanes].astype(f32)
            sig = logistic(z)
            skip = ck_ref[5:6, lanes]
            grad = gag_s[:, lanes]
            ssm = state_ref[:, lanes] + skip * conv
            projg_ref[:, lanes] = (grad * ssm * slope(z, sig)).astype(bf16)
            ssm_grad = grad * z * sig
            sg_s[:, lanes] = ssm_grad.astype(bf16)
            valg_s[:, lanes] = ssm_grad * skip
            convg_ref[5:6, lanes] = jnp.sum(ssm_grad * conv, axis=0, keepdims=True)
        else:
            bc_s[:, 128 * j - RD : 128 * (j + 1) - RD] = conv.astype(bf16)
    fedg_s[...] = jnp.zeros_like(fedg_s)
    bcg_s[:, :NS] = jnp.zeros((count, NS), f32)
    kvg_s[...] = jnp.zeros_like(kvg_s)
    for rows, keys, start in spans(count):
        bar = barred(tok_ref, idr_ref, rows, keys)
        gram = mm(bc_s[rows, NS:], bc_s[keys, :NS], NT)
        gram_grad = jnp.zeros_like(gram)
        for h in range(RH):
            lanes = slice(MP * h, MP * (h + 1))
            decay = jnp.exp(run_s[rows, h : h + 1] - run_t[h : h + 1, keys] + bar)
            grad = sg_s[rows, lanes]
            gram_grad = gram_grad + mm(grad, fed_s[keys, lanes], NT) * decay
            fedg_s[keys, lanes] += mm((gram * decay).astype(bf16), grad, TN)
        gram_low = gram_grad.astype(bf16)
        bcg_s[rows, NS:] = mm(gram_low, bc_s[keys, :NS])
        bcg_s[keys, :NS] += mm(gram_low, bc_s[rows, NS:], TN)
        for h in range(RQ // HD):
            lanes = slice(Q_AT + HD * h, Q_AT + HD * (h + 1))
            query, key = proj_ref[rows, lanes], proj_ref[keys, K_AT : K_AT + HD]
            scores = mm(query, key, NT) * 0.125 + bar
            chances = jnp.exp(scores - jnp.max(scores, axis=-1, keepdims=True))
            probs = chances / jnp.sum(chances, axis=-1, keepdims=True)
            grad = gag_s[rows, RD + HD * h : RD + HD * (h + 1)].astype(bf16)
            prob_grad = mm(grad, proj_ref[keys, K_AT + HD : K_AT + 2 * HD], NT)
            score_grad = probs * (prob_grad - jnp.sum(probs * prob_grad, axis=-1, keepdims=True))
            score_grad = score_grad.astype(bf16)
            projg_ref[rows, lanes] = (mm(score_grad, key) * 0.125).astype(bf16)
            kvg_s[keys, :HD] += mm(score_grad, query, TN) * 0.125
            kvg_s[keys, HD:] += mm(probs.astype(bf16), grad, TN)
    projg_ref[:, K_AT:] = kvg_s[...].astype(bf16)
    head_of = lax.broadcasted_iota(jnp.int32, (RD, 128), 0) // MP
    picks = (head_of == lax.broadcasted_iota(jnp.int32, (RD, 128), 1)).astype(f32)
    run_grad = mm(
        sg_s[...].astype(f32) * state_ref[...] - fed_s[...].astype(f32) * fedg_s[...], picks, precision=highest
    )
    shape = (count, count)
    later = (
        (lax.broadcasted_iota(jnp.int32, shape, 1) >= lax.broadcasted_iota(jnp.int32, shape, 0))
        & (tok_ref[:, 0:1] == idr_ref[0:1, :])
    ).astype(f32)
    rate_grad = mm(later, run_grad, precision=highest)
    dt_grad = mm(vals_s[...] * fedg_s[...], picks, precision=highest) - rate_grad * hp_ref[1:2, :]
    raw_grad = dt_grad * logistic(stepped)
    headg_ref[0:1, :] = jnp.sum(raw_grad, axis=0, keepdims=True)
    headg_ref[1:2, :] = jnp.sum(rate_grad * rate, axis=0, keepdims=True)
    lane = lax.broadcasted_iota(jnp.int32, raw_grad.shape, 1)
    projg_ref[:, RAW_AT : RAW_AT + 128] = jnp.where(lane < RH, raw_grad, 0.0).astype(bf16)
    for j in range(CONVR // 128):
        lanes = slice(128 * j, 128 * (j + 1))
        pre, summed = conv_chunk(proj_ref, ck_ref, tok_ref, j)
        if j < RD // 128:
            grad = valg_s[:, lanes] + fed_chunk(dt, fedg_s[:, lanes], j, count)
        else:
            grad = bcg_s[:, 128 * j - RD : 128 * (j + 1) - RD]
        grad = grad * slope(summed, logistic(summed))
        convg_ref[4:5, lanes] = jnp.sum(grad, axis=0, keepdims=True)
        convg_ref[3:4, lanes] = jnp.sum(grad * pre, axis=0, keepdims=True)
        total = grad * ck_ref[3:4, lanes]
        for by in range(1, CONV):
            kept = grad * tok_ref[:, by : by + 1]
            convg_ref[3 - by : 4 - by, lanes] = jnp.sum(kept * pltpu.roll(pre, by, 0), axis=0, keepdims=True)
            total = total + pltpu.roll(kept * ck_ref[3 - by : 4 - by, lanes], count - by, 0)
        projg_ref[:, RD + 128 * j : RD + 128 * (j + 1)] = total.astype(bf16)
    for half in range(2):
        rows = slice(count // 2 * half, count // 2 * (half + 1))
        split_rows(c_ref, keep_ref, give_ref, half, mm(projg_ref[rows, :], wi_ref[...], NT).astype(bf16))


def back_input_kernel(c_ref, x_ref, own_ref, other_ref, gain_ref, midg_ref, low_ref, gaing_ref):
    count = x_ref.shape[0]
    gain_grad = jnp.zeros((1, D), f32)
    for i in range(count // BLOCK):
        rows = slice(BLOCK * i, BLOCK * (i + 1))
        back, more = norm_back_rows(
            x_ref[rows, :].astype(f32), gain_ref[...], added_rows(c_ref, own_ref, other_ref, i, count)
        )
        gain_grad = gain_grad + more
        low_ref[rows, :] = (midg_ref[rows, :] + back).astype(bf16)
    gaing_ref[...] = gain_grad


def back_half_kernel(c_ref, x_ref, own_ref, gain_ref, midg_ref, low_ref, gaing_ref):
    gain_grad = jnp.zeros((1, D), f32)
    for i in range(own_ref.shape[0] // BLOCK):
        rows = slice(BLOCK * i, BLOCK * (i + 1))
        at = pl.ds(pl.multiple_of(own_ref.shape[0] * c_ref[0] + BLOCK * i, BLOCK), BLOCK)
        back, more = norm_back_rows(x_ref[at, :].astype(f32), gain_ref[...], own_ref[rows, :].astype(f32))
        gain_grad = gain_grad + more
        low_ref[rows, :] = (midg_ref[at, :] + back).astype(bf16)
    gaing_ref[...] = gain_grad


def chosen(shape, source):
    lane = lax.broadcasted_iota(jnp.int32, shape, 1)
    return (lax.broadcasted_iota(jnp.int32, shape, 0) == source(lane)).astype(bf16)


def heads_from(x, width):
    return lambda d: d + x * width + jnp.where(d >= width, width, 0)


def steps_from(x, core):
    return lambda d: jnp.where(d < RH, 12 * core + 3 * x + d + jnp.where(d >= 3, 3, 0), -1)


def keys_from(core):
    return lambda d: HD * core + d + jnp.where(d >= HD, HD, 0)


def aligned(value, by):
    return value if isinstance(value, int) else pl.multiple_of(value, by)


def folded(ref, index, at, rows):
    ref[index + (slice(0, 64), slice(at, at + WIDE))] = rows[:, :WIDE]
    ref[index + (slice(64, 128), slice(at, at + WIDE))] = rows[:, WIDE:]


def prepare_a_kernel(c_ref, mi_ref, ai_ref, mo_ref, ao_ref, free_ref, keep_ref, give_ref):
    core, x = c_ref[0], c_ref[2]
    pick = chosen((2 * RD, RD), heads_from(x, RD // 2))
    pick_query = chosen((2 * RQ, RQ), heads_from(x, HD))
    half = RD // 2
    for t in range(2):
        pick_step = chosen((MH, 128), steps_from(x, t))
        pick_key = chosen((2 * KVD, 2 * HD), keys_from(t))
        for y in range(2):
            rows = slice(128 * y, 128 * (y + 1))
            parts = [mm(mi_ref[DS * h + 2 * RD * t : DS * h + 2 * RD * (t + 1), rows], pick, TN) for h in range(2)]
            parts.append(mi_ref[2 * DS : 2 * DS + 2 * NS, rows].T)
            parts.append(mm(mi_ref[DS + CONVD :, rows], pick_step, TN) + free_ref[...].astype(f32))
            parts.append(mm(ai_ref[rows, 2 * RQ * t : 2 * RQ * (t + 1)], pick_query))
            parts.append(mm(ai_ref[rows, QD:], pick_key))
            if y == 0:
                out = mo_ref[pl.ds(aligned(half * x + 64 * t, 64), 64), :]
            elif t == 0:
                out = mo_ref[pl.ds(aligned(half * x + 128, 64), 64), :]
            else:
                out = ao_ref[pl.ds(aligned(64 * x, 64), 64), :]
            for k, ref in enumerate((keep_ref, give_ref)):

                @pl.when((core == t) if k == 0 else (core != t))
                def _(ref=ref, parts=parts, out=out, y=y):
                    at = 0
                    for part in parts:
                        ref[y, :, at : at + part.shape[1]] = part.astype(bf16)
                        at += part.shape[1]
                    folded(ref, (y,), INC, out)


def prepare_b_kernel(c_ref, gu_ref, dn_ref, keep_ref, give_ref):
    core, x = c_ref[0], c_ref[2]
    for t in range(2):
        for k, ref in enumerate((keep_ref, give_ref)):

            @pl.when((core == t) if k == 0 else (core != t))
            def _(ref=ref, t=t):
                for y in range(2):
                    rows = slice(128 * y, 128 * (y + 1))
                    for h in range(8):
                        at = aligned(RF * h + 256 * t + 128 * x, 128)
                        ref[y, :, 128 * h : 128 * (h + 1)] = gu_ref[rows, pl.ds(at, 128)]
                    at = aligned(256 * t + 128 * x + 64 * y, 64)
                    folded(ref, (y,), 2 * RF, dn_ref[pl.ds(at, 64), :])


def unpack_a_from(c_ref, parts, wi_ref, mine_ref, give_ref):
    for line, y, load in parts:
        wi_ref[pl.ds(aligned(256 * line + 128 * y, 128), 128), :] = load(slice(None), slice(0, INC))
        rows = pl.ds(aligned(128 * lax.rem(line, 2) + 64 * y, 64), 64)
        left = load(slice(0, 64), slice(INC, GROUP_A))
        right = load(slice(64, 128), slice(INC, GROUP_A))

        @pl.when(line // 2 == c_ref[0])
        def _(rows=rows, left=left, right=right):
            mine_ref[rows, :WIDE] = left
            mine_ref[rows, WIDE:] = right

        @pl.when(line // 2 != c_ref[0])
        def _(rows=rows, left=left, right=right):
            give_ref[rows, :WIDE] = left
            give_ref[rows, WIDE:] = right


def unpack_b_from(parts, wgu_ref, wd_ref):
    for line, y, load in parts:
        wgu_ref[pl.ds(aligned(256 * line + 128 * y, 128), 128), :] = load(slice(None), slice(0, 2 * RF))
        rows = pl.ds(aligned(128 * line + 64 * y, 64), 64)
        wd_ref[rows, :WIDE] = load(slice(0, 64), slice(2 * RF, GROUP_B))
        wd_ref[rows, WIDE:] = load(slice(64, 128), slice(2 * RF, GROUP_B))


def halves_of(own, c_ref, keep_ref, got_ref, near_ref, far_ref):
    y, z = c_ref[1], c_ref[3]
    for k in range(4):
        line = lax.rem(z + k, 4)
        yield line, y, lambda *at, line=line: near_ref[(line,) + at]
        if k == 0:
            yield line, 1 - y, lambda *at: jnp.where(
                c_ref[0] == own, keep_ref[(1 - y,) + at], got_ref[(1 - y,) + at]
            )
        else:
            yield line, 1 - y, lambda *at, k=k: far_ref[(k - 1,) + at]


def lines_a_kernel(own, c_ref, keep_ref, got_ref, near_ref, far_ref, wi_ref, mine_ref, give_ref):
    unpack_a_from(c_ref, halves_of(own, c_ref, keep_ref, got_ref, near_ref, far_ref), wi_ref, mine_ref, give_ref)


def whole_a_kernel(c_ref, all_ref, wi_ref, mine_ref, give_ref):
    parts = [(k // 2, k % 2, lambda *at, k=k: all_ref[(k,) + at]) for k in range(8)]
    unpack_a_from(c_ref, parts, wi_ref, mine_ref, give_ref)


def lines_b_kernel(own, c_ref, keep_ref, got_ref, near_ref, far_ref, wgu_ref, wd_ref):
    unpack_b_from(halves_of(own, c_ref, keep_ref, got_ref, near_ref, far_ref), wgu_ref, wd_ref)


def split_halves(c_ref, y, line, refs, width, value, folds):
    def put(ref, index):
        ref[index + (slice(None), slice(0, width))] = value
        folded(ref, index, width, folds)

    if len(refs) == 1:
        put(refs[0], (line, y))
        return
    far = refs[1 + line // 2] if len(refs) == 3 else refs[1]

    @pl.when(c_ref[1] == y)
    def _():
        put(refs[0], (line,))

    @pl.when(c_ref[1] != y)
    def _():
        put(far, (line % 2,) if len(refs) == 3 else (line,))


def grads_b_kernel(c_ref, h_ref, gug_ref, hid_ref, cot_ref, *refs):
    for line in range(4):
        down = mm(hid_ref[:, 128 * line : 128 * (line + 1)], cot_ref[...], TN).astype(bf16)
        for y in range(2):
            at = 256 * line + 128 * y
            grad = mm(h_ref[:, at : at + 128], gug_ref[...], TN).astype(bf16)
            split_halves(c_ref, y, line, refs, 2 * RF, grad, down[64 * y : 64 * (y + 1), :])


def grads_a_kernel(c_ref, h_ref, projg_ref, mine_ref, got_ref, *refs):
    for line in range(4):
        for y in range(2):
            at = 256 * line + 128 * y
            grad = mm(h_ref[:, at : at + 128], projg_ref[...], TN).astype(bf16)
            rows = slice(128 * (line % 2) + 64 * y, 128 * (line % 2) + 64 * y + 64)
            out = jnp.where(c_ref[0] == line // 2, mine_ref[rows, :], got_ref[rows, :])
            split_halves(c_ref, y, line, refs, INC, grad, out)


def final_b_kernel(c_ref, p0, p1, p2, p3, near, far, gu_ref, dn_ref):
    @pl.when(c_ref[0] == 0)
    def _():
        final_b_of(c_ref, [p0, p1, p2, p3], gu_ref, dn_ref)

    @pl.when(c_ref[0] == 1)
    def _():
        final_b_of(c_ref, [near.at[0], far.at[0], near.at[1], far.at[1]], gu_ref, dn_ref)


def final_b_of(c_ref, refs, gu_ref, dn_ref):
    for i, ref in enumerate(refs):
        y, x = lax.rem(c_ref[1] + i // 2, 2), lax.rem(c_ref[2] + i, 2)
        rows = pl.ds(aligned(128 * y, 128), 128)
        for t in range(2):
            for h in range(8):
                at = aligned(RF * h + 256 * t + 128 * x, 128)
                gu_ref[rows, pl.ds(at, 128)] = ref[t, :, 128 * h : 128 * (h + 1)].astype(f32)
            down = pl.ds(aligned(256 * t + 128 * x + 64 * y, 64), 64)
            dn_ref[down, :WIDE] = ref[t, :64, 2 * RF : GROUP_B].astype(f32)
            dn_ref[down, WIDE:] = ref[t, 64:, 2 * RF : GROUP_B].astype(f32)


def final_a_kernel(c_ref, p0, p1, p2, p3, q0, q1, q2, q3, mi_ref, ai_ref, mo_ref, ao_ref):
    @pl.when(c_ref[0] == 0)
    def _():
        final_a_of(c_ref, p0, p1, p2, p3, mi_ref, ai_ref, mo_ref, ao_ref)

    @pl.when(c_ref[0] == 1)
    def _():
        final_a_of(c_ref, q0, q1, q2, q3, mi_ref, ai_ref, mo_ref, ao_ref)


def final_a_of(c_ref, p0, p1, p2, p3, mi_ref, ai_ref, mo_ref, ao_ref):
    half = RD // 2
    for i in range(2):
        y = lax.rem(c_ref[1] + i, 2)
        rows = pl.ds(aligned(128 * y, 128), 128)
        shared = jnp.zeros((128, 2 * NS), f32)
        steps = jnp.zeros((MH, 128), f32)
        keys = jnp.zeros((128, 2 * KVD), f32)
        for t in range(2):
            query = jnp.zeros((128, 2 * RQ), f32)
            for k in range(2):
                ref = (p0, p1, p2, p3)[2 * i + k]
                x = lax.rem(c_ref[2] + k, 2)
                for h in range(2):
                    part = ref[t, :, RD * h : RD * (h + 1)].astype(f32).T
                    for j in range(2):
                        at = aligned(DS * h + 2 * RD * t + RD * j + half * x, 64)
                        mi_ref[pl.ds(at, half), rows] = part[half * j : half * (j + 1), :]
                shared = shared + ref[t, :, 2 * RD : RAW_AT].astype(f32)
                steps = steps + mm(chosen((MH, 128), steps_from(x, t)), ref[t, :, RAW_AT:Q_AT], NT)
                query = query + mm(ref[t, :, Q_AT:K_AT], chosen((2 * RQ, RQ), heads_from(x, HD)), NT)
                keys = keys + mm(ref[t, :, K_AT:INC], chosen((2 * KVD, 2 * HD), keys_from(t)), NT)
                left, right = ref[t, :64, INC:].astype(f32), ref[t, 64:, INC:].astype(f32)

                def put(out_ref, at, left=left, right=right):
                    out_ref[pl.ds(aligned(at, 64), 64), :WIDE] = left
                    out_ref[pl.ds(aligned(at, 64), 64), WIDE:] = right

                @pl.when(y == 0)
                def _(put=put, x=x, t=t):
                    put(mo_ref, half * x + 64 * t)

                @pl.when(y == 1)
                def _(put=put, x=x, t=t):
                    if t == 0:
                        put(mo_ref, half * x + 128)
                    else:
                        put(ao_ref, 64 * x)

            ai_ref[rows, 2 * RQ * t : 2 * RQ * (t + 1)] = query
        mi_ref[2 * DS : 2 * DS + 2 * NS, rows] = shared.T
        mi_ref[DS + CONVD :, rows] = steps
        ai_ref[rows, QD:] = keys


def on_chip(kernel, c, inputs, outs, scratch=(), micros=2):
    inside = pl.BlockSpec(memory_space=pltpu.VMEM)
    return pl.pallas_call(
        kernel,
        in_specs=[pl.BlockSpec(memory_space=pltpu.SMEM)] + [inside] * len(inputs),
        out_specs=[inside] * len(outs),
        out_shape=[jax.ShapeDtypeStruct(*o) for o in outs],
        scratch_shapes=[pltpu.VMEM(*s) for s in scratch],
        compiler_params=pltpu.CompilerParams(vmem_limit_bytes=LIMIT),
        cost_estimate=pl.CostEstimate(flops=micros * 10**9, bytes_accessed=micros * 3 * 10**6, transcendentals=0),
    )(c, *inputs)


def small_parameters(one, per_head, c, x):
    quarter = CONVD // 4
    cut = lax.dynamic_slice_in_dim

    def heads(values, width):
        parts = cut(values, c * 12 * width, 12 * width, values.ndim - 1)
        parts = [cut(parts, (6 * j + 3 * x) * width, 3 * width, values.ndim - 1) for j in range(2)]
        return jnp.concatenate(parts, axis=-1)

    conv = one[:, : 5 * quarter].reshape(4, 5, quarter).transpose(1, 0, 2).reshape(5, CONVD)
    conv = jnp.concatenate([heads(conv[:, :DS], MP), conv[:, DS:]], axis=1)
    at = 5 * quarter
    gains = one[:, at : at + 512].reshape(4, 2, 256).transpose(1, 0, 2).reshape(2, D)
    per_head = heads(per_head, 1)
    skip = jnp.pad(jnp.repeat(per_head[2], MP), (0, CONVR - RD))
    conv = jnp.pad(jnp.concatenate([conv, skip[None]], axis=0), ((0, 2), (0, 0)))
    per_head = jnp.pad(jnp.stack([per_head[0], jnp.exp(per_head[1])]), ((0, 6), (0, 128 - RH)))
    return gains[0:1], gains[1:2], conv, per_head


def small_gradients(conv_grad, head_grad, first_grad, second_grad, c, x, counted):
    def heads(values, width):
        out = jnp.zeros(values.shape[:-1] + (MH * width,), f32)
        for j in range(2):
            part = values[..., 3 * width * j : 3 * width * (j + 1)]
            out = lax.dynamic_update_slice_in_dim(out, part, (12 * c + 6 * j + 3 * x) * width, values.ndim - 1)
        return out

    first = ((c == 0) & (x == 0)).astype(f32)
    wide = jnp.concatenate([heads(conv_grad[:5, :RD], MP), conv_grad[:5, RD:]], axis=1)
    skip = conv_grad[5, :RD].reshape(RH, MP).sum(axis=1)
    per_head = heads(jnp.stack([head_grad[0, :RH], head_grad[1, :RH], skip]), 1)
    flat = jnp.concatenate(
        [wide.reshape(-1), first_grad[0] * counted.astype(f32), second_grad[0] * first, per_head.reshape(-1)]
    )
    return jnp.pad(flat, (0, 88 * 128 - flat.shape[0])).reshape(88, 128)


def summed_small(grads, c, wait, last):
    total = after(jnp.stack(grads), wait)
    total = total + paired_lines(total, 1)
    total = total + paired_lines(total, 2)
    first, second = total[0], total[1]
    total = jnp.where(c == 0, first, second) + swapped(jnp.where(c == 0, second, first), CORE)
    total = total + swapped(after(total, last), COL)
    return total + swapped(total, ROW)


def paired(
    block_input,
    output_grad,
    doc_lengths,
    first_gain,
    mixer_in,
    conv_kernel,
    conv_bias,
    step_bias,
    decay_log,
    skip_gain,
    mixer_out,
    attention_in,
    attention_out,
    second_gain,
    gate_up,
    down_weight,
):
    c, y, x, z = (lax.axis_index(a) for a in AXES)
    at = jnp.stack([c, y, x, z]).astype(jnp.int32)
    cut = lax.dynamic_slice_in_dim
    quarter = CONVD // 4

    free = jnp.concatenate([conv_kernel[0].reshape(-1), conv_bias[0], first_gain[0], second_gain[0]])
    free = jnp.pad(free, (0, FREE * 128 - free.shape[0])).reshape(FREE, 128).T
    free = jnp.pad(free, ((0, 0), (8, 120 - FREE)))

    keep_a, give_a = on_chip(
        prepare_a_kernel,
        at,
        (mixer_in[0].T, attention_in[0], mixer_out[0], attention_out[0], free),
        [((2, 128, GROUP_A), bf16)] * 2,
    )
    got_a = swapped(give_a, CORE)

    def halves(keep, got, s):
        return jnp.where(c == s, lax.dynamic_index_in_dim(keep, y, 0, False), lax.dynamic_index_in_dim(got, y, 0, False))

    half_a0 = halves(keep_a, got_a, 0)
    lines_a0 = lax.all_gather(half_a0, LINE)
    keep_b, give_b = on_chip(
        prepare_b_kernel, after(at, half_a0), (gate_up[0], down_weight[0]), [((2, 128, GROUP_B), bf16)] * 2
    )
    got_b = swapped(give_b, CORE)
    rows_in = jnp.concatenate([block_input[:, 0], output_grad[:, 0]], axis=2)
    rows_in = after(rows_in, half_a0)
    whole = whole_rows(rows_in, y, x)
    x0, cot = whole[:, :D], whole[:, D:]
    per_head = jnp.stack([step_bias[0], decay_log[0], skip_gain[0]])
    per_head = ordered(c, per_head, swapped(after(per_head, half_a0), CORE))

    def small_of(piece):
        return jnp.swapaxes(piece[..., RAW_AT + 8 : RAW_AT + 8 + FREE], -1, -2).astype(f32)

    smalls = [small_parameters(small_of(lines_a0).reshape(4, -1), per_head[0], c, x)]
    doc_sizes = lax.dynamic_index_in_dim(doc_lengths[:, 0], y, 0, False)
    length = x0.shape[0]
    positions = jnp.arange(length, dtype=jnp.int32)
    ids = doc_layout(doc_sizes, positions)[0]
    taps = [(positions >= by) & (jnp.roll(ids, by) == ids) for by in range(1, CONV)]
    tok = jnp.pad(jnp.stack([ids.astype(f32)] + [t.astype(f32) for t in taps], axis=1), ((0, 0), (0, 128 - CONV)))
    idr = jnp.broadcast_to(ids.astype(f32)[None], (8, length))
    half = length // 2
    partial = [((half, D), bf16), ((half, D), bf16)]

    def others(lines):
        return jnp.stack([lax.dynamic_index_in_dim(lines, (z + k) % 4, 0, False) for k in (1, 2, 3)])

    def unpack_a(s, near, far):
        wi, mine, give = on_chip(
            functools.partial(lines_a_kernel, s),
            at,
            (keep_a, got_a, near[:, :, :GROUP_A], far),
            [((D, INC), bf16), ((256, D), bf16), ((256, D), bf16)],
        )
        return wi, mine, swapped(give, CORE)

    def unpack_b(s, near, far):
        return on_chip(
            functools.partial(lines_b_kernel, s),
            at,
            (keep_b, got_b, near[:, :, -GROUP_B:], far),
            [((D, 2 * RF), bf16), ((RF, D), bf16)],
        )

    def first_part(entry, own, other, s, wi, mine, got):
        gain, _, conv, per_head = smalls[s]
        return on_chip(
            first_kernel,
            at,
            (entry, own, other, gain, wi, mine, got, conv, per_head, tok, idr),
            partial
            + [
                ((length, D), bf16),
                ((length, INC), bf16),
                ((length, RD), f32),
                ((length, OUTR), bf16),
                ((length, D), bf16),
                ((OUTR, D), bf16),
            ],
            [
                ((length, RD), f32),
                ((length, 2 * NS), bf16),
                ((length, RD), bf16),
                ((length, 128), f32),
                ((128, length), f32),
            ],
            15,
        )

    def second_part(entry, own, other, s, wgu, wd):
        return on_chip(
            second_kernel,
            at,
            (entry, own, other, smalls[s][1], wgu, wd),
            partial
            + [((length, D), f32), ((length, D), bf16), ((length, 2 * RF), f32), ((length, RF), bf16)],
            micros=8,
        )

    half_b0 = halves(keep_b, got_b, 0)
    lines_b0 = lax.all_gather(after(half_b0, lines_a0), LINE)
    far_a0 = swapped(after(others(lines_a0), whole, tok, idr, per_head), ROW)
    half_a1 = after(halves(keep_a, got_a, 1), lines_b0, far_a0)
    lines_a1 = lax.all_gather(half_a1, (LINE, ROW))
    x0 = after(x0, half_a1)
    wi0, mine, got = unpack_a(0, lines_a0, far_a0)
    far_b0 = swapped(others(lines_b0), ROW)
    keep, give, x0, proj0, state0, ga0, h0, wo0 = first_part(x0, smalls[0][0], smalls[0][0], 0, wi0, mine, got)
    give = after(give, far_b0)
    own, other = quarter_sum(keep, give)
    wgu0, wd0 = unpack_b(0, lines_b0, far_b0)
    keep, give, mid0, g0, gu0, hid0 = second_part(x0, own, other, 0, wgu0, wd0)
    lines_b1 = lax.all_gather(after(halves(keep_b, got_b, 1), lines_a1, keep), LINE)
    smalls.append(small_parameters(small_of(after(lines_a1, mid0)[::2]).reshape(4, -1), per_head[1], c, x))
    own, other = quarter_sum(keep, give)
    wi1, mine, give_out = on_chip(
        whole_a_kernel, at, (lines_a1,), [((D, INC), bf16), ((256, D), bf16), ((256, D), bf16)]
    )
    got = swapped(give_out, CORE)
    keep, give, x1, proj1, state1, ga1, h1, wo1 = first_part(mid0, own, other, 1, wi1, mine, got)
    far_b1 = swapped(others(lines_b1), ROW)
    own, other = quarter_sum(keep, give)
    wgu1, wd1 = unpack_b(1, lines_b1, far_b1)
    late_keep, late_give, mid1, g1, gu1, hid1 = second_part(x1, own, other, 1, wgu1, wd1)

    def back_second(cot, s, gu, wgu, wd):
        return on_chip(
            back_second_kernel, at, (cot, gu, wgu, wd), partial + [((length, 2 * RF), bf16)], micros=7
        )

    def back_first(cot, own, other, s, mid, proj, state, ga, wi, wo):
        gain, conv, per_head = smalls[s][1:]
        return on_chip(
            back_first_kernel,
            at,
            (cot, own, other, mid, gain, proj, state, ga, wi, wo, conv, per_head, tok, idr),
            partial
            + [
                ((256, D), bf16),
                ((256, D), bf16),
                ((length, D), f32),
                ((length, INC), bf16),
                ((1, D), f32),
                ((8, CONVR), f32),
                ((8, 128), f32),
            ],
            [
                ((length, D), bf16),
                ((length, OUTR), f32),
                ((length, RD), f32),
                ((length, 2 * NS), bf16),
                ((length, RD), bf16),
                ((length, 128), f32),
                ((128, length), f32),
                ((length, RD), bf16),
                ((length, RD), f32),
                ((length, 2 * NS), f32),
                ((length, 2 * HD), f32),
                ((length, RD), f32),
            ],
            25,
        )

    def back_input(s, entry, own, other, mid_grad):
        return on_chip(
            back_input_kernel,
            at,
            (entry, own, other, smalls[s][0], mid_grad),
            [((length, D), bf16), ((1, D), f32)],
            micros=4,
        )

    def shapes(split, columns):
        if not split:
            return [((4, 2, 128, columns), bf16)]
        return [((4, 128, columns), bf16)] + [((4 // split, 128, columns), bf16)] * split

    def grads_b(split, *inputs):
        return on_chip(grads_b_kernel, at, inputs, shapes(split, GROUP_B), micros=5)

    def grads_a(split, h, proj_grad, mine, give):
        inputs = (h, proj_grad, mine, swapped(give, CORE))
        return on_chip(grads_a_kernel, at, inputs, shapes(split, GROUP_A), micros=5)

    def added(grads, *got):
        got = jnp.concatenate(got, axis=0) if len(got) > 1 else got[0]
        return (grads[0].astype(f32) + got.astype(f32)).astype(bf16)

    def lines_first(grads):
        columns = grads[0].shape[3]
        sums = scattered(grads[0].reshape(4, 256, columns)).reshape(2, 128, columns)
        mine = lax.dynamic_index_in_dim(sums, y, 0, False)
        theirs = lax.dynamic_index_in_dim(sums, 1 - y, 0, False)
        return (mine.astype(f32) + swapped(theirs, ROW).astype(f32)).astype(bf16)

    def scattered(lines):
        return lax.psum_scatter(lines, LINE, scatter_dimension=0)

    def both_ranks(first, second):
        return ordered(c, jnp.where(c == 0, first, second), swapped(jnp.where(c == 0, second, first), CORE))

    def spread_rows(piece, s):
        given = sent(piece, [(p, (s,) + p[1:]) for p in every if p[0] != s])
        block = jnp.stack([piece, given] if s == 0 else [given, piece])
        return jnp.stack([block, sent(block, [(p, (s, 1 - p[1], p[2], p[3])) for p in every if p[0] == s])])

    def spread_one(piece, s):
        given = sent(piece, [(p, (s,) + p[1:]) for p in every if p[0] != s])
        block = jnp.stack([piece, given] if s == 0 else [given, piece])
        mine = [p for p in every if p[0] == s]
        flips = [[(p, (s, p[1] ^ i, p[2] ^ k, p[3])) for p in mine] for i, k in ((0, 1), (1, 0), (1, 1))]
        return [block] + [sent(block, f) for f in flips]

    cot1 = cot
    keep, give, gu_grad = back_second(cot1, 1, gu1, wgu1, wd1)
    own, other = quarter_sum(keep, give)
    late_give = after(late_give, own)
    late, late_other = quarter_sum(late_keep, late_give)
    gb1 = grads_b(0, g1, gu_grad, hid1, cot1)
    own = after(own, gb1[0])
    sum_b1 = lines_first(gb1)
    keep, give, mine, give_out, mid_grad, proj_grad, second1, conv1, head1 = back_first(
        cot1, own, other, 1, mid1, proj1, state1, ga1, wi1, wo1
    )
    give = after(give, late)
    own, other = quarter_sum(keep, give)
    ga1_ = grads_a(0, h1, proj_grad, mine, give_out)
    own = after(own, ga1_[0], sum_b1, late_other)
    sum_a1 = lines_first(ga1_)
    cot0, first1 = back_input(1, x1, own, other, mid_grad)
    keep, give, gu_grad = back_second(cot0, 0, gu0, wgu0, wd0)
    own, other = quarter_sum(keep, give)
    gb0 = grads_b(1, g0, gu_grad, hid0, cot0)
    gb0_got = swapped(gb0[1], ROW)
    near_b1 = spread_rows(sum_b1, 1)
    own = after(own, gb0[0], near_b1)
    plane_b1 = near_b1, sent(near_b1, [(p, (1, p[1], 1 - p[2], p[3])) for p in every if p[0] == 1])
    keep, give, mine, give_out, mid_grad, proj_grad, second0, conv0, head0 = back_first(
        cot0, own, other, 0, mid0, proj0, state0, ga0, wi0, wo0
    )
    ga0_ = grads_a(2, h0, proj_grad, mine, give_out)
    ga0_got = [swapped(ga0_[1], ROW)]
    ga0_got.append(swapped(after(ga0_[2], ga0_got[0]), ROW))
    lines_gb0 = added(gb0, after(gb0_got, ga0_[0]))
    b0 = scattered(lines_gb0)
    own = half_sum(keep, after(give, ga0_[0]))
    low0, first0 = on_chip(
        back_half_kernel,
        at,
        (x0, own, smalls[0][0], mid_grad),
        [((half, D), bf16), ((1, D), f32)],
        micros=3,
    )
    block = both_ranks(jnp.pad(b0, ((0, 0), (0, GROUP_A - GROUP_B))), sum_a1)
    lines_ga0 = added(ga0_, ga0_got[0], after(ga0_got[1], first0, block, plane_b1[1]))
    a0 = scattered(lines_ga0)
    block = after(block, lines_ga0)
    plane_two = block, swapped(block, COL), swapped(block, ROW), across(block)
    gate_up_grad, down_grad = on_chip(
        final_b_kernel, at, (*plane_two, *plane_b1), [((256, 2 * FF), f32), ((RF, D), f32)], micros=4
    )
    plane_a0 = spread_one(after(a0, *plane_two), 0)
    mixer_in_grad, attention_in_grad, mixer_out_grad, attention_out_grad = on_chip(
        final_a_kernel,
        at,
        (*plane_a0, *plane_two),
        [((DS + CONVD + MH, 256), f32), ((256, QD + 2 * KVD), f32), ((RD, D), f32), ((128, D), f32)],
        micros=40,
    )

    out1 = (mid1 + ordered(c, late, late_other).reshape(length, D).astype(f32)).astype(bf16)
    section_output = back_rows(jnp.where(c == 0, x1, out1), y, x)
    part = lax.dynamic_slice_in_dim(low0, x * (half // 2), half // 2, 0)
    part = after(part, plane_a0[0])
    moved = [sent(part, [(p, (0, p[0], p[2], p[3])) for p in every if p[1] == m]) for m in range(2)]
    input_grad = jnp.where(c == 0, jnp.stack(moved), back_rows(cot0, y, x))
    grads = [
        small_gradients(conv0, head0, first0, second0, c, x, x == 0),
        small_gradients(conv1, head1, first1, second1, c, x, (c == 0) & (x == 0)),
    ]
    sums = summed_small(grads, c, first0, plane_a0[0]).reshape(-1)
    wide = sums[: 5 * CONVD].reshape(5, CONVD)
    start = 5 * CONVD
    conv_out = cut(wide, z * quarter, quarter, 1)
    first_out = cut(sums[start : start + D], z * 256, 256, 0)
    second_out = cut(sums[start + D : start + 2 * D], z * 256, 256, 0)
    head_out = sums[start + 2 * D : start + 2 * D + 3 * MH].reshape(3, MH)
    return (
        section_output[None, :, None],
        input_grad[None, :, None],
        first_out[None],
        mixer_in_grad.T[None],
        conv_out[None, :4],
        conv_out[None, 4],
        head_out[None, 0],
        head_out[None, 1],
        head_out[None, 2],
        mixer_out_grad[None],
        attention_in_grad[None],
        attention_out_grad[None],
        second_out[None],
        gate_up_grad[None],
        down_grad[None],
    )


def paired_specs():
    plane = (ROW, COL)
    rows = P(CORE, LINE, None)
    placed = (
        P(None, LINE, plane, None),
        P(None, LINE, plane, None),
        P(None, LINE, None),
        P(CORE, LINE),
        rows,
        P(CORE, None, LINE),
        P(CORE, LINE),
        P(CORE, None),
        P(CORE, None),
        P(CORE, None),
        rows,
        rows,
        rows,
        P(CORE, LINE),
        rows,
        rows,
    )
    given = (
        P(CORE, None, LINE, plane, None),
        P(CORE, None, LINE, plane, None),
        P(CORE, LINE),
        rows,
        P(CORE, None, LINE),
        P(CORE, LINE),
        P(CORE, None),
        P(CORE, None),
        P(CORE, None),
        rows,
        rows,
        rows,
        P(CORE, LINE),
        rows,
        rows,
    )
    return placed, given


def solution(mesh):
    if tuple(mesh.devices.shape) == (2, 4, 4):
        fine = Mesh(mesh.devices.reshape(2, 2, 2, 4), AXES)
        placed, given = paired_specs()
        return jax.shard_map(paired, mesh=fine, in_specs=placed, out_specs=given, check_vma=False)
    return spread(mesh)
```

```python
import functools
import math

import jax
import jax.numpy as jnp
from jax import lax
from jax.experimental import pallas as pl
from jax.experimental.pallas import tpu as pltpu
from jax.sharding import Mesh, PartitionSpec as P

D = 1024
FF = 2048
MH = 24
MP = 64
NS = 128
QH = 8
KVH = 2
HD = 64
CONV = 4
MICRO = 2
SPAN = 128
KEY_BLOCK = 1024
DS = 1536
CONVD = 1792
QD = 512
KVD = 128


epsilon = 1e-05
masked_value = -1e30
highest = lax.Precision.HIGHEST
weight_names = (
    "first_gain",
    "mixer_in",
    "conv_kernel",
    "conv_bias",
    "mixer_out",
    "attention_in",
    "attention_out",
    "second_gain",
    "gate_up",
    "down_weight",
)


def passed_along(value, axis, by):
    length = lax.axis_size(axis)
    pairs = [(i, i + by) for i in range(length) if 0 <= i + by < length]
    return lax.ppermute(value, axis, pairs)


def prefix(value, axis, combine, identity):
    length, position = (lax.axis_size(axis), lax.axis_index(axis))
    everything = jax.tree.map(
        lambda part, kind: lax.all_gather(part.astype(kind), axis),
        value,
        (jnp.bfloat16, jnp.bfloat16),
    )
    start = jax.tree.map(
        lambda part, zero: jnp.broadcast_to(jnp.asarray(zero, part.dtype), part.shape),
        value,
        identity,
    )

    def step(k, before):
        reached = k < position
        new = combine(
            before, jax.tree.map(lambda part, own: part[k].astype(own.dtype), everything, value)
        )
        return jax.tree.map(lambda a, b: jnp.where(reached, a, b), new, before)

    return lax.fori_loop(0, length, step, start)


def prefix_2(value, axis, join, neutral):
    count = lax.axis_size(axis)
    place = lax.axis_index(axis)
    ahead = count - 1 - place
    gathered = jax.tree.map(
        lambda a, kind: lax.all_gather(a.astype(kind), axis),
        value,
        jax.tree.map(lambda a: jnp.bfloat16 if a.dtype == jnp.float32 else a.dtype, value),
    )
    state = jax.tree.map(lambda a, e: jnp.zeros_like(a) + jnp.asarray(e, a.dtype), value, neutral)

    def one(step, state):
        source = count - 1 - step
        return join(
            state,
            jax.tree.map(
                lambda a, own: lax.dynamic_index_in_dim(a, source, 0, False).astype(own.dtype),
                gathered,
                value,
            ),
        )

    return lax.fori_loop(0, ahead, one, state)


def inner_rows(left, right):
    return lax.dot_general(
        left, right, (((0,), (0,)), ((), ())), preferred_element_type=jnp.float32
    )


def outer_cols(left, right):
    return lax.dot_general(
        left, right, (((1,), (1,)), ((), ())), preferred_element_type=jnp.float32
    )


def norm_apply(hidden_in, gain_vec):
    return (
        hidden_in
        * lax.rsqrt(jnp.mean(hidden_in * hidden_in, axis=-1, keepdims=True) + epsilon)
        * gain_vec
    )


def norm_back(hidden_in, gain_vec, upstream):
    scale = lax.rsqrt(jnp.mean(hidden_in * hidden_in, axis=-1, keepdims=True) + epsilon)
    normed = hidden_in * scale
    weighted = upstream * gain_vec
    hidden_grad = scale * (weighted - normed * jnp.mean(weighted * normed, axis=-1, keepdims=True))
    return (hidden_grad, jnp.sum(upstream * normed, axis=0))


def running_sum(value):
    count = value.shape[0]
    until = lax.broadcasted_iota(jnp.int32, (count, count), 0) >= lax.broadcasted_iota(
        jnp.int32, (count, count), 1
    )
    return jnp.dot(until.astype(jnp.float32), value, precision=highest)


def doc_layout(doc_sizes, positions):
    count = doc_sizes.shape[0]
    until = lax.broadcasted_iota(jnp.int32, (count, count), 0) >= lax.broadcasted_iota(
        jnp.int32, (count, count), 1
    )
    bounds = jnp.sum(jnp.where(until, doc_sizes[None, :], 0), axis=1)[:-1]
    doc_ids = jnp.sum((positions[:, None] >= bounds[None, :]).astype(jnp.int32), axis=1)
    starts = jnp.any(positions[:, None] == bounds[None, :], axis=1)
    return (doc_ids, starts)


def conv_apply(extended, ext_ids, kernel, offset_vec):
    amount = extended.shape[0] - CONV + 1
    own_ids = ext_ids[CONV - 1 :]
    summed = offset_vec[None, :] + jnp.zeros((amount, 1), extended.dtype)
    for tap_index in range(CONV):
        same_doc = (ext_ids[tap_index : tap_index + amount] == own_ids).astype(extended.dtype)
        summed = (
            summed
            + kernel[tap_index][None, :]
            * extended[tap_index : tap_index + amount]
            * same_doc[:, None]
        )
    return jax.nn.silu(summed)


def span_pass(carried_state, pieces):
    values, write_vec, read_vec, step_size, log_decay, doc_ids, before = pieces
    amount = values.shape[0]
    running = running_sum(log_decay)
    row_ids = lax.broadcasted_iota(jnp.int32, (amount, amount), 0)
    col_ids = lax.broadcasted_iota(jnp.int32, (amount, amount), 1)
    allowed = (col_ids <= row_ids) & (doc_ids[:, None] == doc_ids[None, :])
    log_gap = jnp.where(
        allowed[:, :, None], running[:, None, :] - running[None, :, :], masked_value
    )
    intersection = jnp.einsum("in,jn->ij", read_vec, write_vec, precision=highest)
    mixing = intersection[:, :, None] * jnp.exp(log_gap) * step_size[None, :, :]
    within = jnp.einsum("ijh,jhp->ihp", mixing, values, precision=highest)
    inflow = jnp.exp(running) * (doc_ids == before)[:, None].astype(jnp.float32)
    carried = (
        jnp.einsum("in,hpn->ihp", read_vec, carried_state, precision=highest) * inflow[:, :, None]
    )
    to_end = (
        jnp.exp(running[-1][None, :] - running)
        * (doc_ids == doc_ids[-1])[:, None].astype(jnp.float32)
        * step_size
    )
    increment = jnp.einsum("jh,jhp,jn->hpn", to_end, values, write_vec, precision=highest)
    return (inflow[-1][:, None, None] * carried_state + increment, within + carried)


def mixer_local(
    extended,
    raw_rate,
    kernel,
    offset_vec,
    step_bias,
    decay_log,
    skip_gain,
    state_in,
    ext_ids,
    doc_ids,
    starts,
):
    tokens = raw_rate.shape[0]
    conv_out = conv_apply(extended, ext_ids, kernel, offset_vec)
    values = conv_out[:, :DS].reshape(tokens, MH, MP)
    read_vector = conv_out[:, DS + NS :]
    step_size = jax.nn.softplus(raw_rate + step_bias)
    log_decay = -step_size * jnp.exp(decay_log)
    blocks = tokens // SPAN
    pieces = (
        values.reshape(blocks, SPAN, MH, MP),
        conv_out[:, DS : DS + NS].reshape(blocks, SPAN, NS),
        read_vector.reshape(blocks, SPAN, NS),
        step_size.reshape(blocks, SPAN, MH),
        log_decay.reshape(blocks, SPAN, MH),
        doc_ids.reshape(blocks, SPAN),
        doc_ids[::SPAN] - starts[::SPAN].astype(jnp.int32),
    )
    state_out, outputs = lax.scan(span_pass, state_in, pieces)
    result = outputs.reshape(tokens, MH, MP) + skip_gain[None, :, None] * values
    return ((result.reshape(tokens, DS), state_out), (read_vector, log_decay))


def device_inflow(log_decay, doc_ids, starts):
    same_doc = (doc_ids == doc_ids[0] - starts[0].astype(jnp.int32)).astype(jnp.float32)
    return jnp.exp(running_sum(log_decay)) * same_doc[:, None]


def chain_affine(earlier, later):
    return (earlier[0] * later[0], later[0][:, None, None] * earlier[1] + later[1])


def query_groups(flat):
    tokens = flat.shape[0]
    per_group = QH // KVH
    return (
        flat.reshape(tokens, KVH, per_group, HD)
        .transpose(1, 2, 0, 3)
        .reshape(KVH, per_group * tokens, HD)
    )


def query_flat(grouped, tokens):
    per_group = QH // KVH
    return grouped.reshape(KVH, per_group, tokens, HD).transpose(2, 0, 1, 3).reshape(tokens, QD)


def score_block(queries, key_rows, query_pos, query_ids, all_ids, offset, block_len):
    key_block = lax.dynamic_slice_in_dim(key_rows, offset, block_len, 0)
    key_part = key_block[:, :KVD].reshape(block_len, KVH, HD)
    value_part = key_block[:, KVD:].reshape(block_len, KVH, HD)
    key_pos = offset + jnp.arange(block_len, dtype=jnp.int32)
    key_ids = lax.dynamic_slice_in_dim(all_ids, offset, block_len, 0)
    allowed = (key_pos[None, :] <= query_pos[:, None]) & (key_ids[None, :] == query_ids[:, None])
    scores = (
        jnp.einsum("grd,kgd->grk", queries, key_part, preferred_element_type=jnp.float32) * 0.125
    )
    return (jnp.where(allowed[None], scores, masked_value), allowed, key_part, value_part)


def attend_forward(queries_flat, key_rows, positions, doc_ids, all_ids, ctx_index):
    tokens = queries_flat.shape[0]
    per_group = QH // KVH
    queries = query_groups(queries_flat)
    query_pos = jnp.tile(positions, per_group)
    query_ids = jnp.tile(doc_ids, per_group)
    block_len = math.gcd(key_rows.shape[0], KEY_BLOCK)
    block_count = ((ctx_index + 1) * tokens + block_len - 1) // block_len

    def visit_block(block_index, carry):
        running_max, running_sum, accumulated = carry
        scores, allowed, key_part, value_part = score_block(
            queries, key_rows, query_pos, query_ids, all_ids, block_index * block_len, block_len
        )
        new_max = jnp.maximum(running_max, jnp.max(scores, axis=-1))
        chances = jnp.where(allowed[None], jnp.exp(scores - new_max[..., None]), 0.0)
        rescale = jnp.exp(running_max - new_max)
        running_sum = running_sum * rescale + jnp.sum(chances, axis=-1)
        accumulated = accumulated * rescale[..., None] + jnp.einsum(
            "grk,kgd->grd",
            chances.astype(jnp.bfloat16),
            value_part,
            preferred_element_type=jnp.float32,
        )
        return (new_max, running_sum, accumulated)

    row_count = per_group * tokens
    start_carry = (
        jnp.full((KVH, row_count), masked_value, jnp.float32),
        jnp.zeros((KVH, row_count), jnp.float32),
        jnp.zeros((KVH, row_count, HD), jnp.float32),
    )
    running_max, running_sum, accumulated = lax.fori_loop(0, block_count, visit_block, start_carry)
    output = accumulated / running_sum[..., None]
    return (query_flat(output, tokens), running_max + jnp.log(running_sum))


def attend_backward(
    queries_flat,
    key_rows,
    attention_raw,
    log_norm,
    grad_low,
    positions,
    doc_ids,
    all_ids,
    ctx_index,
):
    tokens = queries_flat.shape[0]
    length = key_rows.shape[0]
    per_group = QH // KVH
    queries = query_groups(queries_flat)
    grad_rows = query_groups(grad_low)
    grad_wide = grad_rows.astype(jnp.float32)
    delta = jnp.sum(grad_wide * query_groups(attention_raw), axis=-1)
    query_pos = jnp.tile(positions, per_group)
    query_ids = jnp.tile(doc_ids, per_group)
    block_len = math.gcd(length, KEY_BLOCK)
    block_count = ((ctx_index + 1) * tokens + block_len - 1) // block_len

    def visit_block(block_index, carry):
        query_grad, key_grad, value_grad = carry
        offset = block_index * block_len
        scores, allowed, key_part, value_part = score_block(
            queries, key_rows, query_pos, query_ids, all_ids, offset, block_len
        )
        chances = jnp.where(allowed[None], jnp.exp(scores - log_norm[..., None]), 0.0)
        prob_grad = jnp.einsum(
            "grd,kgd->grk", grad_rows, value_part, preferred_element_type=jnp.float32
        )
        score_grad = (chances * (prob_grad - delta[..., None])).astype(jnp.bfloat16)
        query_grad = query_grad + jnp.einsum(
            "grk,kgd->grd", score_grad, key_part, preferred_element_type=jnp.float32
        )
        key_piece = (
            jnp.einsum("grk,grd->kgd", score_grad, queries, preferred_element_type=jnp.float32)
            * 0.125
        )
        value_piece = jnp.einsum(
            "grk,grd->kgd",
            chances.astype(jnp.bfloat16),
            grad_rows,
            preferred_element_type=jnp.float32,
        )
        key_grad = lax.dynamic_update_slice_in_dim(
            key_grad,
            lax.dynamic_slice_in_dim(key_grad, offset, block_len, 0)
            + key_piece.reshape(block_len, KVD),
            offset,
            0,
        )
        value_grad = lax.dynamic_update_slice_in_dim(
            value_grad,
            lax.dynamic_slice_in_dim(value_grad, offset, block_len, 0)
            + value_piece.reshape(block_len, KVD),
            offset,
            0,
        )
        return (query_grad, key_grad, value_grad)

    start_carry = (
        jnp.zeros((KVH, per_group * tokens, HD), jnp.float32),
        jnp.zeros((length, KVD), jnp.float32),
        jnp.zeros((length, KVD), jnp.float32),
    )
    query_grad, key_grad, value_grad = lax.fori_loop(0, block_count, visit_block, start_carry)
    return (query_flat(query_grad * 0.125, tokens), key_grad, value_grad)


def layer_layout(doc_sizes, tokens, ctx_index, ctx_count):
    positions = ctx_index * tokens + jnp.arange(tokens, dtype=jnp.int32)
    doc_ids, starts = doc_layout(doc_sizes, positions)
    all_ids = doc_layout(doc_sizes, jnp.arange(tokens * ctx_count, dtype=jnp.int32))[0]
    ext_ids = doc_layout(
        doc_sizes, ctx_index * tokens - (CONV - 1) + jnp.arange(tokens + CONV - 1, dtype=jnp.int32)
    )[0]
    return (positions, doc_ids, starts, all_ids, ext_ids)


def layer_forward(hidden_in, weights_full, head_params, doc_sizes, ctx_index, ctx_count):
    tokens = hidden_in.shape[0]
    positions, doc_ids, starts, all_ids, ext_ids = layer_layout(
        doc_sizes, tokens, ctx_index, ctx_count
    )
    normed = norm_apply(hidden_in, weights_full["first_gain"].astype(jnp.float32)).astype(
        jnp.bfloat16
    )
    projected = jnp.dot(
        normed, weights_full["mixer_in"], preferred_element_type=jnp.float32
    ).astype(jnp.bfloat16)
    edge_rows = passed_along(projected[tokens - (CONV - 1) :, DS : DS + CONVD], "ctx", 1)
    extended = jnp.concatenate([edge_rows, projected[:, DS : DS + CONVD]], axis=0).astype(
        jnp.float32
    )
    raw_rate = projected[:, DS + CONVD :].astype(jnp.float32)
    step_bias, decay_log, skip_gain = head_params
    empty_state = jnp.zeros((MH, MP, NS), jnp.float32)
    (partial_out, local_state), (read_vector, log_decay) = mixer_local(
        extended,
        raw_rate,
        weights_full["conv_kernel"].astype(jnp.float32),
        weights_full["conv_bias"].astype(jnp.float32),
        step_bias,
        decay_log,
        skip_gain,
        empty_state,
        ext_ids,
        doc_ids,
        starts,
    )
    inflow = device_inflow(log_decay, doc_ids, starts)
    state_in = prefix(
        (inflow[-1], local_state), "ctx", chain_affine, (jnp.ones((MH,), jnp.float32), empty_state)
    )[1]
    carried = (
        jnp.einsum("tn,hpn->thp", read_vector, state_in, precision=highest) * inflow[:, :, None]
    )
    ssm_out = partial_out + carried.reshape(tokens, DS)
    gate_value = projected[:, :DS].astype(jnp.float32)
    gated_out = (ssm_out * jax.nn.silu(gate_value)).astype(jnp.bfloat16)
    mixer_term = jnp.dot(gated_out, weights_full["mixer_out"], preferred_element_type=jnp.float32)
    heads_in = jnp.dot(
        normed, weights_full["attention_in"], preferred_element_type=jnp.float32
    ).astype(jnp.bfloat16)
    key_rows = lax.all_gather(heads_in[:, QD:], "ctx", axis=0, tiled=True)
    attention_raw, log_norm = attend_forward(
        heads_in[:, :QD], key_rows, positions, doc_ids, all_ids, ctx_index
    )
    attention_term = jnp.dot(
        attention_raw.astype(jnp.bfloat16),
        weights_full["attention_out"],
        preferred_element_type=jnp.float32,
    )
    middle = hidden_in + mixer_term + attention_term
    normed_mid = norm_apply(middle, weights_full["second_gain"].astype(jnp.float32)).astype(
        jnp.bfloat16
    )
    expanded = jnp.dot(normed_mid, weights_full["gate_up"], preferred_element_type=jnp.float32)
    hidden = (jax.nn.silu(expanded[:, :FF]) * expanded[:, FF:]).astype(jnp.bfloat16)
    result = middle + jnp.dot(
        hidden, weights_full["down_weight"], preferred_element_type=jnp.float32
    )
    stored = (
        hidden_in,
        middle,
        projected,
        edge_rows,
        state_in,
        ssm_out,
        heads_in,
        key_rows,
        attention_raw,
        log_norm,
        expanded,
    )
    return (result, stored)


def layer_backward(grad_in, stored, weights_full, head_params, doc_sizes, ctx_index, ctx_count):
    (
        hidden_in,
        middle,
        projected,
        edge_rows,
        state_in,
        ssm_out,
        heads_in,
        key_rows,
        attention_raw,
        log_norm,
        expanded,
    ) = stored
    tokens = hidden_in.shape[0]
    positions, doc_ids, starts, all_ids, ext_ids = layer_layout(
        doc_sizes, tokens, ctx_index, ctx_count
    )
    first_gain = weights_full["first_gain"].astype(jnp.float32)
    second_gain = weights_full["second_gain"].astype(jnp.float32)
    down_low = grad_in.astype(jnp.bfloat16)
    gate_vals = expanded[:, :FF]
    up_vals = expanded[:, FF:]
    gate_sig = jax.nn.sigmoid(gate_vals)
    hidden = (jax.nn.silu(gate_vals) * up_vals).astype(jnp.bfloat16)
    down_weight_grad = inner_rows(hidden, down_low)
    hidden_grad = outer_cols(down_low, weights_full["down_weight"])
    slope = gate_sig * (1.0 + gate_vals * (1.0 - gate_sig))
    expand_grad = jnp.concatenate(
        [hidden_grad * up_vals * slope, hidden_grad * jax.nn.silu(gate_vals)], axis=1
    ).astype(jnp.bfloat16)
    normed_mid = norm_apply(middle, second_gain).astype(jnp.bfloat16)
    gate_up_grad = inner_rows(normed_mid, expand_grad)
    mid_norm_grad, second_gain_grad = norm_back(
        middle, second_gain, outer_cols(expand_grad, weights_full["gate_up"])
    )
    middle_grad = grad_in + mid_norm_grad
    residual_low = middle_grad.astype(jnp.bfloat16)
    attention_out_grad = inner_rows(attention_raw.astype(jnp.bfloat16), residual_low)
    output_low = outer_cols(residual_low, weights_full["attention_out"]).astype(jnp.bfloat16)
    query_grad, key_grad, value_grad = attend_backward(
        heads_in[:, :QD],
        key_rows,
        attention_raw,
        log_norm,
        output_low,
        positions,
        doc_ids,
        all_ids,
        ctx_index,
    )
    key_share, value_share = (
        lax.psum_scatter(
            key_grad.astype(jnp.bfloat16), "ctx", scatter_dimension=0, tiled=True
        ).astype(jnp.float32),
        lax.psum_scatter(
            value_grad.astype(jnp.bfloat16), "ctx", scatter_dimension=0, tiled=True
        ).astype(jnp.float32),
    )
    heads_grad = jnp.concatenate([query_grad, key_share, value_share], axis=1).astype(jnp.bfloat16)
    gate_value = projected[:, :DS].astype(jnp.float32)
    gate_sig_z = jax.nn.sigmoid(gate_value)
    gated_out = (ssm_out * jax.nn.silu(gate_value)).astype(jnp.bfloat16)
    mixer_out_grad = inner_rows(gated_out, residual_low)
    gated_grad = outer_cols(residual_low, weights_full["mixer_out"])
    ssm_grad = gated_grad * jax.nn.silu(gate_value)
    gate_grad = gated_grad * ssm_out * gate_sig_z * (1.0 + gate_value * (1.0 - gate_sig_z))
    extended = jnp.concatenate([edge_rows, projected[:, DS : DS + CONVD]], axis=0).astype(
        jnp.float32
    )
    raw_rate = projected[:, DS + CONVD :].astype(jnp.float32)
    step_bias, decay_log, skip_gain = head_params

    def local_piece(
        extended, raw_rate, kernel, offset_vec, step_bias, decay_log, skip_gain, state_in
    ):
        return mixer_local(
            extended,
            raw_rate,
            kernel,
            offset_vec,
            step_bias,
            decay_log,
            skip_gain,
            state_in,
            ext_ids,
            doc_ids,
            starts,
        )

    primal, pullback, (read_vector, log_decay) = jax.vjp(
        local_piece,
        extended,
        raw_rate,
        weights_full["conv_kernel"].astype(jnp.float32),
        weights_full["conv_bias"].astype(jnp.float32),
        step_bias,
        decay_log,
        skip_gain,
        state_in,
        has_aux=True,
    )
    inflow = device_inflow(log_decay, doc_ids, starts)
    local_grad = jnp.einsum(
        "th,thp,tn->hpn", inflow, ssm_grad.reshape(tokens, MH, MP), read_vector, precision=highest
    )
    state_back = prefix_2(
        (inflow[-1], local_grad),
        "ctx",
        chain_affine,
        (jnp.ones((MH,), jnp.float32), jnp.zeros((MH, MP, NS), jnp.float32)),
    )[1]
    ext_grad, raw_grad, kernel_grad, offset_grad, step_grad, decay_grad, skip_grad, unused = (
        pullback((ssm_grad, state_back))
    )
    rim_grad = passed_along(ext_grad[: CONV - 1], "ctx", -1)
    pre_grad = ext_grad[CONV - 1 :]
    pre_grad = jnp.concatenate(
        [pre_grad[: tokens - (CONV - 1)], pre_grad[tokens - (CONV - 1) :] + rim_grad], axis=0
    )
    mixer_grad = jnp.concatenate([gate_grad, pre_grad, raw_grad], axis=1).astype(jnp.bfloat16)
    normed = norm_apply(hidden_in, first_gain).astype(jnp.bfloat16)
    mixer_in_grad = inner_rows(normed, mixer_grad)
    attention_in_grad = inner_rows(normed, heads_grad)
    normed_grad = outer_cols(mixer_grad, weights_full["mixer_in"]) + outer_cols(
        heads_grad, weights_full["attention_in"]
    )
    in_norm_grad, first_gain_grad = norm_back(hidden_in, first_gain, normed_grad)
    block_grad = middle_grad + in_norm_grad
    weight_grads = (
        first_gain_grad,
        mixer_in_grad,
        kernel_grad,
        offset_grad,
        mixer_out_grad,
        attention_in_grad,
        attention_out_grad,
        second_gain_grad,
        gate_up_grad,
        down_weight_grad,
    )
    return (block_grad, weight_grads, (step_grad, decay_grad, skip_grad))


def local(
    block_input,
    output_grad,
    doc_lengths,
    first_gain,
    mixer_in,
    conv_kernel,
    conv_bias,
    step_bias,
    decay_log,
    skip_gain,
    mixer_out,
    attention_in,
    attention_out,
    second_gain,
    gate_up,
    down_weight,
):
    gathered = (
        lax.all_gather(first_gain[0], "wt", axis=0, tiled=True),
        lax.all_gather(mixer_in[0], "wt", axis=0, tiled=True),
        lax.all_gather(conv_kernel[0], "wt", axis=1, tiled=True),
        lax.all_gather(conv_bias[0], "wt", axis=0, tiled=True),
        lax.all_gather(mixer_out[0], "wt", axis=0, tiled=True),
        lax.all_gather(attention_in[0], "wt", axis=0, tiled=True),
        lax.all_gather(attention_out[0], "wt", axis=0, tiled=True),
        lax.all_gather(second_gain[0], "wt", axis=0, tiled=True),
        lax.all_gather(gate_up[0], "wt", axis=0, tiled=True),
        lax.all_gather(down_weight[0], "wt", axis=0, tiled=True),
    )
    weights_full = dict(zip(weight_names, gathered))
    head_params = (step_bias[0], decay_log[0], skip_gain[0])
    head_section = lax.axis_index("section") == 0
    ctx_index = lax.axis_index("ctx")
    ctx_count = lax.axis_size("ctx")
    tokens = block_input.shape[2]
    received = jnp.zeros((tokens, D), jnp.bfloat16)
    results = []
    stored_list = []
    for moment in range(MICRO + 1):
        own_block = block_input[min(moment, MICRO - 1), 0].astype(jnp.float32)
        entry = jnp.where(head_section, own_block, received.astype(jnp.float32))
        doc_sizes = jnp.where(
            head_section, doc_lengths[min(moment, MICRO - 1), 0], doc_lengths[max(moment - 1, 0), 0]
        )
        layer_result, stored = layer_forward(
            entry, weights_full, head_params, doc_sizes, ctx_index, ctx_count
        )
        sent = layer_result.astype(jnp.bfloat16)
        results.append(sent)
        stored_list.append((stored, doc_sizes))
        if moment < MICRO:
            received = passed_along(sent, "section", 1)
    back_received = jnp.zeros((tokens, D), jnp.bfloat16)
    total_grads = tuple((jnp.zeros(weight_full.shape, jnp.float32) for weight_full in gathered))
    total_heads = tuple((jnp.zeros(param_vec.shape, jnp.float32) for param_vec in head_params))
    sent_grads = []
    for moment in range(MICRO + 1):
        given_grad = output_grad[min(moment, MICRO - 1), 0].astype(jnp.float32)
        cotangent = jnp.where(head_section, back_received.astype(jnp.float32), given_grad)
        chosen = jax.tree.map(
            lambda left, right: jnp.where(head_section, left, right),
            stored_list[max(moment - 1, 0)],
            stored_list[min(moment + 1, MICRO)],
        )
        valid = jnp.where(head_section, moment >= 1, moment < MICRO)
        stored, doc_sizes = chosen
        block_grad, weight_grads, head_grads = layer_backward(
            cotangent, stored, weights_full, head_params, doc_sizes, ctx_index, ctx_count
        )
        total_grads = tuple(
            (old + jnp.where(valid, new, 0.0) for old, new in zip(total_grads, weight_grads))
        )
        total_heads = tuple(
            (old + jnp.where(valid, new, 0.0) for old, new in zip(total_heads, head_grads))
        )
        sent = block_grad.astype(jnp.bfloat16)
        sent_grads.append(sent)
        if moment < MICRO:
            back_received = passed_along(sent, "section", -1)
    section_output = jnp.stack(
        [
            jnp.where(head_section, results[batch_index], results[batch_index + 1])
            for batch_index in range(MICRO)
        ]
    ).reshape(1, MICRO, 1, tokens, D)
    input_grad = jnp.stack(
        [
            jnp.where(head_section, sent_grads[batch_index + 1], sent_grads[batch_index])
            for batch_index in range(MICRO)
        ]
    ).reshape(1, MICRO, 1, tokens, D)
    shares = (
        lax.psum_scatter(
            total_grads[0].astype(jnp.bfloat16), "wt", scatter_dimension=0, tiled=True
        ).astype(jnp.float32),
        lax.psum_scatter(
            total_grads[1].astype(jnp.bfloat16), "wt", scatter_dimension=0, tiled=True
        ).astype(jnp.float32),
        lax.psum_scatter(
            total_grads[2].astype(jnp.bfloat16), "wt", scatter_dimension=1, tiled=True
        ).astype(jnp.float32),
        lax.psum_scatter(
            total_grads[3].astype(jnp.bfloat16), "wt", scatter_dimension=0, tiled=True
        ).astype(jnp.float32),
        lax.psum_scatter(
            total_grads[4].astype(jnp.bfloat16), "wt", scatter_dimension=0, tiled=True
        ).astype(jnp.float32),
        lax.psum_scatter(
            total_grads[5].astype(jnp.bfloat16), "wt", scatter_dimension=0, tiled=True
        ).astype(jnp.float32),
        lax.psum_scatter(
            total_grads[6].astype(jnp.bfloat16), "wt", scatter_dimension=0, tiled=True
        ).astype(jnp.float32),
        lax.psum_scatter(
            total_grads[7].astype(jnp.bfloat16), "wt", scatter_dimension=0, tiled=True
        ).astype(jnp.float32),
        lax.psum_scatter(
            total_grads[8].astype(jnp.bfloat16), "wt", scatter_dimension=0, tiled=True
        ).astype(jnp.float32),
        lax.psum_scatter(
            total_grads[9].astype(jnp.bfloat16), "wt", scatter_dimension=0, tiled=True
        ).astype(jnp.float32),
    )
    reduced = (
        lax.psum(shares[0].astype(jnp.bfloat16), "ctx").astype(jnp.float32),
        lax.psum(shares[1].astype(jnp.bfloat16), "ctx").astype(jnp.float32),
        lax.psum(shares[2].astype(jnp.bfloat16), "ctx").astype(jnp.float32),
        lax.psum(shares[3].astype(jnp.bfloat16), "ctx").astype(jnp.float32),
        lax.psum(shares[4].astype(jnp.bfloat16), "ctx").astype(jnp.float32),
        lax.psum(shares[5].astype(jnp.bfloat16), "ctx").astype(jnp.float32),
        lax.psum(shares[6].astype(jnp.bfloat16), "ctx").astype(jnp.float32),
        lax.psum(shares[7].astype(jnp.bfloat16), "ctx").astype(jnp.float32),
        lax.psum(shares[8].astype(jnp.bfloat16), "ctx").astype(jnp.float32),
        lax.psum(shares[9].astype(jnp.bfloat16), "ctx").astype(jnp.float32),
    )
    head_sums = lax.psum((total_heads[0], total_heads[1], total_heads[2]), ("ctx", "wt"))
    return (
        section_output,
        input_grad,
        reduced[0][None],
        reduced[1][None],
        reduced[2][None],
        reduced[3][None],
        head_sums[0][None],
        head_sums[1][None],
        head_sums[2][None],
        reduced[4][None],
        reduced[5][None],
        reduced[6][None],
        reduced[7][None],
        reduced[8][None],
        reduced[9][None],
    )


def spread(mesh):
    placed = (
        P(None, "wt", "ctx", None),
        P(None, "wt", "ctx", None),
        P(None, "wt", None),
        P("section", "wt"),
        P("section", "wt", None),
        P("section", None, "wt"),
        P("section", "wt"),
        P("section", None),
        P("section", None),
        P("section", None),
        P("section", "wt", None),
        P("section", "wt", None),
        P("section", "wt", None),
        P("section", "wt"),
        P("section", "wt", None),
        P("section", "wt", None),
    )
    return jax.shard_map(
        local,
        mesh=mesh,
        in_specs=placed,
        out_specs=(
            P("section", None, "wt", "ctx", None),
            P("section", None, "wt", "ctx", None),
            P("section", "wt"),
            P("section", "wt", None),
            P("section", None, "wt"),
            P("section", "wt"),
            P("section", None),
            P("section", None),
            P("section", None),
            P("section", "wt", None),
            P("section", "wt", None),
            P("section", "wt", None),
            P("section", "wt"),
            P("section", "wt", None),
            P("section", "wt", None),
        ),
        check_vma=False,
    )


f32, bf16 = jnp.float32, jnp.bfloat16
RH = MH // 4
RD = DS // 4
RQ = QD // 4
RF = FF // 4
RAW_AT = 2 * RD + 2 * NS
Q_AT = RAW_AT + 128
K_AT = Q_AT + RQ
INC = K_AT + 2 * HD
OUTR = RD + RQ
FREE = 22
GROUP_A = INC + D // 2
GROUP_B = 2 * RF + D // 2
AXES = CORE, ROW, COL, LINE = tuple("cyxz")


def swapped(value, axis):
    return lax.ppermute(value, axis, [(0, 1), (1, 0)])


def across(value):
    return lax.ppermute(value, (ROW, COL), [(0, 3), (1, 2), (2, 1), (3, 0)])


def place(p):
    return ((p[0] * 2 + p[1]) * 2 + p[2]) * 4 + p[3]


def sent(value, pairs):
    return lax.ppermute(value, AXES, [(place(a), place(b)) for a, b in pairs])


every = [(c, y, x, z) for c in range(2) for y in range(2) for x in range(2) for z in range(4)]


def turned(value, by):
    return lax.ppermute(value, LINE, [(i, (i + by) % 4) for i in range(4)])


def paired_lines(value, by):
    return lax.ppermute(value, LINE, [(i, i ^ by) for i in range(4)])


def after(value, *others):
    return lax.optimization_barrier((value,) + others)[0]


def ordered(flag, own, other):
    return jnp.where(flag == 0, jnp.stack([own, other]), jnp.stack([other, own]))


def whole_rows(pair, y, x):
    own = lax.dynamic_index_in_dim(pair, y, 0, False)
    other = lax.dynamic_index_in_dim(pair, 1 - y, 0, False)
    near = ordered(x, own, swapped(own, COL))
    far = ordered(x, swapped(other, ROW), across(other))
    return ordered(y, near, far).reshape(4 * own.shape[0], own.shape[1])


def back_rows(rows, y, x):
    blocks = rows.reshape(2, 2, rows.shape[0] // 4, rows.shape[1])
    return ordered(y, blocks[y, x], swapped(blocks[1 - y, x], ROW))


def half_sum(keep, give):
    low = (keep.astype(f32) + swapped(give, CORE).astype(f32)).astype(bf16)
    return (low.astype(f32) + swapped(low, COL).astype(f32)).astype(bf16)


def quarter_sum(keep, give):
    both = half_sum(keep, give)
    return both, swapped(both, CORE)


BLOCK = 128
REACH = 2
CONVR = RD + 2 * NS
OUT_BLOCKS = [(j, y, c) for j in range(2) for y, c in ((0, 0), (0, 1), (1, 0))] + [(0, 1, 1), (1, 1, 1)]
WIDE = D // 2
LIMIT = 56 << 20


def mm(left, right, dims=((1,), (0,)), precision=None):
    return lax.dot_general(left, right, (dims, ((), ())), precision=precision, preferred_element_type=f32)


NT = ((1,), (1,))
TN = ((0,), (0,))


def parts_of(value):
    first = value.astype(bf16)
    rest = value - first.astype(f32)
    second = rest.astype(bf16)
    return first, second, (rest - second.astype(f32)).astype(bf16)


def picked(left, right):
    if left.dtype == bf16:
        return sum(mm(left, p) for p in parts_of(right))
    return sum(mm(p, right) for p in parts_of(left))


def logistic(value):
    return 1.0 / (1.0 + jnp.exp(-value))


def slope(value, sig):
    return sig * (1.0 + value * (1.0 - sig))


def unit_scale(rows):
    return lax.rsqrt(jnp.mean(rows * rows, axis=-1, keepdims=True) + epsilon)


def conv_chunk(proj_ref, ck_ref, tok_ref, j):
    lanes = slice(128 * j, 128 * (j + 1))
    pre = proj_ref[:, RD + 128 * j : RD + 128 * (j + 1)].astype(f32)
    summed = ck_ref[4:5, lanes] + pre * ck_ref[3:4, lanes]
    for by in range(1, CONV):
        summed = summed + pltpu.roll(pre, by, 0) * (ck_ref[3 - by : 4 - by, lanes] * tok_ref[:, by : by + 1])
    return pre, summed


def step_sizes(proj_ref, hp_ref):
    stepped = proj_ref[:, RAW_AT : RAW_AT + 128].astype(f32) + hp_ref[0:1, :]
    dt = jnp.maximum(stepped, 0.0) + jnp.log1p(jnp.exp(-jnp.abs(stepped)))
    return stepped, dt


def running(dt, hp_ref, run_s, run_t):
    count = dt.shape[0]
    rate = -dt * hp_ref[1:2, :]
    until = (
        lax.broadcasted_iota(jnp.int32, (count, count), 0) >= lax.broadcasted_iota(jnp.int32, (count, count), 1)
    ).astype(bf16)
    run = picked(until, rate)
    run_s[...] = run
    run_t[...] = run.T
    return rate


def spans(count):
    for i in range(count // BLOCK):
        start = BLOCK * max(0, i - REACH)
        yield slice(BLOCK * i, BLOCK * (i + 1)), slice(start, BLOCK * (i + 1)), start


def barred(tok_ref, idr_ref, rows, keys):
    shape = (rows.stop - rows.start, keys.stop - keys.start)
    query = lax.broadcasted_iota(jnp.int32, shape, 0) + rows.start
    key = lax.broadcasted_iota(jnp.int32, shape, 1) + keys.start
    ok = (query >= key) & (tok_ref[rows, 0:1] == idr_ref[0:1, keys])
    return jnp.where(ok, 0.0, masked_value)


def fed_chunk(dt, conv, j, count):
    lane = lax.broadcasted_iota(jnp.int32, (count, 128), 1)
    return jnp.where(lane < MP, dt[:, 2 * j : 2 * j + 1], dt[:, 2 * j + 1 : 2 * j + 2]) * conv


def split_rows(c_ref, keep_ref, give_ref, half, value):
    @pl.when(c_ref[0] == half)
    def _():
        keep_ref[...] = value

    @pl.when(c_ref[0] != half)
    def _():
        give_ref[...] = value


def first_kernel(
    c_ref, mid_ref, own_ref, other_ref, gain_ref, wi_ref, mine_ref, got_ref, ck_ref, hp_ref, tok_ref, idr_ref,
    keep_ref, give_ref, x_ref, proj_ref, state_ref, ga_ref, h_s, wo_ref,
    vals_s, bc_s, fed_s, run_s, run_t,
):
    count = mid_ref.shape[0]
    for b, (j, y, c) in enumerate(OUT_BLOCKS):
        rows = slice(128 * j + 64 * y, 128 * j + 64 * y + 64)
        wo_ref[64 * b : 64 * b + 64, :] = jnp.where(c_ref[0] == c, mine_ref[rows, :], got_ref[rows, :])
    for i in range(count // BLOCK):
        rows = slice(BLOCK * i, BLOCK * (i + 1))
        low = mid_ref[rows, :]
        if mid_ref.dtype == f32:
            low = (low + added_rows(c_ref, own_ref, other_ref, i, count)).astype(bf16)
        x_ref[rows, :] = low
        x = low.astype(f32)
        h_s[rows, :] = (x * unit_scale(x) * gain_ref[...]).astype(bf16)
    for at in range(0, INC, 256):
        cols = slice(at, min(at + 256, INC))
        proj_ref[:, cols] = mm(h_s[...], wi_ref[:, cols]).astype(bf16)
    stepped, dt = step_sizes(proj_ref, hp_ref)
    running(dt, hp_ref, run_s, run_t)
    for j in range(CONVR // 128):
        pre, summed = conv_chunk(proj_ref, ck_ref, tok_ref, j)
        conv = summed * logistic(summed)
        if j < RD // 128:
            vals_s[:, 128 * j : 128 * (j + 1)] = conv
            fed_s[:, 128 * j : 128 * (j + 1)] = fed_chunk(dt, conv, j, count).astype(bf16)
        else:
            bc_s[:, 128 * j - RD : 128 * (j + 1) - RD] = conv.astype(bf16)
    for rows, keys, start in spans(count):
        bar = barred(tok_ref, idr_ref, rows, keys)
        gram = mm(bc_s[rows, NS:], bc_s[keys, :NS], NT)
        for h in range(RH):
            lanes = slice(MP * h, MP * (h + 1))
            decay = jnp.exp(run_s[rows, h : h + 1] - run_t[h : h + 1, keys] + bar)
            state_ref[rows, lanes] = mm((gram * decay).astype(bf16), fed_s[keys, lanes])
        for h in range(RQ // HD):
            lanes = slice(Q_AT + HD * h, Q_AT + HD * (h + 1))
            scores = mm(proj_ref[rows, lanes], proj_ref[keys, K_AT : K_AT + HD], NT) * 0.125 + bar
            chances = jnp.exp(scores - jnp.max(scores, axis=-1, keepdims=True))
            probs = (chances / jnp.sum(chances, axis=-1, keepdims=True)).astype(bf16)
            ga_ref[rows, RD + HD * h : RD + HD * (h + 1)] = mm(
                probs, proj_ref[keys, K_AT + HD : K_AT + 2 * HD]
            ).astype(bf16)
        z = proj_ref[rows, :RD].astype(f32)
        ssm = state_ref[rows, :] + ck_ref[5:6, :RD] * vals_s[rows, :]
        ga_ref[rows, :RD] = (ssm * z * logistic(z)).astype(bf16)
    for half in range(2):
        rows = slice(count // 2 * half, count // 2 * (half + 1))
        split_rows(c_ref, keep_ref, give_ref, half, mm(ga_ref[rows, :], wo_ref[...]).astype(bf16))


def added_rows(c_ref, own_ref, other_ref, i, count):
    half, at = divmod(BLOCK * i, count // 2)
    rows = slice(at, at + BLOCK)
    return jnp.where(c_ref[0] == half, own_ref[rows, :], other_ref[rows, :]).astype(f32)


def second_kernel(
    c_ref, x_ref, own_ref, other_ref, gain_ref, wgu_ref, wd_ref,
    keep_ref, give_ref, mid_ref, h_ref, gu_ref, hid_ref,
):
    count = x_ref.shape[0]
    for i in range(count // BLOCK):
        rows = slice(BLOCK * i, BLOCK * (i + 1))
        mid = x_ref[rows, :].astype(f32) + added_rows(c_ref, own_ref, other_ref, i, count)
        mid_ref[rows, :] = mid
        h_ref[rows, :] = (mid * unit_scale(mid) * gain_ref[...]).astype(bf16)
    for at in range(0, RF, 256):
        cols = slice(at, at + 256)
        ups = slice(RF + at, RF + at + 256)
        gate = mm(h_ref[...], wgu_ref[:, cols])
        up = mm(h_ref[...], wgu_ref[:, ups])
        gu_ref[:, cols] = gate
        gu_ref[:, ups] = up
        hid_ref[:, cols] = (gate * logistic(gate) * up).astype(bf16)
    for half in range(2):
        rows = slice(count // 2 * half, count // 2 * (half + 1))
        split_rows(c_ref, keep_ref, give_ref, half, mm(hid_ref[rows, :], wd_ref[...]).astype(bf16))


def back_second_kernel(c_ref, cot_ref, gu_ref, wgu_ref, wd_ref, keep_ref, give_ref, gug_ref):
    count = cot_ref.shape[0]
    for at in range(0, RF, 256):
        cols = slice(at, at + 256)
        ups = slice(RF + at, RF + at + 256)
        hidden_grad = mm(cot_ref[...], wd_ref[cols, :], NT)
        gate, up = gu_ref[:, cols], gu_ref[:, ups]
        sig = logistic(gate)
        gug_ref[:, cols] = (hidden_grad * up * slope(gate, sig)).astype(bf16)
        gug_ref[:, ups] = (hidden_grad * gate * sig).astype(bf16)
    for half in range(2):
        rows = slice(count // 2 * half, count // 2 * (half + 1))
        split_rows(c_ref, keep_ref, give_ref, half, mm(gug_ref[rows, :], wgu_ref[...], NT).astype(bf16))


def norm_back_rows(rows, gain, grad):
    scale = unit_scale(rows)
    normed = rows * scale
    weighted = grad * gain
    back = scale * (weighted - normed * jnp.mean(weighted * normed, axis=-1, keepdims=True))
    return back, jnp.sum(grad * normed, axis=0, keepdims=True)


def back_first_kernel(
    c_ref, cot_ref, own_ref, other_ref, mid_ref, gain_ref, proj_ref, state_ref, ga_ref, wi_ref, wo_ref, ck_ref,
    hp_ref, tok_ref, idr_ref,
    keep_ref, give_ref, outk_ref, outg_ref, midg_ref, projg_ref, gaing_ref, convg_ref, headg_ref,
    low_ref, gag_s, vals_s, bc_s, fed_s, run_s, run_t, sg_s, fedg_s, bcg_s, kvg_s, valg_s,
):
    count = cot_ref.shape[0]
    gain_grad = jnp.zeros((1, D), f32)
    for i in range(count // BLOCK):
        rows = slice(BLOCK * i, BLOCK * (i + 1))
        back, more = norm_back_rows(
            mid_ref[rows, :], gain_ref[...], added_rows(c_ref, own_ref, other_ref, i, count)
        )
        gain_grad = gain_grad + more
        total = cot_ref[rows, :].astype(f32) + back
        midg_ref[rows, :] = total
        low_ref[rows, :] = total.astype(bf16)
    gaing_ref[...] = gain_grad
    for q in range(OUTR // 128):
        grad = mm(ga_ref[:, 128 * q : 128 * (q + 1)], low_ref[...], TN).astype(bf16)
        for b in (2 * q, 2 * q + 1):
            j, y, c = OUT_BLOCKS[b]
            rows = slice(128 * j + 64 * y, 128 * j + 64 * y + 64)
            part = grad[64 * (b % 2) : 64 * (b % 2) + 64, :]

            @pl.when(c_ref[0] == c)
            def _(rows=rows, part=part):
                outk_ref[rows, :] = part

            @pl.when(c_ref[0] != c)
            def _(rows=rows, part=part):
                outg_ref[rows, :] = part

    for at in range(0, OUTR, 256):
        cols = slice(at, at + 256)
        gag_s[:, cols] = mm(low_ref[...], wo_ref[cols, :], NT)
    stepped, dt = step_sizes(proj_ref, hp_ref)
    rate = running(dt, hp_ref, run_s, run_t)
    for j in range(CONVR // 128):
        lanes = slice(128 * j, 128 * (j + 1))
        pre, summed = conv_chunk(proj_ref, ck_ref, tok_ref, j)
        conv = summed * logistic(summed)
        if j < RD // 128:
            vals_s[:, lanes] = conv
            fed_s[:, lanes] = fed_chunk(dt, conv, j, count).astype(bf16)
            z = proj_ref[:, lanes].astype(f32)
            sig = logistic(z)
            skip = ck_ref[5:6, lanes]
            grad = gag_s[:, lanes]
            ssm = state_ref[:, lanes] + skip * conv
            projg_ref[:, lanes] = (grad * ssm * slope(z, sig)).astype(bf16)
            ssm_grad = grad * z * sig
            sg_s[:, lanes] = ssm_grad.astype(bf16)
            valg_s[:, lanes] = ssm_grad * skip
            convg_ref[5:6, lanes] = jnp.sum(ssm_grad * conv, axis=0, keepdims=True)
        else:
            bc_s[:, 128 * j - RD : 128 * (j + 1) - RD] = conv.astype(bf16)
    fedg_s[...] = jnp.zeros_like(fedg_s)
    bcg_s[:, :NS] = jnp.zeros((count, NS), f32)
    kvg_s[...] = jnp.zeros_like(kvg_s)
    for rows, keys, start in spans(count):
        bar = barred(tok_ref, idr_ref, rows, keys)
        gram = mm(bc_s[rows, NS:], bc_s[keys, :NS], NT)
        gram_grad = jnp.zeros_like(gram)
        for h in range(RH):
            lanes = slice(MP * h, MP * (h + 1))
            decay = jnp.exp(run_s[rows, h : h + 1] - run_t[h : h + 1, keys] + bar)
            grad = sg_s[rows, lanes]
            gram_grad = gram_grad + mm(grad, fed_s[keys, lanes], NT) * decay
            fedg_s[keys, lanes] += mm((gram * decay).astype(bf16), grad, TN)
        gram_low = gram_grad.astype(bf16)
        bcg_s[rows, NS:] = mm(gram_low, bc_s[keys, :NS])
        bcg_s[keys, :NS] += mm(gram_low, bc_s[rows, NS:], TN)
        for h in range(RQ // HD):
            lanes = slice(Q_AT + HD * h, Q_AT + HD * (h + 1))
            query, key = proj_ref[rows, lanes], proj_ref[keys, K_AT : K_AT + HD]
            scores = mm(query, key, NT) * 0.125 + bar
            chances = jnp.exp(scores - jnp.max(scores, axis=-1, keepdims=True))
            probs = chances / jnp.sum(chances, axis=-1, keepdims=True)
            grad = gag_s[rows, RD + HD * h : RD + HD * (h + 1)].astype(bf16)
            prob_grad = mm(grad, proj_ref[keys, K_AT + HD : K_AT + 2 * HD], NT)
            score_grad = probs * (prob_grad - jnp.sum(probs * prob_grad, axis=-1, keepdims=True))
            score_grad = score_grad.astype(bf16)
            projg_ref[rows, lanes] = (mm(score_grad, key) * 0.125).astype(bf16)
            kvg_s[keys, :HD] += mm(score_grad, query, TN) * 0.125
            kvg_s[keys, HD:] += mm(probs.astype(bf16), grad, TN)
    projg_ref[:, K_AT:] = kvg_s[...].astype(bf16)
    head_of = lax.broadcasted_iota(jnp.int32, (RD, 128), 0) // MP
    picks = (head_of == lax.broadcasted_iota(jnp.int32, (RD, 128), 1)).astype(bf16)
    run_grad = picked(sg_s[...].astype(f32) * state_ref[...] - fed_s[...].astype(f32) * fedg_s[...], picks)
    shape = (count, count)
    later = (
        (lax.broadcasted_iota(jnp.int32, shape, 1) >= lax.broadcasted_iota(jnp.int32, shape, 0))
        & (tok_ref[:, 0:1] == idr_ref[0:1, :])
    ).astype(bf16)
    rate_grad = picked(later, run_grad)
    dt_grad = picked(vals_s[...] * fedg_s[...], picks) - rate_grad * hp_ref[1:2, :]
    raw_grad = dt_grad * logistic(stepped)
    headg_ref[0:1, :] = jnp.sum(raw_grad, axis=0, keepdims=True)
    headg_ref[1:2, :] = jnp.sum(rate_grad * rate, axis=0, keepdims=True)
    lane = lax.broadcasted_iota(jnp.int32, raw_grad.shape, 1)
    projg_ref[:, RAW_AT : RAW_AT + 128] = jnp.where(lane < RH, raw_grad, 0.0).astype(bf16)
    for j in range(CONVR // 128):
        lanes = slice(128 * j, 128 * (j + 1))
        pre, summed = conv_chunk(proj_ref, ck_ref, tok_ref, j)
        if j < RD // 128:
            grad = valg_s[:, lanes] + fed_chunk(dt, fedg_s[:, lanes], j, count)
        else:
            grad = bcg_s[:, 128 * j - RD : 128 * (j + 1) - RD]
        grad = grad * slope(summed, logistic(summed))
        convg_ref[4:5, lanes] = jnp.sum(grad, axis=0, keepdims=True)
        convg_ref[3:4, lanes] = jnp.sum(grad * pre, axis=0, keepdims=True)
        total = grad * ck_ref[3:4, lanes]
        for by in range(1, CONV):
            kept = grad * tok_ref[:, by : by + 1]
            convg_ref[3 - by : 4 - by, lanes] = jnp.sum(kept * pltpu.roll(pre, by, 0), axis=0, keepdims=True)
            total = total + pltpu.roll(kept * ck_ref[3 - by : 4 - by, lanes], count - by, 0)
        projg_ref[:, RD + 128 * j : RD + 128 * (j + 1)] = total.astype(bf16)
    for half in range(2):
        rows = slice(count // 2 * half, count // 2 * (half + 1))
        split_rows(c_ref, keep_ref, give_ref, half, mm(projg_ref[rows, :], wi_ref[...], NT).astype(bf16))


def back_input_kernel(c_ref, x_ref, own_ref, other_ref, gain_ref, midg_ref, low_ref, gaing_ref):
    count = x_ref.shape[0]
    gain_grad = jnp.zeros((1, D), f32)
    for i in range(count // BLOCK):
        rows = slice(BLOCK * i, BLOCK * (i + 1))
        back, more = norm_back_rows(
            x_ref[rows, :].astype(f32), gain_ref[...], added_rows(c_ref, own_ref, other_ref, i, count)
        )
        gain_grad = gain_grad + more
        low_ref[rows, :] = (midg_ref[rows, :] + back).astype(bf16)
    gaing_ref[...] = gain_grad


def back_half_kernel(c_ref, x_ref, own_ref, gain_ref, midg_ref, low_ref, gaing_ref):
    gain_grad = jnp.zeros((1, D), f32)
    for i in range(own_ref.shape[0] // BLOCK):
        rows = slice(BLOCK * i, BLOCK * (i + 1))
        at = pl.ds(pl.multiple_of(own_ref.shape[0] * c_ref[0] + BLOCK * i, BLOCK), BLOCK)
        back, more = norm_back_rows(x_ref[at, :].astype(f32), gain_ref[...], own_ref[rows, :].astype(f32))
        gain_grad = gain_grad + more
        low_ref[rows, :] = (midg_ref[at, :] + back).astype(bf16)
    gaing_ref[...] = gain_grad


def chosen(shape, source):
    lane = lax.broadcasted_iota(jnp.int32, shape, 1)
    return (lax.broadcasted_iota(jnp.int32, shape, 0) == source(lane)).astype(bf16)


def heads_from(x, width):
    return lambda d: d + x * width + jnp.where(d >= width, width, 0)


def steps_from(x, core):
    return lambda d: jnp.where(d < RH, 12 * core + 3 * x + d + jnp.where(d >= 3, 3, 0), -1)


def keys_from(core):
    return lambda d: HD * core + d + jnp.where(d >= HD, HD, 0)


def aligned(value, by):
    return value if isinstance(value, int) else pl.multiple_of(value, by)


def folded(ref, index, at, rows):
    ref[index + (slice(0, 64), slice(at, at + WIDE))] = rows[:, :WIDE]
    ref[index + (slice(64, 128), slice(at, at + WIDE))] = rows[:, WIDE:]


def prepare_a_kernel(c_ref, mi_ref, ai_ref, mo_ref, ao_ref, free_ref, keep_ref, give_ref):
    core, x = c_ref[0], c_ref[2]
    pick = chosen((2 * RD, RD), heads_from(x, RD // 2))
    pick_query = chosen((2 * RQ, RQ), heads_from(x, HD))
    half = RD // 2
    for t in range(2):
        pick_step = chosen((MH, 128), steps_from(x, t))
        pick_key = chosen((2 * KVD, 2 * HD), keys_from(t))
        for y in range(2):
            rows = slice(128 * y, 128 * (y + 1))
            parts = [mm(mi_ref[DS * h + 2 * RD * t : DS * h + 2 * RD * (t + 1), rows], pick, TN) for h in range(2)]
            parts.append(mi_ref[2 * DS : 2 * DS + 2 * NS, rows].T)
            parts.append(mm(mi_ref[DS + CONVD :, rows], pick_step, TN) + free_ref[...].astype(f32))
            parts.append(mm(ai_ref[rows, 2 * RQ * t : 2 * RQ * (t + 1)], pick_query))
            parts.append(mm(ai_ref[rows, QD:], pick_key))
            if y == 0:
                out = mo_ref[pl.ds(aligned(half * x + 64 * t, 64), 64), :]
            elif t == 0:
                out = mo_ref[pl.ds(aligned(half * x + 128, 64), 64), :]
            else:
                out = ao_ref[pl.ds(aligned(64 * x, 64), 64), :]
            for k, ref in enumerate((keep_ref, give_ref)):

                @pl.when((core == t) if k == 0 else (core != t))
                def _(ref=ref, parts=parts, out=out, y=y):
                    at = 0
                    for part in parts:
                        ref[y, :, at : at + part.shape[1]] = part.astype(bf16)
                        at += part.shape[1]
                    folded(ref, (y,), INC, out)


def prepare_b_kernel(c_ref, gu_ref, dn_ref, keep_ref, give_ref):
    core, x = c_ref[0], c_ref[2]
    for t in range(2):
        for k, ref in enumerate((keep_ref, give_ref)):

            @pl.when((core == t) if k == 0 else (core != t))
            def _(ref=ref, t=t):
                for y in range(2):
                    rows = slice(128 * y, 128 * (y + 1))
                    for h in range(8):
                        at = aligned(RF * h + 256 * t + 128 * x, 128)
                        ref[y, :, 128 * h : 128 * (h + 1)] = gu_ref[rows, pl.ds(at, 128)]
                    at = aligned(256 * t + 128 * x + 64 * y, 64)
                    folded(ref, (y,), 2 * RF, dn_ref[pl.ds(at, 64), :])


def unpack_a_from(c_ref, parts, wi_ref, mine_ref, give_ref):
    for line, y, load in parts:
        wi_ref[pl.ds(aligned(256 * line + 128 * y, 128), 128), :] = load(slice(None), slice(0, INC))
        rows = pl.ds(aligned(128 * lax.rem(line, 2) + 64 * y, 64), 64)
        left = load(slice(0, 64), slice(INC, GROUP_A))
        right = load(slice(64, 128), slice(INC, GROUP_A))

        @pl.when(line // 2 == c_ref[0])
        def _(rows=rows, left=left, right=right):
            mine_ref[rows, :WIDE] = left
            mine_ref[rows, WIDE:] = right

        @pl.when(line // 2 != c_ref[0])
        def _(rows=rows, left=left, right=right):
            give_ref[rows, :WIDE] = left
            give_ref[rows, WIDE:] = right


def unpack_b_from(parts, wgu_ref, wd_ref):
    for line, y, load in parts:
        wgu_ref[pl.ds(aligned(256 * line + 128 * y, 128), 128), :] = load(slice(None), slice(0, 2 * RF))
        rows = pl.ds(aligned(128 * line + 64 * y, 64), 64)
        wd_ref[rows, :WIDE] = load(slice(0, 64), slice(2 * RF, GROUP_B))
        wd_ref[rows, WIDE:] = load(slice(64, 128), slice(2 * RF, GROUP_B))


def halves_of(own, c_ref, keep_ref, got_ref, near_ref, far_ref):
    y, z = c_ref[1], c_ref[3]
    for k in range(4):
        line = lax.rem(z + k, 4)
        yield line, y, lambda *at, line=line: near_ref[(line,) + at]
        if k == 0:
            yield line, 1 - y, lambda *at: jnp.where(
                c_ref[0] == own, keep_ref[(1 - y,) + at], got_ref[(1 - y,) + at]
            )
        else:
            yield line, 1 - y, lambda *at, k=k: far_ref[(k - 1,) + at]


def lines_a_kernel(own, c_ref, keep_ref, got_ref, near_ref, far_ref, wi_ref, mine_ref, give_ref):
    unpack_a_from(c_ref, halves_of(own, c_ref, keep_ref, got_ref, near_ref, far_ref), wi_ref, mine_ref, give_ref)


def whole_a_kernel(c_ref, all_ref, wi_ref, mine_ref, give_ref):
    parts = [(k // 2, k % 2, lambda *at, k=k: all_ref[(k,) + at]) for k in range(8)]
    unpack_a_from(c_ref, parts, wi_ref, mine_ref, give_ref)


def lines_b_kernel(own, c_ref, keep_ref, got_ref, near_ref, far_ref, wgu_ref, wd_ref):
    unpack_b_from(halves_of(own, c_ref, keep_ref, got_ref, near_ref, far_ref), wgu_ref, wd_ref)


def split_halves(c_ref, y, line, refs, width, value, folds):
    def put(ref, index):
        ref[index + (slice(None), slice(0, width))] = value
        folded(ref, index, width, folds)

    if len(refs) == 1:
        put(refs[0], (line, y))
        return
    far = refs[1 + line // 2] if len(refs) == 3 else refs[1]

    @pl.when(c_ref[1] == y)
    def _():
        put(refs[0], (line,))

    @pl.when(c_ref[1] != y)
    def _():
        put(far, (line % 2,) if len(refs) == 3 else (line,))


def grads_b_kernel(c_ref, h_ref, gug_ref, hid_ref, cot_ref, *refs):
    for line in range(4):
        down = mm(hid_ref[:, 128 * line : 128 * (line + 1)], cot_ref[...], TN).astype(bf16)
        for y in range(2):
            at = 256 * line + 128 * y
            grad = mm(h_ref[:, at : at + 128], gug_ref[...], TN).astype(bf16)
            split_halves(c_ref, y, line, refs, 2 * RF, grad, down[64 * y : 64 * (y + 1), :])


def grads_a_kernel(c_ref, h_ref, projg_ref, mine_ref, got_ref, *refs):
    for line in range(4):
        for y in range(2):
            at = 256 * line + 128 * y
            grad = mm(h_ref[:, at : at + 128], projg_ref[...], TN).astype(bf16)
            rows = slice(128 * (line % 2) + 64 * y, 128 * (line % 2) + 64 * y + 64)
            out = jnp.where(c_ref[0] == line // 2, mine_ref[rows, :], got_ref[rows, :])
            split_halves(c_ref, y, line, refs, INC, grad, out)


def final_b_kernel(c_ref, p0, p1, p2, p3, near, far, gu_ref, dn_ref):
    @pl.when(c_ref[0] == 0)
    def _():
        final_b_of(c_ref, [p0, p1, p2, p3], gu_ref, dn_ref)

    @pl.when(c_ref[0] == 1)
    def _():
        final_b_of(c_ref, [near.at[0], far.at[0], near.at[1], far.at[1]], gu_ref, dn_ref)


def final_b_of(c_ref, refs, gu_ref, dn_ref):
    for i, ref in enumerate(refs):
        y, x = lax.rem(c_ref[1] + i // 2, 2), lax.rem(c_ref[2] + i, 2)
        rows = pl.ds(aligned(128 * y, 128), 128)
        for t in range(2):
            for h in range(8):
                at = aligned(RF * h + 256 * t + 128 * x, 128)
                gu_ref[rows, pl.ds(at, 128)] = ref[t, :, 128 * h : 128 * (h + 1)].astype(f32)
            down = pl.ds(aligned(256 * t + 128 * x + 64 * y, 64), 64)
            dn_ref[down, :WIDE] = ref[t, :64, 2 * RF : GROUP_B].astype(f32)
            dn_ref[down, WIDE:] = ref[t, 64:, 2 * RF : GROUP_B].astype(f32)


def final_a_kernel(c_ref, p0, p1, p2, p3, q0, q1, q2, q3, mi_ref, ai_ref, mo_ref, ao_ref):
    @pl.when(c_ref[0] == 0)
    def _():
        final_a_of(c_ref, p0, p1, p2, p3, mi_ref, ai_ref, mo_ref, ao_ref)

    @pl.when(c_ref[0] == 1)
    def _():
        final_a_of(c_ref, q0, q1, q2, q3, mi_ref, ai_ref, mo_ref, ao_ref)


def final_a_of(c_ref, p0, p1, p2, p3, mi_ref, ai_ref, mo_ref, ao_ref):
    half = RD // 2
    for i in range(2):
        y = lax.rem(c_ref[1] + i, 2)
        rows = pl.ds(aligned(128 * y, 128), 128)
        shared = jnp.zeros((128, 2 * NS), f32)
        steps = jnp.zeros((MH, 128), f32)
        keys = jnp.zeros((128, 2 * KVD), f32)
        for t in range(2):
            query = jnp.zeros((128, 2 * RQ), f32)
            for k in range(2):
                ref = (p0, p1, p2, p3)[2 * i + k]
                x = lax.rem(c_ref[2] + k, 2)
                for h in range(2):
                    part = ref[t, :, RD * h : RD * (h + 1)].astype(f32).T
                    for j in range(2):
                        at = aligned(DS * h + 2 * RD * t + RD * j + half * x, 64)
                        mi_ref[pl.ds(at, half), rows] = part[half * j : half * (j + 1), :]
                shared = shared + ref[t, :, 2 * RD : RAW_AT].astype(f32)
                steps = steps + mm(chosen((MH, 128), steps_from(x, t)), ref[t, :, RAW_AT:Q_AT], NT)
                query = query + mm(ref[t, :, Q_AT:K_AT], chosen((2 * RQ, RQ), heads_from(x, HD)), NT)
                keys = keys + mm(ref[t, :, K_AT:INC], chosen((2 * KVD, 2 * HD), keys_from(t)), NT)
                left, right = ref[t, :64, INC:].astype(f32), ref[t, 64:, INC:].astype(f32)

                def put(out_ref, at, left=left, right=right):
                    out_ref[pl.ds(aligned(at, 64), 64), :WIDE] = left
                    out_ref[pl.ds(aligned(at, 64), 64), WIDE:] = right

                @pl.when(y == 0)
                def _(put=put, x=x, t=t):
                    put(mo_ref, half * x + 64 * t)

                @pl.when(y == 1)
                def _(put=put, x=x, t=t):
                    if t == 0:
                        put(mo_ref, half * x + 128)
                    else:
                        put(ao_ref, 64 * x)

            ai_ref[rows, 2 * RQ * t : 2 * RQ * (t + 1)] = query
        mi_ref[2 * DS : 2 * DS + 2 * NS, rows] = shared.T
        mi_ref[DS + CONVD :, rows] = steps
        ai_ref[rows, QD:] = keys


def on_chip(kernel, c, inputs, outs, scratch=(), micros=2):
    inside = pl.BlockSpec(memory_space=pltpu.VMEM)
    return pl.pallas_call(
        kernel,
        in_specs=[pl.BlockSpec(memory_space=pltpu.SMEM)] + [inside] * len(inputs),
        out_specs=[inside] * len(outs),
        out_shape=[jax.ShapeDtypeStruct(*o) for o in outs],
        scratch_shapes=[pltpu.VMEM(*s) for s in scratch],
        compiler_params=pltpu.CompilerParams(vmem_limit_bytes=LIMIT),
        cost_estimate=pl.CostEstimate(flops=micros * 10**9, bytes_accessed=micros * 3 * 10**6, transcendentals=0),
    )(c, *inputs)


def small_parameters(one, per_head, c, x):
    quarter = CONVD // 4
    cut = lax.dynamic_slice_in_dim

    def heads(values, width):
        parts = cut(values, c * 12 * width, 12 * width, values.ndim - 1)
        parts = [cut(parts, (6 * j + 3 * x) * width, 3 * width, values.ndim - 1) for j in range(2)]
        return jnp.concatenate(parts, axis=-1)

    conv = one[:, : 5 * quarter].reshape(4, 5, quarter).transpose(1, 0, 2).reshape(5, CONVD)
    conv = jnp.concatenate([heads(conv[:, :DS], MP), conv[:, DS:]], axis=1)
    at = 5 * quarter
    gains = one[:, at : at + 512].reshape(4, 2, 256).transpose(1, 0, 2).reshape(2, D)
    per_head = heads(per_head, 1)
    skip = jnp.pad(jnp.repeat(per_head[2], MP), (0, CONVR - RD))
    conv = jnp.pad(jnp.concatenate([conv, skip[None]], axis=0), ((0, 2), (0, 0)))
    per_head = jnp.pad(jnp.stack([per_head[0], jnp.exp(per_head[1])]), ((0, 6), (0, 128 - RH)))
    return gains[0:1], gains[1:2], conv, per_head


def small_gradients(conv_grad, head_grad, first_grad, second_grad, c, x, counted):
    def heads(values, width):
        out = jnp.zeros(values.shape[:-1] + (MH * width,), f32)
        for j in range(2):
            part = values[..., 3 * width * j : 3 * width * (j + 1)]
            out = lax.dynamic_update_slice_in_dim(out, part, (12 * c + 6 * j + 3 * x) * width, values.ndim - 1)
        return out

    first = ((c == 0) & (x == 0)).astype(f32)
    wide = jnp.concatenate([heads(conv_grad[:5, :RD], MP), conv_grad[:5, RD:]], axis=1)
    skip = conv_grad[5, :RD].reshape(RH, MP).sum(axis=1)
    per_head = heads(jnp.stack([head_grad[0, :RH], head_grad[1, :RH], skip]), 1)
    flat = jnp.concatenate(
        [wide.reshape(-1), first_grad[0] * counted.astype(f32), second_grad[0] * first, per_head.reshape(-1)]
    )
    return jnp.pad(flat, (0, 88 * 128 - flat.shape[0])).reshape(88, 128)


def summed_small(grads, c, wait, last):
    total = after(jnp.stack(grads), wait)
    total = total + paired_lines(total, 1)
    total = total + paired_lines(total, 2)
    first, second = total[0], total[1]
    total = jnp.where(c == 0, first, second) + swapped(jnp.where(c == 0, second, first), CORE)
    total = total + swapped(after(total, last), COL)
    return total + swapped(total, ROW)


def paired(
    block_input,
    output_grad,
    doc_lengths,
    first_gain,
    mixer_in,
    conv_kernel,
    conv_bias,
    step_bias,
    decay_log,
    skip_gain,
    mixer_out,
    attention_in,
    attention_out,
    second_gain,
    gate_up,
    down_weight,
):
    c, y, x, z = (lax.axis_index(a) for a in AXES)
    at = jnp.stack([c, y, x, z]).astype(jnp.int32)
    cut = lax.dynamic_slice_in_dim
    quarter = CONVD // 4

    free = jnp.concatenate([conv_kernel[0].reshape(-1), conv_bias[0], first_gain[0], second_gain[0]])
    free = jnp.pad(free, (0, FREE * 128 - free.shape[0])).reshape(FREE, 128).T
    free = jnp.pad(free, ((0, 0), (8, 120 - FREE)))

    keep_a, give_a = on_chip(
        prepare_a_kernel,
        at,
        (mixer_in[0].T, attention_in[0], mixer_out[0], attention_out[0], free),
        [((2, 128, GROUP_A), bf16)] * 2,
    )
    got_a = swapped(give_a, CORE)

    def halves(keep, got, s):
        return jnp.where(c == s, lax.dynamic_index_in_dim(keep, y, 0, False), lax.dynamic_index_in_dim(got, y, 0, False))

    half_a0 = halves(keep_a, got_a, 0)
    lines_a0 = lax.all_gather(half_a0, LINE)
    keep_b, give_b = on_chip(
        prepare_b_kernel, after(at, half_a0), (gate_up[0], down_weight[0]), [((2, 128, GROUP_B), bf16)] * 2
    )
    got_b = swapped(give_b, CORE)
    rows_in = jnp.concatenate([block_input[:, 0], output_grad[:, 0]], axis=2)
    rows_in = after(rows_in, half_a0)
    whole = whole_rows(rows_in, y, x)
    x0, cot = whole[:, :D], whole[:, D:]
    per_head = jnp.stack([step_bias[0], decay_log[0], skip_gain[0]])
    per_head = ordered(c, per_head, swapped(after(per_head, half_a0), CORE))

    def small_of(piece):
        return jnp.swapaxes(piece[..., RAW_AT + 8 : RAW_AT + 8 + FREE], -1, -2).astype(f32)

    smalls = [small_parameters(small_of(lines_a0).reshape(4, -1), per_head[0], c, x)]
    doc_sizes = lax.dynamic_index_in_dim(doc_lengths[:, 0], y, 0, False)
    length = x0.shape[0]
    positions = jnp.arange(length, dtype=jnp.int32)
    ids = doc_layout(doc_sizes, positions)[0]
    taps = [(positions >= by) & (jnp.roll(ids, by) == ids) for by in range(1, CONV)]
    tok = jnp.pad(jnp.stack([ids.astype(f32)] + [t.astype(f32) for t in taps], axis=1), ((0, 0), (0, 128 - CONV)))
    idr = jnp.broadcast_to(ids.astype(f32)[None], (8, length))
    half = length // 2
    partial = [((half, D), bf16), ((half, D), bf16)]

    def others(lines):
        return jnp.stack([lax.dynamic_index_in_dim(lines, (z + k) % 4, 0, False) for k in (1, 2, 3)])

    def unpack_a(s, near, far):
        wi, mine, give = on_chip(
            functools.partial(lines_a_kernel, s),
            at,
            (keep_a, got_a, near[:, :, :GROUP_A], far),
            [((D, INC), bf16), ((256, D), bf16), ((256, D), bf16)],
        )
        return wi, mine, swapped(give, CORE)

    def unpack_b(s, near, far):
        return on_chip(
            functools.partial(lines_b_kernel, s),
            at,
            (keep_b, got_b, near[:, :, -GROUP_B:], far),
            [((D, 2 * RF), bf16), ((RF, D), bf16)],
        )

    def first_part(entry, own, other, s, wi, mine, got):
        gain, _, conv, per_head = smalls[s]
        return on_chip(
            first_kernel,
            at,
            (entry, own, other, gain, wi, mine, got, conv, per_head, tok, idr),
            partial
            + [
                ((length, D), bf16),
                ((length, INC), bf16),
                ((length, RD), f32),
                ((length, OUTR), bf16),
                ((length, D), bf16),
                ((OUTR, D), bf16),
            ],
            [
                ((length, RD), f32),
                ((length, 2 * NS), bf16),
                ((length, RD), bf16),
                ((length, 128), f32),
                ((128, length), f32),
            ],
            15,
        )

    def second_part(entry, own, other, s, wgu, wd):
        return on_chip(
            second_kernel,
            at,
            (entry, own, other, smalls[s][1], wgu, wd),
            partial
            + [((length, D), f32), ((length, D), bf16), ((length, 2 * RF), f32), ((length, RF), bf16)],
            micros=8,
        )

    half_b0 = halves(keep_b, got_b, 0)
    lines_b0 = lax.all_gather(after(half_b0, lines_a0), LINE)
    far_a0 = swapped(after(others(lines_a0), whole, tok, idr, per_head), ROW)
    half_a1 = after(halves(keep_a, got_a, 1), lines_b0, far_a0)
    lines_a1 = lax.all_gather(half_a1, (LINE, ROW))
    x0 = after(x0, half_a1)
    wi0, mine, got = unpack_a(0, lines_a0, far_a0)
    far_b0 = swapped(others(lines_b0), ROW)
    keep, give, x0, proj0, state0, ga0, h0, wo0 = first_part(x0, smalls[0][0], smalls[0][0], 0, wi0, mine, got)
    give = after(give, far_b0)
    own, other = quarter_sum(keep, give)
    wgu0, wd0 = unpack_b(0, lines_b0, far_b0)
    keep, give, mid0, g0, gu0, hid0 = second_part(x0, own, other, 0, wgu0, wd0)
    lines_b1 = lax.all_gather(after(halves(keep_b, got_b, 1), lines_a1, keep), LINE)
    smalls.append(small_parameters(small_of(after(lines_a1, mid0)[::2]).reshape(4, -1), per_head[1], c, x))
    own, other = quarter_sum(keep, give)
    wi1, mine, give_out = on_chip(
        whole_a_kernel, at, (lines_a1,), [((D, INC), bf16), ((256, D), bf16), ((256, D), bf16)]
    )
    got = swapped(give_out, CORE)
    keep, give, x1, proj1, state1, ga1, h1, wo1 = first_part(mid0, own, other, 1, wi1, mine, got)
    far_b1 = swapped(others(lines_b1), ROW)
    own, other = quarter_sum(keep, give)
    wgu1, wd1 = unpack_b(1, lines_b1, far_b1)
    late_keep, late_give, mid1, g1, gu1, hid1 = second_part(x1, own, other, 1, wgu1, wd1)

    def back_second(cot, s, gu, wgu, wd):
        return on_chip(
            back_second_kernel, at, (cot, gu, wgu, wd), partial + [((length, 2 * RF), bf16)], micros=7
        )

    def back_first(cot, own, other, s, mid, proj, state, ga, wi, wo):
        gain, conv, per_head = smalls[s][1:]
        return on_chip(
            back_first_kernel,
            at,
            (cot, own, other, mid, gain, proj, state, ga, wi, wo, conv, per_head, tok, idr),
            partial
            + [
                ((256, D), bf16),
                ((256, D), bf16),
                ((length, D), f32),
                ((length, INC), bf16),
                ((1, D), f32),
                ((8, CONVR), f32),
                ((8, 128), f32),
            ],
            [
                ((length, D), bf16),
                ((length, OUTR), f32),
                ((length, RD), f32),
                ((length, 2 * NS), bf16),
                ((length, RD), bf16),
                ((length, 128), f32),
                ((128, length), f32),
                ((length, RD), bf16),
                ((length, RD), f32),
                ((length, 2 * NS), f32),
                ((length, 2 * HD), f32),
                ((length, RD), f32),
            ],
            25,
        )

    def back_input(s, entry, own, other, mid_grad):
        return on_chip(
            back_input_kernel,
            at,
            (entry, own, other, smalls[s][0], mid_grad),
            [((length, D), bf16), ((1, D), f32)],
            micros=4,
        )

    def shapes(split, columns):
        if not split:
            return [((4, 2, 128, columns), bf16)]
        return [((4, 128, columns), bf16)] + [((4 // split, 128, columns), bf16)] * split

    def grads_b(split, *inputs):
        return on_chip(grads_b_kernel, at, inputs, shapes(split, GROUP_B), micros=5)

    def grads_a(split, h, proj_grad, mine, give):
        inputs = (h, proj_grad, mine, swapped(give, CORE))
        return on_chip(grads_a_kernel, at, inputs, shapes(split, GROUP_A), micros=5)

    def added(grads, *got):
        got = jnp.concatenate(got, axis=0) if len(got) > 1 else got[0]
        return (grads[0].astype(f32) + got.astype(f32)).astype(bf16)

    def lines_first(grads):
        columns = grads[0].shape[3]
        sums = scattered(grads[0].reshape(4, 256, columns)).reshape(2, 128, columns)
        mine = lax.dynamic_index_in_dim(sums, y, 0, False)
        theirs = lax.dynamic_index_in_dim(sums, 1 - y, 0, False)
        return (mine.astype(f32) + swapped(theirs, ROW).astype(f32)).astype(bf16)

    def scattered(lines):
        return lax.psum_scatter(lines, LINE, scatter_dimension=0)

    def both_ranks(first, second):
        return ordered(c, jnp.where(c == 0, first, second), swapped(jnp.where(c == 0, second, first), CORE))

    def spread_rows(piece, s):
        given = sent(piece, [(p, (s,) + p[1:]) for p in every if p[0] != s])
        block = jnp.stack([piece, given] if s == 0 else [given, piece])
        return jnp.stack([block, sent(block, [(p, (s, 1 - p[1], p[2], p[3])) for p in every if p[0] == s])])

    def spread_one(piece, s):
        given = sent(piece, [(p, (s,) + p[1:]) for p in every if p[0] != s])
        block = jnp.stack([piece, given] if s == 0 else [given, piece])
        mine = [p for p in every if p[0] == s]
        flips = [[(p, (s, p[1] ^ i, p[2] ^ k, p[3])) for p in mine] for i, k in ((0, 1), (1, 0), (1, 1))]
        return [block] + [sent(block, f) for f in flips]

    cot1 = cot
    keep, give, gu_grad = back_second(cot1, 1, gu1, wgu1, wd1)
    own, other = quarter_sum(keep, give)
    late_give = after(late_give, own)
    late, late_other = quarter_sum(late_keep, late_give)
    gb1 = grads_b(0, g1, gu_grad, hid1, cot1)
    own = after(own, gb1[0])
    sum_b1 = lines_first(gb1)
    keep, give, mine, give_out, mid_grad, proj_grad, second1, conv1, head1 = back_first(
        cot1, own, other, 1, mid1, proj1, state1, ga1, wi1, wo1
    )
    give = after(give, late)
    own, other = quarter_sum(keep, give)
    ga1_ = grads_a(0, h1, proj_grad, mine, give_out)
    own = after(own, ga1_[0], sum_b1, late_other)
    sum_a1 = lines_first(ga1_)
    cot0, first1 = back_input(1, x1, own, other, mid_grad)
    keep, give, gu_grad = back_second(cot0, 0, gu0, wgu0, wd0)
    own, other = quarter_sum(keep, give)
    gb0 = grads_b(1, g0, gu_grad, hid0, cot0)
    gb0_got = swapped(gb0[1], ROW)
    near_b1 = spread_rows(sum_b1, 1)
    own = after(own, gb0[0], near_b1)
    plane_b1 = near_b1, sent(near_b1, [(p, (1, p[1], 1 - p[2], p[3])) for p in every if p[0] == 1])
    keep, give, mine, give_out, mid_grad, proj_grad, second0, conv0, head0 = back_first(
        cot0, own, other, 0, mid0, proj0, state0, ga0, wi0, wo0
    )
    ga0_ = grads_a(2, h0, proj_grad, mine, give_out)
    ga0_got = [swapped(ga0_[1], ROW)]
    ga0_got.append(swapped(after(ga0_[2], ga0_got[0]), ROW))
    lines_gb0 = added(gb0, after(gb0_got, ga0_[0]))
    b0 = scattered(lines_gb0)
    own = half_sum(keep, after(give, ga0_[0]))
    low0, first0 = on_chip(
        back_half_kernel,
        at,
        (x0, own, smalls[0][0], mid_grad),
        [((half, D), bf16), ((1, D), f32)],
        micros=3,
    )
    block = both_ranks(jnp.pad(b0, ((0, 0), (0, GROUP_A - GROUP_B))), sum_a1)
    lines_ga0 = added(ga0_, ga0_got[0], after(ga0_got[1], first0, block, plane_b1[1]))
    a0 = scattered(lines_ga0)
    block = after(block, lines_ga0)
    plane_two = block, swapped(block, COL), swapped(block, ROW), across(block)
    gate_up_grad, down_grad = on_chip(
        final_b_kernel, at, (*plane_two, *plane_b1), [((256, 2 * FF), f32), ((RF, D), f32)], micros=4
    )
    plane_a0 = spread_one(after(a0, *plane_two), 0)
    mixer_in_grad, attention_in_grad, mixer_out_grad, attention_out_grad = on_chip(
        final_a_kernel,
        at,
        (*plane_a0, *plane_two),
        [((DS + CONVD + MH, 256), f32), ((256, QD + 2 * KVD), f32), ((RD, D), f32), ((128, D), f32)],
        micros=40,
    )

    out1 = (mid1 + ordered(c, late, late_other).reshape(length, D).astype(f32)).astype(bf16)
    section_output = back_rows(jnp.where(c == 0, x1, out1), y, x)
    part = lax.dynamic_slice_in_dim(low0, x * (half // 2), half // 2, 0)
    part = after(part, plane_a0[0])
    moved = [sent(part, [(p, (0, p[0], p[2], p[3])) for p in every if p[1] == m]) for m in range(2)]
    input_grad = jnp.where(c == 0, jnp.stack(moved), back_rows(cot0, y, x))
    grads = [
        small_gradients(conv0, head0, first0, second0, c, x, x == 0),
        small_gradients(conv1, head1, first1, second1, c, x, (c == 0) & (x == 0)),
    ]
    sums = summed_small(grads, c, first0, plane_a0[0]).reshape(-1)
    wide = sums[: 5 * CONVD].reshape(5, CONVD)
    start = 5 * CONVD
    conv_out = cut(wide, z * quarter, quarter, 1)
    first_out = cut(sums[start : start + D], z * 256, 256, 0)
    second_out = cut(sums[start + D : start + 2 * D], z * 256, 256, 0)
    head_out = sums[start + 2 * D : start + 2 * D + 3 * MH].reshape(3, MH)
    return (
        section_output[None, :, None],
        input_grad[None, :, None],
        first_out[None],
        mixer_in_grad.T[None],
        conv_out[None, :4],
        conv_out[None, 4],
        head_out[None, 0],
        head_out[None, 1],
        head_out[None, 2],
        mixer_out_grad[None],
        attention_in_grad[None],
        attention_out_grad[None],
        second_out[None],
        gate_up_grad[None],
        down_grad[None],
    )


def paired_specs():
    plane = (ROW, COL)
    rows = P(CORE, LINE, None)
    placed = (
        P(None, LINE, plane, None),
        P(None, LINE, plane, None),
        P(None, LINE, None),
        P(CORE, LINE),
        rows,
        P(CORE, None, LINE),
        P(CORE, LINE),
        P(CORE, None),
        P(CORE, None),
        P(CORE, None),
        rows,
        rows,
        rows,
        P(CORE, LINE),
        rows,
        rows,
    )
    given = (
        P(CORE, None, LINE, plane, None),
        P(CORE, None, LINE, plane, None),
        P(CORE, LINE),
        rows,
        P(CORE, None, LINE),
        P(CORE, LINE),
        P(CORE, None),
        P(CORE, None),
        P(CORE, None),
        rows,
        rows,
        rows,
        P(CORE, LINE),
        rows,
        rows,
    )
    return placed, given


def solution(mesh):
    if tuple(mesh.devices.shape) == (2, 4, 4):
        fine = Mesh(mesh.devices.reshape(2, 2, 2, 4), AXES)
        placed, given = paired_specs()
        return jax.shard_map(paired, mesh=fine, in_specs=placed, out_specs=given, check_vma=False)
    return spread(mesh)
```
